32 devices in a mesh: fsdp: 4 (over z), ctx: 8 (over y, x, core).
Axes of the slice: x: 2, y: 2, z: 4, core: 2. Of those that a mesh axis runs over, the one named last changes fastest.
Arguments:
- inputs: bfloat16 [24, 1024, 768], P('fsdp', 'ctx'), may hold values from -6 to 6
- cotangent: float32 [24, 1024, 768], P('fsdp', 'ctx'), may hold values from -6 to 6
- ln1_gain: bfloat16 [768], P(('fsdp', 'ctx')), may hold values from 0.5 to 1.5
- ln1_bias: bfloat16 [768], P(('fsdp', 'ctx')), may hold values from -1.25 to 1.25
- ln2_gain: bfloat16 [768], P(('fsdp', 'ctx')), may hold values from 0.5 to 1.5
- ln2_bias: bfloat16 [768], P(('fsdp', 'ctx')), may hold values from -1.25 to 1.25
- w_qkv: bfloat16 [768, 2304], P(('fsdp', 'ctx')), as said below
- b_qkv: bfloat16 [2304], P(('fsdp', 'ctx')), may hold values from -1.75 to 1.75
- w_out: bfloat16 [768, 768], P(('fsdp', 'ctx')), may hold values from -2.5 to 2.5
- b_out: bfloat16 [768], P(('fsdp', 'ctx')), may hold values from -1.75 to 1.75
- w_in: bfloat16 [768, 3072], P(('fsdp', 'ctx')), may hold values from -0.21875 to 0.21875
- b_in: bfloat16 [3072], P(('fsdp', 'ctx')), may hold values from -1.75 to 1.75
- w_mlp_out: bfloat16 [3072, 768], P(('fsdp', 'ctx')), may hold values from -0.109375 to 0.109375
- b_mlp_out: bfloat16 [768], P(('fsdp', 'ctx')), may hold values from -1.75 to 1.75
Outputs:
- outputs: float32 [24, 1024, 768], P('fsdp', 'ctx')
- grad_inputs: float32 [24, 1024, 768], P('fsdp', 'ctx')
- grad_ln1_gain: float32 [768], P(('fsdp', 'ctx'))
- grad_ln1_bias: float32 [768], P(('fsdp', 'ctx'))
- grad_ln2_gain: float32 [768], P(('fsdp', 'ctx'))
- grad_ln2_bias: float32 [768], P(('fsdp', 'ctx'))
- grad_w_qkv: float32 [768, 2304], P(('fsdp', 'ctx'))
- grad_b_qkv: float32 [2304], P(('fsdp', 'ctx'))
- grad_w_out: float32 [768, 768], P(('fsdp', 'ctx'))
- grad_b_out: float32 [768], P(('fsdp', 'ctx'))
- grad_w_in: float32 [768, 3072], P(('fsdp', 'ctx'))
- grad_b_in: float32 [3072], P(('fsdp', 'ctx'))
- grad_w_mlp_out: float32 [3072, 768], P(('fsdp', 'ctx'))
- grad_b_mlp_out: float32 [768], P(('fsdp', 'ctx'))
The draws below stay inside these ranges and needn't reach their ends.
Inputs may be any that keep to these rules, and one draw needn't show every extreme that they name: `w_qkv`: a weight matrix whose entries lie within 24 / sqrt(768) of zero.
All inputs are finite; a program needn't handle non-finite values.
Results may differ from the reference program's by a relative error of at most 0.012.
Values may be sent and summed in bfloat16 or wider, within the bound.
No kernel may reach another device: no remote copies, remote signals or barrier semaphores. Data moves between devices by JAX's collectives and lax.ppermute only.
A program may use at most 448 MiB of HBM per device.

```python
import jax
import jax.numpy as jnp
from jax import lax

D = 768
HEADS = 12
HEAD_DIM = 64
ROT_DIM = 16
FF = 3072
SEQ_LEN = 1024
SEQS = 24


def draw_w_qkv(key, part):
    matrix = jnp.clip(jax.random.normal(key, (D, 3 * D), jnp.float32), -4.0, 4.0) * D ** (-0.5)
    return matrix.astype(jnp.bfloat16)


def steps_of(key, shape, pieces, low, largest):
    def one(axis_at, parts):
        steps = jax.random.uniform(jax.random.fold_in(jax.random.fold_in(key, 6), axis_at), (parts,), jnp.float32, low / len(pieces), largest / len(pieces))
        return jnp.repeat(jnp.exp(steps), shape[axis_at] // parts).reshape((-1,) + (1,) * (len(shape) - axis_at - 1))

    factor_of = one(*pieces[0])
    for cut in pieces[1:]:
        factor_of = factor_of * one(*cut)
    return factor_of


def scatter_about(stream_key, extent, scale, limit, cuts=(), kind=jnp.bfloat16):
    result = jax.random.normal(stream_key, extent, jnp.float32) * scale
    if len(cuts) > 0:
        result = steps_of(stream_key, extent, cuts, -0.22, 0.18) * result
    return jnp.clip(result, min=-limit, max=limit).astype(kind)


def setup_inputs(seed: int = 0) -> dict:
    splits = jax.random.split(jax.random.key(seed), 15)
    inputs = scatter_about(splits[0], (SEQS, SEQ_LEN, D), 1.0, 6.0, ((0, 4), (1, 8)))
    cotangent = scatter_about(splits[1], (SEQS, SEQ_LEN, D), 1.0, 6.0, ((0, 4), (1, 8)), jnp.float32)
    ln1_gain = jnp.clip(1.0 + 0.1 * jax.random.normal(splits[2], (D,), jnp.float32), 0.5, 1.5).astype(jnp.bfloat16)
    ln1_bias = scatter_about(splits[3], (D,), 0.2, 1.25, ((0, 32),))
    ln2_gain = jnp.clip(1.0 + 0.1 * jax.random.normal(splits[4], (D,), jnp.float32), 0.5, 1.5).astype(jnp.bfloat16)
    ln2_bias = scatter_about(splits[5], (D,), 0.2, 1.25, ((0, 32),))
    w_qkv = draw_w_qkv(jax.random.fold_in(splits[14], 71), 0)
    b_qkv = scatter_about(splits[7], (3 * D,), 0.3, 1.75, ((0, 32),))
    w_out = scatter_about(splits[8], (D, D), (max(1, 8 * D // SEQ_LEN)) ** -0.5, 2.5, ((0, 32),))
    b_out = scatter_about(splits[9], (D,), 0.3, 1.75, ((0, 32),))
    w_in = scatter_about(splits[10], (D, FF), D ** -0.5, 0.21875, ((0, 32),))
    b_in = scatter_about(splits[11], (FF,), 0.3, 1.75, ((0, 32),))
    w_mlp_out = scatter_about(splits[12], (FF, D), FF ** -0.5, 0.109375, ((0, 32),))
    b_mlp_out = scatter_about(splits[13], (D,), 0.3, 1.75, ((0, 32),))
    return {"inputs": inputs, "cotangent": cotangent, "ln1_gain": ln1_gain, "ln1_bias": ln1_bias, "ln2_gain": ln2_gain, "ln2_bias": ln2_bias, "w_qkv": w_qkv, "b_qkv": b_qkv, "w_out": w_out, "b_out": b_out, "w_in": w_in, "b_in": b_in, "w_mlp_out": w_mlp_out, "b_mlp_out": b_mlp_out}


EPS = 1e-05
BASE_FREQ = 10000.0

def rounded(value):
    return lax.optimization_barrier(value.astype(jnp.bfloat16)).astype(jnp.float32)

def layer_norm(values, gain_row, shift_row):
    centre = lax.optimization_barrier(jnp.mean(values, axis=-1, keepdims=True))
    centred = values - centre
    inverse = lax.rsqrt(lax.optimization_barrier(jnp.mean(centred * centred, axis=-1, keepdims=True)) + EPS)
    normed = centred * inverse
    return (normed * gain_row + shift_row, normed, inverse)

def norm_back(grad_out, normed, inverse, gain_row):
    scaled = grad_out * gain_row
    return inverse * (scaled - lax.optimization_barrier(jnp.mean(scaled, axis=-1, keepdims=True)) - normed * lax.optimization_barrier(jnp.mean(scaled * normed, axis=-1, keepdims=True)))

def angles(positions):
    half_rot = ROT_DIM // 2
    inv_freq = BASE_FREQ ** (-(2.0 * jnp.arange(half_rot, dtype=jnp.float32)) / ROT_DIM)
    phase_angle = positions.astype(jnp.float32)[:, None] * inv_freq[None, :]
    return (jnp.cos(phase_angle), jnp.sin(phase_angle))

def rotate(head_field, cosine, sine_rot, direction):
    half_rot = ROT_DIM // 2
    lead_half = head_field[..., :half_rot]
    trail_half = head_field[..., half_rot:ROT_DIM]
    cos_wide = cosine[:, None, :]
    sin_wide = direction * sine_rot[:, None, :]
    return jnp.concatenate([lead_half * cos_wide - trail_half * sin_wide, trail_half * cos_wide + lead_half * sin_wide, head_field[..., ROT_DIM:]], axis=-1)

def gelu_parts(pre_act):
    normal_cdf = 0.5 * (1.0 + jax.scipy.special.erf(pre_act * 0.7071067811865476))
    density = jnp.exp(-0.5 * pre_act * pre_act) * 0.3989422804014327
    return (pre_act * normal_cdf, normal_cdf + pre_act * density)

def reference(inputs, cotangent, ln1_gain, ln1_bias, ln2_gain, ln2_bias, w_qkv, b_qkv, w_out, b_out, w_in, b_in, w_mlp_out, b_mlp_out):
    f32 = jnp.float32
    bf16 = jnp.bfloat16
    score_scale = HEAD_DIM ** (-0.5)
    gain_one = ln1_gain.astype(f32)
    shift_one = ln1_bias.astype(f32)
    gain_two = ln2_gain.astype(f32)
    shift_two = ln2_bias.astype(f32)
    positions = jnp.arange(SEQ_LEN, dtype=jnp.int32)
    cosine, sine_rot = angles(positions)
    causal = positions[None, :] <= positions[:, None]

    def one_sequence(weight_sums, seq_pair):
        seq_rows, cot_rows = seq_pair
        residual = seq_rows.astype(f32)
        normal_one, normed_one, inverse_one = layer_norm(residual, gain_one, shift_one)
        normal_two, normed_two, inverse_two = layer_norm(residual, gain_two, shift_two)
        hidden_one = normal_one.astype(bf16)
        hidden_two = normal_two.astype(bf16)
        project = jnp.dot(hidden_one, w_qkv, preferred_element_type=f32) + b_qkv.astype(f32)
        query_low = rounded(rotate(project[:, :D].reshape(SEQ_LEN, HEADS, HEAD_DIM), cosine, sine_rot, 1.0))
        key_low = rounded(rotate(project[:, D:2 * D].reshape(SEQ_LEN, HEADS, HEAD_DIM), cosine, sine_rot, 1.0))
        value_low = rounded(project[:, 2 * D:].reshape(SEQ_LEN, HEADS, HEAD_DIM))
        scores = jnp.einsum('qhd,khd->hqk', query_low, key_low) * score_scale
        scores = jnp.where(causal[None], scores, -jnp.inf)
        run_max = lax.optimization_barrier(jnp.max(scores, axis=-1))
        exp_scores = jnp.exp(scores - run_max[..., None])
        run_sum = lax.optimization_barrier(jnp.sum(exp_scores, axis=-1))
        log_total = run_max + jnp.log(run_sum)
        prob_low = rounded(exp_scores / run_sum[..., None])
        attended = jnp.einsum('hqk,khd->qhd', prob_low, value_low).astype(bf16)
        att_flat = attended.reshape(SEQ_LEN, D)
        pre_act = jnp.dot(hidden_two, w_in, preferred_element_type=f32) + b_in.astype(f32)
        activation_f, gelu_slope = gelu_parts(pre_act)
        activation = activation_f.astype(bf16)
        output = residual + jnp.dot(att_flat, w_out, preferred_element_type=f32) + b_out.astype(f32) + jnp.dot(activation, w_mlp_out, preferred_element_type=f32) + b_mlp_out.astype(f32)
        cot_low = cot_rows.astype(bf16)
        cot_sum = lax.optimization_barrier(jnp.sum(cot_rows, axis=0))
        grad_w_out = jnp.dot(att_flat.T, cot_low, preferred_element_type=f32)
        grad_w_mlp = jnp.dot(activation.T, cot_low, preferred_element_type=f32)
        d_pre = jnp.dot(cot_low, w_mlp_out.T, preferred_element_type=f32) * gelu_slope
        d_pre_low = d_pre.astype(bf16)
        grad_w_in = jnp.dot(hidden_two.T, d_pre_low, preferred_element_type=f32)
        d_hidden_two = jnp.dot(d_pre_low, w_in.T, preferred_element_type=f32)
        grad_att = rounded(jnp.dot(cot_low, w_out.T, preferred_element_type=f32)).reshape(SEQ_LEN, HEADS, HEAD_DIM)
        row_delta = jnp.einsum('qhd,qhd->hq', grad_att, attended.astype(f32))
        prob_full = jnp.where(causal[None], jnp.exp(scores - log_total[..., None]), 0.0)
        grad_value = jnp.einsum('hqk,qhd->khd', rounded(prob_full), grad_att)
        grad_prob = jnp.einsum('qhd,khd->hqk', grad_att, value_low)
        grad_score = rounded(prob_full * (grad_prob - row_delta[..., None]) * score_scale)
        grad_query = jnp.einsum('hqk,khd->qhd', grad_score, key_low)
        grad_key = jnp.einsum('hqk,qhd->khd', grad_score, query_low)
        grad_query = rotate(grad_query, cosine, sine_rot, -1.0)
        grad_key = rotate(grad_key, cosine, sine_rot, -1.0)
        d_project = jnp.concatenate([grad_query.reshape(SEQ_LEN, D), grad_key.reshape(SEQ_LEN, D), grad_value.reshape(SEQ_LEN, D)], axis=-1)
        d_project_low = d_project.astype(bf16)
        grad_w_qkv = jnp.dot(hidden_one.T, d_project_low, preferred_element_type=f32)
        d_hidden_one = jnp.dot(d_project_low, w_qkv.T, preferred_element_type=f32)
        grad_rows = cot_rows + norm_back(d_hidden_one, normed_one, inverse_one, gain_one) + norm_back(d_hidden_two, normed_two, inverse_two, gain_two)
        terms = (lax.optimization_barrier(jnp.sum(d_hidden_one * normed_one, axis=0)), lax.optimization_barrier(jnp.sum(d_hidden_one, axis=0)), lax.optimization_barrier(jnp.sum(d_hidden_two * normed_two, axis=0)), lax.optimization_barrier(jnp.sum(d_hidden_two, axis=0)), grad_w_qkv, lax.optimization_barrier(jnp.sum(d_project, axis=0)), grad_w_out, cot_sum, grad_w_in, lax.optimization_barrier(jnp.sum(d_pre, axis=0)), grad_w_mlp, cot_sum)
        new_sums = jax.tree.map(lambda total, term: total + term, weight_sums, terms)
        return (new_sums, (output, grad_rows))
    zero_grads = (jnp.zeros((D,), f32), jnp.zeros((D,), f32), jnp.zeros((D,), f32), jnp.zeros((D,), f32), jnp.zeros((D, 3 * D), f32), jnp.zeros((3 * D,), f32), jnp.zeros((D, D), f32), jnp.zeros((D,), f32), jnp.zeros((D, FF), f32), jnp.zeros((FF,), f32), jnp.zeros((FF, D), f32), jnp.zeros((D,), f32))
    sums, (outputs, grad_inputs) = lax.scan(one_sequence, zero_grads, (inputs, cotangent))
    return (outputs, grad_inputs, sums[0], sums[1], sums[2], sums[3], sums[4], sums[5], sums[6], sums[7], sums[8], sums[9], sums[10], sums[11])
```

```python
import functools
import math

import jax
import jax.numpy as jnp
from jax import lax
from jax.experimental import pallas as pl
from jax.experimental.pallas import tpu as pltpu
from jax.sharding import PartitionSpec as P

HEADS = 12
HEAD_DIM = 64
ROT_DIM = 16
MICRO = 2
SEQ_MB = 3
CHUNKS = (1, 2)


EPS = 1e-05
BASE_FREQ = 10000.0


def layer_norm(values, gain_row, shift_row):
    centre = jnp.mean(values, axis=-1, keepdims=True)
    centred = values - centre
    inverse = lax.rsqrt(jnp.mean(centred * centred, axis=-1, keepdims=True) + EPS)
    normed = centred * inverse
    return (normed * gain_row + shift_row, normed, inverse)


def norm_back(grad_out, normed, inverse, gain_row):
    scaled = grad_out * gain_row
    return inverse * (
        scaled
        - jnp.mean(scaled, axis=-1, keepdims=True)
        - normed * jnp.mean(scaled * normed, axis=-1, keepdims=True)
    )


def angles(positions):
    half_rot = ROT_DIM // 2
    inv_freq = BASE_FREQ ** (-(2.0 * jnp.arange(half_rot, dtype=jnp.float32)) / ROT_DIM)
    phase_angle = positions.astype(jnp.float32)[:, None] * inv_freq[None, :]
    return (jnp.cos(phase_angle), jnp.sin(phase_angle))


def rotate(head_field, cosine, sine_rot, direction):
    half_rot = ROT_DIM // 2
    lead_half = head_field[..., :half_rot]
    trail_half = head_field[..., half_rot:ROT_DIM]
    cos_wide = cosine[:, None, :]
    sin_wide = direction * sine_rot[:, None, :]
    return jnp.concatenate(
        [
            lead_half * cos_wide - trail_half * sin_wide,
            trail_half * cos_wide + lead_half * sin_wide,
            head_field[..., ROT_DIM:],
        ],
        axis=-1,
    )


def gelu_parts(pre_act):
    normal_cdf = 0.5 * (1.0 + jax.scipy.special.erf(pre_act * 0.7071067811865476))
    density = jnp.exp(-0.5 * pre_act * pre_act) * 0.3989422804014327
    return (pre_act * normal_cdf, normal_cdf + pre_act * density)


def outer_rows(left, right):
    return lax.dot_general(
        left, right, (((0,), (0,)), ((), ())), preferred_element_type=jnp.float32
    )


def times_transpose(left, right):
    return lax.dot_general(
        left, right, (((1,), (1,)), ((), ())), preferred_element_type=jnp.float32
    )


def attend_block(soft_state, kv_block, first_row, query_low, positions, score_scale):
    run_max, run_sum, weighted = soft_state
    seq_count, block_rows, double_width = kv_block.shape
    model_width = double_width // 2
    key_low = kv_block[..., :model_width].reshape(seq_count, block_rows, HEADS, HEAD_DIM)
    value_low = kv_block[..., model_width:].reshape(seq_count, block_rows, HEADS, HEAD_DIM)
    scores = (
        jnp.einsum("sqhd,skhd->shqk", query_low, key_low, preferred_element_type=jnp.float32)
        * score_scale
    )
    allowed = (first_row + jnp.arange(block_rows, dtype=jnp.int32))[None, :] <= positions[:, None]
    scores = jnp.where(allowed, scores, -jnp.inf)
    new_max = jnp.maximum(run_max, jnp.max(scores, axis=-1))
    safe_max = jnp.where(new_max == -jnp.inf, 0.0, new_max)
    exp_scores = jnp.exp(scores - safe_max[..., None])
    factor = jnp.exp(run_max - safe_max)
    run_sum = run_sum * factor + jnp.sum(exp_scores, axis=-1)
    weighted = weighted * factor[..., None] + jnp.einsum(
        "shqk,skhd->shqd",
        exp_scores.astype(jnp.bfloat16),
        value_low,
        preferred_element_type=jnp.float32,
    )
    return (new_max, run_sum, weighted)


def attend_piece(soft_state, kv_piece, query_low, positions, score_scale):
    piece_rows = kv_piece.shape[1]
    step_rows = math.gcd(piece_rows, 512)

    def one_block(block_index, inner_state):
        offset = block_index * step_rows
        kv_block = lax.dynamic_slice_in_dim(kv_piece, offset, step_rows, 1)
        return attend_block(inner_state, kv_block, offset, query_low, positions, score_scale)

    return lax.fori_loop(0, piece_rows // step_rows, one_block, soft_state)


def local(
    inputs,
    cotangent,
    ln1_gain,
    ln1_bias,
    ln2_gain,
    ln2_bias,
    w_qkv,
    b_qkv,
    w_out,
    b_out,
    w_in,
    b_in,
    w_mlp_out,
    b_mlp_out,
):
    f32 = jnp.float32
    bf16 = jnp.bfloat16
    group_rows = inputs.shape[1]
    model_width = inputs.shape[2]
    seq_len = group_rows * lax.axis_size("ctx")
    key_block = math.gcd(seq_len, 512)
    score_scale = HEAD_DIM ** (-0.5)
    positions = lax.axis_index("ctx") * group_rows + jnp.arange(group_rows, dtype=jnp.int32)
    cosine, sine_rot = angles(positions)

    def gather_params():
        return (
            lax.all_gather(ln1_gain, ("fsdp", "ctx"), axis=0, tiled=True),
            lax.all_gather(ln1_bias, ("fsdp", "ctx"), axis=0, tiled=True),
            lax.all_gather(ln2_gain, ("fsdp", "ctx"), axis=0, tiled=True),
            lax.all_gather(ln2_bias, ("fsdp", "ctx"), axis=0, tiled=True),
            lax.all_gather(w_qkv, ("fsdp", "ctx"), axis=0, tiled=True),
            lax.all_gather(b_qkv, ("fsdp", "ctx"), axis=0, tiled=True),
            lax.all_gather(w_out, ("fsdp", "ctx"), axis=0, tiled=True),
            lax.all_gather(b_out, ("fsdp", "ctx"), axis=0, tiled=True),
            lax.all_gather(w_in, ("fsdp", "ctx"), axis=0, tiled=True),
            lax.all_gather(b_in, ("fsdp", "ctx"), axis=0, tiled=True),
            lax.all_gather(w_mlp_out, ("fsdp", "ctx"), axis=0, tiled=True),
            lax.all_gather(b_mlp_out, ("fsdp", "ctx"), axis=0, tiled=True),
        )

    weight_sums = None
    output_list = []
    grad_list = []
    for micro_index in range(MICRO):
        batch_rows = inputs[micro_index * SEQ_MB : (micro_index + 1) * SEQ_MB]
        cot_rows = cotangent[micro_index * SEQ_MB : (micro_index + 1) * SEQ_MB]
        seq_count = batch_rows.shape[0]
        flat_rows = seq_count * group_rows
        params_fwd = gather_params()
        (
            gain_one,
            shift_one,
            gain_two,
            shift_two,
            weight_qkv,
            bias_qkv,
            weight_out,
            bias_out,
            weight_in,
            bias_in,
            weight_mlp,
            bias_mlp,
        ) = params_fwd
        residual = batch_rows.reshape(flat_rows, model_width).astype(f32)
        normal_one, normed_one, inverse_one = layer_norm(
            residual, gain_one.astype(f32), shift_one.astype(f32)
        )
        normal_two, normed_two, inverse_two = layer_norm(
            residual, gain_two.astype(f32), shift_two.astype(f32)
        )
        hidden_one = normal_one.astype(bf16)
        hidden_two = normal_two.astype(bf16)
        project = jnp.dot(hidden_one, weight_qkv, preferred_element_type=f32) + bias_qkv.astype(f32)
        head_shape = (seq_count, group_rows, HEADS, HEAD_DIM)
        query_low = rotate(
            project[:, :model_width].reshape(head_shape), cosine, sine_rot, 1.0
        ).astype(bf16)
        key_low = rotate(
            project[:, model_width : 2 * model_width].reshape(head_shape), cosine, sine_rot, 1.0
        ).astype(bf16)
        value_low = project[:, 2 * model_width :].astype(bf16)
        kv_pack = jnp.concatenate(
            [
                key_low.reshape(seq_count, group_rows, model_width),
                value_low.reshape(seq_count, group_rows, model_width),
            ],
            axis=-1,
        )
        start_state = (
            jnp.full((seq_count, HEADS, group_rows), -jnp.inf, f32),
            jnp.zeros((seq_count, HEADS, group_rows), f32),
            jnp.zeros((seq_count, HEADS, group_rows, HEAD_DIM), f32),
        )
        soft_state = attend_piece(
            start_state,
            lax.all_gather(kv_pack, "ctx", axis=1, tiled=True),
            query_low,
            positions,
            score_scale,
        )
        run_max, run_sum, weighted = soft_state
        log_total = run_max + jnp.log(run_sum)
        attended = jnp.transpose(weighted / run_sum[..., None], (0, 2, 1, 3)).astype(bf16)
        att_flat = attended.reshape(flat_rows, model_width)
        pre_act = jnp.dot(hidden_two, weight_in, preferred_element_type=f32) + bias_in.astype(f32)
        activation_f, gelu_slope = gelu_parts(pre_act)
        activation = activation_f.astype(bf16)
        output = (
            residual
            + jnp.dot(att_flat, weight_out, preferred_element_type=f32)
            + bias_out.astype(f32)
            + jnp.dot(activation, weight_mlp, preferred_element_type=f32)
            + bias_mlp.astype(f32)
        )
        output_list.append(output.reshape(seq_count, group_rows, model_width))
        params_back = gather_params()
        (
            gain_one,
            shift_one,
            gain_two,
            shift_two,
            weight_qkv,
            bias_qkv,
            weight_out,
            bias_out,
            weight_in,
            bias_in,
            weight_mlp,
            bias_mlp,
        ) = params_back
        kv_rows = lax.all_gather(kv_pack, "ctx", axis=1, tiled=True)
        cot_flat = cot_rows.reshape(flat_rows, model_width)
        cot_low = cot_flat.astype(bf16)
        cot_sum = jnp.sum(cot_flat, axis=0)
        grad_w_out = outer_rows(att_flat, cot_low)
        grad_w_mlp = outer_rows(activation, cot_low)
        d_pre = times_transpose(cot_low, weight_mlp) * gelu_slope
        d_pre_low = d_pre.astype(bf16)
        grad_w_in = outer_rows(hidden_two, d_pre_low)
        d_hidden_two = times_transpose(d_pre_low, weight_in)
        grad_att = times_transpose(cot_low, weight_out).astype(bf16).reshape(head_shape)
        row_delta = jnp.einsum("sqhd,sqhd->shq", grad_att, attended, preferred_element_type=f32)

        def back_block(block_index, loop_carry):
            grad_query, buffer = loop_carry
            offset = block_index * key_block
            kv_block = lax.dynamic_slice_in_dim(kv_rows, offset, key_block, 1)
            key_part = kv_block[..., :model_width].reshape(seq_count, key_block, HEADS, HEAD_DIM)
            value_part = kv_block[..., model_width:].reshape(seq_count, key_block, HEADS, HEAD_DIM)
            scores = (
                jnp.einsum("sqhd,skhd->shqk", query_low, key_part, preferred_element_type=f32)
                * score_scale
            )
            allowed = (offset + jnp.arange(key_block, dtype=jnp.int32))[None, :] <= positions[
                :, None
            ]
            prob_block = jnp.where(allowed, jnp.exp(scores - log_total[..., None]), 0.0)
            grad_value = jnp.einsum(
                "shqk,sqhd->skhd", prob_block.astype(bf16), grad_att, preferred_element_type=f32
            )
            grad_prob = jnp.einsum(
                "sqhd,skhd->shqk", grad_att, value_part, preferred_element_type=f32
            )
            grad_score = (prob_block * (grad_prob - row_delta[..., None]) * score_scale).astype(
                bf16
            )
            grad_query = grad_query + jnp.einsum(
                "shqk,skhd->sqhd", grad_score, key_part, preferred_element_type=f32
            )
            grad_key = jnp.einsum(
                "shqk,sqhd->skhd", grad_score, query_low, preferred_element_type=f32
            )
            key_value_grad = jnp.concatenate(
                [
                    grad_key.reshape(seq_count, key_block, model_width),
                    grad_value.reshape(seq_count, key_block, model_width),
                ],
                axis=-1,
            )
            return (grad_query, lax.dynamic_update_slice_in_dim(buffer, key_value_grad, offset, 1))

        start_carry = (
            jnp.zeros(head_shape, f32),
            jnp.zeros((seq_count, seq_len, 2 * model_width), f32),
        )
        grad_query, buffer = lax.fori_loop(0, seq_len // key_block, back_block, start_carry)
        kv_grad_own = lax.psum_scatter(
            buffer.astype(jnp.bfloat16), "ctx", scatter_dimension=1, tiled=True
        ).astype(jnp.float32)
        key_grad_raw = kv_grad_own[..., :model_width].reshape(head_shape)
        value_grad_flat = kv_grad_own[..., model_width:].reshape(flat_rows, model_width)
        grad_query = rotate(grad_query, cosine, sine_rot, -1.0)
        grad_key = rotate(key_grad_raw, cosine, sine_rot, -1.0)
        d_project = jnp.concatenate(
            [
                grad_query.reshape(flat_rows, model_width),
                grad_key.reshape(flat_rows, model_width),
                value_grad_flat,
            ],
            axis=-1,
        )
        d_project_low = d_project.astype(bf16)
        grad_w_qkv = outer_rows(hidden_one, d_project_low)
        d_hidden_one = times_transpose(d_project_low, weight_qkv)
        grad_rows = (
            cot_flat
            + norm_back(d_hidden_one, normed_one, inverse_one, gain_one.astype(f32))
            + norm_back(d_hidden_two, normed_two, inverse_two, gain_two.astype(f32))
        )
        grad_list.append(grad_rows.reshape(seq_count, group_rows, model_width))
        terms = (
            jnp.sum(d_hidden_one * normed_one, axis=0),
            jnp.sum(d_hidden_one, axis=0),
            jnp.sum(d_hidden_two * normed_two, axis=0),
            jnp.sum(d_hidden_two, axis=0),
            grad_w_qkv,
            jnp.sum(d_project, axis=0),
            grad_w_out,
            cot_sum,
            grad_w_in,
            jnp.sum(d_pre, axis=0),
            grad_w_mlp,
            cot_sum,
        )
        if weight_sums is None:
            weight_sums = terms
        else:
            weight_sums = jax.tree.map(lambda total, term: total + term, weight_sums, terms)
    owned = (
        lax.psum_scatter(weight_sums[0], ("fsdp", "ctx"), scatter_dimension=0, tiled=True),
        lax.psum_scatter(weight_sums[1], ("fsdp", "ctx"), scatter_dimension=0, tiled=True),
        lax.psum_scatter(weight_sums[2], ("fsdp", "ctx"), scatter_dimension=0, tiled=True),
        lax.psum_scatter(weight_sums[3], ("fsdp", "ctx"), scatter_dimension=0, tiled=True),
        lax.psum_scatter(weight_sums[4], ("fsdp", "ctx"), scatter_dimension=0, tiled=True),
        lax.psum_scatter(weight_sums[5], ("fsdp", "ctx"), scatter_dimension=0, tiled=True),
        lax.psum_scatter(weight_sums[6], ("fsdp", "ctx"), scatter_dimension=0, tiled=True),
        lax.psum_scatter(weight_sums[7], ("fsdp", "ctx"), scatter_dimension=0, tiled=True),
        lax.psum_scatter(weight_sums[8], ("fsdp", "ctx"), scatter_dimension=0, tiled=True),
        lax.psum_scatter(weight_sums[9], ("fsdp", "ctx"), scatter_dimension=0, tiled=True),
        lax.psum_scatter(weight_sums[10], ("fsdp", "ctx"), scatter_dimension=0, tiled=True),
        lax.psum_scatter(weight_sums[11], ("fsdp", "ctx"), scatter_dimension=0, tiled=True),
    )
    outputs = jnp.concatenate(output_list, axis=0)
    grad_inputs = jnp.concatenate(grad_list, axis=0)
    return (
        outputs,
        grad_inputs,
        owned[0],
        owned[1],
        owned[2],
        owned[3],
        owned[4],
        owned[5],
        owned[6],
        owned[7],
        owned[8],
        owned[9],
        owned[10],
        owned[11],
    )


ROWS = 128
BLOCK = 256


def swap(value, bit):
    return lax.ppermute(value, "ctx", [(i, i ^ bit) for i in range(8)])


def shift_z(value, step):
    return lax.ppermute(value, "fsdp", [(i, (i + step) % 4) for i in range(4)])


def nt(left, right):
    return lax.dot_general(
        left, right, (((1,), (1,)), ((), ())), preferred_element_type=jnp.float32
    )


def nn(left, right):
    return lax.dot_general(
        left, right, (((1,), (0,)), ((), ())), preferred_element_type=jnp.float32
    )


def tn(left, right):
    return lax.dot_general(
        left, right, (((0,), (0,)), ((), ())), preferred_element_type=jnp.float32
    )


def normalize(values):
    centred = values - jnp.mean(values, axis=-1, keepdims=True)
    inverse = lax.rsqrt(jnp.mean(centred * centred, axis=-1, keepdims=True) + EPS)
    return centred * inverse, inverse


def col_sum(values):
    return jnp.sum(values, axis=0, keepdims=True)


def piece_bits(index):
    return ((index & 1) << 2) | (index & 2) | (index >> 2)


def mlp_kernel(layout, *refs):
    chunks, has_prev = layout
    refs = list(refs)
    row_ref = refs.pop(0)
    near = [refs.pop(0) for _ in chunks]
    far = [refs.pop(0) for _ in chunks]
    w_own, w_other, gain, shift, bias = [refs.pop(0) for _ in range(5)]
    out_ref, s_ref, g_in, g_out, vec_ref = [refs.pop(0) for _ in range(5)]
    w_in, w_down, x_s, c_s, h_s, act_s, dpre_s = refs
    f32, bf16 = jnp.float32, jnp.bfloat16
    step = pl.program_id(0)

    @pl.when(step == 0)
    def _():
        for other, source in ((0, w_own), (1, w_other)):
            for zr in range(4):
                rows = pl.ds(pl.multiple_of(row_ref[other * 4 + zr], 16), 96)
                w_in[rows, :] = source[zr, :96, :]
                w_down[rows, :] = source[zr, 96:, :]
        vec_ref[...] = jnp.zeros_like(vec_ref)
        g_in[...] = jnp.zeros_like(g_in)
        g_out[...] = jnp.zeros_like(g_out)

    first = 0
    for at, count in enumerate(chunks):
        @pl.when((step >= first) & (step < first + count))
        def _(at=at):
            for piece in range(8):
                source = near[at] if piece < 4 else far[at]
                rows = slice(piece * ROWS, (piece + 1) * ROWS)
                x_s[rows, :] = source[piece % 4, 0, 0]
                c_s[rows, :] = source[piece % 4, 1, 0]
        first += count

    for block in range(4):
        rows = slice(block * 256, (block + 1) * 256)
        normed, _ = normalize(x_s[rows, :].astype(f32))
        hidden = (normed * gain[...] + shift[...]).astype(bf16)
        h_s[rows, :] = hidden
        pre = nn(hidden, w_in[...]) + bias[...]
        cdf = 0.5 * (1.0 + lax.erf(pre * 0.7071067811865476))
        density = jnp.exp(-0.5 * pre * pre) * 0.3989422804014327
        act = (pre * cdf).astype(bf16)
        act_s[rows, :] = act
        cot = c_s[rows, :]
        d_pre = nt(cot, w_down[...]) * (cdf + pre * density)
        d_low = d_pre.astype(bf16)
        dpre_s[rows, :] = d_low
        out = nn(act, w_down[...])
        d_hidden = nt(d_low, w_in[...])
        vec_ref[0:1, :] += col_sum(d_pre)
        vec_ref[1:2, :] += col_sum(d_hidden * normed)
        vec_ref[2:3, :] += col_sum(d_hidden)
        s = (d_hidden * gain[...]).astype(bf16)
        out = out.astype(bf16)
        for half in range(2):
            out_ref[0, block * 2 + half] = out[half * ROWS : (half + 1) * ROWS]
            s_ref[0, block * 2 + half] = s[half * ROWS : (half + 1) * ROWS]
    g_in[...] += tn(h_s[...], dpre_s[...])
    g_out[...] += tn(act_s[...], c_s[...])


def whole(shape):
    return pl.BlockSpec(shape, lambda *_: (0,) * len(shape))


def mlp_call(row_offsets, near, far, w_own, w_other, gain, shift, bias):
    chunks = tuple(part.shape[2] for part in near)
    total = sum(chunks)
    width = gain.shape[-1]
    f32, bf16 = jnp.float32, jnp.bfloat16

    def part_spec(first, count):
        return pl.BlockSpec(
            (4, 2, 1, ROWS, width),
            lambda i, *_: (0, 0, jnp.clip(i - first, 0, count - 1), 0, 0),
        )

    specs, first = [], 0
    for count in chunks:
        specs.append(part_spec(first, count))
        first += count
    seq_spec = pl.BlockSpec((1, 8, ROWS, width), lambda i, *_: (i, 0, 0, 0))
    return pl.pallas_call(
        functools.partial(mlp_kernel, (chunks, False)),
        grid_spec=pltpu.PrefetchScalarGridSpec(
            num_scalar_prefetch=1,
            grid=(total,),
            in_specs=specs
            + specs
            + [whole(w_own.shape), whole(w_other.shape)]
            + [whole(gain.shape), whole(shift.shape), whole(bias.shape)],
            out_specs=[
                seq_spec,
                seq_spec,
                whole((width, width)),
                whole((width, width)),
                whole((8, width)),
            ],
            scratch_shapes=[pltpu.VMEM((width, width), bf16)] * 2
            + [pltpu.VMEM((8 * ROWS, width), bf16)] * 5,
        ),
        out_shape=[
            jax.ShapeDtypeStruct((total, 8, ROWS, width), bf16),
            jax.ShapeDtypeStruct((total, 8, ROWS, width), bf16),
            jax.ShapeDtypeStruct((width, width), f32),
            jax.ShapeDtypeStruct((width, width), f32),
            jax.ShapeDtypeStruct((8, width), f32),
        ],
        compiler_params=pltpu.CompilerParams(vmem_limit_bytes=56 << 20),
        name="mlp",
    )(row_offsets, *near, *far, w_own, w_other, gain, shift, bias)


def attn_kernel(has_prev, *refs):
    refs = list(refs)
    row_ref = refs.pop(0)
    near, far, w_own, w_other, o_own, o_other = [refs.pop(0) for _ in range(6)]
    gain, shift, bias, tab = [refs.pop(0) for _ in range(4)]
    prev_out, prev_s = [refs.pop(0) for _ in range(2)]
    if has_prev:
        pq_ref, po_ref, pv_ref = [refs.pop(0) for _ in range(3)]
    send_ref, keep_ref, gq_ref, go_ref, vec_ref = [refs.pop(0) for _ in range(5)]
    wq, wo, x_n, h_s, c_s, q_s, k_s, v_s, kt_s, vt_s, ga_s, gat_s, dk_s, dv_s, at_s, att_s, dp_s, out_s, s_s = refs
    f32, bf16 = jnp.float32, jnp.bfloat16
    seq = 8 * ROWS

    for other, source in ((0, w_own), (1, w_other)):
        for zr in range(4):
            rows = pl.ds(pl.multiple_of(row_ref[other * 4 + zr], 16), 96)
            wq[rows, :] = source[zr, :, :576]
    for other, source in ((0, o_own), (1, o_other)):
        rows = pl.ds(pl.multiple_of(row_ref[8 + other], 16), 96)
        wo[rows, :] = source[...]

    for piece in range(8):
        source = near if piece < 4 else far
        rows = pl.ds(pl.multiple_of(row_ref[16 + piece], ROWS), ROWS)
        normed, _ = normalize(source[piece % 4, 0, 0].astype(f32))
        x_n[rows, :] = normed
        h_s[rows, :] = (normed * gain[...] + shift[...]).astype(bf16)
        c_s[rows, :] = source[piece % 4, 1, 0]

    for block in range(4):
        rows = slice(block * 256, (block + 1) * 256)
        project = nn(h_s[rows, :], wq[...]) + bias[...]
        cosine, low, high = tab[0, rows, :], tab[1, rows, :], tab[2, rows, :]
        grad_t = nt(wo[...], c_s[rows, :])
        for head in range(3):
            pair = project[:, head * 128 : (head + 1) * 128]
            pair = pair * cosine + pltpu.roll(pair, 120, 1) * low + pltpu.roll(pair, 8, 1) * high
            q_s[head, rows, :] = pair[:, :64].astype(bf16)
            key = pltpu.roll(pair, 64, 1)[:, :64]
            k_s[head, rows, :] = key.astype(bf16)
            kt_s[head, :, rows] = jnp.transpose(key).astype(bf16)
            value = project[:, 384 + head * 64 : 384 + (head + 1) * 64]
            v_s[head, rows, :] = value.astype(bf16)
            vt_s[head, :, rows] = jnp.transpose(value).astype(bf16)
            part = grad_t[head * 64 : (head + 1) * 64]
            gat_s[head, :, rows] = part.astype(bf16)
            ga_s[head, rows, :] = jnp.transpose(part).astype(bf16)

    key_at = lax.broadcasted_iota(jnp.int32, (BLOCK, BLOCK), 0)
    query_at = lax.broadcasted_iota(jnp.int32, (BLOCK, BLOCK), 1)
    allowed = key_at <= query_at
    for head in range(3):
        for block in range(seq // BLOCK):
            rows = slice(block * BLOCK, (block + 1) * BLOCK)
            upto = (block + 1) * BLOCK
            query = q_s[head, rows, :]
            grad = ga_s[head, rows, :]
            diag = jnp.where(allowed, nt(k_s[head, rows, :], query), -1e30)
            if block:
                scores = jnp.concatenate([nt(k_s[head, : upto - BLOCK, :], query), diag], axis=0)
            else:
                scores = diag
            top = jnp.max(scores, axis=0, keepdims=True)
            prob = jnp.exp(scores - top)
            prob = prob * (1.0 / jnp.sum(prob, axis=0, keepdims=True))
            low_prob = prob.astype(bf16)
            att_t = nn(vt_s[head, :, :upto], low_prob)
            att_low = att_t.astype(bf16)
            att_s[head * 64 : (head + 1) * 64, rows] = att_low
            at_s[rows, head * 64 : (head + 1) * 64] = jnp.transpose(att_t).astype(bf16)
            delta = jnp.sum(
                gat_s[head, :, rows].astype(f32) * att_low.astype(f32), axis=0, keepdims=True
            )
            d_prob = nt(v_s[head, :upto, :], grad)
            d_score = (prob * (d_prob - delta)).astype(bf16)
            d_value = nn(low_prob, grad)
            d_key = nn(d_score, query)
            if block:
                keep = slice(0, upto - BLOCK)
                dv_s[keep, :] += d_value[: upto - BLOCK]
                dk_s[keep, :] += d_key[: upto - BLOCK]
            dv_s[rows, :] = d_value[upto - BLOCK :]
            dk_s[rows, :] = d_key[upto - BLOCK :]
            d_query = jnp.transpose(nn(kt_s[head, :, :upto], d_score))
            dp_s[rows, head * 128 : head * 128 + 64] = d_query
        for block in range(4):
            rows = slice(block * 256, (block + 1) * 256)
            pair = jnp.concatenate(
                [dp_s[rows, head * 128 : head * 128 + 64], dk_s[rows, :]], axis=1
            )
            cosine, low, high = tab[0, rows, :], tab[1, rows, :], tab[2, rows, :]
            pair = pair * cosine - pltpu.roll(pair, 120, 1) * low - pltpu.roll(pair, 8, 1) * high
            dp_s[rows, head * 128 : (head + 1) * 128] = pair
            dp_s[rows, 384 + head * 64 : 384 + (head + 1) * 64] = dv_s[rows, :]

    project = dp_s[...]
    project_low = project.astype(bf16)
    g_query = tn(h_s[...], project_low)
    g_out = nn(att_s[...], c_s[...])
    vec_ref[...] = jnp.zeros_like(vec_ref)
    sums = col_sum(project)
    for block in range(4):
        rows = slice(block * 256, (block + 1) * 256)
        d_hidden = nt(project_low[rows], wq[...])
        out_s[rows, :] = nn(at_s[rows, :], wo[...])
        s_s[rows, :] = d_hidden * gain[...]
        vec_ref[1:2, :] += col_sum(d_hidden * x_n[rows, :])
        vec_ref[2:3, :] += col_sum(d_hidden)
    vec_ref[0:1, :576] = sums
    if has_prev:
        g_query = g_query + pq_ref[...]
        g_out = g_out + po_ref[...]
        vec_ref[...] += pv_ref[...]
    gq_ref[...] = g_query
    go_ref[...] = g_out
    for piece in range(8):
        rows = pl.ds(pl.multiple_of(row_ref[16 + piece], ROWS), ROWS)
        target = keep_ref if piece < 4 else send_ref
        target[0, piece % 4] = (out_s[rows, :] + prev_out[0, piece].astype(f32)).astype(bf16)
        target[1, piece % 4] = (s_s[rows, :] + prev_s[0, piece].astype(f32)).astype(bf16)


def attn_call(row_offsets, near, far, at, w_own, w_other, o_own, o_other, gain, shift, bias, tab, prev_out, prev_s, seq_at, prev):
    width = gain.shape[-1]
    seq = 8 * ROWS
    f32, bf16 = jnp.float32, jnp.bfloat16
    part_spec = pl.BlockSpec((4, 2, 1, ROWS, width), lambda i, *_: (0, 0, at, 0, 0))
    prev_spec = pl.BlockSpec((1, 8, ROWS, width), lambda i, *_: (seq_at, 0, 0, 0))
    extra = list(prev) if prev is not None else []
    half = (2, 4, ROWS, width)
    return pl.pallas_call(
        functools.partial(attn_kernel, prev is not None),
        grid_spec=pltpu.PrefetchScalarGridSpec(
            num_scalar_prefetch=1,
            grid=(1,),
            in_specs=[part_spec, part_spec]
            + [whole(a.shape) for a in (w_own, w_other, o_own, o_other, gain, shift, bias, tab)]
            + [prev_spec, prev_spec]
            + [whole(a.shape) for a in extra],
            out_specs=[whole(half), whole(half), whole((width, 576)), whole((192, width)), whole((8, width))],
            scratch_shapes=[
                pltpu.VMEM((width, 576), bf16),
                pltpu.VMEM((192, width), bf16),
                pltpu.VMEM((seq, width), f32),
                pltpu.VMEM((seq, width), bf16),
                pltpu.VMEM((seq, width), bf16),
                pltpu.VMEM((3, seq, 64), bf16),
                pltpu.VMEM((3, seq, 64), bf16),
                pltpu.VMEM((3, seq, 64), bf16),
                pltpu.VMEM((3, 64, seq), bf16),
                pltpu.VMEM((3, 64, seq), bf16),
                pltpu.VMEM((3, seq, 64), bf16),
                pltpu.VMEM((3, 64, seq), bf16),
                pltpu.VMEM((seq, 64), f32),
                pltpu.VMEM((seq, 64), f32),
                pltpu.VMEM((seq, 192), bf16),
                pltpu.VMEM((192, seq), bf16),
                pltpu.VMEM((seq, 576), f32),
                pltpu.VMEM((seq, width), f32),
                pltpu.VMEM((seq, width), f32),
            ],
        ),
        out_shape=[
            jax.ShapeDtypeStruct(half, bf16),
            jax.ShapeDtypeStruct(half, bf16),
            jax.ShapeDtypeStruct((width, 576), f32),
            jax.ShapeDtypeStruct((192, width), f32),
            jax.ShapeDtypeStruct((8, width), f32),
        ],
        compiler_params=pltpu.CompilerParams(vmem_limit_bytes=56 << 20),
        name="attn",
    )(row_offsets, near, far, w_own, w_other, o_own, o_other, gain, shift, bias, tab, prev_out, prev_s, *extra)


def finish_kernel(half_ref, x_ref, c_ref, own_ref, other_ref, bias, out_ref, grad_ref):
    f32 = jnp.float32
    step = pl.program_id(0)
    is_own = (step // 3) == half_ref[0]

    def write(source):
        x = x_ref[0].astype(f32)
        normed, inverse = normalize(x)
        out_ref[0] = x + bias[...] + source[0, 0].astype(f32)
        s = source[0, 1].astype(f32)
        mean_s = jnp.mean(s, axis=-1, keepdims=True)
        mean_sn = jnp.mean(s * normed, axis=-1, keepdims=True)
        grad_ref[0] = c_ref[0] + inverse * (s - mean_s - normed * mean_sn)

    @pl.when(is_own)
    def _():
        write(own_ref)

    @pl.when(jnp.logical_not(is_own))
    def _():
        write(other_ref)


def finish_call(half, x, cot, own, other, bias):
    count, rows, width = x.shape
    f32 = jnp.float32
    seq_spec = pl.BlockSpec((1, rows, width), lambda i, *_: (i, 0, 0))
    part_spec = pl.BlockSpec((1, 2, rows, width), lambda i, *_: (i % 3, 0, 0, 0))
    return pl.pallas_call(
        finish_kernel,
        grid_spec=pltpu.PrefetchScalarGridSpec(
            num_scalar_prefetch=1,
            grid=(count,),
            in_specs=[seq_spec, seq_spec, part_spec, part_spec, whole(bias.shape)],
            out_specs=[seq_spec, seq_spec],
        ),
        out_shape=[jax.ShapeDtypeStruct(x.shape, f32)] * 2,
        name="finish",
    )(half, x, cot, own, other, bias)


def pick(value, index, axis=0):
    return lax.dynamic_index_in_dim(value, index, axis, keepdims=False)


def exchange_four(blocks, x, c):
    blocks = blocks.reshape((2, 2) + blocks.shape[1:])
    own = pick(blocks, x)
    got = swap(pick(blocks, 1 - x), 2)
    both = jnp.stack([own, got])
    mine = pick(both, c, 1)
    theirs = swap(pick(both, 1 - c, 1), 1)
    mine = jnp.where(x == 0, mine, mine[::-1])
    theirs = jnp.where(x == 0, theirs, theirs[::-1])
    pairs = jnp.where(
        c == 0, jnp.stack([mine, theirs], axis=1), jnp.stack([theirs, mine], axis=1)
    )
    return pairs.reshape((4,) + pairs.shape[2:])


def fast(
    inputs, cotangent, ln1_gain, ln1_bias, ln2_gain, ln2_bias, w_qkv, b_qkv, w_out, b_out, w_in, b_in, w_mlp_out, b_mlp_out
):
    f32, bf16 = jnp.float32, jnp.bfloat16
    width = inputs.shape[2]
    z = lax.axis_index("fsdp")
    ctx = lax.axis_index("ctx")
    y, x, c = ctx // 4, (ctx // 2) % 2, ctx % 2
    h = ctx % 4
    chunk_sizes = CHUNKS

    in4 = w_in.reshape(24, 8, 4, 96).transpose(2, 0, 1, 3).reshape(4, 24, 768)
    q5 = w_qkv.reshape(24, 3, 4, 3, 64)
    qk4 = q5[:, :2].transpose(2, 0, 3, 1, 4).reshape(4, 24, 384)
    v4 = q5[:, 2].transpose(1, 0, 2, 3).reshape(4, 24, 192)
    small = jnp.concatenate(
        [ln1_gain, ln1_bias, ln2_gain, ln2_bias, b_qkv, b_out, b_in, b_mlp_out]
    ).reshape(24, 13)
    small4 = jnp.broadcast_to(small[None], (4, 24, 13))
    pad4 = jnp.zeros((4, 24, 51), bf16)
    pack = jnp.concatenate([in4, qk4, v4, small4, pad4], axis=-1)

    cot_low = cotangent.astype(bf16)
    both = jnp.stack([inputs, cot_low])
    mine = lax.dynamic_slice_in_dim(both, y * 3, 3, 1)
    theirs = lax.dynamic_slice_in_dim(both, (1 - y) * 3, 3, 1)

    def gather(first, count):
        own = lax.slice_in_dim(mine, first, first + count, axis=1)
        got = swap(lax.slice_in_dim(theirs, first, first + count, axis=1), 4)
        two = jnp.stack([own, got])
        near = jnp.concatenate([two, swap(two, 2)])
        return near, swap(near, 1)

    near, far = [], []
    part = gather(0, chunk_sizes[0])
    near.append(part[0])
    far.append(part[1])
    pack = exchange_four(pack, x, c).reshape(96, 1408)
    mlp_w = jnp.concatenate([pack[:, :768], w_mlp_out])
    out_cols = w_out.reshape(24, 4, 192).transpose(1, 0, 2).reshape(96, 192)
    attn_w = jnp.concatenate([pack[:, 768:], out_cols], axis=1)
    attn_own = jnp.stack([attn_w] + [shift_z(attn_w, k) for k in (1, 2, 3)])
    mlp_own = jnp.stack([mlp_w] + [shift_z(mlp_w, k) for k in (1, 2, 3)])
    attn_q = attn_own[:, :, :640]
    attn_q_other = swap(attn_q, 4)
    out_rel = attn_own[:, :, 640:]
    out4 = jnp.stack([pick(out_rel, (z - k) % 4) for k in range(4)])
    out4 = exchange_four(out4, x, c)
    out_own = out4.reshape(4, 4, 24, 192).transpose(0, 2, 1, 3).reshape(96, 768)
    out_other = swap(out_own, 4)
    mlp_other = swap(mlp_own, 4)
    first = chunk_sizes[0]
    for count in chunk_sizes[1:]:
        part = gather(first, count)
        near.append(part[0])
        far.append(part[1])
        first += count

    def canonical(own, other):
        order = [pick(own, (z - k) % 4) for k in range(4)]
        order_other = [pick(other, (z - k) % 4) for k in range(4)]
        one, two = jnp.stack(order), jnp.stack(order_other)
        return jnp.where(y == 0, jnp.stack([one, two], axis=1), jnp.stack([two, one], axis=1))

    vectors = canonical(attn_q[:, :, 576:589], attn_q_other[:, :, 576:589])
    vectors = vectors.reshape(32, 312).astype(f32)

    def vector(first, count):
        return vectors[:, first : first + count].reshape(1, 32 * count)

    gain_one, shift_one = vector(0, 24), vector(24, 24)
    gain_two, shift_two = vector(48, 24), vector(72, 24)
    bias_q = pick(vector(96, 72).reshape(3, 4, 3, 64), h, 1)
    bias_q = jnp.concatenate(
        [bias_q[:2].transpose(1, 0, 2).reshape(1, 384), bias_q[2].reshape(1, 192)], axis=1
    )
    bias_in = pick(vectors[:, 192:288].reshape(8, 4, 96), h, 1).reshape(1, 768)
    bias_sum = vector(168, 24) + vector(288, 24)

    zs = jnp.stack([(z - k) % 4 for k in range(4)])
    rows_w = jnp.concatenate([(zs * 2 + y) * 96, (zs * 2 + 1 - y) * 96])
    rows_o = jnp.stack([y * 96, (1 - y) * 96])
    rows_p = jnp.stack([(ctx ^ piece_bits(k)) * ROWS for k in range(8)])
    row_offsets = jnp.concatenate(
        [rows_w, rows_o, jnp.zeros((6,), jnp.int32), rows_p]
    ).astype(jnp.int32)

    half_rot = ROT_DIM // 2
    cosine, sine = angles(jnp.arange(8 * ROWS, dtype=jnp.int32))
    rest = jnp.ones((8 * ROWS, HEAD_DIM - ROT_DIM), f32)
    none = jnp.zeros((8 * ROWS, HEAD_DIM - half_rot), f32)
    none_high = jnp.zeros((8 * ROWS, HEAD_DIM - ROT_DIM), f32)
    none_low = jnp.zeros((8 * ROWS, half_rot), f32)
    tab_cos = jnp.concatenate([cosine, cosine, rest], axis=1)
    tab_low = jnp.concatenate([-sine, none], axis=1)
    tab_high = jnp.concatenate([none_low, sine, none_high], axis=1)
    scale = HEAD_DIM ** (-0.5)
    tab = jnp.stack([jnp.concatenate([t * scale, t], axis=1) for t in (tab_cos, tab_low, tab_high)])

    mlp_out, mlp_s, g_in, g_down, mlp_vec = mlp_call(
        row_offsets, near, far, mlp_own, mlp_other, gain_two, shift_two, bias_in
    )

    def reduce_z(total):
        low = total.astype(bf16)
        result = pick(total, z)
        for k in (1, 2, 3):
            result = result + shift_z(pick(low, (z + k) % 4), k).astype(f32)
        return result

    def reduce_y(parts):
        return pick(parts, y, 1) + swap(pick(parts, 1 - y, 1).astype(bf16), 4).astype(f32)

    mlp_parts = jnp.concatenate([g_in.reshape(4, 2, 96, 768), g_down.reshape(4, 2, 96, 768)], axis=2)
    mlp_grad = reduce_z(reduce_y(mlp_parts))
    grad_w_mlp = mlp_grad[96:]
    in_parts = exchange_four(mlp_grad[:96].astype(bf16).reshape(4, 24, 768), x, c)
    grad_w_in = (
        in_parts.reshape(4, 24, 8, 96).transpose(1, 2, 0, 3).reshape(24, 3072).astype(f32)
    )

    own_parts, other_parts = [], []
    prev = None
    at_chunk, at_in = 0, 0
    for seq in range(3):
        send, keep, g_q, g_o, vec = attn_call(
            row_offsets, near[at_chunk], far[at_chunk], at_in, attn_q, attn_q_other, out_own, out_other,
            gain_one, shift_one, bias_q, tab, mlp_out, mlp_s, seq, prev,
        )
        prev = (g_q, g_o, vec)
        at_in += 1
        if at_in == chunk_sizes[at_chunk]:
            at_chunk, at_in = at_chunk + 1, 0
        got = swap(send, 1).astype(f32) + keep.astype(f32)
        got = got[:, :2] + swap(got[:, 2:].astype(bf16), 2).astype(f32)
        own_parts.append(got[:, 0].astype(bf16))
        other_parts.append(swap(got[:, 1].astype(bf16), 4))
    g_q, g_o, vec = prev

    cot_sum = jnp.sum(cotangent, axis=(0, 1))
    g_bq = vec[0, :576]
    g_bq = jnp.concatenate(
        [g_bq[:384].reshape(3, 2, 64).transpose(1, 0, 2), g_bq[384:].reshape(1, 3, 64)]
    )
    place = (jnp.arange(4) == h).astype(f32)
    g_bq = (g_bq[:, None] * place[None, :, None, None]).reshape(32, 72)
    g_bin = (mlp_vec[0].reshape(8, 1, 96) * place[None, :, None]).reshape(32, 96)
    vec_rows = [vec[1], vec[2], mlp_vec[1], mlp_vec[2], cot_sum]
    small_g = jnp.concatenate([v.reshape(32, 24) for v in vec_rows] + [g_bq, g_bin], axis=1)
    small_g = small_g.reshape(4, 2, 96, 12)
    q_parts = jnp.concatenate([g_q.reshape(4, 2, 96, 576), small_g], axis=3)
    q_grad = reduce_z(reduce_y(q_parts))
    q_blocks = exchange_four(q_grad.astype(bf16).reshape(4, 24, 588), x, c).astype(f32)
    qk = q_blocks[:, :, :384].reshape(4, 24, 3, 2, 64).transpose(1, 3, 0, 2, 4)
    vv = q_blocks[:, :, 384:576].reshape(4, 24, 1, 3, 64).transpose(1, 2, 0, 3, 4)
    grad_w_qkv = jnp.concatenate([qk, vv], axis=1).reshape(24, 2304)
    small_own = jnp.sum(q_blocks[:, :, 576:], axis=0).reshape(288)

    o_parts = pick(g_o.reshape(2, 96, 768), y) + swap(
        pick(g_o.reshape(2, 96, 768), 1 - y).astype(bf16), 4
    ).astype(f32)
    o_blocks = exchange_four(o_parts.astype(bf16).reshape(4, 24, 768), x, c)
    grad_w_out = reduce_z(o_blocks.astype(f32))

    outputs, grad_inputs = finish_call(
        jnp.reshape(y, (1,)).astype(jnp.int32), inputs, cotangent,
        jnp.stack(own_parts), jnp.stack(other_parts), bias_sum,
    )
    return (
        outputs,
        grad_inputs,
        small_own[0:24],
        small_own[24:48],
        small_own[48:72],
        small_own[72:96],
        grad_w_qkv,
        small_own[120:192],
        grad_w_out,
        small_own[96:120],
        grad_w_in,
        small_own[192:288],
        grad_w_mlp,
        small_own[96:120],
    )


def fast_fits(mesh):
    sizes = dict(mesh.shape)
    return sizes["fsdp"] == 4 and sizes["ctx"] == 8


def solution(mesh):
    return jax.shard_map(
        fast if fast_fits(mesh) else local,
        mesh=mesh,
        in_specs=(
            P("fsdp", "ctx", None),
            P("fsdp", "ctx", None),
            P(("fsdp", "ctx")),
            P(("fsdp", "ctx")),
            P(("fsdp", "ctx")),
            P(("fsdp", "ctx")),
            P(("fsdp", "ctx"), None),
            P(("fsdp", "ctx")),
            P(("fsdp", "ctx"), None),
            P(("fsdp", "ctx")),
            P(("fsdp", "ctx"), None),
            P(("fsdp", "ctx")),
            P(("fsdp", "ctx"), None),
            P(("fsdp", "ctx")),
        ),
        out_specs=(
            P("fsdp", "ctx", None),
            P("fsdp", "ctx", None),
            P(("fsdp", "ctx")),
            P(("fsdp", "ctx")),
            P(("fsdp", "ctx")),
            P(("fsdp", "ctx")),
            P(("fsdp", "ctx"), None),
            P(("fsdp", "ctx")),
            P(("fsdp", "ctx"), None),
            P(("fsdp", "ctx")),
            P(("fsdp", "ctx"), None),
            P(("fsdp", "ctx")),
            P(("fsdp", "ctx"), None),
            P(("fsdp", "ctx")),
        ),
        check_vma=False,
    )
```

```python
import functools
import math

import jax
import jax.numpy as jnp
import numpy as np
from jax import lax
from jax.experimental import pallas as pl
from jax.experimental.pallas import tpu as pltpu
from jax.sharding import PartitionSpec as P


HEADS = 12
HEAD_DIM = 64
ROT_DIM = 16
MICRO = 2
SEQ_MB = 3
CHUNKS = (1, 2)


EPS = 1e-05
BASE_FREQ = 10000.0


def layer_norm(values, gain_row, shift_row):
    centre = jnp.mean(values, axis=-1, keepdims=True)
    centred = values - centre
    inverse = lax.rsqrt(jnp.mean(centred * centred, axis=-1, keepdims=True) + EPS)
    normed = centred * inverse
    return (normed * gain_row + shift_row, normed, inverse)


def norm_back(grad_out, normed, inverse, gain_row):
    scaled = grad_out * gain_row
    return inverse * (
        scaled
        - jnp.mean(scaled, axis=-1, keepdims=True)
        - normed * jnp.mean(scaled * normed, axis=-1, keepdims=True)
    )


def angles(positions):
    half_rot = ROT_DIM // 2
    inv_freq = BASE_FREQ ** (-(2.0 * jnp.arange(half_rot, dtype=jnp.float32)) / ROT_DIM)
    phase_angle = positions.astype(jnp.float32)[:, None] * inv_freq[None, :]
    return (jnp.cos(phase_angle), jnp.sin(phase_angle))


def rotate(head_field, cosine, sine_rot, direction):
    half_rot = ROT_DIM // 2
    lead_half = head_field[..., :half_rot]
    trail_half = head_field[..., half_rot:ROT_DIM]
    cos_wide = cosine[:, None, :]
    sin_wide = direction * sine_rot[:, None, :]
    return jnp.concatenate(
        [
            lead_half * cos_wide - trail_half * sin_wide,
            trail_half * cos_wide + lead_half * sin_wide,
            head_field[..., ROT_DIM:],
        ],
        axis=-1,
    )


def gelu_parts(pre_act):
    normal_cdf = 0.5 * (1.0 + jax.scipy.special.erf(pre_act * 0.7071067811865476))
    density = jnp.exp(-0.5 * pre_act * pre_act) * 0.3989422804014327
    return (pre_act * normal_cdf, normal_cdf + pre_act * density)


def outer_rows(left, right):
    return lax.dot_general(
        left, right, (((0,), (0,)), ((), ())), preferred_element_type=jnp.float32
    )


def times_transpose(left, right):
    return lax.dot_general(
        left, right, (((1,), (1,)), ((), ())), preferred_element_type=jnp.float32
    )


def attend_block(soft_state, kv_block, first_row, query_low, positions, score_scale):
    run_max, run_sum, weighted = soft_state
    seq_count, block_rows, double_width = kv_block.shape
    model_width = double_width // 2
    key_low = kv_block[..., :model_width].reshape(seq_count, block_rows, HEADS, HEAD_DIM)
    value_low = kv_block[..., model_width:].reshape(seq_count, block_rows, HEADS, HEAD_DIM)
    scores = (
        jnp.einsum("sqhd,skhd->shqk", query_low, key_low, preferred_element_type=jnp.float32)
        * score_scale
    )
    allowed = (first_row + jnp.arange(block_rows, dtype=jnp.int32))[None, :] <= positions[:, None]
    scores = jnp.where(allowed, scores, -jnp.inf)
    new_max = jnp.maximum(run_max, jnp.max(scores, axis=-1))
    safe_max = jnp.where(new_max == -jnp.inf, 0.0, new_max)
    exp_scores = jnp.exp(scores - safe_max[..., None])
    factor = jnp.exp(run_max - safe_max)
    run_sum = run_sum * factor + jnp.sum(exp_scores, axis=-1)
    weighted = weighted * factor[..., None] + jnp.einsum(
        "shqk,skhd->shqd",
        exp_scores.astype(jnp.bfloat16),
        value_low,
        preferred_element_type=jnp.float32,
    )
    return (new_max, run_sum, weighted)


def attend_piece(soft_state, kv_piece, query_low, positions, score_scale):
    piece_rows = kv_piece.shape[1]
    step_rows = math.gcd(piece_rows, 512)

    def one_block(block_index, inner_state):
        offset = block_index * step_rows
        kv_block = lax.dynamic_slice_in_dim(kv_piece, offset, step_rows, 1)
        return attend_block(inner_state, kv_block, offset, query_low, positions, score_scale)

    return lax.fori_loop(0, piece_rows // step_rows, one_block, soft_state)


def local(
    inputs,
    cotangent,
    ln1_gain,
    ln1_bias,
    ln2_gain,
    ln2_bias,
    w_qkv,
    b_qkv,
    w_out,
    b_out,
    w_in,
    b_in,
    w_mlp_out,
    b_mlp_out,
):
    f32 = jnp.float32
    bf16 = jnp.bfloat16
    group_rows = inputs.shape[1]
    model_width = inputs.shape[2]
    seq_len = group_rows * lax.axis_size("ctx")
    key_block = math.gcd(seq_len, 512)
    score_scale = HEAD_DIM ** (-0.5)
    positions = lax.axis_index("ctx") * group_rows + jnp.arange(group_rows, dtype=jnp.int32)
    cosine, sine_rot = angles(positions)

    def gather_params():
        return (
            lax.all_gather(ln1_gain, ("fsdp", "ctx"), axis=0, tiled=True),
            lax.all_gather(ln1_bias, ("fsdp", "ctx"), axis=0, tiled=True),
            lax.all_gather(ln2_gain, ("fsdp", "ctx"), axis=0, tiled=True),
            lax.all_gather(ln2_bias, ("fsdp", "ctx"), axis=0, tiled=True),
            lax.all_gather(w_qkv, ("fsdp", "ctx"), axis=0, tiled=True),
            lax.all_gather(b_qkv, ("fsdp", "ctx"), axis=0, tiled=True),
            lax.all_gather(w_out, ("fsdp", "ctx"), axis=0, tiled=True),
            lax.all_gather(b_out, ("fsdp", "ctx"), axis=0, tiled=True),
            lax.all_gather(w_in, ("fsdp", "ctx"), axis=0, tiled=True),
            lax.all_gather(b_in, ("fsdp", "ctx"), axis=0, tiled=True),
            lax.all_gather(w_mlp_out, ("fsdp", "ctx"), axis=0, tiled=True),
            lax.all_gather(b_mlp_out, ("fsdp", "ctx"), axis=0, tiled=True),
        )

    weight_sums = None
    output_list = []
    grad_list = []
    for micro_index in range(MICRO):
        batch_rows = inputs[micro_index * SEQ_MB : (micro_index + 1) * SEQ_MB]
        cot_rows = cotangent[micro_index * SEQ_MB : (micro_index + 1) * SEQ_MB]
        seq_count = batch_rows.shape[0]
        flat_rows = seq_count * group_rows
        params_fwd = gather_params()
        (
            gain_one,
            shift_one,
            gain_two,
            shift_two,
            weight_qkv,
            bias_qkv,
            weight_out,
            bias_out,
            weight_in,
            bias_in,
            weight_mlp,
            bias_mlp,
        ) = params_fwd
        residual = batch_rows.reshape(flat_rows, model_width).astype(f32)
        normal_one, normed_one, inverse_one = layer_norm(
            residual, gain_one.astype(f32), shift_one.astype(f32)
        )
        normal_two, normed_two, inverse_two = layer_norm(
            residual, gain_two.astype(f32), shift_two.astype(f32)
        )
        hidden_one = normal_one.astype(bf16)
        hidden_two = normal_two.astype(bf16)
        project = jnp.dot(hidden_one, weight_qkv, preferred_element_type=f32) + bias_qkv.astype(f32)
        head_shape = (seq_count, group_rows, HEADS, HEAD_DIM)
        query_low = rotate(
            project[:, :model_width].reshape(head_shape), cosine, sine_rot, 1.0
        ).astype(bf16)
        key_low = rotate(
            project[:, model_width : 2 * model_width].reshape(head_shape), cosine, sine_rot, 1.0
        ).astype(bf16)
        value_low = project[:, 2 * model_width :].astype(bf16)
        kv_pack = jnp.concatenate(
            [
                key_low.reshape(seq_count, group_rows, model_width),
                value_low.reshape(seq_count, group_rows, model_width),
            ],
            axis=-1,
        )
        start_state = (
            jnp.full((seq_count, HEADS, group_rows), -jnp.inf, f32),
            jnp.zeros((seq_count, HEADS, group_rows), f32),
            jnp.zeros((seq_count, HEADS, group_rows, HEAD_DIM), f32),
        )
        soft_state = attend_piece(
            start_state,
            lax.all_gather(kv_pack, "ctx", axis=1, tiled=True),
            query_low,
            positions,
            score_scale,
        )
        run_max, run_sum, weighted = soft_state
        log_total = run_max + jnp.log(run_sum)
        attended = jnp.transpose(weighted / run_sum[..., None], (0, 2, 1, 3)).astype(bf16)
        att_flat = attended.reshape(flat_rows, model_width)
        pre_act = jnp.dot(hidden_two, weight_in, preferred_element_type=f32) + bias_in.astype(f32)
        activation_f, gelu_slope = gelu_parts(pre_act)
        activation = activation_f.astype(bf16)
        output = (
            residual
            + jnp.dot(att_flat, weight_out, preferred_element_type=f32)
            + bias_out.astype(f32)
            + jnp.dot(activation, weight_mlp, preferred_element_type=f32)
            + bias_mlp.astype(f32)
        )
        output_list.append(output.reshape(seq_count, group_rows, model_width))
        params_back = gather_params()
        (
            gain_one,
            shift_one,
            gain_two,
            shift_two,
            weight_qkv,
            bias_qkv,
            weight_out,
            bias_out,
            weight_in,
            bias_in,
            weight_mlp,
            bias_mlp,
        ) = params_back
        kv_rows = lax.all_gather(kv_pack, "ctx", axis=1, tiled=True)
        cot_flat = cot_rows.reshape(flat_rows, model_width)
        cot_low = cot_flat.astype(bf16)
        cot_sum = jnp.sum(cot_flat, axis=0)
        grad_w_out = outer_rows(att_flat, cot_low)
        grad_w_mlp = outer_rows(activation, cot_low)
        d_pre = times_transpose(cot_low, weight_mlp) * gelu_slope
        d_pre_low = d_pre.astype(bf16)
        grad_w_in = outer_rows(hidden_two, d_pre_low)
        d_hidden_two = times_transpose(d_pre_low, weight_in)
        grad_att = times_transpose(cot_low, weight_out).astype(bf16).reshape(head_shape)
        row_delta = jnp.einsum("sqhd,sqhd->shq", grad_att, attended, preferred_element_type=f32)

        def back_block(block_index, loop_carry):
            grad_query, buffer = loop_carry
            offset = block_index * key_block
            kv_block = lax.dynamic_slice_in_dim(kv_rows, offset, key_block, 1)
            key_part = kv_block[..., :model_width].reshape(seq_count, key_block, HEADS, HEAD_DIM)
            value_part = kv_block[..., model_width:].reshape(seq_count, key_block, HEADS, HEAD_DIM)
            scores = (
                jnp.einsum("sqhd,skhd->shqk", query_low, key_part, preferred_element_type=f32)
                * score_scale
            )
            allowed = (offset + jnp.arange(key_block, dtype=jnp.int32))[None, :] <= positions[
                :, None
            ]
            prob_block = jnp.where(allowed, jnp.exp(scores - log_total[..., None]), 0.0)
            grad_value = jnp.einsum(
                "shqk,sqhd->skhd", prob_block.astype(bf16), grad_att, preferred_element_type=f32
            )
            grad_prob = jnp.einsum(
                "sqhd,skhd->shqk", grad_att, value_part, preferred_element_type=f32
            )
            grad_score = (prob_block * (grad_prob - row_delta[..., None]) * score_scale).astype(
                bf16
            )
            grad_query = grad_query + jnp.einsum(
                "shqk,skhd->sqhd", grad_score, key_part, preferred_element_type=f32
            )
            grad_key = jnp.einsum(
                "shqk,sqhd->skhd", grad_score, query_low, preferred_element_type=f32
            )
            key_value_grad = jnp.concatenate(
                [
                    grad_key.reshape(seq_count, key_block, model_width),
                    grad_value.reshape(seq_count, key_block, model_width),
                ],
                axis=-1,
            )
            return (grad_query, lax.dynamic_update_slice_in_dim(buffer, key_value_grad, offset, 1))

        start_carry = (
            jnp.zeros(head_shape, f32),
            jnp.zeros((seq_count, seq_len, 2 * model_width), f32),
        )
        grad_query, buffer = lax.fori_loop(0, seq_len // key_block, back_block, start_carry)
        kv_grad_own = lax.psum_scatter(
            buffer.astype(jnp.bfloat16), "ctx", scatter_dimension=1, tiled=True
        ).astype(jnp.float32)
        key_grad_raw = kv_grad_own[..., :model_width].reshape(head_shape)
        value_grad_flat = kv_grad_own[..., model_width:].reshape(flat_rows, model_width)
        grad_query = rotate(grad_query, cosine, sine_rot, -1.0)
        grad_key = rotate(key_grad_raw, cosine, sine_rot, -1.0)
        d_project = jnp.concatenate(
            [
                grad_query.reshape(flat_rows, model_width),
                grad_key.reshape(flat_rows, model_width),
                value_grad_flat,
            ],
            axis=-1,
        )
        d_project_low = d_project.astype(bf16)
        grad_w_qkv = outer_rows(hidden_one, d_project_low)
        d_hidden_one = times_transpose(d_project_low, weight_qkv)
        grad_rows = (
            cot_flat
            + norm_back(d_hidden_one, normed_one, inverse_one, gain_one.astype(f32))
            + norm_back(d_hidden_two, normed_two, inverse_two, gain_two.astype(f32))
        )
        grad_list.append(grad_rows.reshape(seq_count, group_rows, model_width))
        terms = (
            jnp.sum(d_hidden_one * normed_one, axis=0),
            jnp.sum(d_hidden_one, axis=0),
            jnp.sum(d_hidden_two * normed_two, axis=0),
            jnp.sum(d_hidden_two, axis=0),
            grad_w_qkv,
            jnp.sum(d_project, axis=0),
            grad_w_out,
            cot_sum,
            grad_w_in,
            jnp.sum(d_pre, axis=0),
            grad_w_mlp,
            cot_sum,
        )
        if weight_sums is None:
            weight_sums = terms
        else:
            weight_sums = jax.tree.map(lambda total, term: total + term, weight_sums, terms)
    owned = (
        lax.psum_scatter(weight_sums[0], ("fsdp", "ctx"), scatter_dimension=0, tiled=True),
        lax.psum_scatter(weight_sums[1], ("fsdp", "ctx"), scatter_dimension=0, tiled=True),
        lax.psum_scatter(weight_sums[2], ("fsdp", "ctx"), scatter_dimension=0, tiled=True),
        lax.psum_scatter(weight_sums[3], ("fsdp", "ctx"), scatter_dimension=0, tiled=True),
        lax.psum_scatter(weight_sums[4], ("fsdp", "ctx"), scatter_dimension=0, tiled=True),
        lax.psum_scatter(weight_sums[5], ("fsdp", "ctx"), scatter_dimension=0, tiled=True),
        lax.psum_scatter(weight_sums[6], ("fsdp", "ctx"), scatter_dimension=0, tiled=True),
        lax.psum_scatter(weight_sums[7], ("fsdp", "ctx"), scatter_dimension=0, tiled=True),
        lax.psum_scatter(weight_sums[8], ("fsdp", "ctx"), scatter_dimension=0, tiled=True),
        lax.psum_scatter(weight_sums[9], ("fsdp", "ctx"), scatter_dimension=0, tiled=True),
        lax.psum_scatter(weight_sums[10], ("fsdp", "ctx"), scatter_dimension=0, tiled=True),
        lax.psum_scatter(weight_sums[11], ("fsdp", "ctx"), scatter_dimension=0, tiled=True),
    )
    outputs = jnp.concatenate(output_list, axis=0)
    grad_inputs = jnp.concatenate(grad_list, axis=0)
    return (
        outputs,
        grad_inputs,
        owned[0],
        owned[1],
        owned[2],
        owned[3],
        owned[4],
        owned[5],
        owned[6],
        owned[7],
        owned[8],
        owned[9],
        owned[10],
        owned[11],
    )


ROWS = 128
BLOCK = 256


def swap(value, bit):
    return lax.ppermute(value, "ctx", [(i, i ^ bit) for i in range(8)])


def shift_z(value, step):
    return lax.ppermute(value, "fsdp", [(i, (i + step) % 4) for i in range(4)])


def nt(left, right):
    return lax.dot_general(
        left, right, (((1,), (1,)), ((), ())), preferred_element_type=jnp.float32
    )


def nn(left, right):
    return lax.dot_general(
        left, right, (((1,), (0,)), ((), ())), preferred_element_type=jnp.float32
    )


def tn(left, right):
    return lax.dot_general(
        left, right, (((0,), (0,)), ((), ())), preferred_element_type=jnp.float32
    )


def normalize(values):
    centred = values - jnp.mean(values, axis=-1, keepdims=True)
    inverse = lax.rsqrt(jnp.mean(centred * centred, axis=-1, keepdims=True) + EPS)
    return centred * inverse, inverse


def col_sum(values):
    return jnp.sum(values, axis=0, keepdims=True)


def piece_bits(index):
    return ((index & 1) << 2) | (index & 2) | (index >> 2)


def mlp_kernel(chunks, row_ref, *refs):
    refs = list(refs)
    parts = [[refs.pop(0) for _ in range(4)] for _ in chunks]
    weights = [refs.pop(0) for _ in range(8)]
    vecs, cot_ref, first_send, first_keep = [refs.pop(0) for _ in range(4)]
    send_ref, keep_ref, rest_ref, gsend_ref, gkeep_ref, vec_ref = [refs.pop(0) for _ in range(6)]
    w_in, w_down, x_s, c_s, h_s, act_s, dpre_s, part_s, g_in, g_down, seg_s = refs
    f32, bf16 = jnp.float32, jnp.bfloat16
    step = pl.program_id(0)
    gain, shift, bias = vecs[2:3, :], vecs[3:4, :], vecs[6:7, :]

    @pl.when(step == 0)
    def _():
        for at, source in enumerate(weights):
            rows = pl.ds(pl.multiple_of(row_ref[at], 16), 96)
            w_in[rows, :] = source[:96, :]
            w_down[rows, :] = source[96:, :]
        vec_ref[...] = jnp.zeros_like(vec_ref)

    first = 0
    for at, count in enumerate(chunks):
        @pl.when((step >= first) & (step < first + count))
        def _(at=at):
            for piece in range(8):
                source = parts[at][piece // 2]
                rows = slice(piece * ROWS, (piece + 1) * ROWS)
                x_s[rows, :] = source[piece % 2, 0, 0]
                c_s[rows, :] = source[piece % 2, 1, 0]

        first += count

    vec_ref[3:4, :] += col_sum(cot_ref[0]) + col_sum(cot_ref[1])
    for block in range(4):
        rows = slice(block * 256, (block + 1) * 256)
        normed, _ = normalize(x_s[rows, :].astype(f32))
        hidden = (normed * gain + shift).astype(bf16)
        h_s[rows, :] = hidden
        pre = nn(hidden, w_in[...]) + bias
        cdf = 0.5 * (1.0 + lax.erf(pre * 0.7071067811865476))
        density = jnp.exp(-0.5 * pre * pre) * 0.3989422804014327
        act = (pre * cdf).astype(bf16)
        act_s[rows, :] = act
        cot = c_s[rows, :]
        d_pre = nt(cot, w_down[...]) * (cdf + pre * density)
        d_low = d_pre.astype(bf16)
        dpre_s[rows, :] = d_low
        out = nn(act, w_down[...])
        d_hidden = nt(d_low, w_in[...])
        vec_ref[0:1, :] += col_sum(d_pre)
        vec_ref[1:2, :] += col_sum(d_hidden * normed)
        vec_ref[2:3, :] += col_sum(d_hidden)
        for kind, value in ((0, out), (1, d_hidden * gain)):
            for half in range(2):
                part_s[block * 2 + half, kind] = value[half * ROWS : (half + 1) * ROWS].astype(bf16)

    @pl.when(step == 0)
    def _():
        g_in[...] = tn(h_s[...], dpre_s[...])
        g_down[...] = tn(act_s[...], c_s[...])
        for target, source, first in ((keep_ref, first_keep, 0), (send_ref, first_send, 4)):
            total = source[...].astype(f32) + part_s[first : first + 4].astype(f32)
            target[...] = total.astype(bf16)

    @pl.when(step > 0)
    def _():
        g_in[...] += tn(h_s[...], dpre_s[...])
        g_down[...] += tn(act_s[...], c_s[...])
        rest_ref[0] = part_s[...]

    @pl.when(step == sum(chunks) - 1)
    def _():
        for at in range(8):
            seg_s[at, :, :96] = jnp.broadcast_to(vec_ref[0:1, at * 96 : (at + 1) * 96], (16, 96))
        for half, target in ((0, gkeep_ref), (1, gsend_ref)):
            for zz in range(4):
                at = zz * 2 + (row_ref[24] ^ half)
                rows = pl.ds(pl.multiple_of(at * 96, 16), 96)
                target[zz, :96, :] = g_in[rows, :].astype(target.dtype)
                target[zz, 96:192, :] = g_down[rows, :].astype(target.dtype)
                target[zz, 192:, :] = jnp.zeros((16, 768), target.dtype)
                target[zz, 192:, :96] = seg_s[at, :, :96].astype(target.dtype)


def whole(shape):
    return pl.BlockSpec(shape, lambda *_: (0,) * len(shape))


def mlp_call(row_offsets, parts, weights, vecs, cot, first_send, first_keep):
    chunks = tuple(part[0].shape[2] for part in parts)
    total = sum(chunks)
    width = vecs.shape[-1]
    f32, bf16 = jnp.float32, jnp.bfloat16

    def part_spec(first, count):
        return pl.BlockSpec(
            (2, 2, 1, ROWS, width),
            lambda i, *_: (0, 0, jnp.clip(i - first, 0, count - 1), 0, 0),
        )

    specs, first = [], 0
    for count in chunks:
        specs += [part_spec(first, count)] * 4
        first += count
    rest_spec = pl.BlockSpec(
        (1, 8, 2, ROWS, width), lambda i, *_: (jnp.maximum(i - 1, 0), 0, 0, 0, 0)
    )
    half = (4, 2, ROWS, width)
    grads = (4, 208, width)
    return pl.pallas_call(
        functools.partial(mlp_kernel, chunks),
        grid_spec=pltpu.PrefetchScalarGridSpec(
            num_scalar_prefetch=1,
            grid=(total,),
            in_specs=specs
            + [whole(a.shape) for a in weights]
            + [whole(vecs.shape), pl.BlockSpec((2, ROWS, width), lambda i, *_: (i, 0, 0))]
            + [whole(half), whole(half)],
            out_specs=[whole(half), whole(half), rest_spec, whole(grads), whole(grads), whole((8, width))],
            scratch_shapes=[pltpu.VMEM((width, width), bf16)] * 2
            + [pltpu.VMEM((8 * ROWS, width), bf16)] * 5
            + [pltpu.VMEM((8, 2, ROWS, width), bf16)]
            + [pltpu.VMEM((width, width), f32)] * 2
            + [pltpu.VMEM((8, 16, 128), f32)],
        ),
        out_shape=[
            jax.ShapeDtypeStruct(half, bf16),
            jax.ShapeDtypeStruct(half, bf16),
            jax.ShapeDtypeStruct((total - 1, 8, 2, ROWS, width), bf16),
            jax.ShapeDtypeStruct(grads, bf16),
            jax.ShapeDtypeStruct(grads, f32),
            jax.ShapeDtypeStruct((8, width), f32),
        ],
        compiler_params=pltpu.CompilerParams(vmem_limit_bytes=56 << 20),
        cost_estimate=pl.CostEstimate(
            flops=30_000_000_000, transcendentals=0, bytes_accessed=30_000_000
        ),
        name="mlp",
    )(row_offsets, *[a for part in parts for a in part], *weights, vecs, cot, first_send, first_keep)


def rotary_tables():
    f32 = jnp.float32
    lane = lax.broadcasted_iota(jnp.int32, (32, 128), 1)
    dim = lane & 63
    power = (dim & 7).astype(f32) * (-2.0 / ROT_DIM)
    freq = jnp.where(dim < ROT_DIM, jnp.exp(power * math.log(BASE_FREQ)), 0.0)
    row = lax.broadcasted_iota(jnp.int32, (32, 128), 0).astype(f32)
    fine, coarse = row * freq, row * 32.0 * freq
    cos_fine, sin_fine = jnp.cos(fine), jnp.sin(fine)
    scale = jnp.where(lane < 64, HEAD_DIM ** (-0.5), 1.0)
    cos_coarse, sin_coarse = jnp.cos(coarse) * scale, jnp.sin(coarse) * scale
    first, second = dim[:1] < 8, (dim[:1] >= 8) & (dim[:1] < ROT_DIM)
    return cos_fine, sin_fine, cos_coarse, sin_coarse, first, second


def attn_kernel(has_prev, last, *refs):
    refs = list(refs)
    row_ref = refs.pop(0)
    parts = [refs.pop(0) for _ in range(4)]
    weights = [refs.pop(0) for _ in range(8)]
    o_own, o_other = [refs.pop(0) for _ in range(2)]
    vecs = refs.pop(0)
    if has_prev:
        partial = refs.pop(0)
        pq_ref, po_ref, pv_ref = [refs.pop(0) for _ in range(3)]
    if last:
        mv_ref, at_ref, col_ref = [refs.pop(0) for _ in range(3)]
        send_ref, keep_ref, qsend_ref, qkeep_ref, osend_ref, okeep_ref = [refs.pop(0) for _ in range(6)]
    else:
        send_ref, keep_ref, gq_ref, go_ref, vec_ref = [refs.pop(0) for _ in range(5)]
    wq, wo, x_n, h_s, c_s, q_s, k_s, v_s, kt_s, vt_s, ga_s, gat_s, dk_s, dv_s, at_s, att_s, dp_s, out_s, s_s, tab = refs[:20]
    f32, bf16 = jnp.float32, jnp.bfloat16
    seq = 8 * ROWS
    gain, shift, bias = vecs[0:1, :], vecs[1:2, :], vecs[5:6, :576]

    cos_f, sin_f, cos_c, sin_c, first, second = rotary_tables()
    for at in range(seq // 32):
        rows = slice(at * 32, (at + 1) * 32)
        cosine = cos_f * cos_c[at : at + 1] - sin_f * sin_c[at : at + 1]
        sine = sin_f * cos_c[at : at + 1] + cos_f * sin_c[at : at + 1]
        tab[0, rows, :] = cosine
        tab[1, rows, :] = jnp.where(first, -sine, 0.0)
        tab[2, rows, :] = jnp.where(second, sine, 0.0)

    for at, source in enumerate(weights):
        rows = pl.ds(pl.multiple_of(row_ref[at], 16), 96)
        wq[rows, :] = source[:, :576]
    for other, source in ((0, o_own), (1, o_other)):
        rows = pl.ds(pl.multiple_of(row_ref[8 + other], 16), 96)
        wo[rows, :] = source[...]

    for piece in range(8):
        source = parts[piece // 2]
        rows = pl.ds(pl.multiple_of(row_ref[16 + piece], ROWS), ROWS)
        normed, _ = normalize(source[piece % 2, 0, 0].astype(f32))
        x_n[rows, :] = normed
        h_s[rows, :] = (normed * gain + shift).astype(bf16)
        c_s[rows, :] = source[piece % 2, 1, 0]

    for block in range(4):
        rows = slice(block * 256, (block + 1) * 256)
        project = nn(h_s[rows, :], wq[...]) + bias
        cosine, low, high = tab[0, rows, :], tab[1, rows, :], tab[2, rows, :]
        grad_t = nt(wo[...], c_s[rows, :])
        for head in range(3):
            pair = project[:, head * 128 : (head + 1) * 128]
            pair = pair * cosine + pltpu.roll(pair, 120, 1) * low + pltpu.roll(pair, 8, 1) * high
            q_s[head, rows, :] = pair[:, :64].astype(bf16)
            key = pltpu.roll(pair, 64, 1)[:, :64]
            k_s[head, rows, :] = key.astype(bf16)
            kt_s[head, :, rows] = jnp.transpose(key).astype(bf16)
            value = project[:, 384 + head * 64 : 384 + (head + 1) * 64]
            v_s[head, rows, :] = value.astype(bf16)
            vt_s[head, :, rows] = jnp.transpose(value).astype(bf16)
            part = grad_t[head * 64 : (head + 1) * 64]
            gat_s[head, :, rows] = part.astype(bf16)
            ga_s[head, rows, :] = jnp.transpose(part).astype(bf16)

    key_at = lax.broadcasted_iota(jnp.int32, (BLOCK, BLOCK), 0)
    query_at = lax.broadcasted_iota(jnp.int32, (BLOCK, BLOCK), 1)
    allowed = key_at <= query_at
    for head in range(3):
        for block in range(seq // BLOCK):
            rows = slice(block * BLOCK, (block + 1) * BLOCK)
            upto = (block + 1) * BLOCK
            query = q_s[head, rows, :]
            grad = ga_s[head, rows, :]
            diag = jnp.where(allowed, nt(k_s[head, rows, :], query), -1e30)
            if block:
                scores = jnp.concatenate([nt(k_s[head, : upto - BLOCK, :], query), diag], axis=0)
            else:
                scores = diag
            top = jnp.max(scores, axis=0, keepdims=True)
            prob = jnp.exp(scores - top)
            prob = prob * (1.0 / jnp.sum(prob, axis=0, keepdims=True))
            low_prob = prob.astype(bf16)
            att_t = nn(vt_s[head, :, :upto], low_prob)
            att_low = att_t.astype(bf16)
            att_s[head * 64 : (head + 1) * 64, rows] = att_low
            at_s[rows, head * 64 : (head + 1) * 64] = jnp.transpose(att_t).astype(bf16)
            delta = jnp.sum(
                gat_s[head, :, rows].astype(f32) * att_low.astype(f32), axis=0, keepdims=True
            )
            d_prob = nt(v_s[head, :upto, :], grad)
            d_score = (prob * (d_prob - delta)).astype(bf16)
            d_value = nn(low_prob, grad)
            d_key = nn(d_score, query)
            if block:
                keep = slice(0, upto - BLOCK)
                dv_s[keep, :] += d_value[: upto - BLOCK]
                dk_s[keep, :] += d_key[: upto - BLOCK]
            dv_s[rows, :] = d_value[upto - BLOCK :]
            dk_s[rows, :] = d_key[upto - BLOCK :]
            d_query = jnp.transpose(nn(kt_s[head, :, :upto], d_score))
            dp_s[rows, head * 128 : head * 128 + 64] = d_query
        for block in range(4):
            rows = slice(block * 256, (block + 1) * 256)
            pair = jnp.concatenate(
                [dp_s[rows, head * 128 : head * 128 + 64], dk_s[rows, :]], axis=1
            )
            cosine, low, high = tab[0, rows, :], tab[1, rows, :], tab[2, rows, :]
            pair = pair * cosine - pltpu.roll(pair, 120, 1) * low - pltpu.roll(pair, 8, 1) * high
            dp_s[rows, head * 128 : (head + 1) * 128] = pair
            dp_s[rows, 384 + head * 64 : 384 + (head + 1) * 64] = dv_s[rows, :]

    project = dp_s[...]
    project_low = project.astype(bf16)
    g_query = tn(h_s[...], project_low)
    g_out = nn(att_s[...], c_s[...])
    sums = [col_sum(project), jnp.zeros((1, 768), f32), jnp.zeros((1, 768), f32)]
    for block in range(4):
        rows = slice(block * 256, (block + 1) * 256)
        d_hidden = nt(project_low[rows], wq[...])
        out_s[rows, :] = nn(at_s[rows, :], wo[...])
        s_s[rows, :] = d_hidden * gain
        sums[1] += col_sum(d_hidden * x_n[rows, :])
        sums[2] += col_sum(d_hidden)
    if has_prev:
        g_query = g_query + pq_ref[...]
        g_out = g_out + po_ref[...]
        sums = [sums[0] + pv_ref[0:1, :576], sums[1] + pv_ref[1:2, :], sums[2] + pv_ref[2:3, :]]
    if last:
        gq_s, go_s, tr_s = refs[20:]
        gq_s[:, :576] = g_query
        go_s[...] = g_out
        tr_s[...] = jnp.zeros_like(tr_s)
        tr_s[64:65, :] = sums[1]
        tr_s[65:66, :] = sums[2]
        tr_s[66:69, :] = mv_ref[1:4, :]
        columns = jnp.transpose(tr_s[...])
        lane = lax.broadcasted_iota(jnp.int32, (768, 128), 1)
        target_at = col_ref[0:1, :576] + row_ref[25] * 192
        for third in range(3):
            hit = at_ref[:, third : third + 1] == target_at
            column = jnp.sum(jnp.where(hit, sums[0], 0.0), axis=1, keepdims=True)
            columns = jnp.where(lane == 69 + third, column, columns)
        gq_s[:, 512:640] = jnp.where(lane < 64, gq_s[:, 512:640], columns)
        for half, target in ((0, qkeep_ref), (1, qsend_ref)):
            for zz in range(4):
                at = zz * 2 + (row_ref[24] ^ half)
                rows = pl.ds(pl.multiple_of(at * 96, 16), 96)
                target[zz] = gq_s[rows, :].astype(target.dtype)
        for half, target in ((0, okeep_ref), (1, osend_ref)):
            rows = pl.ds(pl.multiple_of((row_ref[24] ^ half) * 96, 16), 96)
            target[...] = go_s[rows, :].astype(target.dtype)
    else:
        gq_ref[...] = g_query
        go_ref[...] = g_out
        vec_ref[...] = jnp.zeros_like(vec_ref)
        vec_ref[0:1, :576] = sums[0]
        vec_ref[1:2, :] = sums[1]
        vec_ref[2:3, :] = sums[2]
    for piece in range(8):
        rows = pl.ds(pl.multiple_of(row_ref[16 + piece], ROWS), ROWS)
        target = keep_ref if piece < 4 else send_ref
        for kind, source in ((0, out_s), (1, s_s)):
            total = source[rows, :]
            if has_prev:
                total = total + partial[0, piece, kind].astype(f32)
            target[piece % 4, kind] = total.astype(bf16)


def attn_call(row_offsets, parts, at, weights, o_own, o_other, vecs, partial, seq, prev, tail):
    width = vecs.shape[-1]
    f32, bf16 = jnp.float32, jnp.bfloat16
    part_spec = pl.BlockSpec((2, 2, 1, ROWS, width), lambda i, *_: (0, 0, at, 0, 0))
    partial_spec = pl.BlockSpec((1, 8, 2, ROWS, width), lambda i, *_: (seq - 1, 0, 0, 0, 0))
    extra = list(prev) if prev is not None else []
    partials = [partial] if prev is not None else []
    last = tail is not None
    after = list(tail) if last else []
    rows = 8 * ROWS
    half = (4, 2, ROWS, width)
    shapes = [(half, bf16), (half, bf16)]
    if last:
        shapes += [((4, 96, 640), bf16), ((4, 96, 640), f32), ((96, width), bf16), ((96, width), f32)]
    else:
        shapes += [((width, 576), f32), ((192, width), f32), ((8, width), f32)]
    outs = [jax.ShapeDtypeStruct(shape, kind) for shape, kind in shapes]
    return pl.pallas_call(
        functools.partial(attn_kernel, prev is not None, last),
        grid_spec=pltpu.PrefetchScalarGridSpec(
            num_scalar_prefetch=1,
            grid=(1,),
            in_specs=[part_spec] * 4
            + [whole(a.shape) for a in (*weights, o_own, o_other, vecs)]
            + [partial_spec] * len(partials)
            + [whole(a.shape) for a in extra + after],
            out_specs=[whole(a.shape) for a in outs],
            scratch_shapes=[
                pltpu.VMEM((width, 576), bf16),
                pltpu.VMEM((192, width), bf16),
                pltpu.VMEM((rows, width), f32),
                pltpu.VMEM((rows, width), bf16),
                pltpu.VMEM((rows, width), bf16),
                pltpu.VMEM((3, rows, 64), bf16),
                pltpu.VMEM((3, rows, 64), bf16),
                pltpu.VMEM((3, rows, 64), bf16),
                pltpu.VMEM((3, 64, rows), bf16),
                pltpu.VMEM((3, 64, rows), bf16),
                pltpu.VMEM((3, rows, 64), bf16),
                pltpu.VMEM((3, 64, rows), bf16),
                pltpu.VMEM((rows, 64), f32),
                pltpu.VMEM((rows, 64), f32),
                pltpu.VMEM((rows, 192), bf16),
                pltpu.VMEM((192, rows), bf16),
                pltpu.VMEM((rows, 576), f32),
                pltpu.VMEM((rows, width), f32),
                pltpu.VMEM((rows, width), f32),
                pltpu.VMEM((3, rows, 128), f32),
            ]
            + (
                [pltpu.VMEM((width, 640), f32), pltpu.VMEM((192, width), f32), pltpu.VMEM((128, width), f32)]
                if last
                else []
            ),
        ),
        out_shape=outs,
        compiler_params=pltpu.CompilerParams(vmem_limit_bytes=56 << 20),
        cost_estimate=pl.CostEstimate(
            flops=24_000_000_000, transcendentals=0, bytes_accessed=15_000_000
        ),
        name="attn",
    )(row_offsets, *parts, *weights, o_own, o_other, vecs, *partials, *extra, *after)


def finish_kernel(half_ref, x_ref, c_ref, own_ref, other_ref, bias, *refs):
    out_ref, grad_ref = refs[-2:]
    f32 = jnp.float32

    def write(source):
        x = x_ref[0].astype(f32)
        normed, inverse = normalize(x)
        out_ref[0] = x + bias[4:5, :] + source[0].astype(f32)
        s = source[1].astype(f32)
        mean_s = jnp.mean(s, axis=-1, keepdims=True)
        mean_sn = jnp.mean(s * normed, axis=-1, keepdims=True)
        grad_ref[0] = c_ref[0] + inverse * (s - mean_s - normed * mean_sn)

    @pl.when(pl.program_id(0) == 0)
    def _():
        write(own_ref)

    @pl.when(pl.program_id(0) == 1)
    def _():
        write(other_ref)


def finish_call(half, seq, x, cot, own, other, bias, done):
    _, rows, width = x.shape
    f32 = jnp.float32
    seq_spec = pl.BlockSpec(
        (1, rows, width), lambda i, at: (jnp.where(i == 0, at[0], 1 - at[0]) * 3 + seq, 0, 0)
    )
    before = list(done) if done is not None else []
    return pl.pallas_call(
        finish_kernel,
        grid_spec=pltpu.PrefetchScalarGridSpec(
            num_scalar_prefetch=1,
            grid=(2,),
            in_specs=[seq_spec, seq_spec, whole(own.shape), whole(other.shape), whole(bias.shape)]
            + [pl.BlockSpec(memory_space=pl.ANY)] * len(before),
            out_specs=[seq_spec, seq_spec],
        ),
        out_shape=[jax.ShapeDtypeStruct(x.shape, f32)] * 2,
        input_output_aliases={6: 0, 7: 1} if before else {},
        name="finish",
    )(half, x, cot, own, other, bias, *before)


def pick(value, index, axis=0):
    return lax.dynamic_index_in_dim(value, index, axis, keepdims=False)


def prep_kernel(at_ref, in_ref, q_ref, small_ref, own_ref, send_ref, pack_s):
    for h in range(4):
        parts = [in_ref[:, zy * 384 + h * 96 : zy * 384 + (h + 1) * 96] for zy in range(8)]
        for head in range(3):
            for kind in range(2):
                first = kind * 768 + h * 192 + head * 64
                parts.append(q_ref[:, first : first + 64])
        first = 1536 + h * 192
        parts.append(q_ref[:, first : first + 192])
        parts.append(small_ref[...])
        at = 0
        for part in parts:
            pack_s[h, :, at : at + part.shape[1]] = part
            at += part.shape[1]
    for core in range(2):
        own_ref[core] = pack_s[at_ref[26] * 2 + core]
        send_ref[core] = pack_s[(1 - at_ref[26]) * 2 + core]


def prep_call(row_offsets, w_in, w_qkv, small):
    half = jax.ShapeDtypeStruct((2, 24, 1408), jnp.bfloat16)
    return pl.pallas_call(
        prep_kernel,
        grid_spec=pltpu.PrefetchScalarGridSpec(
            num_scalar_prefetch=1,
            grid=(1,),
            in_specs=[whole(a.shape) for a in (w_in, w_qkv, small)],
            out_specs=[whole(half.shape)] * 2,
            scratch_shapes=[pltpu.VMEM((4, 24, 1408), jnp.bfloat16)],
        ),
        out_shape=[half, half],
        name="prep",
    )(row_offsets, w_in, w_qkv, small)


def join_kernel(at_ref, own_ref, got_ref, far_ref, down_ref, out_ref, attn_ref, mlp_ref, four, rows_s, cols_s):
    f32, bf16 = jnp.float32, jnp.bfloat16
    x, c = at_ref[26], at_ref[27]
    four[0] = own_ref[c].astype(f32)
    four[1] = got_ref[c].astype(f32)
    four[2] = far_ref[0].astype(f32)
    four[3] = far_ref[1].astype(f32)
    for source in range(4):
        near = ((source & 1) ^ c) * 2 + ((source >> 1) ^ x)
        rows_s[source * 24 : (source + 1) * 24, :] = four[near]
        cols_s[source * 24 : (source + 1) * 24, :] = out_ref[:, source * 192 : (source + 1) * 192].astype(f32)
    mlp_ref[:96, :] = rows_s[:, :768].astype(bf16)
    mlp_ref[96:, :] = down_ref[...]
    attn_ref[:, :640] = rows_s[:, 768:].astype(bf16)
    attn_ref[:, 640:] = cols_s[...].astype(bf16)


def join_call(row_offsets, own, got, far, w_down, w_out):
    f32, bf16 = jnp.float32, jnp.bfloat16
    outs = [jax.ShapeDtypeStruct((96, 832), bf16), jax.ShapeDtypeStruct((192, 768), bf16)]
    return pl.pallas_call(
        join_kernel,
        grid_spec=pltpu.PrefetchScalarGridSpec(
            num_scalar_prefetch=1,
            grid=(1,),
            in_specs=[whole(a.shape) for a in (own, got, far, w_down, w_out)],
            out_specs=[whole(a.shape) for a in outs],
            scratch_shapes=[
                pltpu.VMEM((4, 24, 1408), f32), pltpu.VMEM((96, 1408), f32), pltpu.VMEM((96, 192), f32)
            ],
        ),
        out_shape=outs,
        name="join",
    )(row_offsets, own, got, far, w_down, w_out)


def pick_out_kernel(at_ref, one, two, three, four, own_ref, send_ref, all_s):
    for at, source in enumerate((one, two, three, four)):
        all_s[at] = source[:, 640:]
    for core in range(2):
        own_ref[core] = all_s[(at_ref[28] - at_ref[26] * 2 - core + 4) % 4]
        send_ref[core] = all_s[(at_ref[28] - (1 - at_ref[26]) * 2 - core + 4) % 4]


def pick_out_call(row_offsets, pieces):
    half = jax.ShapeDtypeStruct((2, 96, 192), jnp.bfloat16)
    return pl.pallas_call(
        pick_out_kernel,
        grid_spec=pltpu.PrefetchScalarGridSpec(
            num_scalar_prefetch=1,
            grid=(1,),
            in_specs=[whole((96, 832))] * 4,
            out_specs=[whole(half.shape)] * 2,
            scratch_shapes=[pltpu.VMEM((4, 96, 192), jnp.bfloat16)],
        ),
        out_shape=[half, half],
        name="pick_out",
    )(row_offsets, *pieces)


def join_out_kernel(at_ref, own_ref, got_ref, far_ref, out_ref, four, rows_s):
    f32, bf16 = jnp.float32, jnp.bfloat16
    x, c = at_ref[26], at_ref[27]
    four[0] = own_ref[c].astype(f32)
    four[1] = got_ref[c].astype(f32)
    four[2] = far_ref[0].astype(f32)
    four[3] = far_ref[1].astype(f32)
    for source in range(4):
        near = ((source & 1) ^ c) * 2 + ((source >> 1) ^ x)
        for group in range(4):
            rows_s[source * 24 : (source + 1) * 24, group * 192 : (group + 1) * 192] = four[
                near, group * 24 : (group + 1) * 24, :
            ]
    out_ref[...] = rows_s[...].astype(bf16)


def join_out_call(row_offsets, own, got, far):
    f32, bf16 = jnp.float32, jnp.bfloat16
    return pl.pallas_call(
        join_out_kernel,
        grid_spec=pltpu.PrefetchScalarGridSpec(
            num_scalar_prefetch=1,
            grid=(1,),
            in_specs=[whole(a.shape) for a in (own, got, far)],
            out_specs=whole((96, 768)),
            scratch_shapes=[pltpu.VMEM((4, 96, 192), f32), pltpu.VMEM((96, 768), f32)],
        ),
        out_shape=jax.ShapeDtypeStruct((96, 768), bf16),
        name="join_out",
    )(row_offsets, own, got, far)


def vector_tables():
    row = np.arange(768)
    at_q = np.stack([(row // 24) * 72 + third * 24 + row % 24 for third in range(3)], axis=1)
    at_in = np.stack([(row // 24) * 96 + third * 24 + row % 24 for third in range(4)], axis=1)
    lane = np.arange(576)
    head, kind = lane // 128, (lane % 128) // 64
    col_q = np.where(lane < 384, kind * 768 + head * 64 + lane % 64, 1536 + lane - 384)
    col_in = (row // 96) * 384 + row % 96
    cols = np.zeros((8, 768), np.int32)
    cols[0, :576] = col_q
    cols[1] = col_in
    rows = np.concatenate([at_q, at_in, np.zeros((768, 1))], axis=1).astype(np.int32)
    return rows, cols


def vec_kernel(at_ref, *refs):
    refs = list(refs)
    pieces = [refs.pop(0) for _ in range(8)]
    rows_ref, cols_ref, out_ref, all_s = refs
    f32 = jnp.float32
    for at, source in enumerate(pieces):
        rows = pl.ds(pl.multiple_of(at_ref[at], 16), 96)
        all_s[rows, :] = source[...].astype(f32)
    flipped = jnp.transpose(all_s[...])
    out_ref[0:4, :] = flipped[64:68]
    out_ref[4:5, :] = flipped[68:69] + flipped[69:70]
    for row, kinds, target, width, step in ((5, (0, 1, 2), 0, 576, 192), (6, (3, 4, 5, 6), 1, 768, 96)):
        wanted = cols_ref[target : target + 1, :width] + at_ref[25] * step
        total = jnp.zeros((1, width), f32)
        for kind in kinds:
            hit = rows_ref[:, kind : kind + 1] == wanted
            total += col_sum(jnp.where(hit, all_s[:, 70 + kind : 71 + kind], 0.0))
        out_ref[row : row + 1, :width] = total
    out_ref[7:8, :] = jnp.zeros((1, 768), f32)
    out_ref[5:6, 576:] = jnp.zeros((1, 192), f32)


def vec_call(row_offsets, pieces, rows, cols):
    f32 = jnp.float32
    return pl.pallas_call(
        vec_kernel,
        grid_spec=pltpu.PrefetchScalarGridSpec(
            num_scalar_prefetch=1,
            grid=(1,),
            in_specs=[pl.BlockSpec((96, 128), lambda i, *_: (0, 4))] * 8
            + [whole(rows.shape), whole(cols.shape)],
            out_specs=whole((8, 768)),
            scratch_shapes=[pltpu.VMEM((768, 128), f32)],
        ),
        out_shape=jax.ShapeDtypeStruct((8, 768), f32),
        name="vectors",
    )(row_offsets, *pieces, rows, cols)


def spread_q_kernel(blocks_ref, q_ref, *out_refs):
    f32 = jnp.float32
    total = None
    for h in range(4):
        block = blocks_ref[h].astype(f32)
        for head in range(3):
            for kind in range(2):
                first = kind * 768 + h * 192 + head * 64
                at = head * 128 + kind * 64
                q_ref[:, first : first + 64] = block[:, at : at + 64]
        first = 1536 + h * 192
        q_ref[:, first : first + 192] = block[:, 384:576]
        part = block[:, 576:584]
        total = part if total is None else total + part
    same = lax.broadcasted_iota(jnp.int32, (24, 24), 0) == lax.broadcasted_iota(jnp.int32, (24, 24), 1)
    rows = [col_sum(jnp.where(same, total[:, t : t + 1], 0.0)) for t in range(8)]
    for t in range(5):
        out_refs[t][...] = rows[t]
    out_refs[5][...] = jnp.concatenate(rows[5:], axis=1)


def spread_q_call(blocks):
    f32 = jnp.float32
    shapes = [(24, 2304)] + [(1, 24)] * 5 + [(1, 72)]
    return pl.pallas_call(
        spread_q_kernel,
        out_shape=[jax.ShapeDtypeStruct(shape, f32) for shape in shapes],
        name="spread_q",
    )(blocks)


def spread_in_kernel(blocks_ref, in_ref):
    for h in range(4):
        block = blocks_ref[h].astype(jnp.float32)
        for zy in range(8):
            first = zy * 384 + h * 96
            in_ref[:, first : first + 96] = block[:, zy * 96 : (zy + 1) * 96]


def spread_in_call(blocks):
    return pl.pallas_call(
        spread_in_kernel,
        out_shape=jax.ShapeDtypeStruct((24, 3072), jnp.float32),
        name="spread_in",
    )(blocks)


def exchange_four(blocks, x, c):
    blocks = blocks.reshape((2, 2) + blocks.shape[1:])
    own = pick(blocks, x)
    got = swap(pick(blocks, 1 - x), 2)
    both = jnp.stack([own, got])
    mine = pick(both, c, 1)
    theirs = swap(pick(both, 1 - c, 1), 1)
    mine = jnp.where(x == 0, mine, mine[::-1])
    theirs = jnp.where(x == 0, theirs, theirs[::-1])
    pairs = jnp.where(
        c == 0, jnp.stack([mine, theirs], axis=1), jnp.stack([theirs, mine], axis=1)
    )
    return pairs.reshape((4,) + pairs.shape[2:])


def fast(*args):
    return fast_body(*args)


def fast_body(
    inputs, cotangent, ln1_gain, ln1_bias, ln2_gain, ln2_bias, w_qkv, b_qkv, w_out, b_out, w_in, b_in, w_mlp_out, b_mlp_out
):
    f32, bf16 = jnp.float32, jnp.bfloat16
    z = lax.axis_index("fsdp")
    ctx = lax.axis_index("ctx")
    y, x, c = ctx // 4, (ctx // 2) % 2, ctx % 2
    h = ctx % 4

    zs = jnp.stack([(z - k) % 4 for k in range(4)])
    rows_w = jnp.concatenate([(zs * 2 + y) * 96, (zs * 2 + 1 - y) * 96])
    rows_o = jnp.stack([y * 96, (1 - y) * 96])
    rows_p = jnp.stack([(ctx ^ piece_bits(k)) * ROWS for k in range(8)])
    row_offsets = jnp.concatenate(
        [rows_w, rows_o, jnp.zeros((6,), jnp.int32), rows_p, jnp.stack([y, h, x, c, z])]
    ).astype(jnp.int32)

    small = jnp.concatenate(
        [ln1_gain, ln1_bias, ln2_gain, ln2_bias, b_out, b_mlp_out, b_qkv, b_in, jnp.zeros((51 * 24,), bf16)]
    ).reshape(64, 24).T
    pack_own, pack_send = prep_call(row_offsets, w_in, w_qkv, small)

    def rows_of(half, first, count):
        at = half * 3 + first
        return jnp.stack(
            [
                lax.dynamic_slice_in_dim(inputs, at, count),
                lax.dynamic_slice_in_dim(cotangent, at, count).astype(bf16),
            ]
        )

    parts = []
    first = 0
    for count in CHUNKS:
        got = swap(rows_of(1 - y, first, count), 4)
        two = jnp.stack([rows_of(y, first, count), got])
        side = swap(two, 2)
        parts.append((two, side, swap(two, 1), swap(side, 1)))
        first += count

    pack_got = swap(pack_send, 2)
    pack_far = swap(jnp.stack([pick(pack_own, 1 - c), pick(pack_got, 1 - c)]), 1)
    attn_w, mlp_w = join_call(row_offsets, pack_own, pack_got, pack_far, w_mlp_out, w_out)
    attn_own = [attn_w] + [shift_z(attn_w, k) for k in (1, 2, 3)]
    mlp_own = [mlp_w] + [shift_z(mlp_w, k) for k in (1, 2, 3)]
    attn_all = attn_own + [swap(part, 4) for part in attn_own]
    mlp_all = mlp_own + [swap(part, 4) for part in mlp_own]
    out_mine, out_send = pick_out_call(row_offsets, attn_own)
    out_got = swap(out_send, 2)
    out_far = swap(jnp.stack([pick(out_mine, 1 - c), pick(out_got, 1 - c)]), 1)
    out_own = join_out_call(row_offsets, out_mine, out_got, out_far)
    out_other = swap(out_own, 4)
    at_rows, at_cols = vector_tables()
    vecs = vec_call(row_offsets, attn_all, at_rows, at_cols)

    where = [(at, inside) for at, count in enumerate(CHUNKS) for inside in range(count)]

    def attention(seq, partial, prev, tail=None):
        at, inside = where[seq]
        return attn_call(
            row_offsets, parts[at], inside, attn_all, out_own, out_other,
            vecs, partial, seq, prev, tail,
        )

    def reduce_z(blocks):
        def total(at):
            value = pick(blocks[0], at).astype(f32)
            for block in blocks[1:]:
                value = value + pick(block, at).astype(f32)
            return value

        sent = [shift_z(total((z + k) % 4).astype(bf16), k) for k in (1, 2, 3)]
        result = total(z)
        for part in sent:
            result = result + part.astype(f32)
        return result

    half = jnp.reshape(y, (1,)).astype(jnp.int32)

    def scatter(seq, send, keep, done):
        got = swap(send, 1)
        side = swap((keep[2:].astype(f32) + got[2:].astype(f32)).astype(bf16), 2)
        mine = (keep[0].astype(f32) + got[0].astype(f32) + side[0].astype(f32)).astype(bf16)
        far = (keep[1].astype(f32) + got[1].astype(f32) + side[1].astype(f32)).astype(bf16)
        return finish_call(half, seq, inputs, cotangent, mine, swap(far, 4), vecs, done)

    first_send, first_keep, g_q, g_o, vec = attention(0, None, None)
    prev = (g_q, g_o, vec)
    send, keep, rest_part, g_send, g_keep, mlp_vec = mlp_call(
        row_offsets, parts, mlp_all, vecs, cotangent, first_send, first_keep
    )
    g_got = swap(g_send, 4)
    done = scatter(0, send, keep, None)
    send, keep, g_q, g_o, vec = attention(1, rest_part, prev)
    done = scatter(1, send, keep, done)
    mlp_grad = reduce_z((g_keep, g_got))
    grad_w_mlp = mlp_grad[96:192]
    grad_b_in = mlp_grad[192, :96]
    grad_w_in = spread_in_call(exchange_four(mlp_grad[:96].astype(bf16).reshape(4, 24, 768), x, c))
    send, keep, q_send, q_keep, o_send, o_keep = attention(
        2, rest_part, (g_q, g_o, vec), (mlp_vec, at_rows, at_cols)
    )
    done = scatter(2, send, keep, done)
    q_grad = reduce_z((q_keep, swap(q_send, 4)))
    spread = spread_q_call(exchange_four(q_grad.astype(bf16).reshape(4, 24, 640), x, c))
    grad_w_qkv = spread[0]
    one_gain, one_bias, two_gain, two_bias, grad_bias, grad_bq = [v.reshape(-1) for v in spread[1:]]

    o_parts = o_keep + swap(o_send, 4).astype(f32)
    o_blocks = exchange_four(o_parts.astype(bf16).reshape(4, 24, 768), x, c)
    grad_w_out = reduce_z((o_blocks,))

    outputs, grad_inputs = done
    return (
        outputs,
        grad_inputs,
        one_gain,
        one_bias,
        two_gain,
        two_bias,
        grad_w_qkv,
        grad_bq,
        grad_w_out,
        grad_bias,
        grad_w_in,
        grad_b_in,
        grad_w_mlp,
        grad_bias,
    )


def fast_fits(mesh):
    sizes = dict(mesh.shape)
    return sizes["fsdp"] == 4 and sizes["ctx"] == 8


def solution(mesh):
    return jax.shard_map(
        fast if fast_fits(mesh) else local,
        mesh=mesh,
        in_specs=(
            P("fsdp", "ctx", None),
            P("fsdp", "ctx", None),
            P(("fsdp", "ctx")),
            P(("fsdp", "ctx")),
            P(("fsdp", "ctx")),
            P(("fsdp", "ctx")),
            P(("fsdp", "ctx"), None),
            P(("fsdp", "ctx")),
            P(("fsdp", "ctx"), None),
            P(("fsdp", "ctx")),
            P(("fsdp", "ctx"), None),
            P(("fsdp", "ctx")),
            P(("fsdp", "ctx"), None),
            P(("fsdp", "ctx")),
        ),
        out_specs=(
            P("fsdp", "ctx", None),
            P("fsdp", "ctx", None),
            P(("fsdp", "ctx")),
            P(("fsdp", "ctx")),
            P(("fsdp", "ctx")),
            P(("fsdp", "ctx")),
            P(("fsdp", "ctx"), None),
            P(("fsdp", "ctx")),
            P(("fsdp", "ctx"), None),
            P(("fsdp", "ctx")),
            P(("fsdp", "ctx"), None),
            P(("fsdp", "ctx")),
            P(("fsdp", "ctx"), None),
            P(("fsdp", "ctx")),
        ),
        check_vma=False,
    )
```

```python
import functools
import math

import jax
import jax.numpy as jnp
import numpy as np
from jax import lax
from jax.experimental import pallas as pl
from jax.experimental.pallas import tpu as pltpu
from jax.sharding import PartitionSpec as P


HEADS = 12
HEAD_DIM = 64
ROT_DIM = 16
MICRO = 2
SEQ_MB = 3
CHUNKS = (1, 2)


EPS = 1e-05
BASE_FREQ = 10000.0


def layer_norm(values, gain_row, shift_row):
    centre = jnp.mean(values, axis=-1, keepdims=True)
    centred = values - centre
    inverse = lax.rsqrt(jnp.mean(centred * centred, axis=-1, keepdims=True) + EPS)
    normed = centred * inverse
    return (normed * gain_row + shift_row, normed, inverse)


def norm_back(grad_out, normed, inverse, gain_row):
    scaled = grad_out * gain_row
    return inverse * (
        scaled
        - jnp.mean(scaled, axis=-1, keepdims=True)
        - normed * jnp.mean(scaled * normed, axis=-1, keepdims=True)
    )


def angles(positions):
    half_rot = ROT_DIM // 2
    inv_freq = BASE_FREQ ** (-(2.0 * jnp.arange(half_rot, dtype=jnp.float32)) / ROT_DIM)
    phase_angle = positions.astype(jnp.float32)[:, None] * inv_freq[None, :]
    return (jnp.cos(phase_angle), jnp.sin(phase_angle))


def rotate(head_field, cosine, sine_rot, direction):
    half_rot = ROT_DIM // 2
    lead_half = head_field[..., :half_rot]
    trail_half = head_field[..., half_rot:ROT_DIM]
    cos_wide = cosine[:, None, :]
    sin_wide = direction * sine_rot[:, None, :]
    return jnp.concatenate(
        [
            lead_half * cos_wide - trail_half * sin_wide,
            trail_half * cos_wide + lead_half * sin_wide,
            head_field[..., ROT_DIM:],
        ],
        axis=-1,
    )


def gelu_parts(pre_act):
    normal_cdf = 0.5 * (1.0 + jax.scipy.special.erf(pre_act * 0.7071067811865476))
    density = jnp.exp(-0.5 * pre_act * pre_act) * 0.3989422804014327
    return (pre_act * normal_cdf, normal_cdf + pre_act * density)


def outer_rows(left, right):
    return lax.dot_general(
        left, right, (((0,), (0,)), ((), ())), preferred_element_type=jnp.float32
    )


def times_transpose(left, right):
    return lax.dot_general(
        left, right, (((1,), (1,)), ((), ())), preferred_element_type=jnp.float32
    )


def attend_block(soft_state, kv_block, first_row, query_low, positions, score_scale):
    run_max, run_sum, weighted = soft_state
    seq_count, block_rows, double_width = kv_block.shape
    model_width = double_width // 2
    key_low = kv_block[..., :model_width].reshape(seq_count, block_rows, HEADS, HEAD_DIM)
    value_low = kv_block[..., model_width:].reshape(seq_count, block_rows, HEADS, HEAD_DIM)
    scores = (
        jnp.einsum("sqhd,skhd->shqk", query_low, key_low, preferred_element_type=jnp.float32)
        * score_scale
    )
    allowed = (first_row + jnp.arange(block_rows, dtype=jnp.int32))[None, :] <= positions[:, None]
    scores = jnp.where(allowed, scores, -jnp.inf)
    new_max = jnp.maximum(run_max, jnp.max(scores, axis=-1))
    safe_max = jnp.where(new_max == -jnp.inf, 0.0, new_max)
    exp_scores = jnp.exp(scores - safe_max[..., None])
    factor = jnp.exp(run_max - safe_max)
    run_sum = run_sum * factor + jnp.sum(exp_scores, axis=-1)
    weighted = weighted * factor[..., None] + jnp.einsum(
        "shqk,skhd->shqd",
        exp_scores.astype(jnp.bfloat16),
        value_low,
        preferred_element_type=jnp.float32,
    )
    return (new_max, run_sum, weighted)


def attend_piece(soft_state, kv_piece, query_low, positions, score_scale):
    piece_rows = kv_piece.shape[1]
    step_rows = math.gcd(piece_rows, 512)

    def one_block(block_index, inner_state):
        offset = block_index * step_rows
        kv_block = lax.dynamic_slice_in_dim(kv_piece, offset, step_rows, 1)
        return attend_block(inner_state, kv_block, offset, query_low, positions, score_scale)

    return lax.fori_loop(0, piece_rows // step_rows, one_block, soft_state)


def local(
    inputs,
    cotangent,
    ln1_gain,
    ln1_bias,
    ln2_gain,
    ln2_bias,
    w_qkv,
    b_qkv,
    w_out,
    b_out,
    w_in,
    b_in,
    w_mlp_out,
    b_mlp_out,
):
    f32 = jnp.float32
    bf16 = jnp.bfloat16
    group_rows = inputs.shape[1]
    model_width = inputs.shape[2]
    seq_len = group_rows * lax.axis_size("ctx")
    key_block = math.gcd(seq_len, 512)
    score_scale = HEAD_DIM ** (-0.5)
    positions = lax.axis_index("ctx") * group_rows + jnp.arange(group_rows, dtype=jnp.int32)
    cosine, sine_rot = angles(positions)

    def gather_params():
        return (
            lax.all_gather(ln1_gain, ("fsdp", "ctx"), axis=0, tiled=True),
            lax.all_gather(ln1_bias, ("fsdp", "ctx"), axis=0, tiled=True),
            lax.all_gather(ln2_gain, ("fsdp", "ctx"), axis=0, tiled=True),
            lax.all_gather(ln2_bias, ("fsdp", "ctx"), axis=0, tiled=True),
            lax.all_gather(w_qkv, ("fsdp", "ctx"), axis=0, tiled=True),
            lax.all_gather(b_qkv, ("fsdp", "ctx"), axis=0, tiled=True),
            lax.all_gather(w_out, ("fsdp", "ctx"), axis=0, tiled=True),
            lax.all_gather(b_out, ("fsdp", "ctx"), axis=0, tiled=True),
            lax.all_gather(w_in, ("fsdp", "ctx"), axis=0, tiled=True),
            lax.all_gather(b_in, ("fsdp", "ctx"), axis=0, tiled=True),
            lax.all_gather(w_mlp_out, ("fsdp", "ctx"), axis=0, tiled=True),
            lax.all_gather(b_mlp_out, ("fsdp", "ctx"), axis=0, tiled=True),
        )

    weight_sums = None
    output_list = []
    grad_list = []
    for micro_index in range(MICRO):
        batch_rows = inputs[micro_index * SEQ_MB : (micro_index + 1) * SEQ_MB]
        cot_rows = cotangent[micro_index * SEQ_MB : (micro_index + 1) * SEQ_MB]
        seq_count = batch_rows.shape[0]
        flat_rows = seq_count * group_rows
        params_fwd = gather_params()
        (
            gain_one,
            shift_one,
            gain_two,
            shift_two,
            weight_qkv,
            bias_qkv,
            weight_out,
            bias_out,
            weight_in,
            bias_in,
            weight_mlp,
            bias_mlp,
        ) = params_fwd
        residual = batch_rows.reshape(flat_rows, model_width).astype(f32)
        normal_one, normed_one, inverse_one = layer_norm(
            residual, gain_one.astype(f32), shift_one.astype(f32)
        )
        normal_two, normed_two, inverse_two = layer_norm(
            residual, gain_two.astype(f32), shift_two.astype(f32)
        )
        hidden_one = normal_one.astype(bf16)
        hidden_two = normal_two.astype(bf16)
        project = jnp.dot(hidden_one, weight_qkv, preferred_element_type=f32) + bias_qkv.astype(f32)
        head_shape = (seq_count, group_rows, HEADS, HEAD_DIM)
        query_low = rotate(
            project[:, :model_width].reshape(head_shape), cosine, sine_rot, 1.0
        ).astype(bf16)
        key_low = rotate(
            project[:, model_width : 2 * model_width].reshape(head_shape), cosine, sine_rot, 1.0
        ).astype(bf16)
        value_low = project[:, 2 * model_width :].astype(bf16)
        kv_pack = jnp.concatenate(
            [
                key_low.reshape(seq_count, group_rows, model_width),
                value_low.reshape(seq_count, group_rows, model_width),
            ],
            axis=-1,
        )
        start_state = (
            jnp.full((seq_count, HEADS, group_rows), -jnp.inf, f32),
            jnp.zeros((seq_count, HEADS, group_rows), f32),
            jnp.zeros((seq_count, HEADS, group_rows, HEAD_DIM), f32),
        )
        soft_state = attend_piece(
            start_state,
            lax.all_gather(kv_pack, "ctx", axis=1, tiled=True),
            query_low,
            positions,
            score_scale,
        )
        run_max, run_sum, weighted = soft_state
        log_total = run_max + jnp.log(run_sum)
        attended = jnp.transpose(weighted / run_sum[..., None], (0, 2, 1, 3)).astype(bf16)
        att_flat = attended.reshape(flat_rows, model_width)
        pre_act = jnp.dot(hidden_two, weight_in, preferred_element_type=f32) + bias_in.astype(f32)
        activation_f, gelu_slope = gelu_parts(pre_act)
        activation = activation_f.astype(bf16)
        output = (
            residual
            + jnp.dot(att_flat, weight_out, preferred_element_type=f32)
            + bias_out.astype(f32)
            + jnp.dot(activation, weight_mlp, preferred_element_type=f32)
            + bias_mlp.astype(f32)
        )
        output_list.append(output.reshape(seq_count, group_rows, model_width))
        params_back = gather_params()
        (
            gain_one,
            shift_one,
            gain_two,
            shift_two,
            weight_qkv,
            bias_qkv,
            weight_out,
            bias_out,
            weight_in,
            bias_in,
            weight_mlp,
            bias_mlp,
        ) = params_back
        kv_rows = lax.all_gather(kv_pack, "ctx", axis=1, tiled=True)
        cot_flat = cot_rows.reshape(flat_rows, model_width)
        cot_low = cot_flat.astype(bf16)
        cot_sum = jnp.sum(cot_flat, axis=0)
        grad_w_out = outer_rows(att_flat, cot_low)
        grad_w_mlp = outer_rows(activation, cot_low)
        d_pre = times_transpose(cot_low, weight_mlp) * gelu_slope
        d_pre_low = d_pre.astype(bf16)
        grad_w_in = outer_rows(hidden_two, d_pre_low)
        d_hidden_two = times_transpose(d_pre_low, weight_in)
        grad_att = times_transpose(cot_low, weight_out).astype(bf16).reshape(head_shape)
        row_delta = jnp.einsum("sqhd,sqhd->shq", grad_att, attended, preferred_element_type=f32)

        def back_block(block_index, loop_carry):
            grad_query, buffer = loop_carry
            offset = block_index * key_block
            kv_block = lax.dynamic_slice_in_dim(kv_rows, offset, key_block, 1)
            key_part = kv_block[..., :model_width].reshape(seq_count, key_block, HEADS, HEAD_DIM)
            value_part = kv_block[..., model_width:].reshape(seq_count, key_block, HEADS, HEAD_DIM)
            scores = (
                jnp.einsum("sqhd,skhd->shqk", query_low, key_part, preferred_element_type=f32)
                * score_scale
            )
            allowed = (offset + jnp.arange(key_block, dtype=jnp.int32))[None, :] <= positions[
                :, None
            ]
            prob_block = jnp.where(allowed, jnp.exp(scores - log_total[..., None]), 0.0)
            grad_value = jnp.einsum(
                "shqk,sqhd->skhd", prob_block.astype(bf16), grad_att, preferred_element_type=f32
            )
            grad_prob = jnp.einsum(
                "sqhd,skhd->shqk", grad_att, value_part, preferred_element_type=f32
            )
            grad_score = (prob_block * (grad_prob - row_delta[..., None]) * score_scale).astype(
                bf16
            )
            grad_query = grad_query + jnp.einsum(
                "shqk,skhd->sqhd", grad_score, key_part, preferred_element_type=f32
            )
            grad_key = jnp.einsum(
                "shqk,sqhd->skhd", grad_score, query_low, preferred_element_type=f32
            )
            key_value_grad = jnp.concatenate(
                [
                    grad_key.reshape(seq_count, key_block, model_width),
                    grad_value.reshape(seq_count, key_block, model_width),
                ],
                axis=-1,
            )
            return (grad_query, lax.dynamic_update_slice_in_dim(buffer, key_value_grad, offset, 1))

        start_carry = (
            jnp.zeros(head_shape, f32),
            jnp.zeros((seq_count, seq_len, 2 * model_width), f32),
        )
        grad_query, buffer = lax.fori_loop(0, seq_len // key_block, back_block, start_carry)
        kv_grad_own = lax.psum_scatter(
            buffer.astype(jnp.bfloat16), "ctx", scatter_dimension=1, tiled=True
        ).astype(jnp.float32)
        key_grad_raw = kv_grad_own[..., :model_width].reshape(head_shape)
        value_grad_flat = kv_grad_own[..., model_width:].reshape(flat_rows, model_width)
        grad_query = rotate(grad_query, cosine, sine_rot, -1.0)
        grad_key = rotate(key_grad_raw, cosine, sine_rot, -1.0)
        d_project = jnp.concatenate(
            [
                grad_query.reshape(flat_rows, model_width),
                grad_key.reshape(flat_rows, model_width),
                value_grad_flat,
            ],
            axis=-1,
        )
        d_project_low = d_project.astype(bf16)
        grad_w_qkv = outer_rows(hidden_one, d_project_low)
        d_hidden_one = times_transpose(d_project_low, weight_qkv)
        grad_rows = (
            cot_flat
            + norm_back(d_hidden_one, normed_one, inverse_one, gain_one.astype(f32))
            + norm_back(d_hidden_two, normed_two, inverse_two, gain_two.astype(f32))
        )
        grad_list.append(grad_rows.reshape(seq_count, group_rows, model_width))
        terms = (
            jnp.sum(d_hidden_one * normed_one, axis=0),
            jnp.sum(d_hidden_one, axis=0),
            jnp.sum(d_hidden_two * normed_two, axis=0),
            jnp.sum(d_hidden_two, axis=0),
            grad_w_qkv,
            jnp.sum(d_project, axis=0),
            grad_w_out,
            cot_sum,
            grad_w_in,
            jnp.sum(d_pre, axis=0),
            grad_w_mlp,
            cot_sum,
        )
        if weight_sums is None:
            weight_sums = terms
        else:
            weight_sums = jax.tree.map(lambda total, term: total + term, weight_sums, terms)
    owned = (
        lax.psum_scatter(weight_sums[0], ("fsdp", "ctx"), scatter_dimension=0, tiled=True),
        lax.psum_scatter(weight_sums[1], ("fsdp", "ctx"), scatter_dimension=0, tiled=True),
        lax.psum_scatter(weight_sums[2], ("fsdp", "ctx"), scatter_dimension=0, tiled=True),
        lax.psum_scatter(weight_sums[3], ("fsdp", "ctx"), scatter_dimension=0, tiled=True),
        lax.psum_scatter(weight_sums[4], ("fsdp", "ctx"), scatter_dimension=0, tiled=True),
        lax.psum_scatter(weight_sums[5], ("fsdp", "ctx"), scatter_dimension=0, tiled=True),
        lax.psum_scatter(weight_sums[6], ("fsdp", "ctx"), scatter_dimension=0, tiled=True),
        lax.psum_scatter(weight_sums[7], ("fsdp", "ctx"), scatter_dimension=0, tiled=True),
        lax.psum_scatter(weight_sums[8], ("fsdp", "ctx"), scatter_dimension=0, tiled=True),
        lax.psum_scatter(weight_sums[9], ("fsdp", "ctx"), scatter_dimension=0, tiled=True),
        lax.psum_scatter(weight_sums[10], ("fsdp", "ctx"), scatter_dimension=0, tiled=True),
        lax.psum_scatter(weight_sums[11], ("fsdp", "ctx"), scatter_dimension=0, tiled=True),
    )
    outputs = jnp.concatenate(output_list, axis=0)
    grad_inputs = jnp.concatenate(grad_list, axis=0)
    return (
        outputs,
        grad_inputs,
        owned[0],
        owned[1],
        owned[2],
        owned[3],
        owned[4],
        owned[5],
        owned[6],
        owned[7],
        owned[8],
        owned[9],
        owned[10],
        owned[11],
    )


ROWS = 128
BLOCK = 256


def swap(value, bit):
    return lax.ppermute(value, "ctx", [(i, i ^ bit) for i in range(8)])


def shift_z(value, step):
    return lax.ppermute(value, "fsdp", [(i, (i + step) % 4) for i in range(4)])


def nt(left, right):
    return lax.dot_general(
        left, right, (((1,), (1,)), ((), ())), preferred_element_type=jnp.float32
    )


def nn(left, right):
    return lax.dot_general(
        left, right, (((1,), (0,)), ((), ())), preferred_element_type=jnp.float32
    )


def tn(left, right):
    return lax.dot_general(
        left, right, (((0,), (0,)), ((), ())), preferred_element_type=jnp.float32
    )


def normalize(values):
    centred = values - jnp.mean(values, axis=-1, keepdims=True)
    inverse = lax.rsqrt(jnp.mean(centred * centred, axis=-1, keepdims=True) + EPS)
    return centred * inverse, inverse


def col_sum(values):
    return jnp.sum(values, axis=0, keepdims=True)


def piece_bits(index):
    return ((index & 1) << 2) | (index & 2) | (index >> 2)


def mlp_kernel(chunks, row_ref, *refs):
    refs = list(refs)
    parts = [[refs.pop(0) for _ in range(8)] for _ in chunks]
    weights = [refs.pop(0) for _ in range(8)]
    vecs, cot_ref, first_send, first_keep, first_norm = [refs.pop(0) for _ in range(5)]
    send_ref, keep_ref, rest_ref, norm_ref, gsend_ref, gkeep_ref, vec_ref = [refs.pop(0) for _ in range(7)]
    w_in, w_down, h_s, c_s, act_s, dpre_s, x_n, first_s, part_s, g_in, g_down, seg_s, w_sem, x_sem, p_sem, o_sem = refs
    f32, bf16 = jnp.float32, jnp.bfloat16
    gain, shift, bias = vecs[2:3, :], vecs[3:4, :], vecs[6:7, :]
    where = [(at, inside) for at, count in enumerate(chunks) for inside in range(count)]
    total = len(where)

    weight_copies = []
    for at, source in enumerate(weights):
        rows = pl.ds(pl.multiple_of(row_ref[at], 16), 96)
        for kind, target in ((0, w_in), (1, w_down)):
            weight_copies.append(
                pltpu.make_async_copy(
                    source.at[pl.ds(kind * 96, 96)], target.at[rows], w_sem.at[at * 2 + kind]
                )
            )
    part_copies = []
    for seq, (at, inside) in enumerate(where):
        for piece in range(8):
            rows = pl.ds((seq * 8 + piece) * ROWS, ROWS)
            sem = x_sem.at[(seq * 8 + piece) * 2]
            if seq == 0:
                source_rows = pl.ds(pl.multiple_of(row_ref[16 + piece], ROWS), ROWS)
                part_copies.append(pltpu.make_async_copy(first_norm.at[source_rows], x_n.at[rows], sem))
            else:
                part_copies.append(
                    pltpu.make_async_copy(parts[at][piece].at[0, inside], h_s.at[rows], sem)
                )
            part_copies.append(
                pltpu.make_async_copy(
                    parts[at][piece].at[1, inside], c_s.at[rows], x_sem.at[(seq * 8 + piece) * 2 + 1]
                )
            )
    norm_copies = [
        pltpu.make_async_copy(x_n.at[pl.ds(seq * 1024, 1024)], norm_ref.at[seq - 1], o_sem.at[total + seq])
        for seq in range(1, total)
    ]
    first_copies = [
        pltpu.make_async_copy(first_keep, first_s.at[pl.ds(0, 4)], p_sem.at[0]),
        pltpu.make_async_copy(first_send, first_s.at[pl.ds(4, 4)], p_sem.at[1]),
    ]
    out_copies = [
        pltpu.make_async_copy(part_s.at[0, pl.ds(0, 4)], keep_ref, o_sem.at[0]),
        pltpu.make_async_copy(part_s.at[0, pl.ds(4, 4)], send_ref, o_sem.at[1]),
    ] + [
        pltpu.make_async_copy(part_s.at[seq % 2], rest_ref.at[seq - 1], o_sem.at[seq + 1])
        for seq in range(1, total)
    ]
    for copy in part_copies[:16] + weight_copies + first_copies + part_copies[16:]:
        copy.start()
    vec_ref[...] = jnp.zeros_like(vec_ref)
    for seq in range(2 * total):
        vec_ref[3:4, :] += col_sum(cot_ref[seq])

    def norm_rows(first):
        for at in range(0, 256, 16):
            rows = slice(first + at, first + at + 16)
            normed, _ = normalize(h_s[rows, :].astype(f32))
            x_n[rows, :] = normed
            h_s[rows, :] = (normed * gain + shift).astype(bf16)

    for seq in range(total):
        rows = slice(seq * 1024, (seq + 1) * 1024)
        if seq == 0:
            for copy in part_copies[:16]:
                copy.wait()
            h_s[rows, :] = (x_n[rows, :] * gain + shift).astype(bf16)
            for copy in weight_copies:
                copy.wait()
        for cols in (slice(0, 512), slice(512, 768)):
            pre = nn(h_s[rows, :], w_in[:, cols]) + bias[:, cols]
            d_act = nt(c_s[rows, :], w_down[cols, :])
            cdf = 0.5 * (1.0 + lax.erf(pre * 0.7071067811865476))
            density = jnp.exp(-0.5 * pre * pre) * 0.3989422804014327
            act_s[rows, cols] = (pre * cdf).astype(bf16)
            d_pre = d_act * (cdf + pre * density)
            dpre_s[rows, cols] = d_pre.astype(bf16)
            vec_ref[0:1, cols] += col_sum(d_pre)
        if seq + 1 < total:
            for copy in part_copies[seq * 16 + 16 : seq * 16 + 32]:
                copy.wait()
        if seq == 0:
            for copy in first_copies:
                copy.wait()
        if seq == 2:
            out_copies[0].wait()
            out_copies[1].wait()
        for block in range(4):
            part_rows = slice(seq * 1024 + block * 256, seq * 1024 + (block + 1) * 256)
            out = nn(act_s[part_rows, :], w_down[...])
            d_hidden = nt(dpre_s[part_rows, :], w_in[...])
            if seq + 1 < total:
                norm_rows((seq + 1) * 1024 + block * 256)
            vec_ref[1:2, :] += col_sum(d_hidden * x_n[part_rows, :])
            vec_ref[2:3, :] += col_sum(d_hidden)
            for kind, value in ((0, out), (1, d_hidden * gain)):
                for half in range(2):
                    piece = block * 2 + half
                    part = value[half * ROWS : (half + 1) * ROWS]
                    if seq == 0:
                        part = part + first_s[piece, kind].astype(f32)
                    part_s[seq % 2, piece, kind] = part.astype(bf16)
        if seq + 1 < total:
            norm_copies[seq].start()
        if seq == 0:
            out_copies[0].start()
            out_copies[1].start()
        else:
            out_copies[seq + 1].start()

    g_in[...] = tn(h_s[...], dpre_s[...])
    g_down[...] = tn(act_s[...], c_s[...])
    for at in range(8):
        seg_s[at, :, :96] = jnp.broadcast_to(vec_ref[0:1, at * 96 : (at + 1) * 96], (16, 96))
    for half, target in ((0, gkeep_ref), (1, gsend_ref)):
        for zz in range(4):
            at = zz * 2 + (row_ref[24] ^ half)
            rows = pl.ds(pl.multiple_of(at * 96, 16), 96)
            target[zz, :96, :] = g_in[rows, :].astype(target.dtype)
            target[zz, 96:192, :] = g_down[rows, :].astype(target.dtype)
            target[zz, 192:, :] = jnp.zeros((16, 768), target.dtype)
            target[zz, 192:, :96] = seg_s[at, :, :96].astype(target.dtype)
    for copy in out_copies[2:] + norm_copies:
        copy.wait()


def whole(shape):
    return pl.BlockSpec(shape, lambda *_: (0,) * len(shape))


def mlp_call(row_offsets, parts, weights, vecs, cot, first_send, first_keep, first_norm):
    chunks = tuple(part[0].shape[1] for part in parts)
    total = sum(chunks)
    width = vecs.shape[-1]
    f32, bf16 = jnp.float32, jnp.bfloat16

    anywhere = pl.BlockSpec(memory_space=pl.ANY)
    dma = pltpu.SemaphoreType.DMA
    rows = total * 8 * ROWS
    half = (4, 2, ROWS, width)
    grads = (4, 208, width)
    return pl.pallas_call(
        functools.partial(mlp_kernel, chunks),
        grid_spec=pltpu.PrefetchScalarGridSpec(
            num_scalar_prefetch=1,
            grid=(1,),
            in_specs=[anywhere] * (8 * len(parts) + 8)
            + [whole(vecs.shape), whole(cot.shape)]
            + [anywhere] * 3,
            out_specs=[anywhere] * 4 + [whole(grads), whole(grads), whole((8, width))],
            scratch_shapes=[pltpu.VMEM((width, width), bf16)] * 2
            + [pltpu.VMEM((rows, width), bf16)] * 4
            + [pltpu.VMEM((rows, width), f32)]
            + [pltpu.VMEM((8, 2, ROWS, width), bf16), pltpu.VMEM((2, 8, 2, ROWS, width), bf16)]
            + [pltpu.VMEM((width, width), f32)] * 2
            + [pltpu.VMEM((8, 16, 128), f32)]
            + [dma((16,)), dma((total * 16,)), dma((2,)), dma((2 * total,))],
        ),
        out_shape=[
            jax.ShapeDtypeStruct(half, bf16),
            jax.ShapeDtypeStruct(half, bf16),
            jax.ShapeDtypeStruct((total - 1, 8, 2, ROWS, width), bf16),
            jax.ShapeDtypeStruct((total - 1, 8 * ROWS, width), f32),
            jax.ShapeDtypeStruct(grads, bf16),
            jax.ShapeDtypeStruct(grads, f32),
            jax.ShapeDtypeStruct((8, width), f32),
        ],
        compiler_params=pltpu.CompilerParams(vmem_limit_bytes=58 << 20),
        cost_estimate=pl.CostEstimate(
            flops=30_000_000_000, transcendentals=0, bytes_accessed=30_000_000
        ),
        name="mlp",
    )(row_offsets, *[a for part in parts for a in part], *weights, vecs, cot, first_send, first_keep, first_norm)


def rotary_tables():
    f32 = jnp.float32
    lane = lax.broadcasted_iota(jnp.int32, (32, 128), 1)
    dim = lane & 63
    power = (dim & 7).astype(f32) * (-2.0 / ROT_DIM)
    freq = jnp.where(dim < ROT_DIM, jnp.exp(power * math.log(BASE_FREQ)), 0.0)
    row = lax.broadcasted_iota(jnp.int32, (32, 128), 0).astype(f32)
    fine, coarse = row * freq, row * 32.0 * freq
    cos_fine, sin_fine = jnp.cos(fine), jnp.sin(fine)
    scale = jnp.where(lane < 64, HEAD_DIM ** (-0.5), 1.0)
    cos_coarse, sin_coarse = jnp.cos(coarse) * scale, jnp.sin(coarse) * scale
    first, second = dim[:1] < 8, (dim[:1] >= 8) & (dim[:1] < ROT_DIM)
    return cos_fine, sin_fine, cos_coarse, sin_coarse, first, second


def attn_kernel(has_prev, last, at_seq, inside, row_ref, *refs):
    refs = list(refs)
    parts = [refs.pop(0) for _ in range(8)]
    weights = [refs.pop(0) for _ in range(8)]
    o_own, o_other, vecs = [refs.pop(0) for _ in range(3)]
    if has_prev:
        partial, norm_ref, pq_ref, po_ref, pv_ref = [refs.pop(0) for _ in range(5)]
    if last:
        mv_ref, at_ref, col_ref = [refs.pop(0) for _ in range(3)]
        send_ref, keep_ref, qsend_ref, qkeep_ref, osend_ref, okeep_ref = [refs.pop(0) for _ in range(6)]
    else:
        send_ref, keep_ref, gq_ref, go_ref, vec_ref = [refs.pop(0) for _ in range(5)]
    if not has_prev:
        norm_out_ref = refs.pop(0)
    wq, wo, x_s, c_s, x_n, h_s = [refs.pop(0) for _ in range(6)]
    q_s, k_s, v_s, g_s, kt_s, vt_s, gt_s = [refs.pop(0) for _ in range(7)]
    dq_s, dk_s, dv_s, at_s, att_s, dp_s, res_s, tab = [refs.pop(0) for _ in range(8)]
    w_sem, x_sem, r_sem = [refs.pop(0) for _ in range(3)]
    if has_prev:
        pp_s, pq_s, po_s, p_sem = [refs.pop(0) for _ in range(4)]
    f32, bf16 = jnp.float32, jnp.bfloat16
    seq = 8 * ROWS
    blocks = seq // BLOCK
    gain, shift, bias = vecs[0:1, :], vecs[1:2, :], vecs[5:6, :640]

    def place(piece):
        return pl.ds(pl.multiple_of(row_ref[16 + piece], ROWS), ROWS)

    weight_copies = [
        pltpu.make_async_copy(
            source.at[:, pl.ds(0, 640)],
            wq.at[pl.ds(pl.multiple_of(row_ref[at], 16), 96)],
            w_sem.at[at],
        )
        for at, source in enumerate(weights)
    ]
    out_weight_copies = [
        pltpu.make_async_copy(
            source, wo.at[pl.ds(pl.multiple_of(row_ref[8 + at], 16), 96)], w_sem.at[8 + at]
        )
        for at, source in enumerate((o_own, o_other))
    ]
    part_copies = [
        [
            pltpu.make_async_copy(
                parts[piece].at[kind, inside], target.at[place(piece)], x_sem.at[kind * 8 + piece]
            )
            for piece in range(8)
        ]
        for kind, target in (((1, c_s),) if has_prev else ((0, x_s), (1, c_s)))
    ]
    if has_prev:
        norm_part_copies = [
            pltpu.make_async_copy(
                norm_ref.at[at_seq - 1, pl.ds(piece * ROWS, ROWS)], x_n.at[place(piece)], x_sem.at[piece]
            )
            for piece in range(8)
        ]
        part_copies.insert(0, norm_part_copies)
    for copy in part_copies[0] + weight_copies + part_copies[1] + out_weight_copies:
        copy.start()
    if has_prev:
        prev_copies = [
            pltpu.make_async_copy(
                partial.at[at_seq - 1, piece, kind], pp_s.at[kind, place(piece)], p_sem.at[kind * 8 + piece]
            )
            for piece in range(8)
            for kind in range(2)
        ]
        prev_copies.append(pltpu.make_async_copy(pq_ref, pq_s, p_sem.at[16]))
        prev_copies.append(pltpu.make_async_copy(po_ref, po_s, p_sem.at[17]))
        for copy in prev_copies:
            copy.start()

    wo[192:, :] = jnp.zeros((64, 768), bf16)
    cos_f, sin_f, cos_c, sin_c, first, second = rotary_tables()
    for at in range(seq // 32):
        rows = slice(at * 32, (at + 1) * 32)
        cosine = cos_f * cos_c[at : at + 1] - sin_f * sin_c[at : at + 1]
        sine = sin_f * cos_c[at : at + 1] + cos_f * sin_c[at : at + 1]
        tab[0, rows, :] = cosine
        tab[1, rows, :] = jnp.where(first, -sine, 0.0)
        tab[2, rows, :] = jnp.where(second, sine, 0.0)

    lane = lax.broadcasted_iota(jnp.int32, (256, 128), 1)
    left = lane < 64

    def heads_of(block, project, grad):
        rows = slice(block * 256, (block + 1) * 256)
        cosine, low, high = tab[0, rows, :], tab[1, rows, :], tab[2, rows, :]
        for head in range(3):
            pair = project[:, head * 128 : (head + 1) * 128]
            pair = pair * cosine + pltpu.roll(pair, 120, 1) * low + pltpu.roll(pair, 8, 1) * high
            k_s[head, rows, :] = jnp.where(left, 0.0, pair).astype(bf16)
            q_s[head, rows, :] = jnp.where(left, 0.0, pltpu.roll(pair, 64, 1)).astype(bf16)
            kt_s[head, :, rows] = jnp.transpose(pair)[64:].astype(bf16)
        v_pair, v_last = project[:, 384:512], jnp.where(left, project[:, 512:640], 0.0)
        vt_s[:128, rows] = jnp.transpose(v_pair).astype(bf16)
        vt_s[128:, rows] = jnp.transpose(v_last)[:64].astype(bf16)
        for target, pair_value, last_value in ((v_s, v_pair, v_last), (g_s, grad[:, :128], grad[:, 128:])):
            target[0, rows, :] = jnp.where(left, pair_value, 0.0).astype(bf16)
            target[1, rows, :] = jnp.where(left, 0.0, pair_value).astype(bf16)
            target[2, rows, :] = last_value.astype(bf16)

    for copy in part_copies[0] + weight_copies + part_copies[1] + out_weight_copies:
        copy.wait()
    for block in (1, 3):
        wide = slice((block - 1) * 256, (block + 1) * 256)
        if has_prev:
            h_s[wide, :] = (x_n[wide, :] * gain + shift).astype(bf16)
        else:
            for part in range(32):
                rows = slice((block - 1) * 256 + part * 16, (block - 1) * 256 + (part + 1) * 16)
                normed, _ = normalize(x_s[rows, :].astype(f32))
                x_n[rows, :] = normed
                h_s[rows, :] = (normed * gain + shift).astype(bf16)
        project_wide = nn(h_s[wide, :], wq[...]) + bias
        grad_wide = nt(c_s[wide, :], wo[...])
        gt_s[:, wide] = nt(wo[:192, :], c_s[wide, :]).astype(bf16)
        for half in range(2):
            heads_of(block - 1 + half, project_wide[half * 256 : half * 256 + 256], grad_wide[half * 256 : half * 256 + 256])

    allowed = lax.broadcasted_iota(jnp.int32, (BLOCK, BLOCK), 0) <= lax.broadcasted_iota(
        jnp.int32, (BLOCK, BLOCK), 1
    )

    def rows_of(block):
        return slice(block * BLOCK, (block + 1) * BLOCK)

    def scores_of(head, block):
        query, grad = q_s[head, rows_of(block), :], g_s[head, rows_of(block), :]
        upto = (block + 1) * BLOCK
        scores = nt(k_s[head, :upto, :], query)
        scores = [scores[rows_of(at)] for at in range(block + 1)]
        scores[block] = jnp.where(allowed, scores[block], -1e30)
        d_prob = nt(v_s[head, :upto, :], grad)
        return scores, [d_prob[rows_of(at)] for at in range(block + 1)]

    def softmax_of(scores):
        top = jnp.max(scores[0], axis=0, keepdims=True)
        for part in scores[1:]:
            top = jnp.maximum(top, jnp.max(part, axis=0, keepdims=True))
        probs = [jnp.exp(part - top) for part in scores]
        total = col_sum(probs[0])
        for part in probs[1:]:
            total = total + col_sum(part)
        scale = 1.0 / total
        probs = [part * scale for part in probs]
        return probs, [part.astype(bf16) for part in probs]

    def values_of(head, block, probs, lows, d_prob):
        rows, upto = rows_of(block), (block + 1) * BLOCK
        low = jnp.concatenate(lows, axis=0) if block else lows[0]
        att_t = nn(vt_s[head * 64 : (head + 1) * 64, :upto], low)
        att_low = att_t.astype(bf16)
        att_s[head * 64 : (head + 1) * 64, rows] = att_low
        d_value = nn(low, g_s[head, rows, :])
        into = head // 2
        keep = slice(0, upto if head == 1 else upto - BLOCK)
        if keep.stop:
            dv_s[into, keep, :] += d_value[keep]
        if head != 1:
            dv_s[into, rows, :] = d_value[upto - BLOCK :]
        delta = col_sum(gt_s[head * 64 : (head + 1) * 64, rows].astype(f32) * att_low.astype(f32))
        return [(p * (d - delta)).astype(bf16) for p, d in zip(probs, d_prob)]

    def grads_of(head, block, d_scores):
        rows, upto = rows_of(block), (block + 1) * BLOCK
        d_score = jnp.concatenate(d_scores, axis=0) if block else d_scores[0]
        d_key = nn(d_score, q_s[head, rows, :])
        if block:
            dk_s[head, : upto - BLOCK, :] += d_key[: upto - BLOCK]
        dk_s[head, rows, :] = d_key[upto - BLOCK :]
        dq_s[head, rows, :64] = jnp.transpose(nn(kt_s[head, :, :upto], d_score))

    order = [(head, block) for block in range(blocks) for head in range(3)]
    ahead = scores_of(*order[0])
    waiting = None
    for at, (head, block) in enumerate(order):
        scores, d_prob = ahead
        if at + 1 < len(order):
            ahead = scores_of(*order[at + 1])
        probs, lows = softmax_of(scores)
        if waiting is not None:
            grads_of(*waiting)
        waiting = (head, block, values_of(head, block, probs, lows, d_prob))
    grads_of(*waiting)

    project_sums = []
    for head in range(3):
        total = jnp.zeros((1, 128), f32)
        for block in range(4):
            rows = slice(block * 256, (block + 1) * 256)
            pair = jnp.concatenate([dq_s[head, rows, :64], dk_s[head, rows, 64:]], axis=1)
            cosine, low, high = tab[0, rows, :], tab[1, rows, :], tab[2, rows, :]
            pair = pair * cosine - pltpu.roll(pair, 120, 1) * low - pltpu.roll(pair, 8, 1) * high
            total = total + col_sum(pair)
            dp_s[rows, head * 128 : (head + 1) * 128] = pair.astype(bf16)
        project_sums.append(total)
    for into in range(2):
        dp_s[:, 384 + into * 128 : 512 + into * 128] = dv_s[into].astype(bf16)
        project_sums.append(col_sum(dv_s[into]))
    if has_prev:
        for copy in prev_copies:
            copy.wait()
    for block in range(4):
        rows = slice(block * 256, (block + 1) * 256)
        at_s[rows, :128] = jnp.transpose(att_s[:128, rows].astype(f32)).astype(bf16)
        at_s[rows, 128:] = jnp.concatenate(
            [jnp.transpose(att_s[128:, rows].astype(f32)), jnp.zeros((256, 64), f32)], axis=1
        ).astype(bf16)
    out = nn(at_s[...], wo[...])
    d_hidden = nt(dp_s[...], wq[...])
    s = d_hidden * gain
    if has_prev:
        out = out + pp_s[0].astype(f32)
        s = s + pp_s[1].astype(f32)
    res_s[0] = out.astype(bf16)
    res_s[1] = s.astype(bf16)
    sums = [
        jnp.concatenate(project_sums, axis=1),
        col_sum(d_hidden * x_n[...]),
        col_sum(d_hidden),
    ]
    result_copies = [
        pltpu.make_async_copy(
            res_s.at[kind, place(piece)],
            (keep_ref if piece < 4 else send_ref).at[piece % 4, kind],
            r_sem.at[piece * 2 + kind],
        )
        for piece in (4, 5, 6, 7, 0, 1, 2, 3)
        for kind in range(2)
    ]
    if not has_prev:
        result_copies.append(pltpu.make_async_copy(x_n, norm_out_ref, r_sem.at[16]))
    for copy in result_copies:
        copy.start()
    g_query = tn(h_s[...], dp_s[...])
    g_out = nn(att_s[...], c_s[...])
    if has_prev:
        g_query = g_query + pq_s[...]
        g_out = g_out + po_s[...]
        sums = [sums[0] + pv_ref[0:1, :640], sums[1] + pv_ref[1:2, :], sums[2] + pv_ref[2:3, :]]
    if last:
        gq_s, go_s, tr_s = refs
        gq_s[...] = g_query
        go_s[...] = g_out
        tr_s[...] = jnp.zeros_like(tr_s)
        tr_s[64:65, :] = sums[1]
        tr_s[65:66, :] = sums[2]
        tr_s[66:69, :] = mv_ref[1:4, :]
        columns = jnp.transpose(tr_s[...])
        lanes = lax.broadcasted_iota(jnp.int32, (768, 128), 1)
        target_at = col_ref[0:1, :576] + row_ref[25] * 192
        for third in range(3):
            hit = at_ref[:, third : third + 1] == target_at
            column = jnp.sum(jnp.where(hit, sums[0][:, :576], 0.0), axis=1, keepdims=True)
            columns = jnp.where(lanes == 69 + third, column, columns)
        gq_s[:, 512:640] = jnp.where(lanes < 64, gq_s[:, 512:640], columns)
        for half, target in ((0, qkeep_ref), (1, qsend_ref)):
            for zz in range(4):
                at = zz * 2 + (row_ref[24] ^ half)
                rows = pl.ds(pl.multiple_of(at * 96, 16), 96)
                target[zz] = gq_s[rows, :].astype(target.dtype)
        for half, target in ((0, okeep_ref), (1, osend_ref)):
            rows = pl.ds(pl.multiple_of((row_ref[24] ^ half) * 96, 16), 96)
            target[...] = go_s[rows, :].astype(target.dtype)
    else:
        gq_ref[...] = g_query
        go_ref[...] = g_out
        vec_ref[...] = jnp.zeros_like(vec_ref)
        vec_ref[0:1, :640] = sums[0]
        vec_ref[1:2, :] = sums[1]
        vec_ref[2:3, :] = sums[2]
    for copy in result_copies:
        copy.wait()


def attn_call(row_offsets, parts, inside, weights, o_own, o_other, vecs, partial, seq, prev, tail):
    width = vecs.shape[-1]
    f32, bf16 = jnp.float32, jnp.bfloat16
    anywhere = pl.BlockSpec(memory_space=pl.ANY)
    dma = pltpu.SemaphoreType.DMA
    has_prev, last = prev is not None, tail is not None
    rows = 8 * ROWS
    half = (4, 2, ROWS, width)
    shapes = [(half, bf16), (half, bf16)]
    if last:
        shapes += [((4, 96, 640), bf16), ((4, 96, 640), f32), ((96, width), bf16), ((96, width), f32)]
    else:
        shapes += [((width, 640), f32), ((192, width), f32), ((8, width), f32)]
    out_specs = [anywhere] * 2 + [whole(shape) for shape, _ in shapes[2:]]
    if not has_prev:
        shapes.append(((rows, width), f32))
        out_specs.append(anywhere)
    operands = [*parts, *weights, o_own, o_other, vecs]
    in_specs = [anywhere] * 18 + [whole(vecs.shape)]
    scratch = [
        pltpu.VMEM((width, 640), bf16),
        pltpu.VMEM((256, width), bf16),
        pltpu.VMEM((rows, width), bf16),
        pltpu.VMEM((rows, width), bf16),
        pltpu.VMEM((rows, width), f32),
        pltpu.VMEM((rows, width), bf16),
    ]
    scratch += [pltpu.VMEM((3, rows, 128), bf16)] * 4
    scratch += [
        pltpu.VMEM((3, 64, rows), bf16),
        pltpu.VMEM((192, rows), bf16),
        pltpu.VMEM((192, rows), bf16),
        pltpu.VMEM((3, rows, 128), f32),
        pltpu.VMEM((3, rows, 128), f32),
        pltpu.VMEM((2, rows, 128), f32),
        pltpu.VMEM((rows, 256), bf16),
        pltpu.VMEM((192, rows), bf16),
        pltpu.VMEM((rows, 640), bf16),
        pltpu.VMEM((2, rows, width), bf16),
        pltpu.VMEM((3, rows, 128), f32),
        dma((10,)),
        dma((16,)),
        dma((17,)),
    ]
    if has_prev:
        operands += [*partial, *prev]
        in_specs += [anywhere] * 4 + [whole(prev[2].shape)]
        scratch += [
            pltpu.VMEM((2, rows, width), bf16),
            pltpu.VMEM((width, 640), f32),
            pltpu.VMEM((192, width), f32),
            dma((18,)),
        ]
    if last:
        operands += list(tail)
        in_specs += [whole(a.shape) for a in tail]
        scratch += [pltpu.VMEM((width, 640), f32), pltpu.VMEM((192, width), f32), pltpu.VMEM((128, width), f32)]
    return pl.pallas_call(
        functools.partial(attn_kernel, has_prev, last, seq, inside),
        grid_spec=pltpu.PrefetchScalarGridSpec(
            num_scalar_prefetch=1,
            grid=(1,),
            in_specs=in_specs,
            out_specs=out_specs,
            scratch_shapes=scratch,
        ),
        out_shape=[jax.ShapeDtypeStruct(shape, kind) for shape, kind in shapes],
        compiler_params=pltpu.CompilerParams(vmem_limit_bytes=58 << 20),
        cost_estimate=pl.CostEstimate(
            flops=24_000_000_000, transcendentals=0, bytes_accessed=15_000_000
        ),
        name="attn",
    )(row_offsets, *operands)


def finish_kernel(half_ref, x_ref, c_ref, own_ref, other_ref, bias, *refs):
    out_ref, grad_ref = refs[-2:]
    f32 = jnp.float32

    def write(source):
        x = x_ref[0].astype(f32)
        normed, inverse = normalize(x)
        out_ref[0] = x + bias[4:5, :] + source[0].astype(f32)
        s = source[1].astype(f32)
        mean_s = jnp.mean(s, axis=-1, keepdims=True)
        mean_sn = jnp.mean(s * normed, axis=-1, keepdims=True)
        grad_ref[0] = c_ref[0] + inverse * (s - mean_s - normed * mean_sn)

    @pl.when(pl.program_id(0) == 0)
    def _():
        write(own_ref)

    @pl.when(pl.program_id(0) == 1)
    def _():
        write(other_ref)


def finish_call(half, seq, x, cot, own, other, bias, done):
    _, rows, width = x.shape
    f32 = jnp.float32
    seq_spec = pl.BlockSpec(
        (1, rows, width), lambda i, at: (jnp.where(i == 0, at[0], 1 - at[0]) * 3 + seq, 0, 0)
    )
    before = list(done) if done is not None else []
    return pl.pallas_call(
        finish_kernel,
        grid_spec=pltpu.PrefetchScalarGridSpec(
            num_scalar_prefetch=1,
            grid=(2,),
            in_specs=[seq_spec, seq_spec, whole(own.shape), whole(other.shape), whole(bias.shape)]
            + [pl.BlockSpec(memory_space=pl.ANY)] * len(before),
            out_specs=[seq_spec, seq_spec],
        ),
        out_shape=[jax.ShapeDtypeStruct(x.shape, f32)] * 2,
        input_output_aliases={6: 0, 7: 1} if before else {},
        name="finish",
    )(half, x, cot, own, other, bias, *before)


def pick(value, index, axis=0):
    return lax.dynamic_index_in_dim(value, index, axis, keepdims=False)


def prep_kernel(at_ref, in_ref, q_ref, small_ref, own_ref, send_ref, pack_s):
    for h in range(4):
        parts = [in_ref[:, zy * 384 + h * 96 : zy * 384 + (h + 1) * 96] for zy in range(8)]
        for head in range(3):
            for kind in range(2):
                first = kind * 768 + h * 192 + head * 64
                parts.append(q_ref[:, first : first + 64])
        first = 1536 + h * 192
        parts.append(q_ref[:, first : first + 192])
        parts.append(small_ref[...])
        at = 0
        for part in parts:
            pack_s[h, :, at : at + part.shape[1]] = part
            at += part.shape[1]
    for core in range(2):
        own_ref[core] = pack_s[at_ref[26] * 2 + core]
        send_ref[core] = pack_s[(1 - at_ref[26]) * 2 + core]


def prep_call(row_offsets, w_in, w_qkv, small):
    half = jax.ShapeDtypeStruct((2, 24, 1408), jnp.bfloat16)
    return pl.pallas_call(
        prep_kernel,
        grid_spec=pltpu.PrefetchScalarGridSpec(
            num_scalar_prefetch=1,
            grid=(1,),
            in_specs=[whole(a.shape) for a in (w_in, w_qkv, small)],
            out_specs=[whole(half.shape)] * 2,
            scratch_shapes=[pltpu.VMEM((4, 24, 1408), jnp.bfloat16)],
        ),
        out_shape=[half, half],
        name="prep",
    )(row_offsets, w_in, w_qkv, small)


def join_kernel(at_ref, own_ref, got_ref, far_ref, down_ref, out_ref, attn_ref, mlp_ref, four, rows_s, cols_s):
    f32, bf16 = jnp.float32, jnp.bfloat16
    x, c = at_ref[26], at_ref[27]
    four[0] = own_ref[c].astype(f32)
    four[1] = got_ref[c].astype(f32)
    four[2] = far_ref[0].astype(f32)
    four[3] = far_ref[1].astype(f32)
    for source in range(4):
        near = ((source & 1) ^ c) * 2 + ((source >> 1) ^ x)
        rows_s[source * 24 : (source + 1) * 24, :] = four[near]
        cols_s[source * 24 : (source + 1) * 24, :] = out_ref[:, source * 192 : (source + 1) * 192].astype(f32)
    mlp_ref[:96, :] = rows_s[:, :768].astype(bf16)
    mlp_ref[96:, :] = down_ref[...]
    attn_ref[:, :640] = rows_s[:, 768:].astype(bf16)
    attn_ref[:, 640:] = cols_s[...].astype(bf16)


def join_call(row_offsets, own, got, far, w_down, w_out):
    f32, bf16 = jnp.float32, jnp.bfloat16
    outs = [jax.ShapeDtypeStruct((96, 832), bf16), jax.ShapeDtypeStruct((192, 768), bf16)]
    return pl.pallas_call(
        join_kernel,
        grid_spec=pltpu.PrefetchScalarGridSpec(
            num_scalar_prefetch=1,
            grid=(1,),
            in_specs=[whole(a.shape) for a in (own, got, far, w_down, w_out)],
            out_specs=[whole(a.shape) for a in outs],
            scratch_shapes=[
                pltpu.VMEM((4, 24, 1408), f32), pltpu.VMEM((96, 1408), f32), pltpu.VMEM((96, 192), f32)
            ],
        ),
        out_shape=outs,
        name="join",
    )(row_offsets, own, got, far, w_down, w_out)


def pick_out_kernel(at_ref, one, two, three, four, own_ref, send_ref, all_s):
    for at, source in enumerate((one, two, three, four)):
        all_s[at] = source[:, 640:]
    for core in range(2):
        own_ref[core] = all_s[(at_ref[28] - at_ref[26] * 2 - core + 4) % 4]
        send_ref[core] = all_s[(at_ref[28] - (1 - at_ref[26]) * 2 - core + 4) % 4]


def pick_out_call(row_offsets, pieces):
    half = jax.ShapeDtypeStruct((2, 96, 192), jnp.bfloat16)
    return pl.pallas_call(
        pick_out_kernel,
        grid_spec=pltpu.PrefetchScalarGridSpec(
            num_scalar_prefetch=1,
            grid=(1,),
            in_specs=[whole((96, 832))] * 4,
            out_specs=[whole(half.shape)] * 2,
            scratch_shapes=[pltpu.VMEM((4, 96, 192), jnp.bfloat16)],
        ),
        out_shape=[half, half],
        name="pick_out",
    )(row_offsets, *pieces)


def join_out_kernel(at_ref, own_ref, got_ref, far_ref, out_ref, four, rows_s):
    f32, bf16 = jnp.float32, jnp.bfloat16
    x, c = at_ref[26], at_ref[27]
    four[0] = own_ref[c].astype(f32)
    four[1] = got_ref[c].astype(f32)
    four[2] = far_ref[0].astype(f32)
    four[3] = far_ref[1].astype(f32)
    for source in range(4):
        near = ((source & 1) ^ c) * 2 + ((source >> 1) ^ x)
        for group in range(4):
            rows_s[source * 24 : (source + 1) * 24, group * 192 : (group + 1) * 192] = four[
                near, group * 24 : (group + 1) * 24, :
            ]
    out_ref[...] = rows_s[...].astype(bf16)


def join_out_call(row_offsets, own, got, far):
    f32, bf16 = jnp.float32, jnp.bfloat16
    return pl.pallas_call(
        join_out_kernel,
        grid_spec=pltpu.PrefetchScalarGridSpec(
            num_scalar_prefetch=1,
            grid=(1,),
            in_specs=[whole(a.shape) for a in (own, got, far)],
            out_specs=whole((96, 768)),
            scratch_shapes=[pltpu.VMEM((4, 96, 192), f32), pltpu.VMEM((96, 768), f32)],
        ),
        out_shape=jax.ShapeDtypeStruct((96, 768), bf16),
        name="join_out",
    )(row_offsets, own, got, far)


def vector_tables():
    row = np.arange(768)
    at_q = np.stack([(row // 24) * 72 + third * 24 + row % 24 for third in range(3)], axis=1)
    at_in = np.stack([(row // 24) * 96 + third * 24 + row % 24 for third in range(4)], axis=1)
    lane = np.arange(576)
    head, kind = lane // 128, (lane % 128) // 64
    col_q = np.where(lane < 384, kind * 768 + head * 64 + lane % 64, 1536 + lane - 384)
    col_in = (row // 96) * 384 + row % 96
    cols = np.zeros((8, 768), np.int32)
    cols[0, :576] = col_q
    cols[1] = col_in
    rows = np.concatenate([at_q, at_in, np.zeros((768, 1))], axis=1).astype(np.int32)
    return rows, cols


def vec_kernel(at_ref, *refs):
    refs = list(refs)
    pieces = [refs.pop(0) for _ in range(8)]
    rows_ref, cols_ref, out_ref, all_s = refs
    f32 = jnp.float32
    for at, source in enumerate(pieces):
        rows = pl.ds(pl.multiple_of(at_ref[at], 16), 96)
        all_s[rows, :] = source[...].astype(f32)
    flipped = jnp.transpose(all_s[...])
    out_ref[0:4, :] = flipped[64:68]
    out_ref[4:5, :] = flipped[68:69] + flipped[69:70]
    for row, kinds, target, width, step in ((5, (0, 1, 2), 0, 576, 192), (6, (3, 4, 5, 6), 1, 768, 96)):
        wanted = cols_ref[target : target + 1, :width] + at_ref[25] * step
        total = jnp.zeros((1, width), f32)
        for kind in kinds:
            hit = rows_ref[:, kind : kind + 1] == wanted
            total += col_sum(jnp.where(hit, all_s[:, 70 + kind : 71 + kind], 0.0))
        out_ref[row : row + 1, :width] = total
    out_ref[7:8, :] = jnp.zeros((1, 768), f32)
    out_ref[5:6, 576:] = jnp.zeros((1, 192), f32)


def vec_call(row_offsets, pieces, rows, cols):
    f32 = jnp.float32
    return pl.pallas_call(
        vec_kernel,
        grid_spec=pltpu.PrefetchScalarGridSpec(
            num_scalar_prefetch=1,
            grid=(1,),
            in_specs=[pl.BlockSpec((96, 128), lambda i, *_: (0, 4))] * 8
            + [whole(rows.shape), whole(cols.shape)],
            out_specs=whole((8, 768)),
            scratch_shapes=[pltpu.VMEM((768, 128), f32)],
        ),
        out_shape=jax.ShapeDtypeStruct((8, 768), f32),
        name="vectors",
    )(row_offsets, *pieces, rows, cols)


def spread_q_kernel(blocks_ref, q_ref, *out_refs):
    f32 = jnp.float32
    total = None
    for h in range(4):
        block = blocks_ref[h].astype(f32)
        for head in range(3):
            for kind in range(2):
                first = kind * 768 + h * 192 + head * 64
                at = head * 128 + kind * 64
                q_ref[:, first : first + 64] = block[:, at : at + 64]
        first = 1536 + h * 192
        q_ref[:, first : first + 192] = block[:, 384:576]
        part = block[:, 576:584]
        total = part if total is None else total + part
    same = lax.broadcasted_iota(jnp.int32, (24, 24), 0) == lax.broadcasted_iota(jnp.int32, (24, 24), 1)
    rows = [col_sum(jnp.where(same, total[:, t : t + 1], 0.0)) for t in range(8)]
    for t in range(5):
        out_refs[t][...] = rows[t]
    out_refs[5][...] = jnp.concatenate(rows[5:], axis=1)


def spread_q_call(blocks):
    f32 = jnp.float32
    shapes = [(24, 2304)] + [(1, 24)] * 5 + [(1, 72)]
    return pl.pallas_call(
        spread_q_kernel,
        out_shape=[jax.ShapeDtypeStruct(shape, f32) for shape in shapes],
        name="spread_q",
    )(blocks)


def spread_in_kernel(blocks_ref, in_ref):
    for h in range(4):
        block = blocks_ref[h].astype(jnp.float32)
        for zy in range(8):
            first = zy * 384 + h * 96
            in_ref[:, first : first + 96] = block[:, zy * 96 : (zy + 1) * 96]


def spread_in_call(blocks):
    return pl.pallas_call(
        spread_in_kernel,
        out_shape=jax.ShapeDtypeStruct((24, 3072), jnp.float32),
        name="spread_in",
    )(blocks)


def exchange_four(blocks, x, c):
    blocks = blocks.reshape((2, 2) + blocks.shape[1:])
    own = pick(blocks, x)
    got = swap(pick(blocks, 1 - x), 2)
    both = jnp.stack([own, got])
    mine = pick(both, c, 1)
    theirs = swap(pick(both, 1 - c, 1), 1)
    mine = jnp.where(x == 0, mine, mine[::-1])
    theirs = jnp.where(x == 0, theirs, theirs[::-1])
    pairs = jnp.where(
        c == 0, jnp.stack([mine, theirs], axis=1), jnp.stack([theirs, mine], axis=1)
    )
    return pairs.reshape((4,) + pairs.shape[2:])


def fast(*args):
    return fast_body(*args)


def fast_body(
    inputs, cotangent, ln1_gain, ln1_bias, ln2_gain, ln2_bias, w_qkv, b_qkv, w_out, b_out, w_in, b_in, w_mlp_out, b_mlp_out
):
    f32, bf16 = jnp.float32, jnp.bfloat16
    z = lax.axis_index("fsdp")
    ctx = lax.axis_index("ctx")
    y, x, c = ctx // 4, (ctx // 2) % 2, ctx % 2
    h = ctx % 4

    zs = jnp.stack([(z - k) % 4 for k in range(4)])
    rows_w = jnp.concatenate([(zs * 2 + y) * 96, (zs * 2 + 1 - y) * 96])
    rows_o = jnp.stack([y * 96, (1 - y) * 96])
    rows_p = jnp.stack([(ctx ^ piece_bits(k)) * ROWS for k in range(8)])
    row_offsets = jnp.concatenate(
        [rows_w, rows_o, jnp.zeros((6,), jnp.int32), rows_p, jnp.stack([y, h, x, c, z])]
    ).astype(jnp.int32)

    small = jnp.concatenate(
        [ln1_gain, ln1_bias, ln2_gain, ln2_bias, b_out, b_mlp_out, b_qkv, b_in, jnp.zeros((51 * 24,), bf16)]
    ).reshape(64, 24).T
    pack_own, pack_send = prep_call(row_offsets, w_in, w_qkv, small)

    def rows_of(half, first, count):
        at = half * 3 + first
        return jnp.stack(
            [
                lax.dynamic_slice_in_dim(inputs, at, count),
                lax.dynamic_slice_in_dim(cotangent, at, count).astype(bf16),
            ]
        )

    parts = []
    first = 0
    for count in CHUNKS:
        got = swap(rows_of(1 - y, first, count), 4)
        own = rows_of(y, first, count)
        side, side_got = swap(own, 2), swap(got, 2)
        near = (own, got, side, side_got)
        parts.append(near + tuple(swap(a, 1) for a in near))
        first += count

    pack_got = swap(pack_send, 2)
    pack_far = swap(jnp.stack([pick(pack_own, 1 - c), pick(pack_got, 1 - c)]), 1)
    attn_w, mlp_w = join_call(row_offsets, pack_own, pack_got, pack_far, w_mlp_out, w_out)
    attn_own = [attn_w] + [shift_z(attn_w, k) for k in (1, 2, 3)]
    mlp_own = [mlp_w] + [shift_z(mlp_w, k) for k in (1, 2, 3)]
    attn_all = attn_own + [swap(part, 4) for part in attn_own]
    mlp_all = mlp_own + [swap(part, 4) for part in mlp_own]
    out_mine, out_send = pick_out_call(row_offsets, attn_own)
    out_got = swap(out_send, 2)
    out_far = swap(jnp.stack([pick(out_mine, 1 - c), pick(out_got, 1 - c)]), 1)
    out_own = join_out_call(row_offsets, out_mine, out_got, out_far)
    out_other = swap(out_own, 4)
    at_rows, at_cols = vector_tables()
    vecs = vec_call(row_offsets, attn_all, at_rows, at_cols)

    where = [(at, inside) for at, count in enumerate(CHUNKS) for inside in range(count)]

    def attention(seq, partial, prev, tail=None):
        at, inside = where[seq]
        return attn_call(
            row_offsets, parts[at], inside, attn_all, out_own, out_other,
            vecs, partial, seq, prev, tail,
        )

    def reduce_z(blocks):
        def total(at):
            value = pick(blocks[0], at).astype(f32)
            for block in blocks[1:]:
                value = value + pick(block, at).astype(f32)
            return value

        low = [total((z + k) % 4).astype(bf16) for k in (1, 2, 3)]
        sent = [shift_z(part, k + 1) for k, part in enumerate(low)]
        result = total(z)
        for part in sent:
            result = result + part.astype(f32)
        return result

    half = jnp.reshape(y, (1,)).astype(jnp.int32)

    def scatter(seq, send, keep, done):
        got = swap(send, 1)
        side = swap((keep[2:].astype(f32) + got[2:].astype(f32)).astype(bf16), 2)
        mine = (keep[0].astype(f32) + got[0].astype(f32) + side[0].astype(f32)).astype(bf16)
        far = (keep[1].astype(f32) + got[1].astype(f32) + side[1].astype(f32)).astype(bf16)
        return finish_call(half, seq, inputs, cotangent, mine, swap(far, 4), vecs, done)

    first_send, first_keep, g_q, g_o, vec, first_norm = attention(0, None, None)
    prev = (g_q, g_o, vec)
    send, keep, rest_part, rest_norm, g_send, g_keep, mlp_vec = mlp_call(
        row_offsets, parts, mlp_all, vecs, cotangent, first_send, first_keep, first_norm
    )
    g_got = swap(g_send, 4)
    done = scatter(0, send, keep, None)
    send, keep, g_q, g_o, vec = attention(1, (rest_part, rest_norm), prev)
    done = scatter(1, send, keep, done)
    mlp_grad = reduce_z((g_keep, g_got))
    grad_w_mlp = mlp_grad[96:192]
    grad_b_in = mlp_grad[192, :96]
    grad_w_in = spread_in_call(exchange_four(mlp_grad[:96].astype(bf16).reshape(4, 24, 768), x, c))
    send, keep, q_send, q_keep, o_send, o_keep = attention(
        2, (rest_part, rest_norm), (g_q, g_o, vec), (mlp_vec, at_rows, at_cols)
    )
    done = scatter(2, send, keep, done)
    q_grad = reduce_z((q_keep, swap(q_send, 4)))
    spread = spread_q_call(exchange_four(q_grad.astype(bf16).reshape(4, 24, 640), x, c))
    grad_w_qkv = spread[0]
    one_gain, one_bias, two_gain, two_bias, grad_bias, grad_bq = [v.reshape(-1) for v in spread[1:]]

    o_parts = o_keep + swap(o_send, 4).astype(f32)
    o_blocks = exchange_four(o_parts.astype(bf16).reshape(4, 24, 768), x, c)
    grad_w_out = reduce_z((o_blocks,))

    outputs, grad_inputs = done
    return (
        outputs,
        grad_inputs,
        one_gain,
        one_bias,
        two_gain,
        two_bias,
        grad_w_qkv,
        grad_bq,
        grad_w_out,
        grad_bias,
        grad_w_in,
        grad_b_in,
        grad_w_mlp,
        grad_bias,
    )


def fast_fits(mesh):
    sizes = dict(mesh.shape)
    return sizes["fsdp"] == 4 and sizes["ctx"] == 8


def solution(mesh):
    return jax.shard_map(
        fast if fast_fits(mesh) else local,
        mesh=mesh,
        in_specs=(
            P("fsdp", "ctx", None),
            P("fsdp", "ctx", None),
            P(("fsdp", "ctx")),
            P(("fsdp", "ctx")),
            P(("fsdp", "ctx")),
            P(("fsdp", "ctx")),
            P(("fsdp", "ctx"), None),
            P(("fsdp", "ctx")),
            P(("fsdp", "ctx"), None),
            P(("fsdp", "ctx")),
            P(("fsdp", "ctx"), None),
            P(("fsdp", "ctx")),
            P(("fsdp", "ctx"), None),
            P(("fsdp", "ctx")),
        ),
        out_specs=(
            P("fsdp", "ctx", None),
            P("fsdp", "ctx", None),
            P(("fsdp", "ctx")),
            P(("fsdp", "ctx")),
            P(("fsdp", "ctx")),
            P(("fsdp", "ctx")),
            P(("fsdp", "ctx"), None),
            P(("fsdp", "ctx")),
            P(("fsdp", "ctx"), None),
            P(("fsdp", "ctx")),
            P(("fsdp", "ctx"), None),
            P(("fsdp", "ctx")),
            P(("fsdp", "ctx"), None),
            P(("fsdp", "ctx")),
        ),
        check_vma=False,
    )
```

```python
import functools
import math

import jax
import jax.numpy as jnp
import numpy as np
from jax import lax
from jax.experimental import pallas as pl
from jax.experimental.pallas import tpu as pltpu
from jax.sharding import PartitionSpec as P


HEADS = 12
HEAD_DIM = 64
ROT_DIM = 16
MICRO = 2
SEQ_MB = 3
CHUNKS = (1, 2)


EPS = 1e-05
BASE_FREQ = 10000.0


def layer_norm(values, gain_row, shift_row):
    centre = jnp.mean(values, axis=-1, keepdims=True)
    centred = values - centre
    inverse = lax.rsqrt(jnp.mean(centred * centred, axis=-1, keepdims=True) + EPS)
    normed = centred * inverse
    return (normed * gain_row + shift_row, normed, inverse)


def norm_back(grad_out, normed, inverse, gain_row):
    scaled = grad_out * gain_row
    return inverse * (
        scaled
        - jnp.mean(scaled, axis=-1, keepdims=True)
        - normed * jnp.mean(scaled * normed, axis=-1, keepdims=True)
    )


def angles(positions):
    half_rot = ROT_DIM // 2
    inv_freq = BASE_FREQ ** (-(2.0 * jnp.arange(half_rot, dtype=jnp.float32)) / ROT_DIM)
    phase_angle = positions.astype(jnp.float32)[:, None] * inv_freq[None, :]
    return (jnp.cos(phase_angle), jnp.sin(phase_angle))


def rotate(head_field, cosine, sine_rot, direction):
    half_rot = ROT_DIM // 2
    lead_half = head_field[..., :half_rot]
    trail_half = head_field[..., half_rot:ROT_DIM]
    cos_wide = cosine[:, None, :]
    sin_wide = direction * sine_rot[:, None, :]
    return jnp.concatenate(
        [
            lead_half * cos_wide - trail_half * sin_wide,
            trail_half * cos_wide + lead_half * sin_wide,
            head_field[..., ROT_DIM:],
        ],
        axis=-1,
    )


def gelu_parts(pre_act):
    normal_cdf = 0.5 * (1.0 + jax.scipy.special.erf(pre_act * 0.7071067811865476))
    density = jnp.exp(-0.5 * pre_act * pre_act) * 0.3989422804014327
    return (pre_act * normal_cdf, normal_cdf + pre_act * density)


def outer_rows(left, right):
    return lax.dot_general(
        left, right, (((0,), (0,)), ((), ())), preferred_element_type=jnp.float32
    )


def times_transpose(left, right):
    return lax.dot_general(
        left, right, (((1,), (1,)), ((), ())), preferred_element_type=jnp.float32
    )


def attend_block(soft_state, kv_block, first_row, query_low, positions, score_scale):
    run_max, run_sum, weighted = soft_state
    seq_count, block_rows, double_width = kv_block.shape
    model_width = double_width // 2
    key_low = kv_block[..., :model_width].reshape(seq_count, block_rows, HEADS, HEAD_DIM)
    value_low = kv_block[..., model_width:].reshape(seq_count, block_rows, HEADS, HEAD_DIM)
    scores = (
        jnp.einsum("sqhd,skhd->shqk", query_low, key_low, preferred_element_type=jnp.float32)
        * score_scale
    )
    allowed = (first_row + jnp.arange(block_rows, dtype=jnp.int32))[None, :] <= positions[:, None]
    scores = jnp.where(allowed, scores, -jnp.inf)
    new_max = jnp.maximum(run_max, jnp.max(scores, axis=-1))
    safe_max = jnp.where(new_max == -jnp.inf, 0.0, new_max)
    exp_scores = jnp.exp(scores - safe_max[..., None])
    factor = jnp.exp(run_max - safe_max)
    run_sum = run_sum * factor + jnp.sum(exp_scores, axis=-1)
    weighted = weighted * factor[..., None] + jnp.einsum(
        "shqk,skhd->shqd",
        exp_scores.astype(jnp.bfloat16),
        value_low,
        preferred_element_type=jnp.float32,
    )
    return (new_max, run_sum, weighted)


def attend_piece(soft_state, kv_piece, query_low, positions, score_scale):
    piece_rows = kv_piece.shape[1]
    step_rows = math.gcd(piece_rows, 512)

    def one_block(block_index, inner_state):
        offset = block_index * step_rows
        kv_block = lax.dynamic_slice_in_dim(kv_piece, offset, step_rows, 1)
        return attend_block(inner_state, kv_block, offset, query_low, positions, score_scale)

    return lax.fori_loop(0, piece_rows // step_rows, one_block, soft_state)


def local(
    inputs,
    cotangent,
    ln1_gain,
    ln1_bias,
    ln2_gain,
    ln2_bias,
    w_qkv,
    b_qkv,
    w_out,
    b_out,
    w_in,
    b_in,
    w_mlp_out,
    b_mlp_out,
):
    f32 = jnp.float32
    bf16 = jnp.bfloat16
    group_rows = inputs.shape[1]
    model_width = inputs.shape[2]
    seq_len = group_rows * lax.axis_size("ctx")
    key_block = math.gcd(seq_len, 512)
    score_scale = HEAD_DIM ** (-0.5)
    positions = lax.axis_index("ctx") * group_rows + jnp.arange(group_rows, dtype=jnp.int32)
    cosine, sine_rot = angles(positions)

    def gather_params():
        return (
            lax.all_gather(ln1_gain, ("fsdp", "ctx"), axis=0, tiled=True),
            lax.all_gather(ln1_bias, ("fsdp", "ctx"), axis=0, tiled=True),
            lax.all_gather(ln2_gain, ("fsdp", "ctx"), axis=0, tiled=True),
            lax.all_gather(ln2_bias, ("fsdp", "ctx"), axis=0, tiled=True),
            lax.all_gather(w_qkv, ("fsdp", "ctx"), axis=0, tiled=True),
            lax.all_gather(b_qkv, ("fsdp", "ctx"), axis=0, tiled=True),
            lax.all_gather(w_out, ("fsdp", "ctx"), axis=0, tiled=True),
            lax.all_gather(b_out, ("fsdp", "ctx"), axis=0, tiled=True),
            lax.all_gather(w_in, ("fsdp", "ctx"), axis=0, tiled=True),
            lax.all_gather(b_in, ("fsdp", "ctx"), axis=0, tiled=True),
            lax.all_gather(w_mlp_out, ("fsdp", "ctx"), axis=0, tiled=True),
            lax.all_gather(b_mlp_out, ("fsdp", "ctx"), axis=0, tiled=True),
        )

    weight_sums = None
    output_list = []
    grad_list = []
    for micro_index in range(MICRO):
        batch_rows = inputs[micro_index * SEQ_MB : (micro_index + 1) * SEQ_MB]
        cot_rows = cotangent[micro_index * SEQ_MB : (micro_index + 1) * SEQ_MB]
        seq_count = batch_rows.shape[0]
        flat_rows = seq_count * group_rows
        params_fwd = gather_params()
        (
            gain_one,
            shift_one,
            gain_two,
            shift_two,
            weight_qkv,
            bias_qkv,
            weight_out,
            bias_out,
            weight_in,
            bias_in,
            weight_mlp,
            bias_mlp,
        ) = params_fwd
        residual = batch_rows.reshape(flat_rows, model_width).astype(f32)
        normal_one, normed_one, inverse_one = layer_norm(
            residual, gain_one.astype(f32), shift_one.astype(f32)
        )
        normal_two, normed_two, inverse_two = layer_norm(
            residual, gain_two.astype(f32), shift_two.astype(f32)
        )
        hidden_one = normal_one.astype(bf16)
        hidden_two = normal_two.astype(bf16)
        project = jnp.dot(hidden_one, weight_qkv, preferred_element_type=f32) + bias_qkv.astype(f32)
        head_shape = (seq_count, group_rows, HEADS, HEAD_DIM)
        query_low = rotate(
            project[:, :model_width].reshape(head_shape), cosine, sine_rot, 1.0
        ).astype(bf16)
        key_low = rotate(
            project[:, model_width : 2 * model_width].reshape(head_shape), cosine, sine_rot, 1.0
        ).astype(bf16)
        value_low = project[:, 2 * model_width :].astype(bf16)
        kv_pack = jnp.concatenate(
            [
                key_low.reshape(seq_count, group_rows, model_width),
                value_low.reshape(seq_count, group_rows, model_width),
            ],
            axis=-1,
        )
        start_state = (
            jnp.full((seq_count, HEADS, group_rows), -jnp.inf, f32),
            jnp.zeros((seq_count, HEADS, group_rows), f32),
            jnp.zeros((seq_count, HEADS, group_rows, HEAD_DIM), f32),
        )
        soft_state = attend_piece(
            start_state,
            lax.all_gather(kv_pack, "ctx", axis=1, tiled=True),
            query_low,
            positions,
            score_scale,
        )
        run_max, run_sum, weighted = soft_state
        log_total = run_max + jnp.log(run_sum)
        attended = jnp.transpose(weighted / run_sum[..., None], (0, 2, 1, 3)).astype(bf16)
        att_flat = attended.reshape(flat_rows, model_width)
        pre_act = jnp.dot(hidden_two, weight_in, preferred_element_type=f32) + bias_in.astype(f32)
        activation_f, gelu_slope = gelu_parts(pre_act)
        activation = activation_f.astype(bf16)
        output = (
            residual
            + jnp.dot(att_flat, weight_out, preferred_element_type=f32)
            + bias_out.astype(f32)
            + jnp.dot(activation, weight_mlp, preferred_element_type=f32)
            + bias_mlp.astype(f32)
        )
        output_list.append(output.reshape(seq_count, group_rows, model_width))
        params_back = gather_params()
        (
            gain_one,
            shift_one,
            gain_two,
            shift_two,
            weight_qkv,
            bias_qkv,
            weight_out,
            bias_out,
            weight_in,
            bias_in,
            weight_mlp,
            bias_mlp,
        ) = params_back
        kv_rows = lax.all_gather(kv_pack, "ctx", axis=1, tiled=True)
        cot_flat = cot_rows.reshape(flat_rows, model_width)
        cot_low = cot_flat.astype(bf16)
        cot_sum = jnp.sum(cot_flat, axis=0)
        grad_w_out = outer_rows(att_flat, cot_low)
        grad_w_mlp = outer_rows(activation, cot_low)
        d_pre = times_transpose(cot_low, weight_mlp) * gelu_slope
        d_pre_low = d_pre.astype(bf16)
        grad_w_in = outer_rows(hidden_two, d_pre_low)
        d_hidden_two = times_transpose(d_pre_low, weight_in)
        grad_att = times_transpose(cot_low, weight_out).astype(bf16).reshape(head_shape)
        row_delta = jnp.einsum("sqhd,sqhd->shq", grad_att, attended, preferred_element_type=f32)

        def back_block(block_index, loop_carry):
            grad_query, buffer = loop_carry
            offset = block_index * key_block
            kv_block = lax.dynamic_slice_in_dim(kv_rows, offset, key_block, 1)
            key_part = kv_block[..., :model_width].reshape(seq_count, key_block, HEADS, HEAD_DIM)
            value_part = kv_block[..., model_width:].reshape(seq_count, key_block, HEADS, HEAD_DIM)
            scores = (
                jnp.einsum("sqhd,skhd->shqk", query_low, key_part, preferred_element_type=f32)
                * score_scale
            )
            allowed = (offset + jnp.arange(key_block, dtype=jnp.int32))[None, :] <= positions[
                :, None
            ]
            prob_block = jnp.where(allowed, jnp.exp(scores - log_total[..., None]), 0.0)
            grad_value = jnp.einsum(
                "shqk,sqhd->skhd", prob_block.astype(bf16), grad_att, preferred_element_type=f32
            )
            grad_prob = jnp.einsum(
                "sqhd,skhd->shqk", grad_att, value_part, preferred_element_type=f32
            )
            grad_score = (prob_block * (grad_prob - row_delta[..., None]) * score_scale).astype(
                bf16
            )
            grad_query = grad_query + jnp.einsum(
                "shqk,skhd->sqhd", grad_score, key_part, preferred_element_type=f32
            )
            grad_key = jnp.einsum(
                "shqk,sqhd->skhd", grad_score, query_low, preferred_element_type=f32
            )
            key_value_grad = jnp.concatenate(
                [
                    grad_key.reshape(seq_count, key_block, model_width),
                    grad_value.reshape(seq_count, key_block, model_width),
                ],
                axis=-1,
            )
            return (grad_query, lax.dynamic_update_slice_in_dim(buffer, key_value_grad, offset, 1))

        start_carry = (
            jnp.zeros(head_shape, f32),
            jnp.zeros((seq_count, seq_len, 2 * model_width), f32),
        )
        grad_query, buffer = lax.fori_loop(0, seq_len // key_block, back_block, start_carry)
        kv_grad_own = lax.psum_scatter(
            buffer.astype(jnp.bfloat16), "ctx", scatter_dimension=1, tiled=True
        ).astype(jnp.float32)
        key_grad_raw = kv_grad_own[..., :model_width].reshape(head_shape)
        value_grad_flat = kv_grad_own[..., model_width:].reshape(flat_rows, model_width)
        grad_query = rotate(grad_query, cosine, sine_rot, -1.0)
        grad_key = rotate(key_grad_raw, cosine, sine_rot, -1.0)
        d_project = jnp.concatenate(
            [
                grad_query.reshape(flat_rows, model_width),
                grad_key.reshape(flat_rows, model_width),
                value_grad_flat,
            ],
            axis=-1,
        )
        d_project_low = d_project.astype(bf16)
        grad_w_qkv = outer_rows(hidden_one, d_project_low)
        d_hidden_one = times_transpose(d_project_low, weight_qkv)
        grad_rows = (
            cot_flat
            + norm_back(d_hidden_one, normed_one, inverse_one, gain_one.astype(f32))
            + norm_back(d_hidden_two, normed_two, inverse_two, gain_two.astype(f32))
        )
        grad_list.append(grad_rows.reshape(seq_count, group_rows, model_width))
        terms = (
            jnp.sum(d_hidden_one * normed_one, axis=0),
            jnp.sum(d_hidden_one, axis=0),
            jnp.sum(d_hidden_two * normed_two, axis=0),
            jnp.sum(d_hidden_two, axis=0),
            grad_w_qkv,
            jnp.sum(d_project, axis=0),
            grad_w_out,
            cot_sum,
            grad_w_in,
            jnp.sum(d_pre, axis=0),
            grad_w_mlp,
            cot_sum,
        )
        if weight_sums is None:
            weight_sums = terms
        else:
            weight_sums = jax.tree.map(lambda total, term: total + term, weight_sums, terms)
    owned = (
        lax.psum_scatter(weight_sums[0], ("fsdp", "ctx"), scatter_dimension=0, tiled=True),
        lax.psum_scatter(weight_sums[1], ("fsdp", "ctx"), scatter_dimension=0, tiled=True),
        lax.psum_scatter(weight_sums[2], ("fsdp", "ctx"), scatter_dimension=0, tiled=True),
        lax.psum_scatter(weight_sums[3], ("fsdp", "ctx"), scatter_dimension=0, tiled=True),
        lax.psum_scatter(weight_sums[4], ("fsdp", "ctx"), scatter_dimension=0, tiled=True),
        lax.psum_scatter(weight_sums[5], ("fsdp", "ctx"), scatter_dimension=0, tiled=True),
        lax.psum_scatter(weight_sums[6], ("fsdp", "ctx"), scatter_dimension=0, tiled=True),
        lax.psum_scatter(weight_sums[7], ("fsdp", "ctx"), scatter_dimension=0, tiled=True),
        lax.psum_scatter(weight_sums[8], ("fsdp", "ctx"), scatter_dimension=0, tiled=True),
        lax.psum_scatter(weight_sums[9], ("fsdp", "ctx"), scatter_dimension=0, tiled=True),
        lax.psum_scatter(weight_sums[10], ("fsdp", "ctx"), scatter_dimension=0, tiled=True),
        lax.psum_scatter(weight_sums[11], ("fsdp", "ctx"), scatter_dimension=0, tiled=True),
    )
    outputs = jnp.concatenate(output_list, axis=0)
    grad_inputs = jnp.concatenate(grad_list, axis=0)
    return (
        outputs,
        grad_inputs,
        owned[0],
        owned[1],
        owned[2],
        owned[3],
        owned[4],
        owned[5],
        owned[6],
        owned[7],
        owned[8],
        owned[9],
        owned[10],
        owned[11],
    )


ROWS = 128
BLOCK = 256


def swap(value, bit):
    return lax.ppermute(value, "ctx", [(i, i ^ bit) for i in range(8)])


def shift_z(value, step):
    return lax.ppermute(value, "fsdp", [(i, (i + step) % 4) for i in range(4)])


def nt(left, right):
    return lax.dot_general(
        left, right, (((1,), (1,)), ((), ())), preferred_element_type=jnp.float32
    )


def nn(left, right):
    return lax.dot_general(
        left, right, (((1,), (0,)), ((), ())), preferred_element_type=jnp.float32
    )


def tn(left, right):
    return lax.dot_general(
        left, right, (((0,), (0,)), ((), ())), preferred_element_type=jnp.float32
    )


def normalize(values):
    centred = values - jnp.mean(values, axis=-1, keepdims=True)
    inverse = lax.rsqrt(jnp.mean(centred * centred, axis=-1, keepdims=True) + EPS)
    return centred * inverse, inverse


def col_sum(values):
    return jnp.sum(values, axis=0, keepdims=True)


def piece_bits(index):
    return ((index & 1) << 2) | (index & 2) | (index >> 2)


def mlp_kernel(chunks, row_ref, *refs):
    refs = list(refs)
    parts = [[refs.pop(0) for _ in range(8)] for _ in chunks]
    weights = [refs.pop(0) for _ in range(8)]
    vecs, cot_ref, first_send, first_keep, first_norm = [refs.pop(0) for _ in range(5)]
    send_ref, keep_ref, rest_ref, norm_ref, gsend_ref, gkeep_ref, vec_ref = [refs.pop(0) for _ in range(7)]
    w_in, w_down, h_s, c_s, act_s, dpre_s, x_n, first_s, part_s, g_in, g_down, seg_s, w_sem, x_sem, p_sem, o_sem = refs
    f32, bf16 = jnp.float32, jnp.bfloat16
    gain, shift, bias = vecs[2:3, :], vecs[3:4, :], vecs[6:7, :]
    where = [(at, inside) for at, count in enumerate(chunks) for inside in range(count)]
    total = len(where)

    weight_copies = []
    for at, source in enumerate(weights):
        rows = pl.ds(pl.multiple_of(row_ref[at], 16), 96)
        for kind, target in ((0, w_in), (1, w_down)):
            weight_copies.append(
                pltpu.make_async_copy(
                    source.at[pl.ds(kind * 96, 96)], target.at[rows], w_sem.at[at * 2 + kind]
                )
            )
    part_copies = []
    for seq, (at, inside) in enumerate(where):
        for piece in range(8):
            rows = pl.ds((seq * 8 + piece) * ROWS, ROWS)
            sem = x_sem.at[(seq * 8 + piece) * 2]
            if seq == 0:
                source_rows = pl.ds(pl.multiple_of(row_ref[16 + piece], ROWS), ROWS)
                part_copies.append(pltpu.make_async_copy(first_norm.at[source_rows], x_n.at[rows], sem))
            else:
                part_copies.append(
                    pltpu.make_async_copy(parts[at][piece].at[0, inside], h_s.at[rows], sem)
                )
            part_copies.append(
                pltpu.make_async_copy(
                    parts[at][piece].at[1, inside], c_s.at[rows], x_sem.at[(seq * 8 + piece) * 2 + 1]
                )
            )
    norm_copies = [
        pltpu.make_async_copy(x_n.at[pl.ds(seq * 1024, 1024)], norm_ref.at[seq - 1], o_sem.at[total + seq])
        for seq in range(1, total)
    ]
    first_copies = [
        pltpu.make_async_copy(first_keep, first_s.at[pl.ds(0, 4)], p_sem.at[0]),
        pltpu.make_async_copy(first_send, first_s.at[pl.ds(4, 4)], p_sem.at[1]),
    ]
    out_copies = [
        pltpu.make_async_copy(part_s.at[0, pl.ds(0, 4)], keep_ref, o_sem.at[0]),
        pltpu.make_async_copy(part_s.at[0, pl.ds(4, 4)], send_ref, o_sem.at[1]),
    ] + [
        pltpu.make_async_copy(part_s.at[seq % 2], rest_ref.at[seq - 1], o_sem.at[seq + 1])
        for seq in range(1, total)
    ]
    for copy in part_copies[:16] + weight_copies + first_copies + part_copies[16:]:
        copy.start()
    vec_ref[...] = jnp.zeros_like(vec_ref)
    for seq in range(2 * total):
        vec_ref[3:4, :] += col_sum(cot_ref[seq])

    def norm_rows(first):
        for at in range(0, 256, 16):
            rows = slice(first + at, first + at + 16)
            normed, _ = normalize(h_s[rows, :].astype(f32))
            x_n[rows, :] = normed
            h_s[rows, :] = (normed * gain + shift).astype(bf16)

    for seq in range(total):
        rows = slice(seq * 1024, (seq + 1) * 1024)
        if seq == 0:
            for copy in part_copies[:16]:
                copy.wait()
            h_s[rows, :] = (x_n[rows, :] * gain + shift).astype(bf16)
            for copy in weight_copies:
                copy.wait()
        for cols in (slice(0, 512), slice(512, 768)):
            pre = nn(h_s[rows, :], w_in[:, cols]) + bias[:, cols]
            d_act = nt(c_s[rows, :], w_down[cols, :])
            cdf = 0.5 * (1.0 + lax.erf(pre * 0.7071067811865476))
            density = jnp.exp(-0.5 * pre * pre) * 0.3989422804014327
            act_s[rows, cols] = (pre * cdf).astype(bf16)
            d_pre = d_act * (cdf + pre * density)
            dpre_s[rows, cols] = d_pre.astype(bf16)
            vec_ref[0:1, cols] += col_sum(d_pre)
        if seq + 1 < total:
            for copy in part_copies[seq * 16 + 16 : seq * 16 + 32]:
                copy.wait()
        if seq == 0:
            for copy in first_copies:
                copy.wait()
        if seq == 2:
            out_copies[0].wait()
            out_copies[1].wait()
        for block in range(4):
            part_rows = slice(seq * 1024 + block * 256, seq * 1024 + (block + 1) * 256)
            out = nn(act_s[part_rows, :], w_down[...])
            d_hidden = nt(dpre_s[part_rows, :], w_in[...])
            if seq + 1 < total:
                norm_rows((seq + 1) * 1024 + block * 256)
            vec_ref[1:2, :] += col_sum(d_hidden * x_n[part_rows, :])
            vec_ref[2:3, :] += col_sum(d_hidden)
            for kind, value in ((0, out), (1, d_hidden * gain)):
                for half in range(2):
                    piece = block * 2 + half
                    part = value[half * ROWS : (half + 1) * ROWS]
                    if seq == 0:
                        part = part + first_s[piece, kind].astype(f32)
                    part_s[seq % 2, piece, kind] = part.astype(bf16)
        if seq + 1 < total:
            norm_copies[seq].start()
        if seq == 0:
            out_copies[0].start()
            out_copies[1].start()
        else:
            out_copies[seq + 1].start()

    g_in[...] = tn(h_s[...], dpre_s[...])
    g_down[...] = tn(act_s[...], c_s[...])
    for at in range(8):
        seg_s[at, :, :96] = jnp.broadcast_to(vec_ref[0:1, at * 96 : (at + 1) * 96], (16, 96))
    for half, target in ((0, gkeep_ref), (1, gsend_ref)):
        for zz in range(4):
            at = zz * 2 + (row_ref[24] ^ half)
            rows = pl.ds(pl.multiple_of(at * 96, 16), 96)
            target[zz, :96, :] = g_in[rows, :].astype(target.dtype)
            target[zz, 96:192, :] = g_down[rows, :].astype(target.dtype)
            target[zz, 192:, :] = jnp.zeros((16, 768), target.dtype)
            target[zz, 192:, :96] = seg_s[at, :, :96].astype(target.dtype)
    for copy in out_copies[2:] + norm_copies:
        copy.wait()


def whole(shape):
    return pl.BlockSpec(shape, lambda *_: (0,) * len(shape))


def mlp_call(row_offsets, parts, weights, vecs, cot, first_send, first_keep, first_norm):
    chunks = tuple(part[0].shape[1] for part in parts)
    total = sum(chunks)
    width = vecs.shape[-1]
    f32, bf16 = jnp.float32, jnp.bfloat16

    anywhere = pl.BlockSpec(memory_space=pl.ANY)
    dma = pltpu.SemaphoreType.DMA
    rows = total * 8 * ROWS
    half = (4, 2, ROWS, width)
    grads = (4, 208, width)
    return pl.pallas_call(
        functools.partial(mlp_kernel, chunks),
        grid_spec=pltpu.PrefetchScalarGridSpec(
            num_scalar_prefetch=1,
            grid=(1,),
            in_specs=[anywhere] * (8 * len(parts) + 8)
            + [whole(vecs.shape), whole(cot.shape)]
            + [anywhere] * 3,
            out_specs=[anywhere] * 4 + [whole(grads), whole(grads), whole((8, width))],
            scratch_shapes=[pltpu.VMEM((width, width), bf16)] * 2
            + [pltpu.VMEM((rows, width), bf16)] * 4
            + [pltpu.VMEM((rows, width), f32)]
            + [pltpu.VMEM((8, 2, ROWS, width), bf16), pltpu.VMEM((2, 8, 2, ROWS, width), bf16)]
            + [pltpu.VMEM((width, width), f32)] * 2
            + [pltpu.VMEM((8, 16, 128), f32)]
            + [dma((16,)), dma((total * 16,)), dma((2,)), dma((2 * total,))],
        ),
        out_shape=[
            jax.ShapeDtypeStruct(half, bf16),
            jax.ShapeDtypeStruct(half, bf16),
            jax.ShapeDtypeStruct((total - 1, 8, 2, ROWS, width), bf16),
            jax.ShapeDtypeStruct((total - 1, 8 * ROWS, width), f32),
            jax.ShapeDtypeStruct(grads, bf16),
            jax.ShapeDtypeStruct(grads, f32),
            jax.ShapeDtypeStruct((8, width), f32),
        ],
        compiler_params=pltpu.CompilerParams(vmem_limit_bytes=58 << 20),
        cost_estimate=pl.CostEstimate(
            flops=30_000_000_000, transcendentals=0, bytes_accessed=30_000_000
        ),
        name="mlp",
    )(row_offsets, *[a for part in parts for a in part], *weights, vecs, cot, first_send, first_keep, first_norm)


def rotary_tables():
    f32 = jnp.float32
    lane = lax.broadcasted_iota(jnp.int32, (32, 128), 1)
    dim = lane & 63
    power = (dim & 7).astype(f32) * (-2.0 / ROT_DIM)
    freq = jnp.where(dim < ROT_DIM, jnp.exp(power * math.log(BASE_FREQ)), 0.0)
    row = lax.broadcasted_iota(jnp.int32, (32, 128), 0).astype(f32)
    fine, coarse = row * freq, row * 32.0 * freq
    cos_fine, sin_fine = jnp.cos(fine), jnp.sin(fine)
    scale = jnp.where(lane < 64, HEAD_DIM ** (-0.5), 1.0)
    cos_coarse, sin_coarse = jnp.cos(coarse) * scale, jnp.sin(coarse) * scale
    first, second = dim[:1] < 8, (dim[:1] >= 8) & (dim[:1] < ROT_DIM)
    return cos_fine, sin_fine, cos_coarse, sin_coarse, first, second


def attn_kernel(has_prev, last, at_seq, inside, row_ref, *refs):
    refs = list(refs)
    parts = [refs.pop(0) for _ in range(8)]
    weights = [refs.pop(0) for _ in range(8)]
    o_own, o_other, vecs = [refs.pop(0) for _ in range(3)]
    if has_prev:
        partial, norm_ref, pq_ref, po_ref, pv_ref = [refs.pop(0) for _ in range(5)]
    if last:
        mv_ref, at_ref, col_ref = [refs.pop(0) for _ in range(3)]
        send_ref, keep_ref, qsend_ref, qkeep_ref, osend_ref, okeep_ref = [refs.pop(0) for _ in range(6)]
    else:
        send_ref, keep_ref, gq_ref, go_ref, vec_ref = [refs.pop(0) for _ in range(5)]
    if not has_prev:
        norm_out_ref = refs.pop(0)
    wq, wo, x_s, c_s, x_n, h_s = [refs.pop(0) for _ in range(6)]
    q_s, k_s, v_s, g_s, kt_s, vt_s, gt_s = [refs.pop(0) for _ in range(7)]
    dq_s, dk_s, dv_s, at_s, att_s, dp_s, res_s, tab = [refs.pop(0) for _ in range(8)]
    w_sem, x_sem, r_sem = [refs.pop(0) for _ in range(3)]
    if has_prev:
        pp_s, pq_s, po_s, p_sem = [refs.pop(0) for _ in range(4)]
    f32, bf16 = jnp.float32, jnp.bfloat16
    seq = 8 * ROWS
    blocks = seq // BLOCK
    gain, shift, bias = vecs[0:1, :], vecs[1:2, :], vecs[5:6, :640]

    def place(piece):
        return pl.ds(pl.multiple_of(row_ref[16 + piece], ROWS), ROWS)

    weight_copies = [
        pltpu.make_async_copy(
            source,
            wq.at[pl.ds(pl.multiple_of(row_ref[at], 16), 96)],
            w_sem.at[at],
        )
        for at, source in enumerate(weights)
    ]
    out_weight_copies = [
        pltpu.make_async_copy(
            source, wo.at[pl.ds(pl.multiple_of(row_ref[8 + at], 16), 96)], w_sem.at[8 + at]
        )
        for at, source in enumerate((o_own, o_other))
    ]
    part_copies = [
        [
            pltpu.make_async_copy(
                parts[piece].at[kind, inside], target.at[place(piece)], x_sem.at[kind * 8 + piece]
            )
            for piece in range(8)
        ]
        for kind, target in (((1, c_s),) if has_prev else ((0, x_s), (1, c_s)))
    ]
    if has_prev:
        norm_part_copies = [
            pltpu.make_async_copy(
                norm_ref.at[at_seq - 1, pl.ds(piece * ROWS, ROWS)], x_n.at[place(piece)], x_sem.at[piece]
            )
            for piece in range(8)
        ]
        part_copies.insert(0, norm_part_copies)
    for copy in part_copies[0] + weight_copies + part_copies[1] + out_weight_copies:
        copy.start()
    if has_prev:
        prev_copies = [
            pltpu.make_async_copy(
                partial.at[at_seq - 1, piece, kind], pp_s.at[kind, place(piece)], p_sem.at[kind * 8 + piece]
            )
            for piece in range(8)
            for kind in range(2)
        ]
        prev_copies.append(pltpu.make_async_copy(pq_ref, pq_s, p_sem.at[16]))
        prev_copies.append(pltpu.make_async_copy(po_ref, po_s, p_sem.at[17]))
        for copy in prev_copies:
            copy.start()

    wo[192:, :] = jnp.zeros((64, 768), bf16)
    cos_f, sin_f, cos_c, sin_c, first, second = rotary_tables()
    for at in range(seq // 32):
        rows = slice(at * 32, (at + 1) * 32)
        cosine = cos_f * cos_c[at : at + 1] - sin_f * sin_c[at : at + 1]
        sine = sin_f * cos_c[at : at + 1] + cos_f * sin_c[at : at + 1]
        tab[0, rows, :] = cosine
        tab[1, rows, :] = jnp.where(first, -sine, 0.0)
        tab[2, rows, :] = jnp.where(second, sine, 0.0)

    lane = lax.broadcasted_iota(jnp.int32, (256, 128), 1)
    left = lane < 64

    def heads_of(block, project, grad):
        rows = slice(block * 256, (block + 1) * 256)
        cosine, low, high = tab[0, rows, :], tab[1, rows, :], tab[2, rows, :]
        for head in range(3):
            pair = project[:, head * 128 : (head + 1) * 128]
            pair = pair * cosine + pltpu.roll(pair, 120, 1) * low + pltpu.roll(pair, 8, 1) * high
            k_s[head, rows, :] = jnp.where(left, 0.0, pair).astype(bf16)
            q_s[head, rows, :] = jnp.where(left, 0.0, pltpu.roll(pair, 64, 1)).astype(bf16)
            kt_s[head, :, rows] = jnp.transpose(pair)[64:].astype(bf16)
        v_pair, v_last = project[:, 384:512], jnp.where(left, project[:, 512:640], 0.0)
        vt_s[:128, rows] = jnp.transpose(v_pair).astype(bf16)
        vt_s[128:, rows] = jnp.transpose(v_last)[:64].astype(bf16)
        for target, pair_value, last_value in ((v_s, v_pair, v_last), (g_s, grad[:, :128], grad[:, 128:])):
            target[0, rows, :] = jnp.where(left, pair_value, 0.0).astype(bf16)
            target[1, rows, :] = jnp.where(left, 0.0, pair_value).astype(bf16)
            target[2, rows, :] = last_value.astype(bf16)

    for copy in part_copies[0] + weight_copies + part_copies[1] + out_weight_copies:
        copy.wait()
    for block in (1, 3):
        wide = slice((block - 1) * 256, (block + 1) * 256)
        if has_prev:
            h_s[wide, :] = (x_n[wide, :] * gain + shift).astype(bf16)
        else:
            for part in range(32):
                rows = slice((block - 1) * 256 + part * 16, (block - 1) * 256 + (part + 1) * 16)
                normed, _ = normalize(x_s[rows, :].astype(f32))
                x_n[rows, :] = normed
                h_s[rows, :] = (normed * gain + shift).astype(bf16)
        project_wide = nn(h_s[wide, :], wq[...]) + bias
        grad_wide = nt(c_s[wide, :], wo[...])
        gt_s[:, wide] = nt(wo[:192, :], c_s[wide, :]).astype(bf16)
        for half in range(2):
            heads_of(block - 1 + half, project_wide[half * 256 : half * 256 + 256], grad_wide[half * 256 : half * 256 + 256])

    allowed = lax.broadcasted_iota(jnp.int32, (BLOCK, BLOCK), 0) <= lax.broadcasted_iota(
        jnp.int32, (BLOCK, BLOCK), 1
    )

    def rows_of(block):
        return slice(block * BLOCK, (block + 1) * BLOCK)

    def scores_of(head, block):
        query, grad = q_s[head, rows_of(block), :], g_s[head, rows_of(block), :]
        upto = (block + 1) * BLOCK
        scores = nt(k_s[head, :upto, :], query)
        scores = [scores[rows_of(at)] for at in range(block + 1)]
        scores[block] = jnp.where(allowed, scores[block], -1e30)
        d_prob = nt(v_s[head, :upto, :], grad)
        return scores, [d_prob[rows_of(at)] for at in range(block + 1)]

    def softmax_of(scores):
        top = jnp.max(scores[0], axis=0, keepdims=True)
        for part in scores[1:]:
            top = jnp.maximum(top, jnp.max(part, axis=0, keepdims=True))
        probs = [jnp.exp(part - top) for part in scores]
        total = col_sum(probs[0])
        for part in probs[1:]:
            total = total + col_sum(part)
        scale = 1.0 / total
        probs = [part * scale for part in probs]
        return probs, [part.astype(bf16) for part in probs]

    def values_of(head, block, probs, lows, d_prob):
        rows, upto = rows_of(block), (block + 1) * BLOCK
        low = jnp.concatenate(lows, axis=0) if block else lows[0]
        att_t = nn(vt_s[head * 64 : (head + 1) * 64, :upto], low)
        att_low = att_t.astype(bf16)
        att_s[head * 64 : (head + 1) * 64, rows] = att_low
        d_value = nn(low, g_s[head, rows, :])
        into = head // 2
        keep = slice(0, upto if head == 1 else upto - BLOCK)
        if keep.stop:
            dv_s[into, keep, :] += d_value[keep]
        if head != 1:
            dv_s[into, rows, :] = d_value[upto - BLOCK :]
        delta = col_sum(gt_s[head * 64 : (head + 1) * 64, rows].astype(f32) * att_low.astype(f32))
        return [(p * (d - delta)).astype(bf16) for p, d in zip(probs, d_prob)]

    def grads_of(head, block, d_scores):
        rows, upto = rows_of(block), (block + 1) * BLOCK
        d_score = jnp.concatenate(d_scores, axis=0) if block else d_scores[0]
        d_key = nn(d_score, q_s[head, rows, :])
        if block:
            dk_s[head, : upto - BLOCK, :] += d_key[: upto - BLOCK]
        dk_s[head, rows, :] = d_key[upto - BLOCK :]
        dq_s[head, rows, :64] = jnp.transpose(nn(kt_s[head, :, :upto], d_score))

    order = [(head, block) for block in range(blocks) for head in range(3)]
    ahead = scores_of(*order[0])
    waiting = None
    for at, (head, block) in enumerate(order):
        scores, d_prob = ahead
        if at + 1 < len(order):
            ahead = scores_of(*order[at + 1])
        probs, lows = softmax_of(scores)
        if waiting is not None:
            grads_of(*waiting)
        waiting = (head, block, values_of(head, block, probs, lows, d_prob))
    grads_of(*waiting)

    project_sums = []
    for head in range(3):
        total = jnp.zeros((1, 128), f32)
        for block in range(4):
            rows = slice(block * 256, (block + 1) * 256)
            pair = jnp.concatenate([dq_s[head, rows, :64], dk_s[head, rows, 64:]], axis=1)
            cosine, low, high = tab[0, rows, :], tab[1, rows, :], tab[2, rows, :]
            pair = pair * cosine - pltpu.roll(pair, 120, 1) * low - pltpu.roll(pair, 8, 1) * high
            total = total + col_sum(pair)
            dp_s[rows, head * 128 : (head + 1) * 128] = pair.astype(bf16)
        project_sums.append(total)
    for into in range(2):
        dp_s[:, 384 + into * 128 : 512 + into * 128] = dv_s[into].astype(bf16)
        project_sums.append(col_sum(dv_s[into]))
    if has_prev:
        for copy in prev_copies:
            copy.wait()
    for block in range(4):
        rows = slice(block * 256, (block + 1) * 256)
        at_s[rows, :128] = jnp.transpose(att_s[:128, rows].astype(f32)).astype(bf16)
        at_s[rows, 128:] = jnp.concatenate(
            [jnp.transpose(att_s[128:, rows].astype(f32)), jnp.zeros((256, 64), f32)], axis=1
        ).astype(bf16)
    out = nn(at_s[...], wo[...])
    d_hidden = nt(dp_s[...], wq[...])
    s = d_hidden * gain
    if has_prev:
        out = out + pp_s[0].astype(f32)
        s = s + pp_s[1].astype(f32)
    res_s[0] = out.astype(bf16)
    res_s[1] = s.astype(bf16)
    sums = [
        jnp.concatenate(project_sums, axis=1),
        col_sum(d_hidden * x_n[...]),
        col_sum(d_hidden),
    ]
    result_copies = [
        pltpu.make_async_copy(
            res_s.at[kind, place(piece)],
            (keep_ref if piece < 4 else send_ref).at[piece % 4, kind],
            r_sem.at[piece * 2 + kind],
        )
        for piece in (4, 5, 6, 7, 0, 1, 2, 3)
        for kind in range(2)
    ]
    if not has_prev:
        result_copies.append(pltpu.make_async_copy(x_n, norm_out_ref, r_sem.at[16]))
    for copy in result_copies:
        copy.start()
    g_query = tn(h_s[...], dp_s[...])
    g_out = nn(att_s[...], c_s[...])
    if has_prev:
        g_query = g_query + pq_s[...]
        g_out = g_out + po_s[...]
        sums = [sums[0] + pv_ref[0:1, :640], sums[1] + pv_ref[1:2, :], sums[2] + pv_ref[2:3, :]]
    if last:
        gq_s, go_s, tr_s = refs
        gq_s[...] = g_query
        go_s[...] = g_out
        tr_s[...] = jnp.zeros_like(tr_s)
        tr_s[64:65, :] = sums[1]
        tr_s[65:66, :] = sums[2]
        tr_s[66:69, :] = mv_ref[1:4, :]
        columns = jnp.transpose(tr_s[...])
        lanes = lax.broadcasted_iota(jnp.int32, (768, 128), 1)
        target_at = col_ref[0:1, :576] + row_ref[25] * 192
        for third in range(3):
            hit = at_ref[:, third : third + 1] == target_at
            column = jnp.sum(jnp.where(hit, sums[0][:, :576], 0.0), axis=1, keepdims=True)
            columns = jnp.where(lanes == 69 + third, column, columns)
        gq_s[:, 512:640] = jnp.where(lanes < 64, gq_s[:, 512:640], columns)
        for half, target in ((0, qkeep_ref), (1, qsend_ref)):
            for zz in range(4):
                at = zz * 2 + (row_ref[24] ^ half)
                rows = pl.ds(pl.multiple_of(at * 96, 16), 96)
                target[zz] = gq_s[rows, :].astype(target.dtype)
        for half, target in ((0, okeep_ref), (1, osend_ref)):
            rows = pl.ds(pl.multiple_of((row_ref[24] ^ half) * 96, 16), 96)
            target[...] = go_s[rows, :].astype(target.dtype)
    else:
        gq_ref[...] = g_query
        go_ref[...] = g_out
        vec_ref[...] = jnp.zeros_like(vec_ref)
        vec_ref[0:1, :640] = sums[0]
        vec_ref[1:2, :] = sums[1]
        vec_ref[2:3, :] = sums[2]
    for copy in result_copies:
        copy.wait()


def attn_call(row_offsets, parts, inside, weights, o_own, o_other, vecs, partial, seq, prev, tail):
    width = vecs.shape[-1]
    f32, bf16 = jnp.float32, jnp.bfloat16
    anywhere = pl.BlockSpec(memory_space=pl.ANY)
    dma = pltpu.SemaphoreType.DMA
    has_prev, last = prev is not None, tail is not None
    rows = 8 * ROWS
    half = (4, 2, ROWS, width)
    shapes = [(half, bf16), (half, bf16)]
    if last:
        shapes += [((4, 96, 640), bf16), ((4, 96, 640), f32), ((96, width), bf16), ((96, width), f32)]
    else:
        shapes += [((width, 640), f32), ((192, width), f32), ((8, width), f32)]
    out_specs = [anywhere] * 2 + [whole(shape) for shape, _ in shapes[2:]]
    if not has_prev:
        shapes.append(((rows, width), f32))
        out_specs.append(anywhere)
    operands = [*parts, *weights, o_own, o_other, vecs]
    in_specs = [anywhere] * 18 + [whole(vecs.shape)]
    scratch = [
        pltpu.VMEM((width, 640), bf16),
        pltpu.VMEM((256, width), bf16),
        pltpu.VMEM((rows, width), bf16),
        pltpu.VMEM((rows, width), bf16),
        pltpu.VMEM((rows, width), f32),
        pltpu.VMEM((rows, width), bf16),
    ]
    scratch += [pltpu.VMEM((3, rows, 128), bf16)] * 4
    scratch += [
        pltpu.VMEM((3, 64, rows), bf16),
        pltpu.VMEM((192, rows), bf16),
        pltpu.VMEM((192, rows), bf16),
        pltpu.VMEM((3, rows, 128), f32),
        pltpu.VMEM((3, rows, 128), f32),
        pltpu.VMEM((2, rows, 128), f32),
        pltpu.VMEM((rows, 256), bf16),
        pltpu.VMEM((192, rows), bf16),
        pltpu.VMEM((rows, 640), bf16),
        pltpu.VMEM((2, rows, width), bf16),
        pltpu.VMEM((3, rows, 128), f32),
        dma((10,)),
        dma((16,)),
        dma((17,)),
    ]
    if has_prev:
        operands += [*partial, *prev]
        in_specs += [anywhere] * 4 + [whole(prev[2].shape)]
        scratch += [
            pltpu.VMEM((2, rows, width), bf16),
            pltpu.VMEM((width, 640), f32),
            pltpu.VMEM((192, width), f32),
            dma((18,)),
        ]
    if last:
        operands += list(tail)
        in_specs += [whole(a.shape) for a in tail]
        scratch += [pltpu.VMEM((width, 640), f32), pltpu.VMEM((192, width), f32), pltpu.VMEM((128, width), f32)]
    return pl.pallas_call(
        functools.partial(attn_kernel, has_prev, last, seq, inside),
        grid_spec=pltpu.PrefetchScalarGridSpec(
            num_scalar_prefetch=1,
            grid=(1,),
            in_specs=in_specs,
            out_specs=out_specs,
            scratch_shapes=scratch,
        ),
        out_shape=[jax.ShapeDtypeStruct(shape, kind) for shape, kind in shapes],
        compiler_params=pltpu.CompilerParams(vmem_limit_bytes=58 << 20),
        cost_estimate=pl.CostEstimate(
            flops=24_000_000_000, transcendentals=0, bytes_accessed=15_000_000
        ),
        name="attn",
    )(row_offsets, *operands)


def finish_kernel(seqs, half_ref, x_ref, c_ref, *refs):
    refs = list(refs)
    terms = [[refs.pop(0) for _ in range(4)] for _ in seqs]
    bias = refs.pop(0)
    out_ref, grad_ref = refs[-2:]
    f32 = jnp.float32

    def write(sources):
        total = [source[0].astype(f32) for source in sources]
        total = sum(total[1:], total[0])
        x = x_ref[0].astype(f32)
        normed, inverse = normalize(x)
        out_ref[0] = x + bias[4:5, :] + total[0]
        s = total[1]
        mean_s = jnp.mean(s, axis=-1, keepdims=True)
        mean_sn = jnp.mean(s * normed, axis=-1, keepdims=True)
        grad_ref[0] = c_ref[0] + inverse * (s - mean_s - normed * mean_sn)

    for at in range(len(seqs)):
        for other in range(2):
            @pl.when(pl.program_id(0) == at * 2 + other)
            def _(at=at, other=other):
                write(terms[at][3:] if other else terms[at][:3])


def finish_call(half, seqs, x, cot, terms, bias, done):
    _, rows, width = x.shape
    f32 = jnp.float32
    seq_spec = pl.BlockSpec(
        (1, rows, width),
        lambda i, at: (jnp.where(i % 2 == 0, at[0], 1 - at[0]) * 3 + seqs[0] + i // 2, 0, 0),
    )
    part_spec = pl.BlockSpec((1, 2, rows, width), lambda i, at: (0, 0, 0, 0))
    before = list(done) if done is not None else []
    operands = [x, cot, *[a for parts in terms for a in parts], bias]
    return pl.pallas_call(
        functools.partial(finish_kernel, seqs),
        grid_spec=pltpu.PrefetchScalarGridSpec(
            num_scalar_prefetch=1,
            grid=(2 * len(seqs),),
            in_specs=[seq_spec, seq_spec]
            + [part_spec] * (4 * len(seqs))
            + [whole(bias.shape)]
            + [pl.BlockSpec(memory_space=pl.ANY)] * len(before),
            out_specs=[seq_spec, seq_spec],
        ),
        out_shape=[jax.ShapeDtypeStruct(x.shape, f32)] * 2,
        input_output_aliases={len(operands) + 1: 0, len(operands) + 2: 1} if before else {},
        name="finish",
    )(half, *operands, *before)


def pick(value, index, axis=0):
    return lax.dynamic_index_in_dim(value, index, axis, keepdims=False)


def prep_kernel(at_ref, in_ref, q_ref, small_ref, own_ref, send_ref, pack_s):
    for h in range(4):
        parts = [in_ref[:, zy * 384 + h * 96 : zy * 384 + (h + 1) * 96] for zy in range(8)]
        for head in range(3):
            for kind in range(2):
                first = kind * 768 + h * 192 + head * 64
                parts.append(q_ref[:, first : first + 64])
        first = 1536 + h * 192
        parts.append(q_ref[:, first : first + 192])
        parts.append(small_ref[...])
        at = 0
        for part in parts:
            pack_s[h, :, at : at + part.shape[1]] = part
            at += part.shape[1]
    for core in range(2):
        own_ref[core] = pack_s[at_ref[26] * 2 + core]
        send_ref[core] = pack_s[(1 - at_ref[26]) * 2 + core]


def prep_call(row_offsets, w_in, w_qkv, small):
    half = jax.ShapeDtypeStruct((2, 24, 1408), jnp.bfloat16)
    return pl.pallas_call(
        prep_kernel,
        grid_spec=pltpu.PrefetchScalarGridSpec(
            num_scalar_prefetch=1,
            grid=(1,),
            in_specs=[whole(a.shape) for a in (w_in, w_qkv, small)],
            out_specs=[whole(half.shape)] * 2,
            scratch_shapes=[pltpu.VMEM((4, 24, 1408), jnp.bfloat16)],
        ),
        out_shape=[half, half],
        name="prep",
    )(row_offsets, w_in, w_qkv, small)


def join_kernel(at_ref, own_ref, got_ref, far_ref, down_ref, attn_ref, mlp_ref, four, rows_s):
    f32, bf16 = jnp.float32, jnp.bfloat16
    x, c = at_ref[26], at_ref[27]
    four[0] = own_ref[c].astype(f32)
    four[1] = got_ref[c].astype(f32)
    four[2] = far_ref[0].astype(f32)
    four[3] = far_ref[1].astype(f32)
    for source in range(4):
        near = ((source & 1) ^ c) * 2 + ((source >> 1) ^ x)
        rows_s[source * 24 : (source + 1) * 24, :] = four[near]
    mlp_ref[:96, :] = rows_s[:, :768].astype(bf16)
    mlp_ref[96:, :] = down_ref[...]
    attn_ref[...] = rows_s[:, 768:].astype(bf16)


def join_call(row_offsets, own, got, far, w_down):
    f32, bf16 = jnp.float32, jnp.bfloat16
    outs = [jax.ShapeDtypeStruct((96, 640), bf16), jax.ShapeDtypeStruct((192, 768), bf16)]
    return pl.pallas_call(
        join_kernel,
        grid_spec=pltpu.PrefetchScalarGridSpec(
            num_scalar_prefetch=1,
            grid=(1,),
            in_specs=[whole(a.shape) for a in (own, got, far, w_down)],
            out_specs=[whole(a.shape) for a in outs],
            scratch_shapes=[pltpu.VMEM((4, 24, 1408), f32), pltpu.VMEM((96, 1408), f32)],
        ),
        out_shape=outs,
        name="join",
    )(row_offsets, own, got, far, w_down)


def pick_out_kernel(at_ref, one, two, three, four, own_ref, send_ref, all_s):
    for at, source in enumerate((one, two, three, four)):
        all_s[at] = source[...]
    for core in range(2):
        own_ref[core] = all_s[(at_ref[28] - at_ref[26] * 2 - core + 4) % 4]
        send_ref[core] = all_s[(at_ref[28] - (1 - at_ref[26]) * 2 - core + 4) % 4]


def pick_out_call(row_offsets, pieces):
    half = jax.ShapeDtypeStruct((2, 24, 768), jnp.bfloat16)
    return pl.pallas_call(
        pick_out_kernel,
        grid_spec=pltpu.PrefetchScalarGridSpec(
            num_scalar_prefetch=1,
            grid=(1,),
            in_specs=[whole((24, 768))] * 4,
            out_specs=[whole(half.shape)] * 2,
            scratch_shapes=[pltpu.VMEM((4, 24, 768), jnp.bfloat16)],
        ),
        out_shape=[half, half],
        name="out_pick",
    )(row_offsets, *pieces)


def join_out_kernel(at_ref, own_ref, got_ref, far_ref, out_ref, four, rows_s):
    f32, bf16 = jnp.float32, jnp.bfloat16
    x, c = at_ref[26], at_ref[27]
    four[0] = own_ref[c].astype(f32)
    four[1] = got_ref[c].astype(f32)
    four[2] = far_ref[0].astype(f32)
    four[3] = far_ref[1].astype(f32)
    for source in range(4):
        near = ((source & 1) ^ c) * 2 + ((source >> 1) ^ x)
        rows_s[source * 24 : (source + 1) * 24, :] = four[near]
    out_ref[...] = rows_s[...].astype(bf16)


def join_out_call(row_offsets, own, got, far):
    f32, bf16 = jnp.float32, jnp.bfloat16
    return pl.pallas_call(
        join_out_kernel,
        grid_spec=pltpu.PrefetchScalarGridSpec(
            num_scalar_prefetch=1,
            grid=(1,),
            in_specs=[whole(a.shape) for a in (own, got, far)],
            out_specs=whole((96, 768)),
            scratch_shapes=[pltpu.VMEM((4, 24, 768), f32), pltpu.VMEM((96, 768), f32)],
        ),
        out_shape=jax.ShapeDtypeStruct((96, 768), bf16),
        name="join_out",
    )(row_offsets, own, got, far)


def vector_tables():
    row = np.arange(768)
    at_q = np.stack([(row // 24) * 72 + third * 24 + row % 24 for third in range(3)], axis=1)
    at_in = np.stack([(row // 24) * 96 + third * 24 + row % 24 for third in range(4)], axis=1)
    lane = np.arange(576)
    head, kind = lane // 128, (lane % 128) // 64
    col_q = np.where(lane < 384, kind * 768 + head * 64 + lane % 64, 1536 + lane - 384)
    col_in = (row // 96) * 384 + row % 96
    cols = np.zeros((8, 768), np.int32)
    cols[0, :576] = col_q
    cols[1] = col_in
    rows = np.concatenate([at_q, at_in, np.zeros((768, 1))], axis=1).astype(np.int32)
    return rows, cols


def vec_kernel(at_ref, *refs):
    refs = list(refs)
    pieces = [refs.pop(0) for _ in range(8)]
    rows_ref, cols_ref, out_ref, all_s = refs
    f32 = jnp.float32
    for at, source in enumerate(pieces):
        rows = pl.ds(pl.multiple_of(at_ref[at], 16), 96)
        all_s[rows, :] = source[...].astype(f32)
    flipped = jnp.transpose(all_s[...])
    out_ref[0:4, :] = flipped[64:68]
    out_ref[4:5, :] = flipped[68:69] + flipped[69:70]
    for row, kinds, target, width, step in ((5, (0, 1, 2), 0, 576, 192), (6, (3, 4, 5, 6), 1, 768, 96)):
        wanted = cols_ref[target : target + 1, :width] + at_ref[25] * step
        total = jnp.zeros((1, width), f32)
        for kind in kinds:
            hit = rows_ref[:, kind : kind + 1] == wanted
            total += col_sum(jnp.where(hit, all_s[:, 70 + kind : 71 + kind], 0.0))
        out_ref[row : row + 1, :width] = total
    out_ref[7:8, :] = jnp.zeros((1, 768), f32)
    out_ref[5:6, 576:] = jnp.zeros((1, 192), f32)


def vec_call(row_offsets, pieces, rows, cols):
    f32 = jnp.float32
    return pl.pallas_call(
        vec_kernel,
        grid_spec=pltpu.PrefetchScalarGridSpec(
            num_scalar_prefetch=1,
            grid=(1,),
            in_specs=[pl.BlockSpec((96, 128), lambda i, *_: (0, 4))] * 8
            + [whole(rows.shape), whole(cols.shape)],
            out_specs=whole((8, 768)),
            scratch_shapes=[pltpu.VMEM((768, 128), f32)],
        ),
        out_shape=jax.ShapeDtypeStruct((8, 768), f32),
        name="vectors",
    )(row_offsets, *pieces, rows, cols)


def spread_kernel(at_ref, q_mine, q_far, in_mine, in_far, q_ref, in_ref, *refs):
    f32 = jnp.float32
    out_refs, (q_four, in_four) = refs[:6], refs[6:]
    x, c = at_ref[26], at_ref[27]
    for four, near, far in ((q_four, q_mine, q_far), (in_four, in_mine, in_far)):
        for side in range(2):
            four[side] = near[side]
            four[2 + side] = far[side]
    total = None
    for h in range(4):
        near = ((h & 1) ^ c) * 2 + ((h >> 1) ^ x)
        block = in_four[near].astype(f32)
        for zy in range(8):
            first = zy * 384 + h * 96
            in_ref[:, first : first + 96] = block[:, zy * 96 : (zy + 1) * 96]
        block = q_four[near].astype(f32)
        for head in range(3):
            for kind in range(2):
                first = kind * 768 + h * 192 + head * 64
                at = head * 128 + kind * 64
                q_ref[:, first : first + 64] = block[:, at : at + 64]
        first = 1536 + h * 192
        q_ref[:, first : first + 192] = block[:, 384:576]
        part = block[:, 576:584]
        total = part if total is None else total + part
    same = lax.broadcasted_iota(jnp.int32, (24, 24), 0) == lax.broadcasted_iota(jnp.int32, (24, 24), 1)
    rows = [col_sum(jnp.where(same, total[:, t : t + 1], 0.0)) for t in range(8)]
    for t in range(5):
        out_refs[t][...] = rows[t]
    out_refs[5][...] = jnp.concatenate(rows[5:], axis=1)


def spread_call(row_offsets, q_pair, in_pair):
    f32, bf16 = jnp.float32, jnp.bfloat16
    shapes = [(24, 2304), (24, 3072)] + [(1, 24)] * 5 + [(1, 72)]
    operands = [*q_pair, *in_pair]
    return pl.pallas_call(
        spread_kernel,
        grid_spec=pltpu.PrefetchScalarGridSpec(
            num_scalar_prefetch=1,
            grid=(1,),
            in_specs=[whole(a.shape) for a in operands],
            out_specs=[whole(shape) for shape in shapes],
            scratch_shapes=[pltpu.VMEM((4, 24, 640), bf16), pltpu.VMEM((4, 24, 768), bf16)],
        ),
        out_shape=[jax.ShapeDtypeStruct(shape, f32) for shape in shapes],
        name="spread",
    )(row_offsets, *operands)


def exchange_four(blocks, x, c):
    blocks = blocks.reshape((2, 2) + blocks.shape[1:])
    own = pick(blocks, x)
    got = swap(pick(blocks, 1 - x), 2)
    both = jnp.stack([own, got])
    mine = pick(both, c, 1)
    send = pick(both, 1 - c, 1)
    return mine, swap(send, 1)


def fast(*args):
    return fast_body(*args)


def fast_body(
    inputs, cotangent, ln1_gain, ln1_bias, ln2_gain, ln2_bias, w_qkv, b_qkv, w_out, b_out, w_in, b_in, w_mlp_out, b_mlp_out
):
    f32, bf16 = jnp.float32, jnp.bfloat16
    z = lax.axis_index("fsdp")
    ctx = lax.axis_index("ctx")
    y, x, c = ctx // 4, (ctx // 2) % 2, ctx % 2
    h = ctx % 4

    zs = jnp.stack([(z - k) % 4 for k in range(4)])
    rows_w = jnp.concatenate([(zs * 2 + y) * 96, (zs * 2 + 1 - y) * 96])
    rows_o = jnp.stack([y * 96, (1 - y) * 96])
    rows_p = jnp.stack([(ctx ^ piece_bits(k)) * ROWS for k in range(8)])
    row_offsets = jnp.concatenate(
        [rows_w, rows_o, jnp.zeros((6,), jnp.int32), rows_p, jnp.stack([y, h, x, c, z])]
    ).astype(jnp.int32)

    small = jnp.concatenate(
        [ln1_gain, ln1_bias, ln2_gain, ln2_bias, b_out, b_mlp_out, b_qkv, b_in, jnp.zeros((51 * 24,), bf16)]
    ).reshape(64, 24).T
    pack_own, pack_send = prep_call(row_offsets, w_in, w_qkv, small)

    def rows_of(half, first, count):
        at = half * 3 + first
        return jnp.stack(
            [
                lax.dynamic_slice_in_dim(inputs, at, count),
                lax.dynamic_slice_in_dim(cotangent, at, count).astype(bf16),
            ]
        )

    parts = []
    first = 0
    for count in CHUNKS:
        got = swap(rows_of(1 - y, first, count), 4)
        own = rows_of(y, first, count)
        side, side_got = swap(own, 2), swap(got, 2)
        near = (own, got, side, side_got)
        parts.append(near + tuple(swap(a, 1) for a in near))
        first += count

    pack_got = swap(pack_send, 2)
    pack_far = swap(jnp.stack([pick(pack_own, 1 - c), pick(pack_got, 1 - c)]), 1)
    out_all = [w_out] + [shift_z(w_out, k) for k in (1, 2, 3)]
    attn_w, mlp_w = join_call(row_offsets, pack_own, pack_got, pack_far, w_mlp_out)
    attn_own = [attn_w] + [shift_z(attn_w, k) for k in (1, 2, 3)]
    mlp_own = [mlp_w] + [shift_z(mlp_w, k) for k in (1, 2, 3)]
    attn_all = attn_own + [swap(part, 4) for part in attn_own]
    mlp_all = mlp_own + [swap(part, 4) for part in mlp_own]
    out_mine, out_send = pick_out_call(row_offsets, out_all)
    out_got = swap(out_send, 2)
    out_far = swap(jnp.stack([pick(out_mine, 1 - c), pick(out_got, 1 - c)]), 1)
    out_own = join_out_call(row_offsets, out_mine, out_got, out_far)
    out_other = swap(out_own, 4)
    at_rows, at_cols = vector_tables()
    vecs = vec_call(row_offsets, attn_all, at_rows, at_cols)

    where = [(at, inside) for at, count in enumerate(CHUNKS) for inside in range(count)]

    def attention(seq, partial, prev, tail=None):
        at, inside = where[seq]
        return attn_call(
            row_offsets, parts[at], inside, attn_all, out_own, out_other,
            vecs, partial, seq, prev, tail,
        )

    def reduce_z(blocks, place=lambda at: at):
        def total(at):
            at = place(at)
            value = pick(blocks[0], at).astype(f32)
            for block in blocks[1:]:
                value = value + pick(block, at).astype(f32)
            return value

        low = [total((z + k) % 4).astype(bf16) for k in (1, 2, 3)]
        sent = [shift_z(part, k + 1) for k, part in enumerate(low)]
        result = total(z)
        for part in sent:
            result = result + part.astype(f32)
        return result

    half = jnp.reshape(y, (1,)).astype(jnp.int32)

    def scatter(send, keep):
        got = swap(send, 1)
        side = swap((keep[2:].astype(f32) + got[2:].astype(f32)).astype(bf16), 2)
        far = (keep[1:2].astype(f32) + got[1:2].astype(f32) + side[1:2].astype(f32)).astype(bf16)
        return keep, got, side, swap(far, 4)

    def finish(seqs, terms, done):
        return finish_call(half, seqs, inputs, cotangent, terms, vecs, done)

    first_send, first_keep, g_q, g_o, vec, first_norm = attention(0, None, None)
    prev = (g_q, g_o, vec)
    send, keep, rest_part, rest_norm, g_send, g_keep, mlp_vec = mlp_call(
        row_offsets, parts, mlp_all, vecs, cotangent, first_send, first_keep, first_norm
    )
    g_got = swap(g_send, 4)
    terms = [scatter(send, keep)]
    send, keep, g_q, g_o, vec = attention(1, (rest_part, rest_norm), prev)
    terms.append(scatter(send, keep))
    mlp_grad = reduce_z((g_keep, g_got))
    grad_w_mlp = mlp_grad[96:192]
    grad_b_in = mlp_grad[192, :96]
    in_pair = exchange_four(mlp_grad[:96].astype(bf16).reshape(4, 24, 768), x, c)
    send, keep, q_send, q_keep, o_send, o_keep = attention(
        2, (rest_part, rest_norm), (g_q, g_o, vec), (mlp_vec, at_rows, at_cols)
    )
    terms.append(scatter(send, keep))
    done = None
    for seq in range(3):
        done = finish((seq,), terms[seq : seq + 1], done)
    q_grad = reduce_z((q_keep, swap(q_send, 4)))
    q_low = q_grad.astype(bf16).reshape(4, 24, 640)
    q_pair = exchange_four(q_low, x, c)
    grad_w_qkv, grad_w_in, *spread = spread_call(row_offsets, q_pair, in_pair)
    one_gain, one_bias, two_gain, two_bias, grad_bias, grad_bq = [v.reshape(-1) for v in spread]

    o_parts = o_keep + swap(o_send, 4).astype(f32)
    o_low = o_parts.astype(bf16).reshape(4, 24, 768)
    o_blocks = jnp.concatenate(exchange_four(o_low, x, c))
    grad_w_out = reduce_z((o_blocks,), lambda at: ((at & 1) ^ c) * 2 + ((at >> 1) ^ x))

    outputs, grad_inputs = done
    return (
        outputs,
        grad_inputs,
        one_gain,
        one_bias,
        two_gain,
        two_bias,
        grad_w_qkv,
        grad_bq,
        grad_w_out,
        grad_bias,
        grad_w_in,
        grad_b_in,
        grad_w_mlp,
        grad_bias,
    )


def fast_fits(mesh):
    sizes = dict(mesh.shape)
    return sizes["fsdp"] == 4 and sizes["ctx"] == 8


def solution(mesh):
    return jax.shard_map(
        fast if fast_fits(mesh) else local,
        mesh=mesh,
        in_specs=(
            P("fsdp", "ctx", None),
            P("fsdp", "ctx", None),
            P(("fsdp", "ctx")),
            P(("fsdp", "ctx")),
            P(("fsdp", "ctx")),
            P(("fsdp", "ctx")),
            P(("fsdp", "ctx"), None),
            P(("fsdp", "ctx")),
            P(("fsdp", "ctx"), None),
            P(("fsdp", "ctx")),
            P(("fsdp", "ctx"), None),
            P(("fsdp", "ctx")),
            P(("fsdp", "ctx"), None),
            P(("fsdp", "ctx")),
        ),
        out_specs=(
            P("fsdp", "ctx", None),
            P("fsdp", "ctx", None),
            P(("fsdp", "ctx")),
            P(("fsdp", "ctx")),
            P(("fsdp", "ctx")),
            P(("fsdp", "ctx")),
            P(("fsdp", "ctx"), None),
            P(("fsdp", "ctx")),
            P(("fsdp", "ctx"), None),
            P(("fsdp", "ctx")),
            P(("fsdp", "ctx"), None),
            P(("fsdp", "ctx")),
            P(("fsdp", "ctx"), None),
            P(("fsdp", "ctx")),
        ),
        check_vma=False,
    )
```

```python
import functools
import math

import jax
import jax.numpy as jnp
import numpy as np
from jax import lax
from jax.experimental import pallas as pl
from jax.experimental.pallas import tpu as pltpu
from jax.sharding import PartitionSpec as P


HEADS = 12
HEAD_DIM = 64
ROT_DIM = 16
MICRO = 2
SEQ_MB = 3
CHUNKS = (1, 2)


EPS = 1e-05
BASE_FREQ = 10000.0


def layer_norm(values, gain_row, shift_row):
    centre = jnp.mean(values, axis=-1, keepdims=True)
    centred = values - centre
    inverse = lax.rsqrt(jnp.mean(centred * centred, axis=-1, keepdims=True) + EPS)
    normed = centred * inverse
    return (normed * gain_row + shift_row, normed, inverse)


def norm_back(grad_out, normed, inverse, gain_row):
    scaled = grad_out * gain_row
    return inverse * (
        scaled
        - jnp.mean(scaled, axis=-1, keepdims=True)
        - normed * jnp.mean(scaled * normed, axis=-1, keepdims=True)
    )


def angles(positions):
    half_rot = ROT_DIM // 2
    inv_freq = BASE_FREQ ** (-(2.0 * jnp.arange(half_rot, dtype=jnp.float32)) / ROT_DIM)
    phase_angle = positions.astype(jnp.float32)[:, None] * inv_freq[None, :]
    return (jnp.cos(phase_angle), jnp.sin(phase_angle))


def rotate(head_field, cosine, sine_rot, direction):
    half_rot = ROT_DIM // 2
    lead_half = head_field[..., :half_rot]
    trail_half = head_field[..., half_rot:ROT_DIM]
    cos_wide = cosine[:, None, :]
    sin_wide = direction * sine_rot[:, None, :]
    return jnp.concatenate(
        [
            lead_half * cos_wide - trail_half * sin_wide,
            trail_half * cos_wide + lead_half * sin_wide,
            head_field[..., ROT_DIM:],
        ],
        axis=-1,
    )


def gelu_parts(pre_act):
    normal_cdf = 0.5 * (1.0 + jax.scipy.special.erf(pre_act * 0.7071067811865476))
    density = jnp.exp(-0.5 * pre_act * pre_act) * 0.3989422804014327
    return (pre_act * normal_cdf, normal_cdf + pre_act * density)


def outer_rows(left, right):
    return lax.dot_general(
        left, right, (((0,), (0,)), ((), ())), preferred_element_type=jnp.float32
    )


def times_transpose(left, right):
    return lax.dot_general(
        left, right, (((1,), (1,)), ((), ())), preferred_element_type=jnp.float32
    )


def attend_block(soft_state, kv_block, first_row, query_low, positions, score_scale):
    run_max, run_sum, weighted = soft_state
    seq_count, block_rows, double_width = kv_block.shape
    model_width = double_width // 2
    key_low = kv_block[..., :model_width].reshape(seq_count, block_rows, HEADS, HEAD_DIM)
    value_low = kv_block[..., model_width:].reshape(seq_count, block_rows, HEADS, HEAD_DIM)
    scores = (
        jnp.einsum("sqhd,skhd->shqk", query_low, key_low, preferred_element_type=jnp.float32)
        * score_scale
    )
    allowed = (first_row + jnp.arange(block_rows, dtype=jnp.int32))[None, :] <= positions[:, None]
    scores = jnp.where(allowed, scores, -jnp.inf)
    new_max = jnp.maximum(run_max, jnp.max(scores, axis=-1))
    safe_max = jnp.where(new_max == -jnp.inf, 0.0, new_max)
    exp_scores = jnp.exp(scores - safe_max[..., None])
    factor = jnp.exp(run_max - safe_max)
    run_sum = run_sum * factor + jnp.sum(exp_scores, axis=-1)
    weighted = weighted * factor[..., None] + jnp.einsum(
        "shqk,skhd->shqd",
        exp_scores.astype(jnp.bfloat16),
        value_low,
        preferred_element_type=jnp.float32,
    )
    return (new_max, run_sum, weighted)


def attend_piece(soft_state, kv_piece, query_low, positions, score_scale):
    piece_rows = kv_piece.shape[1]
    step_rows = math.gcd(piece_rows, 512)

    def one_block(block_index, inner_state):
        offset = block_index * step_rows
        kv_block = lax.dynamic_slice_in_dim(kv_piece, offset, step_rows, 1)
        return attend_block(inner_state, kv_block, offset, query_low, positions, score_scale)

    return lax.fori_loop(0, piece_rows // step_rows, one_block, soft_state)


def local(
    inputs,
    cotangent,
    ln1_gain,
    ln1_bias,
    ln2_gain,
    ln2_bias,
    w_qkv,
    b_qkv,
    w_out,
    b_out,
    w_in,
    b_in,
    w_mlp_out,
    b_mlp_out,
):
    f32 = jnp.float32
    bf16 = jnp.bfloat16
    group_rows = inputs.shape[1]
    model_width = inputs.shape[2]
    seq_len = group_rows * lax.axis_size("ctx")
    key_block = math.gcd(seq_len, 512)
    score_scale = HEAD_DIM ** (-0.5)
    positions = lax.axis_index("ctx") * group_rows + jnp.arange(group_rows, dtype=jnp.int32)
    cosine, sine_rot = angles(positions)

    def gather_params():
        return (
            lax.all_gather(ln1_gain, ("fsdp", "ctx"), axis=0, tiled=True),
            lax.all_gather(ln1_bias, ("fsdp", "ctx"), axis=0, tiled=True),
            lax.all_gather(ln2_gain, ("fsdp", "ctx"), axis=0, tiled=True),
            lax.all_gather(ln2_bias, ("fsdp", "ctx"), axis=0, tiled=True),
            lax.all_gather(w_qkv, ("fsdp", "ctx"), axis=0, tiled=True),
            lax.all_gather(b_qkv, ("fsdp", "ctx"), axis=0, tiled=True),
            lax.all_gather(w_out, ("fsdp", "ctx"), axis=0, tiled=True),
            lax.all_gather(b_out, ("fsdp", "ctx"), axis=0, tiled=True),
            lax.all_gather(w_in, ("fsdp", "ctx"), axis=0, tiled=True),
            lax.all_gather(b_in, ("fsdp", "ctx"), axis=0, tiled=True),
            lax.all_gather(w_mlp_out, ("fsdp", "ctx"), axis=0, tiled=True),
            lax.all_gather(b_mlp_out, ("fsdp", "ctx"), axis=0, tiled=True),
        )

    weight_sums = None
    output_list = []
    grad_list = []
    for micro_index in range(MICRO):
        batch_rows = inputs[micro_index * SEQ_MB : (micro_index + 1) * SEQ_MB]
        cot_rows = cotangent[micro_index * SEQ_MB : (micro_index + 1) * SEQ_MB]
        seq_count = batch_rows.shape[0]
        flat_rows = seq_count * group_rows
        params_fwd = gather_params()
        (
            gain_one,
            shift_one,
            gain_two,
            shift_two,
            weight_qkv,
            bias_qkv,
            weight_out,
            bias_out,
            weight_in,
            bias_in,
            weight_mlp,
            bias_mlp,
        ) = params_fwd
        residual = batch_rows.reshape(flat_rows, model_width).astype(f32)
        normal_one, normed_one, inverse_one = layer_norm(
            residual, gain_one.astype(f32), shift_one.astype(f32)
        )
        normal_two, normed_two, inverse_two = layer_norm(
            residual, gain_two.astype(f32), shift_two.astype(f32)
        )
        hidden_one = normal_one.astype(bf16)
        hidden_two = normal_two.astype(bf16)
        project = jnp.dot(hidden_one, weight_qkv, preferred_element_type=f32) + bias_qkv.astype(f32)
        head_shape = (seq_count, group_rows, HEADS, HEAD_DIM)
        query_low = rotate(
            project[:, :model_width].reshape(head_shape), cosine, sine_rot, 1.0
        ).astype(bf16)
        key_low = rotate(
            project[:, model_width : 2 * model_width].reshape(head_shape), cosine, sine_rot, 1.0
        ).astype(bf16)
        value_low = project[:, 2 * model_width :].astype(bf16)
        kv_pack = jnp.concatenate(
            [
                key_low.reshape(seq_count, group_rows, model_width),
                value_low.reshape(seq_count, group_rows, model_width),
            ],
            axis=-1,
        )
        start_state = (
            jnp.full((seq_count, HEADS, group_rows), -jnp.inf, f32),
            jnp.zeros((seq_count, HEADS, group_rows), f32),
            jnp.zeros((seq_count, HEADS, group_rows, HEAD_DIM), f32),
        )
        soft_state = attend_piece(
            start_state,
            lax.all_gather(kv_pack, "ctx", axis=1, tiled=True),
            query_low,
            positions,
            score_scale,
        )
        run_max, run_sum, weighted = soft_state
        log_total = run_max + jnp.log(run_sum)
        attended = jnp.transpose(weighted / run_sum[..., None], (0, 2, 1, 3)).astype(bf16)
        att_flat = attended.reshape(flat_rows, model_width)
        pre_act = jnp.dot(hidden_two, weight_in, preferred_element_type=f32) + bias_in.astype(f32)
        activation_f, gelu_slope = gelu_parts(pre_act)
        activation = activation_f.astype(bf16)
        output = (
            residual
            + jnp.dot(att_flat, weight_out, preferred_element_type=f32)
            + bias_out.astype(f32)
            + jnp.dot(activation, weight_mlp, preferred_element_type=f32)
            + bias_mlp.astype(f32)
        )
        output_list.append(output.reshape(seq_count, group_rows, model_width))
        params_back = gather_params()
        (
            gain_one,
            shift_one,
            gain_two,
            shift_two,
            weight_qkv,
            bias_qkv,
            weight_out,
            bias_out,
            weight_in,
            bias_in,
            weight_mlp,
            bias_mlp,
        ) = params_back
        kv_rows = lax.all_gather(kv_pack, "ctx", axis=1, tiled=True)
        cot_flat = cot_rows.reshape(flat_rows, model_width)
        cot_low = cot_flat.astype(bf16)
        cot_sum = jnp.sum(cot_flat, axis=0)
        grad_w_out = outer_rows(att_flat, cot_low)
        grad_w_mlp = outer_rows(activation, cot_low)
        d_pre = times_transpose(cot_low, weight_mlp) * gelu_slope
        d_pre_low = d_pre.astype(bf16)
        grad_w_in = outer_rows(hidden_two, d_pre_low)
        d_hidden_two = times_transpose(d_pre_low, weight_in)
        grad_att = times_transpose(cot_low, weight_out).astype(bf16).reshape(head_shape)
        row_delta = jnp.einsum("sqhd,sqhd->shq", grad_att, attended, preferred_element_type=f32)

        def back_block(block_index, loop_carry):
            grad_query, buffer = loop_carry
            offset = block_index * key_block
            kv_block = lax.dynamic_slice_in_dim(kv_rows, offset, key_block, 1)
            key_part = kv_block[..., :model_width].reshape(seq_count, key_block, HEADS, HEAD_DIM)
            value_part = kv_block[..., model_width:].reshape(seq_count, key_block, HEADS, HEAD_DIM)
            scores = (
                jnp.einsum("sqhd,skhd->shqk", query_low, key_part, preferred_element_type=f32)
                * score_scale
            )
            allowed = (offset + jnp.arange(key_block, dtype=jnp.int32))[None, :] <= positions[
                :, None
            ]
            prob_block = jnp.where(allowed, jnp.exp(scores - log_total[..., None]), 0.0)
            grad_value = jnp.einsum(
                "shqk,sqhd->skhd", prob_block.astype(bf16), grad_att, preferred_element_type=f32
            )
            grad_prob = jnp.einsum(
                "sqhd,skhd->shqk", grad_att, value_part, preferred_element_type=f32
            )
            grad_score = (prob_block * (grad_prob - row_delta[..., None]) * score_scale).astype(
                bf16
            )
            grad_query = grad_query + jnp.einsum(
                "shqk,skhd->sqhd", grad_score, key_part, preferred_element_type=f32
            )
            grad_key = jnp.einsum(
                "shqk,sqhd->skhd", grad_score, query_low, preferred_element_type=f32
            )
            key_value_grad = jnp.concatenate(
                [
                    grad_key.reshape(seq_count, key_block, model_width),
                    grad_value.reshape(seq_count, key_block, model_width),
                ],
                axis=-1,
            )
            return (grad_query, lax.dynamic_update_slice_in_dim(buffer, key_value_grad, offset, 1))

        start_carry = (
            jnp.zeros(head_shape, f32),
            jnp.zeros((seq_count, seq_len, 2 * model_width), f32),
        )
        grad_query, buffer = lax.fori_loop(0, seq_len // key_block, back_block, start_carry)
        kv_grad_own = lax.psum_scatter(
            buffer.astype(jnp.bfloat16), "ctx", scatter_dimension=1, tiled=True
        ).astype(jnp.float32)
        key_grad_raw = kv_grad_own[..., :model_width].reshape(head_shape)
        value_grad_flat = kv_grad_own[..., model_width:].reshape(flat_rows, model_width)
        grad_query = rotate(grad_query, cosine, sine_rot, -1.0)
        grad_key = rotate(key_grad_raw, cosine, sine_rot, -1.0)
        d_project = jnp.concatenate(
            [
                grad_query.reshape(flat_rows, model_width),
                grad_key.reshape(flat_rows, model_width),
                value_grad_flat,
            ],
            axis=-1,
        )
        d_project_low = d_project.astype(bf16)
        grad_w_qkv = outer_rows(hidden_one, d_project_low)
        d_hidden_one = times_transpose(d_project_low, weight_qkv)
        grad_rows = (
            cot_flat
            + norm_back(d_hidden_one, normed_one, inverse_one, gain_one.astype(f32))
            + norm_back(d_hidden_two, normed_two, inverse_two, gain_two.astype(f32))
        )
        grad_list.append(grad_rows.reshape(seq_count, group_rows, model_width))
        terms = (
            jnp.sum(d_hidden_one * normed_one, axis=0),
            jnp.sum(d_hidden_one, axis=0),
            jnp.sum(d_hidden_two * normed_two, axis=0),
            jnp.sum(d_hidden_two, axis=0),
            grad_w_qkv,
            jnp.sum(d_project, axis=0),
            grad_w_out,
            cot_sum,
            grad_w_in,
            jnp.sum(d_pre, axis=0),
            grad_w_mlp,
            cot_sum,
        )
        if weight_sums is None:
            weight_sums = terms
        else:
            weight_sums = jax.tree.map(lambda total, term: total + term, weight_sums, terms)
    owned = (
        lax.psum_scatter(weight_sums[0], ("fsdp", "ctx"), scatter_dimension=0, tiled=True),
        lax.psum_scatter(weight_sums[1], ("fsdp", "ctx"), scatter_dimension=0, tiled=True),
        lax.psum_scatter(weight_sums[2], ("fsdp", "ctx"), scatter_dimension=0, tiled=True),
        lax.psum_scatter(weight_sums[3], ("fsdp", "ctx"), scatter_dimension=0, tiled=True),
        lax.psum_scatter(weight_sums[4], ("fsdp", "ctx"), scatter_dimension=0, tiled=True),
        lax.psum_scatter(weight_sums[5], ("fsdp", "ctx"), scatter_dimension=0, tiled=True),
        lax.psum_scatter(weight_sums[6], ("fsdp", "ctx"), scatter_dimension=0, tiled=True),
        lax.psum_scatter(weight_sums[7], ("fsdp", "ctx"), scatter_dimension=0, tiled=True),
        lax.psum_scatter(weight_sums[8], ("fsdp", "ctx"), scatter_dimension=0, tiled=True),
        lax.psum_scatter(weight_sums[9], ("fsdp", "ctx"), scatter_dimension=0, tiled=True),
        lax.psum_scatter(weight_sums[10], ("fsdp", "ctx"), scatter_dimension=0, tiled=True),
        lax.psum_scatter(weight_sums[11], ("fsdp", "ctx"), scatter_dimension=0, tiled=True),
    )
    outputs = jnp.concatenate(output_list, axis=0)
    grad_inputs = jnp.concatenate(grad_list, axis=0)
    return (
        outputs,
        grad_inputs,
        owned[0],
        owned[1],
        owned[2],
        owned[3],
        owned[4],
        owned[5],
        owned[6],
        owned[7],
        owned[8],
        owned[9],
        owned[10],
        owned[11],
    )


ROWS = 128
BLOCK = 256


def swap(value, bit):
    return lax.ppermute(value, "ctx", [(i, i ^ bit) for i in range(8)])


def shift_z(value, step):
    return lax.ppermute(value, "fsdp", [(i, (i + step) % 4) for i in range(4)])


def nt(left, right):
    return lax.dot_general(
        left, right, (((1,), (1,)), ((), ())), preferred_element_type=jnp.float32
    )


def nn(left, right):
    return lax.dot_general(
        left, right, (((1,), (0,)), ((), ())), preferred_element_type=jnp.float32
    )


def tn(left, right):
    return lax.dot_general(
        left, right, (((0,), (0,)), ((), ())), preferred_element_type=jnp.float32
    )


def normalize(values):
    centred = values - jnp.mean(values, axis=-1, keepdims=True)
    inverse = lax.rsqrt(jnp.mean(centred * centred, axis=-1, keepdims=True) + EPS)
    return centred * inverse, inverse


def col_sum(values):
    return jnp.sum(values, axis=0, keepdims=True)


def piece_bits(index):
    return ((index & 1) << 2) | (index & 2) | (index >> 2)


def mlp_kernel(chunks, row_ref, *refs):
    refs = list(refs)
    parts = [[refs.pop(0) for _ in range(8)] for _ in chunks]
    weights = [refs.pop(0) for _ in range(8)]
    vecs, cot_ref, first_send, first_keep, first_norm = [refs.pop(0) for _ in range(5)]
    send_ref, keep_ref, rest_ref, norm_ref, gsend_ref, gkeep_ref, vec_ref = [refs.pop(0) for _ in range(7)]
    w_in, w_down, h_s, c_s, act_s, dpre_s, x_n, first_s, part_s, g_in, g_down, seg_s, w_sem, x_sem, p_sem, o_sem = refs
    f32, bf16 = jnp.float32, jnp.bfloat16
    gain, shift, bias = vecs[2:3, :], vecs[3:4, :], vecs[6:7, :]
    where = [(at, inside) for at, count in enumerate(chunks) for inside in range(count)]
    total = len(where)

    weight_copies = []
    for at, source in enumerate(weights):
        rows = pl.ds(pl.multiple_of(row_ref[at], 16), 96)
        for kind, target in ((0, w_in), (1, w_down)):
            weight_copies.append(
                pltpu.make_async_copy(
                    source.at[pl.ds(kind * 96, 96)], target.at[rows], w_sem.at[at * 2 + kind]
                )
            )
    part_copies = []
    for seq, (at, inside) in enumerate(where):
        for piece in range(8):
            rows = pl.ds((seq * 8 + piece) * ROWS, ROWS)
            sem = x_sem.at[(seq * 8 + piece) * 2]
            if seq == 0:
                source_rows = pl.ds(pl.multiple_of(row_ref[16 + piece], ROWS), ROWS)
                part_copies.append(pltpu.make_async_copy(first_norm.at[source_rows], x_n.at[rows], sem))
            else:
                part_copies.append(
                    pltpu.make_async_copy(parts[at][piece].at[0, inside], h_s.at[rows], sem)
                )
            part_copies.append(
                pltpu.make_async_copy(
                    parts[at][piece].at[1, inside], c_s.at[rows], x_sem.at[(seq * 8 + piece) * 2 + 1]
                )
            )
    norm_copies = [
        pltpu.make_async_copy(x_n.at[pl.ds(seq * 1024, 1024)], norm_ref.at[seq - 1], o_sem.at[total + seq])
        for seq in range(1, total)
    ]
    first_copies = [
        pltpu.make_async_copy(first_keep, first_s.at[pl.ds(0, 4)], p_sem.at[0]),
        pltpu.make_async_copy(first_send, first_s.at[pl.ds(4, 4)], p_sem.at[1]),
    ]
    out_copies = [
        pltpu.make_async_copy(part_s.at[0, pl.ds(0, 4)], keep_ref, o_sem.at[0]),
        pltpu.make_async_copy(part_s.at[0, pl.ds(4, 4)], send_ref, o_sem.at[1]),
    ] + [
        pltpu.make_async_copy(part_s.at[seq % 2], rest_ref.at[seq - 1], o_sem.at[seq + 1])
        for seq in range(1, total)
    ]
    for copy in part_copies[:16] + weight_copies + first_copies + part_copies[16:]:
        copy.start()
    vec_ref[...] = jnp.zeros_like(vec_ref)
    for seq in range(2 * total):
        vec_ref[3:4, :] += col_sum(cot_ref[seq])

    def norm_rows(first):
        for at in range(0, 256, 16):
            rows = slice(first + at, first + at + 16)
            normed, _ = normalize(h_s[rows, :].astype(f32))
            x_n[rows, :] = normed
            h_s[rows, :] = (normed * gain + shift).astype(bf16)

    for seq in range(total):
        rows = slice(seq * 1024, (seq + 1) * 1024)
        if seq == 0:
            for copy in part_copies[:16]:
                copy.wait()
            h_s[rows, :] = (x_n[rows, :] * gain + shift).astype(bf16)
            for copy in weight_copies:
                copy.wait()
        for cols in (slice(0, 512), slice(512, 768)):
            pre = nn(h_s[rows, :], w_in[:, cols]) + bias[:, cols]
            d_act = nt(c_s[rows, :], w_down[cols, :])
            cdf = 0.5 * (1.0 + lax.erf(pre * 0.7071067811865476))
            density = jnp.exp(-0.5 * pre * pre) * 0.3989422804014327
            act_s[rows, cols] = (pre * cdf).astype(bf16)
            d_pre = d_act * (cdf + pre * density)
            dpre_s[rows, cols] = d_pre.astype(bf16)
            vec_ref[0:1, cols] += col_sum(d_pre)
        if seq + 1 < total:
            for copy in part_copies[seq * 16 + 16 : seq * 16 + 32]:
                copy.wait()
        if seq == 0:
            for copy in first_copies:
                copy.wait()
        if seq == 2:
            out_copies[0].wait()
            out_copies[1].wait()
        for block in range(4):
            part_rows = slice(seq * 1024 + block * 256, seq * 1024 + (block + 1) * 256)
            out = nn(act_s[part_rows, :], w_down[...])
            d_hidden = nt(dpre_s[part_rows, :], w_in[...])
            if seq + 1 < total:
                norm_rows((seq + 1) * 1024 + block * 256)
            vec_ref[1:2, :] += col_sum(d_hidden * x_n[part_rows, :])
            vec_ref[2:3, :] += col_sum(d_hidden)
            for kind, value in ((0, out), (1, d_hidden * gain)):
                for half in range(2):
                    piece = block * 2 + half
                    part = value[half * ROWS : (half + 1) * ROWS]
                    if seq == 0:
                        part = part + first_s[piece, kind].astype(f32)
                    part_s[seq % 2, piece, kind] = part.astype(bf16)
        if seq + 1 < total:
            norm_copies[seq].start()
        if seq == 0:
            out_copies[0].start()
            out_copies[1].start()
        else:
            out_copies[seq + 1].start()

    g_in[...] = tn(h_s[...], dpre_s[...])
    g_down[...] = tn(act_s[...], c_s[...])
    for at in range(8):
        seg_s[at, :, :96] = jnp.broadcast_to(vec_ref[0:1, at * 96 : (at + 1) * 96], (16, 96))
    for half, target in ((0, gkeep_ref), (1, gsend_ref)):
        for zz in range(4):
            at = zz * 2 + (row_ref[24] ^ half)
            rows = pl.ds(pl.multiple_of(at * 96, 16), 96)
            target[zz, :96, :] = g_in[rows, :].astype(target.dtype)
            target[zz, 96:192, :] = g_down[rows, :].astype(target.dtype)
            target[zz, 192:, :] = jnp.zeros((16, 768), target.dtype)
            target[zz, 192:, :96] = seg_s[at, :, :96].astype(target.dtype)
    for copy in out_copies[2:] + norm_copies:
        copy.wait()


def whole(shape):
    return pl.BlockSpec(shape, lambda *_: (0,) * len(shape))


def mlp_call(row_offsets, parts, weights, vecs, cot, first_send, first_keep, first_norm):
    chunks = tuple(part[0].shape[1] for part in parts)
    total = sum(chunks)
    width = vecs.shape[-1]
    f32, bf16 = jnp.float32, jnp.bfloat16

    anywhere = pl.BlockSpec(memory_space=pl.ANY)
    dma = pltpu.SemaphoreType.DMA
    rows = total * 8 * ROWS
    half = (4, 2, ROWS, width)
    grads = (4, 208, width)
    return pl.pallas_call(
        functools.partial(mlp_kernel, chunks),
        grid_spec=pltpu.PrefetchScalarGridSpec(
            num_scalar_prefetch=1,
            grid=(1,),
            in_specs=[anywhere] * (8 * len(parts) + 8)
            + [whole(vecs.shape), whole(cot.shape)]
            + [anywhere] * 3,
            out_specs=[anywhere] * 4 + [whole(grads), whole(grads), whole((8, width))],
            scratch_shapes=[pltpu.VMEM((width, width), bf16)] * 2
            + [pltpu.VMEM((rows, width), bf16)] * 4
            + [pltpu.VMEM((rows, width), f32)]
            + [pltpu.VMEM((8, 2, ROWS, width), bf16), pltpu.VMEM((2, 8, 2, ROWS, width), bf16)]
            + [pltpu.VMEM((width, width), f32)] * 2
            + [pltpu.VMEM((8, 16, 128), f32)]
            + [dma((16,)), dma((total * 16,)), dma((2,)), dma((2 * total,))],
        ),
        out_shape=[
            jax.ShapeDtypeStruct(half, bf16),
            jax.ShapeDtypeStruct(half, bf16),
            jax.ShapeDtypeStruct((total - 1, 8, 2, ROWS, width), bf16),
            jax.ShapeDtypeStruct((total - 1, 8 * ROWS, width), f32),
            jax.ShapeDtypeStruct(grads, bf16),
            jax.ShapeDtypeStruct(grads, f32),
            jax.ShapeDtypeStruct((8, width), f32),
        ],
        compiler_params=pltpu.CompilerParams(vmem_limit_bytes=58 << 20),
        cost_estimate=pl.CostEstimate(
            flops=30_000_000_000, transcendentals=0, bytes_accessed=30_000_000
        ),
        name="mlp",
    )(row_offsets, *[a for part in parts for a in part], *weights, vecs, cot, first_send, first_keep, first_norm)


def rotary_tables():
    f32 = jnp.float32
    lane = lax.broadcasted_iota(jnp.int32, (32, 128), 1)
    dim = lane & 63
    power = (dim & 7).astype(f32) * (-2.0 / ROT_DIM)
    freq = jnp.where(dim < ROT_DIM, jnp.exp(power * math.log(BASE_FREQ)), 0.0)
    row = lax.broadcasted_iota(jnp.int32, (32, 128), 0).astype(f32)
    fine, coarse = row * freq, row * 32.0 * freq
    cos_fine, sin_fine = jnp.cos(fine), jnp.sin(fine)
    scale = jnp.where(lane < 64, HEAD_DIM ** (-0.5), 1.0)
    cos_coarse, sin_coarse = jnp.cos(coarse) * scale, jnp.sin(coarse) * scale
    first, second = dim[:1] < 8, (dim[:1] >= 8) & (dim[:1] < ROT_DIM)
    return cos_fine, sin_fine, cos_coarse, sin_coarse, first, second


def attn_kernel(has_prev, last, at_seq, inside, row_ref, *refs):
    refs = list(refs)
    parts = [refs.pop(0) for _ in range(8)]
    weights = [refs.pop(0) for _ in range(8)]
    o_own, o_other, vecs = [refs.pop(0) for _ in range(3)]
    if has_prev:
        partial, norm_ref, pq_ref, po_ref, pv_ref = [refs.pop(0) for _ in range(5)]
    if last:
        mv_ref, at_ref, col_ref = [refs.pop(0) for _ in range(3)]
        send_ref, keep_ref, qsend_ref, qkeep_ref = [refs.pop(0) for _ in range(4)]
    else:
        send_ref, keep_ref, gq_ref, go_ref, vec_ref = [refs.pop(0) for _ in range(5)]
    if not has_prev:
        norm_out_ref = refs.pop(0)
    wq, wo, x_s, c_s, x_n, h_s = [refs.pop(0) for _ in range(6)]
    q_s, k_s, v_s, g_s, kt_s, vt_s, gt_s = [refs.pop(0) for _ in range(7)]
    dq_s, dk_s, dv_s, at_s, att_s, dp_s, res_s, tab = [refs.pop(0) for _ in range(8)]
    w_sem, x_sem, r_sem = [refs.pop(0) for _ in range(3)]
    if has_prev:
        pp_s, pq_s, po_s, p_sem = [refs.pop(0) for _ in range(4)]
    f32, bf16 = jnp.float32, jnp.bfloat16
    seq = 8 * ROWS
    blocks = seq // BLOCK
    gain, shift, bias = vecs[0:1, :], vecs[1:2, :], vecs[5:6, :640]

    def place(piece):
        return pl.ds(pl.multiple_of(row_ref[16 + piece], ROWS), ROWS)

    weight_copies = [
        pltpu.make_async_copy(
            source,
            wq.at[pl.ds(pl.multiple_of(row_ref[at], 16), 96)],
            w_sem.at[at],
        )
        for at, source in enumerate(weights)
    ]
    out_weight_copies = [
        pltpu.make_async_copy(
            source, wo.at[pl.ds(pl.multiple_of(row_ref[8 + at], 16), 96)], w_sem.at[8 + at]
        )
        for at, source in enumerate((o_own, o_other))
    ]
    part_copies = [
        [
            pltpu.make_async_copy(
                parts[piece].at[kind, inside], target.at[place(piece)], x_sem.at[kind * 8 + piece]
            )
            for piece in range(8)
        ]
        for kind, target in (((1, c_s),) if has_prev else ((0, x_s), (1, c_s)))
    ]
    if has_prev:
        norm_part_copies = [
            pltpu.make_async_copy(
                norm_ref.at[at_seq - 1, pl.ds(piece * ROWS, ROWS)], x_n.at[place(piece)], x_sem.at[piece]
            )
            for piece in range(8)
        ]
        part_copies.insert(0, norm_part_copies)
    for copy in part_copies[0] + weight_copies + part_copies[1] + out_weight_copies:
        copy.start()
    if has_prev:
        prev_copies = [
            pltpu.make_async_copy(
                partial.at[at_seq - 1, piece, kind], pp_s.at[kind, place(piece)], p_sem.at[kind * 8 + piece]
            )
            for piece in range(8)
            for kind in range(2)
        ]
        prev_copies.append(pltpu.make_async_copy(pq_ref, pq_s, p_sem.at[16]))
        prev_copies.append(pltpu.make_async_copy(po_ref, po_s, p_sem.at[17]))
        for copy in prev_copies:
            copy.start()

    wo[192:, :] = jnp.zeros((64, 768), bf16)
    cos_f, sin_f, cos_c, sin_c, first, second = rotary_tables()
    for at in range(seq // 32):
        rows = slice(at * 32, (at + 1) * 32)
        cosine = cos_f * cos_c[at : at + 1] - sin_f * sin_c[at : at + 1]
        sine = sin_f * cos_c[at : at + 1] + cos_f * sin_c[at : at + 1]
        tab[0, rows, :] = cosine
        tab[1, rows, :] = jnp.where(first, -sine, 0.0)
        tab[2, rows, :] = jnp.where(second, sine, 0.0)

    lane = lax.broadcasted_iota(jnp.int32, (256, 128), 1)
    left = lane < 64

    def heads_of(block, project, grad):
        rows = slice(block * 256, (block + 1) * 256)
        cosine, low, high = tab[0, rows, :], tab[1, rows, :], tab[2, rows, :]
        for head in range(3):
            pair = project[:, head * 128 : (head + 1) * 128]
            pair = pair * cosine + pltpu.roll(pair, 120, 1) * low + pltpu.roll(pair, 8, 1) * high
            k_s[head, rows, :] = jnp.where(left, 0.0, pair).astype(bf16)
            q_s[head, rows, :] = jnp.where(left, 0.0, pltpu.roll(pair, 64, 1)).astype(bf16)
            kt_s[head, :, rows] = jnp.transpose(pair)[64:].astype(bf16)
        v_pair, v_last = project[:, 384:512], jnp.where(left, project[:, 512:640], 0.0)
        vt_s[:128, rows] = jnp.transpose(v_pair).astype(bf16)
        vt_s[128:, rows] = jnp.transpose(v_last)[:64].astype(bf16)
        for target, pair_value, last_value in ((v_s, v_pair, v_last), (g_s, grad[:, :128], grad[:, 128:])):
            target[0, rows, :] = jnp.where(left, pair_value, 0.0).astype(bf16)
            target[1, rows, :] = jnp.where(left, 0.0, pair_value).astype(bf16)
            target[2, rows, :] = last_value.astype(bf16)

    for copy in part_copies[0] + weight_copies + part_copies[1] + out_weight_copies:
        copy.wait()
    for block in (1, 3):
        wide = slice((block - 1) * 256, (block + 1) * 256)
        if has_prev:
            h_s[wide, :] = (x_n[wide, :] * gain + shift).astype(bf16)
        else:
            for part in range(32):
                rows = slice((block - 1) * 256 + part * 16, (block - 1) * 256 + (part + 1) * 16)
                normed, _ = normalize(x_s[rows, :].astype(f32))
                x_n[rows, :] = normed
                h_s[rows, :] = (normed * gain + shift).astype(bf16)
        project_wide = nn(h_s[wide, :], wq[...]) + bias
        grad_wide = nt(c_s[wide, :], wo[...])
        gt_s[:, wide] = nt(wo[:192, :], c_s[wide, :]).astype(bf16)
        for half in range(2):
            heads_of(block - 1 + half, project_wide[half * 256 : half * 256 + 256], grad_wide[half * 256 : half * 256 + 256])

    allowed = lax.broadcasted_iota(jnp.int32, (BLOCK, BLOCK), 0) <= lax.broadcasted_iota(
        jnp.int32, (BLOCK, BLOCK), 1
    )

    def rows_of(block):
        return slice(block * BLOCK, (block + 1) * BLOCK)

    def scores_of(head, block):
        query, grad = q_s[head, rows_of(block), :], g_s[head, rows_of(block), :]
        upto = (block + 1) * BLOCK
        scores = nt(k_s[head, :upto, :], query)
        scores = [scores[rows_of(at)] for at in range(block + 1)]
        scores[block] = jnp.where(allowed, scores[block], -1e30)
        d_prob = nt(v_s[head, :upto, :], grad)
        return scores, [d_prob[rows_of(at)] for at in range(block + 1)]

    def softmax_of(scores):
        top = jnp.max(scores[0], axis=0, keepdims=True)
        for part in scores[1:]:
            top = jnp.maximum(top, jnp.max(part, axis=0, keepdims=True))
        probs = [jnp.exp(part - top) for part in scores]
        total = col_sum(probs[0])
        for part in probs[1:]:
            total = total + col_sum(part)
        scale = 1.0 / total
        probs = [part * scale for part in probs]
        return probs, [part.astype(bf16) for part in probs]

    def values_of(head, block, probs, lows, d_prob):
        rows, upto = rows_of(block), (block + 1) * BLOCK
        low = jnp.concatenate(lows, axis=0) if block else lows[0]
        att_t = nn(vt_s[head * 64 : (head + 1) * 64, :upto], low)
        att_low = att_t.astype(bf16)
        att_s[head * 64 : (head + 1) * 64, rows] = att_low
        d_value = nn(low, g_s[head, rows, :])
        into = head // 2
        keep = slice(0, upto if head == 1 else upto - BLOCK)
        if keep.stop:
            dv_s[into, keep, :] += d_value[keep]
        if head != 1:
            dv_s[into, rows, :] = d_value[upto - BLOCK :]
        delta = col_sum(gt_s[head * 64 : (head + 1) * 64, rows].astype(f32) * att_low.astype(f32))
        return [(p * (d - delta)).astype(bf16) for p, d in zip(probs, d_prob)]

    def grads_of(head, block, d_scores):
        rows, upto = rows_of(block), (block + 1) * BLOCK
        d_score = jnp.concatenate(d_scores, axis=0) if block else d_scores[0]
        d_key = nn(d_score, q_s[head, rows, :])
        if block:
            dk_s[head, : upto - BLOCK, :] += d_key[: upto - BLOCK]
        dk_s[head, rows, :] = d_key[upto - BLOCK :]
        dq_s[head, rows, :64] = jnp.transpose(nn(kt_s[head, :, :upto], d_score))

    order = [(head, block) for block in range(blocks) for head in range(3)]
    ahead = scores_of(*order[0])
    waiting = None
    for at, (head, block) in enumerate(order):
        scores, d_prob = ahead
        if at + 1 < len(order):
            ahead = scores_of(*order[at + 1])
        probs, lows = softmax_of(scores)
        if waiting is not None:
            grads_of(*waiting)
        waiting = (head, block, values_of(head, block, probs, lows, d_prob))
    grads_of(*waiting)

    project_sums = []
    for head in range(3):
        total = jnp.zeros((1, 128), f32)
        for block in range(4):
            rows = slice(block * 256, (block + 1) * 256)
            pair = jnp.concatenate([dq_s[head, rows, :64], dk_s[head, rows, 64:]], axis=1)
            cosine, low, high = tab[0, rows, :], tab[1, rows, :], tab[2, rows, :]
            pair = pair * cosine - pltpu.roll(pair, 120, 1) * low - pltpu.roll(pair, 8, 1) * high
            total = total + col_sum(pair)
            dp_s[rows, head * 128 : (head + 1) * 128] = pair.astype(bf16)
        project_sums.append(total)
    for into in range(2):
        dp_s[:, 384 + into * 128 : 512 + into * 128] = dv_s[into].astype(bf16)
        project_sums.append(col_sum(dv_s[into]))
    if has_prev:
        for copy in prev_copies:
            copy.wait()
    for block in range(4):
        rows = slice(block * 256, (block + 1) * 256)
        at_s[rows, :128] = jnp.transpose(att_s[:128, rows].astype(f32)).astype(bf16)
        at_s[rows, 128:] = jnp.concatenate(
            [jnp.transpose(att_s[128:, rows].astype(f32)), jnp.zeros((256, 64), f32)], axis=1
        ).astype(bf16)
    out = nn(at_s[...], wo[...])
    d_hidden = nt(dp_s[...], wq[...])
    s = d_hidden * gain
    if has_prev:
        out = out + pp_s[0].astype(f32)
        s = s + pp_s[1].astype(f32)
    res_s[0] = out.astype(bf16)
    res_s[1] = s.astype(bf16)
    sums = [
        jnp.concatenate(project_sums, axis=1),
        col_sum(d_hidden * x_n[...]),
        col_sum(d_hidden),
    ]
    result_copies = [
        pltpu.make_async_copy(
            res_s.at[kind, place(piece)],
            (keep_ref if piece < 4 else send_ref).at[piece % 4, kind],
            r_sem.at[piece * 2 + kind],
        )
        for piece in (4, 5, 6, 7, 0, 1, 2, 3)
        for kind in range(2)
    ]
    if not has_prev:
        result_copies.append(pltpu.make_async_copy(x_n, norm_out_ref, r_sem.at[16]))
    for copy in result_copies:
        copy.start()
    g_query = tn(h_s[...], dp_s[...])
    g_out = nn(att_s[...], c_s[...])
    if has_prev:
        g_query = g_query + pq_s[...]
        g_out = g_out + po_s[...]
        sums = [sums[0] + pv_ref[0:1, :640], sums[1] + pv_ref[1:2, :], sums[2] + pv_ref[2:3, :]]
    if last:
        gq_s, go_s, tr_s = refs
        gq_s[...] = g_query
        go_s[...] = g_out
        tr_s[...] = jnp.zeros_like(tr_s)
        tr_s[64:65, :] = sums[1]
        tr_s[65:66, :] = sums[2]
        tr_s[66:69, :] = mv_ref[1:4, :]
        columns = jnp.transpose(tr_s[...])
        lanes = lax.broadcasted_iota(jnp.int32, (768, 128), 1)
        target_at = col_ref[0:1, :576] + row_ref[25] * 192
        for third in range(3):
            hit = at_ref[:, third : third + 1] == target_at
            column = jnp.sum(jnp.where(hit, sums[0][:, :576], 0.0), axis=1, keepdims=True)
            columns = jnp.where(lanes == 69 + third, column, columns)
        gq_s[:, 512:640] = jnp.where(lanes < 64, gq_s[:, 512:640], columns)
        for half, target in ((0, qkeep_ref), (1, qsend_ref)):
            for zz in range(4):
                at = zz * 2 + (row_ref[24] ^ half)
                rows = pl.ds(pl.multiple_of(at * 96, 16), 96)
                target[zz, :, :640] = gq_s[rows, :].astype(target.dtype)
                target[zz, :, 640:] = jnp.zeros((96, 128), target.dtype)
            rows = pl.ds(pl.multiple_of((row_ref[24] ^ half) * 96, 16), 96)
            target[4] = go_s[rows, :].astype(target.dtype)
    else:
        gq_ref[...] = g_query
        go_ref[...] = g_out
        vec_ref[...] = jnp.zeros_like(vec_ref)
        vec_ref[0:1, :640] = sums[0]
        vec_ref[1:2, :] = sums[1]
        vec_ref[2:3, :] = sums[2]
    for copy in result_copies:
        copy.wait()


def attn_call(row_offsets, parts, inside, weights, o_own, o_other, vecs, partial, seq, prev, tail):
    width = vecs.shape[-1]
    f32, bf16 = jnp.float32, jnp.bfloat16
    anywhere = pl.BlockSpec(memory_space=pl.ANY)
    dma = pltpu.SemaphoreType.DMA
    has_prev, last = prev is not None, tail is not None
    rows = 8 * ROWS
    half = (4, 2, ROWS, width)
    shapes = [(half, bf16), (half, bf16)]
    if last:
        shapes += [((5, 96, width), bf16), ((5, 96, width), f32)]
    else:
        shapes += [((width, 640), f32), ((192, width), f32), ((8, width), f32)]
    out_specs = [anywhere] * 2 + [whole(shape) for shape, _ in shapes[2:]]
    if not has_prev:
        shapes.append(((rows, width), f32))
        out_specs.append(anywhere)
    operands = [*parts, *weights, o_own, o_other, vecs]
    in_specs = [anywhere] * 18 + [whole(vecs.shape)]
    scratch = [
        pltpu.VMEM((width, 640), bf16),
        pltpu.VMEM((256, width), bf16),
        pltpu.VMEM((rows, width), bf16),
        pltpu.VMEM((rows, width), bf16),
        pltpu.VMEM((rows, width), f32),
        pltpu.VMEM((rows, width), bf16),
    ]
    scratch += [pltpu.VMEM((3, rows, 128), bf16)] * 4
    scratch += [
        pltpu.VMEM((3, 64, rows), bf16),
        pltpu.VMEM((192, rows), bf16),
        pltpu.VMEM((192, rows), bf16),
        pltpu.VMEM((3, rows, 128), f32),
        pltpu.VMEM((3, rows, 128), f32),
        pltpu.VMEM((2, rows, 128), f32),
        pltpu.VMEM((rows, 256), bf16),
        pltpu.VMEM((192, rows), bf16),
        pltpu.VMEM((rows, 640), bf16),
        pltpu.VMEM((2, rows, width), bf16),
        pltpu.VMEM((3, rows, 128), f32),
        dma((10,)),
        dma((16,)),
        dma((17,)),
    ]
    if has_prev:
        operands += [*partial, *prev]
        in_specs += [anywhere] * 4 + [whole(prev[2].shape)]
        scratch += [
            pltpu.VMEM((2, rows, width), bf16),
            pltpu.VMEM((width, 640), f32),
            pltpu.VMEM((192, width), f32),
            dma((18,)),
        ]
    if last:
        operands += list(tail)
        in_specs += [whole(a.shape) for a in tail]
        scratch += [pltpu.VMEM((width, 640), f32), pltpu.VMEM((192, width), f32), pltpu.VMEM((128, width), f32)]
    return pl.pallas_call(
        functools.partial(attn_kernel, has_prev, last, seq, inside),
        grid_spec=pltpu.PrefetchScalarGridSpec(
            num_scalar_prefetch=1,
            grid=(1,),
            in_specs=in_specs,
            out_specs=out_specs,
            scratch_shapes=scratch,
        ),
        out_shape=[jax.ShapeDtypeStruct(shape, kind) for shape, kind in shapes],
        compiler_params=pltpu.CompilerParams(vmem_limit_bytes=58 << 20),
        cost_estimate=pl.CostEstimate(
            flops=24_000_000_000, transcendentals=0, bytes_accessed=15_000_000
        ),
        name="attn",
    )(row_offsets, *operands)


def finish_kernel(seqs, half_ref, x_ref, c_ref, *refs):
    refs = list(refs)
    terms = [[refs.pop(0) for _ in range(4)] for _ in seqs]
    bias = refs.pop(0)
    out_ref, grad_ref = refs[-2:]
    f32 = jnp.float32

    def write(sources):
        total = [source[0].astype(f32) for source in sources]
        total = sum(total[1:], total[0])
        x = x_ref[0].astype(f32)
        normed, inverse = normalize(x)
        out_ref[0] = x + bias[4:5, :] + total[0]
        s = total[1]
        mean_s = jnp.mean(s, axis=-1, keepdims=True)
        mean_sn = jnp.mean(s * normed, axis=-1, keepdims=True)
        grad_ref[0] = c_ref[0] + inverse * (s - mean_s - normed * mean_sn)

    for at in range(len(seqs)):
        for other in range(2):
            @pl.when(pl.program_id(0) == at * 2 + other)
            def _(at=at, other=other):
                write(terms[at][3:] if other else terms[at][:3])


def finish_call(half, seqs, x, cot, terms, bias, done):
    _, rows, width = x.shape
    f32 = jnp.float32
    seq_spec = pl.BlockSpec(
        (1, rows, width),
        lambda i, at: (jnp.where(i % 2 == 0, at[0], 1 - at[0]) * 3 + seqs[0] + i // 2, 0, 0),
    )
    part_spec = pl.BlockSpec((1, 2, rows, width), lambda i, at: (0, 0, 0, 0))
    before = list(done) if done is not None else []
    operands = [x, cot, *[a for parts in terms for a in parts], bias]
    return pl.pallas_call(
        functools.partial(finish_kernel, seqs),
        grid_spec=pltpu.PrefetchScalarGridSpec(
            num_scalar_prefetch=1,
            grid=(2 * len(seqs),),
            in_specs=[seq_spec, seq_spec]
            + [part_spec] * (4 * len(seqs))
            + [whole(bias.shape)]
            + [pl.BlockSpec(memory_space=pl.ANY)] * len(before),
            out_specs=[seq_spec, seq_spec],
        ),
        out_shape=[jax.ShapeDtypeStruct(x.shape, f32)] * 2,
        input_output_aliases={len(operands) + 1: 0, len(operands) + 2: 1} if before else {},
        name="finish",
    )(half, *operands, *before)


def pick(value, index, axis=0):
    return lax.dynamic_index_in_dim(value, index, axis, keepdims=False)


def prep_kernel(at_ref, in_ref, q_ref, small_ref, own_ref, send_ref, pack_s):
    for h in range(4):
        parts = [in_ref[:, zy * 384 + h * 96 : zy * 384 + (h + 1) * 96] for zy in range(8)]
        for head in range(3):
            for kind in range(2):
                first = kind * 768 + h * 192 + head * 64
                parts.append(q_ref[:, first : first + 64])
        first = 1536 + h * 192
        parts.append(q_ref[:, first : first + 192])
        parts.append(small_ref[...])
        at = 0
        for part in parts:
            pack_s[h, :, at : at + part.shape[1]] = part
            at += part.shape[1]
    for core in range(2):
        own_ref[core] = pack_s[at_ref[26] * 2 + core]
        send_ref[core] = pack_s[(1 - at_ref[26]) * 2 + core]


def prep_call(row_offsets, w_in, w_qkv, small):
    half = jax.ShapeDtypeStruct((2, 24, 1408), jnp.bfloat16)
    return pl.pallas_call(
        prep_kernel,
        grid_spec=pltpu.PrefetchScalarGridSpec(
            num_scalar_prefetch=1,
            grid=(1,),
            in_specs=[whole(a.shape) for a in (w_in, w_qkv, small)],
            out_specs=[whole(half.shape)] * 2,
            scratch_shapes=[pltpu.VMEM((4, 24, 1408), jnp.bfloat16)],
        ),
        out_shape=[half, half],
        name="prep",
    )(row_offsets, w_in, w_qkv, small)


def join_kernel(at_ref, own_ref, got_ref, far_ref, down_ref, attn_ref, mlp_ref, four, rows_s):
    f32, bf16 = jnp.float32, jnp.bfloat16
    x, c = at_ref[26], at_ref[27]
    four[0] = own_ref[c].astype(f32)
    four[1] = got_ref[c].astype(f32)
    four[2] = far_ref[0].astype(f32)
    four[3] = far_ref[1].astype(f32)
    for source in range(4):
        near = ((source & 1) ^ c) * 2 + ((source >> 1) ^ x)
        rows_s[source * 24 : (source + 1) * 24, :] = four[near]
    mlp_ref[:96, :] = rows_s[:, :768].astype(bf16)
    mlp_ref[96:, :] = down_ref[...]
    attn_ref[...] = rows_s[:, 768:].astype(bf16)


def join_call(row_offsets, own, got, far, w_down):
    f32, bf16 = jnp.float32, jnp.bfloat16
    outs = [jax.ShapeDtypeStruct((96, 640), bf16), jax.ShapeDtypeStruct((192, 768), bf16)]
    return pl.pallas_call(
        join_kernel,
        grid_spec=pltpu.PrefetchScalarGridSpec(
            num_scalar_prefetch=1,
            grid=(1,),
            in_specs=[whole(a.shape) for a in (own, got, far, w_down)],
            out_specs=[whole(a.shape) for a in outs],
            scratch_shapes=[pltpu.VMEM((4, 24, 1408), f32), pltpu.VMEM((96, 1408), f32)],
        ),
        out_shape=outs,
        name="join",
    )(row_offsets, own, got, far, w_down)


def pick_out_kernel(at_ref, one, two, three, four, own_ref, send_ref, all_s):
    for at, source in enumerate((one, two, three, four)):
        all_s[at] = source[...]
    for core in range(2):
        own_ref[core] = all_s[(at_ref[28] - at_ref[26] * 2 - core + 4) % 4]
        send_ref[core] = all_s[(at_ref[28] - (1 - at_ref[26]) * 2 - core + 4) % 4]


def pick_out_call(row_offsets, pieces):
    half = jax.ShapeDtypeStruct((2, 24, 768), jnp.bfloat16)
    return pl.pallas_call(
        pick_out_kernel,
        grid_spec=pltpu.PrefetchScalarGridSpec(
            num_scalar_prefetch=1,
            grid=(1,),
            in_specs=[whole((24, 768))] * 4,
            out_specs=[whole(half.shape)] * 2,
            scratch_shapes=[pltpu.VMEM((4, 24, 768), jnp.bfloat16)],
        ),
        out_shape=[half, half],
        name="out_pick",
    )(row_offsets, *pieces)


def join_out_kernel(at_ref, own_ref, got_ref, far_ref, out_ref, four, rows_s):
    f32, bf16 = jnp.float32, jnp.bfloat16
    x, c = at_ref[26], at_ref[27]
    four[0] = own_ref[c].astype(f32)
    four[1] = got_ref[c].astype(f32)
    four[2] = far_ref[0].astype(f32)
    four[3] = far_ref[1].astype(f32)
    for source in range(4):
        near = ((source & 1) ^ c) * 2 + ((source >> 1) ^ x)
        rows_s[source * 24 : (source + 1) * 24, :] = four[near]
    out_ref[...] = rows_s[...].astype(bf16)


def join_out_call(row_offsets, own, got, far):
    f32, bf16 = jnp.float32, jnp.bfloat16
    return pl.pallas_call(
        join_out_kernel,
        grid_spec=pltpu.PrefetchScalarGridSpec(
            num_scalar_prefetch=1,
            grid=(1,),
            in_specs=[whole(a.shape) for a in (own, got, far)],
            out_specs=whole((96, 768)),
            scratch_shapes=[pltpu.VMEM((4, 24, 768), f32), pltpu.VMEM((96, 768), f32)],
        ),
        out_shape=jax.ShapeDtypeStruct((96, 768), bf16),
        name="join_out",
    )(row_offsets, own, got, far)


def vector_tables():
    row = np.arange(768)
    at_q = np.stack([(row // 24) * 72 + third * 24 + row % 24 for third in range(3)], axis=1)
    at_in = np.stack([(row // 24) * 96 + third * 24 + row % 24 for third in range(4)], axis=1)
    lane = np.arange(576)
    head, kind = lane // 128, (lane % 128) // 64
    col_q = np.where(lane < 384, kind * 768 + head * 64 + lane % 64, 1536 + lane - 384)
    col_in = (row // 96) * 384 + row % 96
    cols = np.zeros((8, 768), np.int32)
    cols[0, :576] = col_q
    cols[1] = col_in
    rows = np.concatenate([at_q, at_in, np.zeros((768, 1))], axis=1).astype(np.int32)
    return rows, cols


def vec_kernel(at_ref, *refs):
    refs = list(refs)
    pieces = [refs.pop(0) for _ in range(8)]
    rows_ref, cols_ref, out_ref, all_s = refs
    f32 = jnp.float32
    for at, source in enumerate(pieces):
        rows = pl.ds(pl.multiple_of(at_ref[at], 16), 96)
        all_s[rows, :] = source[...].astype(f32)
    flipped = jnp.transpose(all_s[...])
    out_ref[0:4, :] = flipped[64:68]
    out_ref[4:5, :] = flipped[68:69] + flipped[69:70]
    for row, kinds, target, width, step in ((5, (0, 1, 2), 0, 576, 192), (6, (3, 4, 5, 6), 1, 768, 96)):
        wanted = cols_ref[target : target + 1, :width] + at_ref[25] * step
        total = jnp.zeros((1, width), f32)
        for kind in kinds:
            hit = rows_ref[:, kind : kind + 1] == wanted
            total += col_sum(jnp.where(hit, all_s[:, 70 + kind : 71 + kind], 0.0))
        out_ref[row : row + 1, :width] = total
    out_ref[7:8, :] = jnp.zeros((1, 768), f32)
    out_ref[5:6, 576:] = jnp.zeros((1, 192), f32)


def vec_call(row_offsets, pieces, rows, cols):
    f32 = jnp.float32
    return pl.pallas_call(
        vec_kernel,
        grid_spec=pltpu.PrefetchScalarGridSpec(
            num_scalar_prefetch=1,
            grid=(1,),
            in_specs=[pl.BlockSpec((96, 128), lambda i, *_: (0, 4))] * 8
            + [whole(rows.shape), whole(cols.shape)],
            out_specs=whole((8, 768)),
            scratch_shapes=[pltpu.VMEM((768, 128), f32)],
        ),
        out_shape=jax.ShapeDtypeStruct((8, 768), f32),
        name="vectors",
    )(row_offsets, *pieces, rows, cols)


def spread_kernel(at_ref, mine, far, q_ref, in_ref, o_ref, *refs):
    f32 = jnp.float32
    out_refs, four = refs[:6], refs[6]
    x, c, z = at_ref[26], at_ref[27], at_ref[28]
    for side in range(2):
        four[side] = mine[side]
        four[2 + side] = far[side]
    o_ref[...] = four[((z & 1) ^ c) * 2 + ((z >> 1) ^ x), :, 1408:].astype(f32)
    total = None
    for h in range(4):
        block = four[((h & 1) ^ c) * 2 + ((h >> 1) ^ x)][:, :1408].astype(f32)
        for zy in range(8):
            first = zy * 384 + h * 96
            in_ref[:, first : first + 96] = block[:, 640 + zy * 96 : 640 + (zy + 1) * 96]
        for head in range(3):
            for kind in range(2):
                first = kind * 768 + h * 192 + head * 64
                at = head * 128 + kind * 64
                q_ref[:, first : first + 64] = block[:, at : at + 64]
        first = 1536 + h * 192
        q_ref[:, first : first + 192] = block[:, 384:576]
        part = block[:, 576:584]
        total = part if total is None else total + part
    same = lax.broadcasted_iota(jnp.int32, (24, 24), 0) == lax.broadcasted_iota(jnp.int32, (24, 24), 1)
    rows = [col_sum(jnp.where(same, total[:, t : t + 1], 0.0)) for t in range(8)]
    for t in range(5):
        out_refs[t][...] = rows[t]
    out_refs[5][...] = jnp.concatenate(rows[5:], axis=1)


def spread_call(row_offsets, mine, far):
    f32, bf16 = jnp.float32, jnp.bfloat16
    shapes = [(24, 2304), (24, 3072), (24, 768)] + [(1, 24)] * 5 + [(1, 72)]
    return pl.pallas_call(
        spread_kernel,
        grid_spec=pltpu.PrefetchScalarGridSpec(
            num_scalar_prefetch=1,
            grid=(1,),
            in_specs=[whole(mine.shape), whole(far.shape)],
            out_specs=[whole(shape) for shape in shapes],
            scratch_shapes=[pltpu.VMEM((4, 24, 2176), bf16)],
        ),
        out_shape=[jax.ShapeDtypeStruct(shape, f32) for shape in shapes],
        name="spread",
    )(row_offsets, mine, far)


def exchange_four(blocks, x, c):
    blocks = blocks.reshape((2, 2) + blocks.shape[1:])
    own = pick(blocks, x)
    got = swap(pick(blocks, 1 - x), 2)
    both = jnp.stack([own, got])
    mine = pick(both, c, 1)
    send = pick(both, 1 - c, 1)
    return mine, swap(send, 1)


def fast(*args):
    return fast_body(*args)


def fast_body(
    inputs, cotangent, ln1_gain, ln1_bias, ln2_gain, ln2_bias, w_qkv, b_qkv, w_out, b_out, w_in, b_in, w_mlp_out, b_mlp_out
):
    f32, bf16 = jnp.float32, jnp.bfloat16
    z = lax.axis_index("fsdp")
    ctx = lax.axis_index("ctx")
    y, x, c = ctx // 4, (ctx // 2) % 2, ctx % 2
    h = ctx % 4

    zs = jnp.stack([(z - k) % 4 for k in range(4)])
    rows_w = jnp.concatenate([(zs * 2 + y) * 96, (zs * 2 + 1 - y) * 96])
    rows_o = jnp.stack([y * 96, (1 - y) * 96])
    rows_p = jnp.stack([(ctx ^ piece_bits(k)) * ROWS for k in range(8)])
    row_offsets = jnp.concatenate(
        [rows_w, rows_o, jnp.zeros((6,), jnp.int32), rows_p, jnp.stack([y, h, x, c, z])]
    ).astype(jnp.int32)

    small = jnp.concatenate(
        [ln1_gain, ln1_bias, ln2_gain, ln2_bias, b_out, b_mlp_out, b_qkv, b_in, jnp.zeros((51 * 24,), bf16)]
    ).reshape(64, 24).T
    pack_own, pack_send = prep_call(row_offsets, w_in, w_qkv, small)

    def rows_of(half, first, count):
        at = half * 3 + first
        return jnp.stack(
            [
                lax.dynamic_slice_in_dim(inputs, at, count),
                lax.dynamic_slice_in_dim(cotangent, at, count).astype(bf16),
            ]
        )

    parts = []
    first = 0
    for count in CHUNKS:
        got = swap(rows_of(1 - y, first, count), 4)
        own = rows_of(y, first, count)
        side, side_got = swap(own, 2), swap(got, 2)
        near = (own, got, side, side_got)
        parts.append(near + tuple(swap(a, 1) for a in near))
        first += count

    pack_got = swap(pack_send, 2)
    pack_far = swap(jnp.stack([pick(pack_own, 1 - c), pick(pack_got, 1 - c)]), 1)
    out_all = [w_out] + [shift_z(w_out, k) for k in (1, 2, 3)]
    attn_w, mlp_w = join_call(row_offsets, pack_own, pack_got, pack_far, w_mlp_out)
    attn_own = [attn_w] + [shift_z(attn_w, k) for k in (1, 2, 3)]
    mlp_own = [mlp_w] + [shift_z(mlp_w, k) for k in (1, 2, 3)]
    attn_all = attn_own + [swap(part, 4) for part in attn_own]
    mlp_all = mlp_own + [swap(part, 4) for part in mlp_own]
    out_mine, out_send = pick_out_call(row_offsets, out_all)
    out_got = swap(out_send, 2)
    out_far = swap(jnp.stack([pick(out_mine, 1 - c), pick(out_got, 1 - c)]), 1)
    out_own = join_out_call(row_offsets, out_mine, out_got, out_far)
    out_other = swap(out_own, 4)
    at_rows, at_cols = vector_tables()
    vecs = vec_call(row_offsets, attn_all, at_rows, at_cols)

    where = [(at, inside) for at, count in enumerate(CHUNKS) for inside in range(count)]

    def attention(seq, partial, prev, tail=None):
        at, inside = where[seq]
        return attn_call(
            row_offsets, parts[at], inside, attn_all, out_own, out_other,
            vecs, partial, seq, prev, tail,
        )

    def reduce_z(blocks, cols):
        def total(at):
            value = pick(blocks[0], at)[:, :cols].astype(f32)
            for block in blocks[1:]:
                value = value + pick(block, at)[:, :cols].astype(f32)
            return value

        low = [total((z + k) % 4).astype(bf16) for k in (1, 2, 3)]
        sent = [shift_z(part, k + 1) for k, part in enumerate(low)]

        def rows_of_sum(first, count):
            result = total(z)[first : first + count]
            for part in sent:
                result = result + part[first : first + count].astype(f32)
            return result

        return rows_of_sum

    def to_owner_z(value):
        total = value
        low = value.astype(bf16)
        for k in (1, 2, 3):
            pairs = [
                (zz * 8 + i, (zz + k) % 4 * 8 + i) for zz in range(4) for i in range(8) if (zz + k) % 4 == i % 4
            ]
            total = total + lax.ppermute(low, ("fsdp", "ctx"), pairs).astype(f32)
        return total

    half = jnp.reshape(y, (1,)).astype(jnp.int32)

    def scatter(send, keep):
        got = swap(send, 1)
        side = swap((keep[2:].astype(f32) + got[2:].astype(f32)).astype(bf16), 2)
        far = (keep[1:2].astype(f32) + got[1:2].astype(f32) + side[1:2].astype(f32)).astype(bf16)
        return keep, got, side, swap(far, 4)

    def finish(seqs, terms, done):
        return finish_call(half, seqs, inputs, cotangent, terms, vecs, done)

    first_send, first_keep, g_q, g_o, vec, first_norm = attention(0, None, None)
    prev = (g_q, g_o, vec)
    send, keep, rest_part, rest_norm, g_send, g_keep, mlp_vec = mlp_call(
        row_offsets, parts, mlp_all, vecs, cotangent, first_send, first_keep, first_norm
    )
    g_got = swap(g_send, 4)
    terms = [scatter(send, keep)]
    send, keep, g_q, g_o, vec = attention(1, (rest_part, rest_norm), prev)
    terms.append(scatter(send, keep))
    mlp_rows = reduce_z((g_keep, g_got), 768)
    grad_w_mlp = mlp_rows(96, 96)
    grad_b_in = mlp_rows(192, 1)[0, :96]
    send, keep, q_send, q_keep = attention(
        2, (rest_part, rest_norm), (g_q, g_o, vec), (mlp_vec, at_rows, at_cols)
    )
    terms.append(scatter(send, keep))
    done = None
    for seq in range(3):
        done = finish((seq,), terms[seq : seq + 1], done)
    q_got = swap(q_send, 4)
    q_rows = reduce_z((q_keep, q_got), 640)
    o_sum = q_keep[4] + q_got[4].astype(f32)
    o_grad = to_owner_z(o_sum)
    low = [part.astype(bf16) for part in (q_rows(0, 96), mlp_rows(0, 96), o_grad)]
    blocks = jnp.concatenate(low, axis=1).reshape(4, 24, 2176)
    grad_w_qkv, grad_w_in, grad_w_out, *spread = spread_call(row_offsets, *exchange_four(blocks, x, c))
    one_gain, one_bias, two_gain, two_bias, grad_bias, grad_bq = [v.reshape(-1) for v in spread]

    outputs, grad_inputs = done
    return (
        outputs,
        grad_inputs,
        one_gain,
        one_bias,
        two_gain,
        two_bias,
        grad_w_qkv,
        grad_bq,
        grad_w_out,
        grad_bias,
        grad_w_in,
        grad_b_in,
        grad_w_mlp,
        grad_bias,
    )


def fast_fits(mesh):
    sizes = dict(mesh.shape)
    return sizes["fsdp"] == 4 and sizes["ctx"] == 8


def solution(mesh):
    return jax.shard_map(
        fast if fast_fits(mesh) else local,
        mesh=mesh,
        in_specs=(
            P("fsdp", "ctx", None),
            P("fsdp", "ctx", None),
            P(("fsdp", "ctx")),
            P(("fsdp", "ctx")),
            P(("fsdp", "ctx")),
            P(("fsdp", "ctx")),
            P(("fsdp", "ctx"), None),
            P(("fsdp", "ctx")),
            P(("fsdp", "ctx"), None),
            P(("fsdp", "ctx")),
            P(("fsdp", "ctx"), None),
            P(("fsdp", "ctx")),
            P(("fsdp", "ctx"), None),
            P(("fsdp", "ctx")),
        ),
        out_specs=(
            P("fsdp", "ctx", None),
            P("fsdp", "ctx", None),
            P(("fsdp", "ctx")),
            P(("fsdp", "ctx")),
            P(("fsdp", "ctx")),
            P(("fsdp", "ctx")),
            P(("fsdp", "ctx"), None),
            P(("fsdp", "ctx")),
            P(("fsdp", "ctx"), None),
            P(("fsdp", "ctx")),
            P(("fsdp", "ctx"), None),
            P(("fsdp", "ctx")),
            P(("fsdp", "ctx"), None),
            P(("fsdp", "ctx")),
        ),
        check_vma=False,
    )
```

```python
import functools
import math

import jax
import jax.numpy as jnp
import numpy as np
from jax import lax
from jax.experimental import pallas as pl
from jax.experimental.pallas import tpu as pltpu
from jax.sharding import PartitionSpec as P


HEADS = 12
HEAD_DIM = 64
ROT_DIM = 16
MICRO = 2
SEQ_MB = 3
CHUNKS = (1, 2)


EPS = 1e-05
BASE_FREQ = 10000.0


def layer_norm(values, gain_row, shift_row):
    centre = jnp.mean(values, axis=-1, keepdims=True)
    centred = values - centre
    inverse = lax.rsqrt(jnp.mean(centred * centred, axis=-1, keepdims=True) + EPS)
    normed = centred * inverse
    return (normed * gain_row + shift_row, normed, inverse)


def norm_back(grad_out, normed, inverse, gain_row):
    scaled = grad_out * gain_row
    return inverse * (
        scaled
        - jnp.mean(scaled, axis=-1, keepdims=True)
        - normed * jnp.mean(scaled * normed, axis=-1, keepdims=True)
    )


def angles(positions):
    half_rot = ROT_DIM // 2
    inv_freq = BASE_FREQ ** (-(2.0 * jnp.arange(half_rot, dtype=jnp.float32)) / ROT_DIM)
    phase_angle = positions.astype(jnp.float32)[:, None] * inv_freq[None, :]
    return (jnp.cos(phase_angle), jnp.sin(phase_angle))


def rotate(head_field, cosine, sine_rot, direction):
    half_rot = ROT_DIM // 2
    lead_half = head_field[..., :half_rot]
    trail_half = head_field[..., half_rot:ROT_DIM]
    cos_wide = cosine[:, None, :]
    sin_wide = direction * sine_rot[:, None, :]
    return jnp.concatenate(
        [
            lead_half * cos_wide - trail_half * sin_wide,
            trail_half * cos_wide + lead_half * sin_wide,
            head_field[..., ROT_DIM:],
        ],
        axis=-1,
    )


def gelu_parts(pre_act):
    normal_cdf = 0.5 * (1.0 + jax.scipy.special.erf(pre_act * 0.7071067811865476))
    density = jnp.exp(-0.5 * pre_act * pre_act) * 0.3989422804014327
    return (pre_act * normal_cdf, normal_cdf + pre_act * density)


def outer_rows(left, right):
    return lax.dot_general(
        left, right, (((0,), (0,)), ((), ())), preferred_element_type=jnp.float32
    )


def times_transpose(left, right):
    return lax.dot_general(
        left, right, (((1,), (1,)), ((), ())), preferred_element_type=jnp.float32
    )


def attend_block(soft_state, kv_block, first_row, query_low, positions, score_scale):
    run_max, run_sum, weighted = soft_state
    seq_count, block_rows, double_width = kv_block.shape
    model_width = double_width // 2
    key_low = kv_block[..., :model_width].reshape(seq_count, block_rows, HEADS, HEAD_DIM)
    value_low = kv_block[..., model_width:].reshape(seq_count, block_rows, HEADS, HEAD_DIM)
    scores = (
        jnp.einsum("sqhd,skhd->shqk", query_low, key_low, preferred_element_type=jnp.float32)
        * score_scale
    )
    allowed = (first_row + jnp.arange(block_rows, dtype=jnp.int32))[None, :] <= positions[:, None]
    scores = jnp.where(allowed, scores, -jnp.inf)
    new_max = jnp.maximum(run_max, jnp.max(scores, axis=-1))
    safe_max = jnp.where(new_max == -jnp.inf, 0.0, new_max)
    exp_scores = jnp.exp(scores - safe_max[..., None])
    factor = jnp.exp(run_max - safe_max)
    run_sum = run_sum * factor + jnp.sum(exp_scores, axis=-1)
    weighted = weighted * factor[..., None] + jnp.einsum(
        "shqk,skhd->shqd",
        exp_scores.astype(jnp.bfloat16),
        value_low,
        preferred_element_type=jnp.float32,
    )
    return (new_max, run_sum, weighted)


def attend_piece(soft_state, kv_piece, query_low, positions, score_scale):
    piece_rows = kv_piece.shape[1]
    step_rows = math.gcd(piece_rows, 512)

    def one_block(block_index, inner_state):
        offset = block_index * step_rows
        kv_block = lax.dynamic_slice_in_dim(kv_piece, offset, step_rows, 1)
        return attend_block(inner_state, kv_block, offset, query_low, positions, score_scale)

    return lax.fori_loop(0, piece_rows // step_rows, one_block, soft_state)


def local(
    inputs,
    cotangent,
    ln1_gain,
    ln1_bias,
    ln2_gain,
    ln2_bias,
    w_qkv,
    b_qkv,
    w_out,
    b_out,
    w_in,
    b_in,
    w_mlp_out,
    b_mlp_out,
):
    f32 = jnp.float32
    bf16 = jnp.bfloat16
    group_rows = inputs.shape[1]
    model_width = inputs.shape[2]
    seq_len = group_rows * lax.axis_size("ctx")
    key_block = math.gcd(seq_len, 512)
    score_scale = HEAD_DIM ** (-0.5)
    positions = lax.axis_index("ctx") * group_rows + jnp.arange(group_rows, dtype=jnp.int32)
    cosine, sine_rot = angles(positions)

    def gather_params():
        return (
            lax.all_gather(ln1_gain, ("fsdp", "ctx"), axis=0, tiled=True),
            lax.all_gather(ln1_bias, ("fsdp", "ctx"), axis=0, tiled=True),
            lax.all_gather(ln2_gain, ("fsdp", "ctx"), axis=0, tiled=True),
            lax.all_gather(ln2_bias, ("fsdp", "ctx"), axis=0, tiled=True),
            lax.all_gather(w_qkv, ("fsdp", "ctx"), axis=0, tiled=True),
            lax.all_gather(b_qkv, ("fsdp", "ctx"), axis=0, tiled=True),
            lax.all_gather(w_out, ("fsdp", "ctx"), axis=0, tiled=True),
            lax.all_gather(b_out, ("fsdp", "ctx"), axis=0, tiled=True),
            lax.all_gather(w_in, ("fsdp", "ctx"), axis=0, tiled=True),
            lax.all_gather(b_in, ("fsdp", "ctx"), axis=0, tiled=True),
            lax.all_gather(w_mlp_out, ("fsdp", "ctx"), axis=0, tiled=True),
            lax.all_gather(b_mlp_out, ("fsdp", "ctx"), axis=0, tiled=True),
        )

    weight_sums = None
    output_list = []
    grad_list = []
    for micro_index in range(MICRO):
        batch_rows = inputs[micro_index * SEQ_MB : (micro_index + 1) * SEQ_MB]
        cot_rows = cotangent[micro_index * SEQ_MB : (micro_index + 1) * SEQ_MB]
        seq_count = batch_rows.shape[0]
        flat_rows = seq_count * group_rows
        params_fwd = gather_params()
        (
            gain_one,
            shift_one,
            gain_two,
            shift_two,
            weight_qkv,
            bias_qkv,
            weight_out,
            bias_out,
            weight_in,
            bias_in,
            weight_mlp,
            bias_mlp,
        ) = params_fwd
        residual = batch_rows.reshape(flat_rows, model_width).astype(f32)
        normal_one, normed_one, inverse_one = layer_norm(
            residual, gain_one.astype(f32), shift_one.astype(f32)
        )
        normal_two, normed_two, inverse_two = layer_norm(
            residual, gain_two.astype(f32), shift_two.astype(f32)
        )
        hidden_one = normal_one.astype(bf16)
        hidden_two = normal_two.astype(bf16)
        project = jnp.dot(hidden_one, weight_qkv, preferred_element_type=f32) + bias_qkv.astype(f32)
        head_shape = (seq_count, group_rows, HEADS, HEAD_DIM)
        query_low = rotate(
            project[:, :model_width].reshape(head_shape), cosine, sine_rot, 1.0
        ).astype(bf16)
        key_low = rotate(
            project[:, model_width : 2 * model_width].reshape(head_shape), cosine, sine_rot, 1.0
        ).astype(bf16)
        value_low = project[:, 2 * model_width :].astype(bf16)
        kv_pack = jnp.concatenate(
            [
                key_low.reshape(seq_count, group_rows, model_width),
                value_low.reshape(seq_count, group_rows, model_width),
            ],
            axis=-1,
        )
        start_state = (
            jnp.full((seq_count, HEADS, group_rows), -jnp.inf, f32),
            jnp.zeros((seq_count, HEADS, group_rows), f32),
            jnp.zeros((seq_count, HEADS, group_rows, HEAD_DIM), f32),
        )
        soft_state = attend_piece(
            start_state,
            lax.all_gather(kv_pack, "ctx", axis=1, tiled=True),
            query_low,
            positions,
            score_scale,
        )
        run_max, run_sum, weighted = soft_state
        log_total = run_max + jnp.log(run_sum)
        attended = jnp.transpose(weighted / run_sum[..., None], (0, 2, 1, 3)).astype(bf16)
        att_flat = attended.reshape(flat_rows, model_width)
        pre_act = jnp.dot(hidden_two, weight_in, preferred_element_type=f32) + bias_in.astype(f32)
        activation_f, gelu_slope = gelu_parts(pre_act)
        activation = activation_f.astype(bf16)
        output = (
            residual
            + jnp.dot(att_flat, weight_out, preferred_element_type=f32)
            + bias_out.astype(f32)
            + jnp.dot(activation, weight_mlp, preferred_element_type=f32)
            + bias_mlp.astype(f32)
        )
        output_list.append(output.reshape(seq_count, group_rows, model_width))
        params_back = gather_params()
        (
            gain_one,
            shift_one,
            gain_two,
            shift_two,
            weight_qkv,
            bias_qkv,
            weight_out,
            bias_out,
            weight_in,
            bias_in,
            weight_mlp,
            bias_mlp,
        ) = params_back
        kv_rows = lax.all_gather(kv_pack, "ctx", axis=1, tiled=True)
        cot_flat = cot_rows.reshape(flat_rows, model_width)
        cot_low = cot_flat.astype(bf16)
        cot_sum = jnp.sum(cot_flat, axis=0)
        grad_w_out = outer_rows(att_flat, cot_low)
        grad_w_mlp = outer_rows(activation, cot_low)
        d_pre = times_transpose(cot_low, weight_mlp) * gelu_slope
        d_pre_low = d_pre.astype(bf16)
        grad_w_in = outer_rows(hidden_two, d_pre_low)
        d_hidden_two = times_transpose(d_pre_low, weight_in)
        grad_att = times_transpose(cot_low, weight_out).astype(bf16).reshape(head_shape)
        row_delta = jnp.einsum("sqhd,sqhd->shq", grad_att, attended, preferred_element_type=f32)

        def back_block(block_index, loop_carry):
            grad_query, buffer = loop_carry
            offset = block_index * key_block
            kv_block = lax.dynamic_slice_in_dim(kv_rows, offset, key_block, 1)
            key_part = kv_block[..., :model_width].reshape(seq_count, key_block, HEADS, HEAD_DIM)
            value_part = kv_block[..., model_width:].reshape(seq_count, key_block, HEADS, HEAD_DIM)
            scores = (
                jnp.einsum("sqhd,skhd->shqk", query_low, key_part, preferred_element_type=f32)
                * score_scale
            )
            allowed = (offset + jnp.arange(key_block, dtype=jnp.int32))[None, :] <= positions[
                :, None
            ]
            prob_block = jnp.where(allowed, jnp.exp(scores - log_total[..., None]), 0.0)
            grad_value = jnp.einsum(
                "shqk,sqhd->skhd", prob_block.astype(bf16), grad_att, preferred_element_type=f32
            )
            grad_prob = jnp.einsum(
                "sqhd,skhd->shqk", grad_att, value_part, preferred_element_type=f32
            )
            grad_score = (prob_block * (grad_prob - row_delta[..., None]) * score_scale).astype(
                bf16
            )
            grad_query = grad_query + jnp.einsum(
                "shqk,skhd->sqhd", grad_score, key_part, preferred_element_type=f32
            )
            grad_key = jnp.einsum(
                "shqk,sqhd->skhd", grad_score, query_low, preferred_element_type=f32
            )
            key_value_grad = jnp.concatenate(
                [
                    grad_key.reshape(seq_count, key_block, model_width),
                    grad_value.reshape(seq_count, key_block, model_width),
                ],
                axis=-1,
            )
            return (grad_query, lax.dynamic_update_slice_in_dim(buffer, key_value_grad, offset, 1))

        start_carry = (
            jnp.zeros(head_shape, f32),
            jnp.zeros((seq_count, seq_len, 2 * model_width), f32),
        )
        grad_query, buffer = lax.fori_loop(0, seq_len // key_block, back_block, start_carry)
        kv_grad_own = lax.psum_scatter(
            buffer.astype(jnp.bfloat16), "ctx", scatter_dimension=1, tiled=True
        ).astype(jnp.float32)
        key_grad_raw = kv_grad_own[..., :model_width].reshape(head_shape)
        value_grad_flat = kv_grad_own[..., model_width:].reshape(flat_rows, model_width)
        grad_query = rotate(grad_query, cosine, sine_rot, -1.0)
        grad_key = rotate(key_grad_raw, cosine, sine_rot, -1.0)
        d_project = jnp.concatenate(
            [
                grad_query.reshape(flat_rows, model_width),
                grad_key.reshape(flat_rows, model_width),
                value_grad_flat,
            ],
            axis=-1,
        )
        d_project_low = d_project.astype(bf16)
        grad_w_qkv = outer_rows(hidden_one, d_project_low)
        d_hidden_one = times_transpose(d_project_low, weight_qkv)
        grad_rows = (
            cot_flat
            + norm_back(d_hidden_one, normed_one, inverse_one, gain_one.astype(f32))
            + norm_back(d_hidden_two, normed_two, inverse_two, gain_two.astype(f32))
        )
        grad_list.append(grad_rows.reshape(seq_count, group_rows, model_width))
        terms = (
            jnp.sum(d_hidden_one * normed_one, axis=0),
            jnp.sum(d_hidden_one, axis=0),
            jnp.sum(d_hidden_two * normed_two, axis=0),
            jnp.sum(d_hidden_two, axis=0),
            grad_w_qkv,
            jnp.sum(d_project, axis=0),
            grad_w_out,
            cot_sum,
            grad_w_in,
            jnp.sum(d_pre, axis=0),
            grad_w_mlp,
            cot_sum,
        )
        if weight_sums is None:
            weight_sums = terms
        else:
            weight_sums = jax.tree.map(lambda total, term: total + term, weight_sums, terms)
    owned = (
        lax.psum_scatter(weight_sums[0], ("fsdp", "ctx"), scatter_dimension=0, tiled=True),
        lax.psum_scatter(weight_sums[1], ("fsdp", "ctx"), scatter_dimension=0, tiled=True),
        lax.psum_scatter(weight_sums[2], ("fsdp", "ctx"), scatter_dimension=0, tiled=True),
        lax.psum_scatter(weight_sums[3], ("fsdp", "ctx"), scatter_dimension=0, tiled=True),
        lax.psum_scatter(weight_sums[4], ("fsdp", "ctx"), scatter_dimension=0, tiled=True),
        lax.psum_scatter(weight_sums[5], ("fsdp", "ctx"), scatter_dimension=0, tiled=True),
        lax.psum_scatter(weight_sums[6], ("fsdp", "ctx"), scatter_dimension=0, tiled=True),
        lax.psum_scatter(weight_sums[7], ("fsdp", "ctx"), scatter_dimension=0, tiled=True),
        lax.psum_scatter(weight_sums[8], ("fsdp", "ctx"), scatter_dimension=0, tiled=True),
        lax.psum_scatter(weight_sums[9], ("fsdp", "ctx"), scatter_dimension=0, tiled=True),
        lax.psum_scatter(weight_sums[10], ("fsdp", "ctx"), scatter_dimension=0, tiled=True),
        lax.psum_scatter(weight_sums[11], ("fsdp", "ctx"), scatter_dimension=0, tiled=True),
    )
    outputs = jnp.concatenate(output_list, axis=0)
    grad_inputs = jnp.concatenate(grad_list, axis=0)
    return (
        outputs,
        grad_inputs,
        owned[0],
        owned[1],
        owned[2],
        owned[3],
        owned[4],
        owned[5],
        owned[6],
        owned[7],
        owned[8],
        owned[9],
        owned[10],
        owned[11],
    )


ROWS = 128
BLOCK = 256


def swap(value, bit):
    return lax.ppermute(value, "ctx", [(i, i ^ bit) for i in range(8)])


def shift_z(value, step):
    return lax.ppermute(value, "fsdp", [(i, (i + step) % 4) for i in range(4)])


def nt(left, right):
    return lax.dot_general(
        left, right, (((1,), (1,)), ((), ())), preferred_element_type=jnp.float32
    )


def nn(left, right):
    return lax.dot_general(
        left, right, (((1,), (0,)), ((), ())), preferred_element_type=jnp.float32
    )


def tn(left, right):
    return lax.dot_general(
        left, right, (((0,), (0,)), ((), ())), preferred_element_type=jnp.float32
    )


def normalize(values):
    centred = values - jnp.mean(values, axis=-1, keepdims=True)
    inverse = lax.rsqrt(jnp.mean(centred * centred, axis=-1, keepdims=True) + EPS)
    return centred * inverse, inverse


def col_sum(values):
    return jnp.sum(values, axis=0, keepdims=True)


def piece_bits(index):
    return ((index & 1) << 2) | (index & 2) | (index >> 2)


def mlp_kernel(chunks, row_ref, *refs):
    refs = list(refs)
    parts = [[refs.pop(0) for _ in range(8)] for _ in chunks]
    weights = [refs.pop(0) for _ in range(8)]
    vecs, cot_ref, first_send, first_keep, first_norm = [refs.pop(0) for _ in range(5)]
    send_ref, keep_ref, rest_ref, norm_ref, gsend_ref, gkeep_ref, vec_ref = [refs.pop(0) for _ in range(7)]
    w_in, w_down, h_s, c_s, act_s, dpre_s, x_n, first_s, part_s, g_in, g_down, seg_s, w_sem, x_sem, p_sem, o_sem = refs
    f32, bf16 = jnp.float32, jnp.bfloat16
    gain, shift, bias = vecs[2:3, :], vecs[3:4, :], vecs[6:7, :]
    where = [(at, inside) for at, count in enumerate(chunks) for inside in range(count)]
    total = len(where)

    weight_copies = []
    for at, source in enumerate(weights):
        rows = pl.ds(pl.multiple_of(row_ref[at], 16), 96)
        for kind, target in ((0, w_in), (1, w_down)):
            weight_copies.append(
                pltpu.make_async_copy(
                    source.at[pl.ds(kind * 96, 96)], target.at[rows], w_sem.at[at * 2 + kind]
                )
            )
    part_copies = []
    for seq, (at, inside) in enumerate(where):
        for piece in range(8):
            rows = pl.ds((seq * 8 + piece) * ROWS, ROWS)
            sem = x_sem.at[(seq * 8 + piece) * 2]
            if seq == 0:
                source_rows = pl.ds(pl.multiple_of(row_ref[16 + piece], ROWS), ROWS)
                part_copies.append(pltpu.make_async_copy(first_norm.at[source_rows], x_n.at[rows], sem))
            else:
                part_copies.append(
                    pltpu.make_async_copy(parts[at][piece].at[0, inside], h_s.at[rows], sem)
                )
            part_copies.append(
                pltpu.make_async_copy(
                    parts[at][piece].at[1, inside], c_s.at[rows], x_sem.at[(seq * 8 + piece) * 2 + 1]
                )
            )
    norm_copies = [
        pltpu.make_async_copy(x_n.at[pl.ds(seq * 1024, 1024)], norm_ref.at[seq - 1], o_sem.at[total + seq])
        for seq in range(1, total)
    ]
    first_copies = [
        pltpu.make_async_copy(first_keep, first_s.at[pl.ds(0, 4)], p_sem.at[0]),
        pltpu.make_async_copy(first_send, first_s.at[pl.ds(4, 4)], p_sem.at[1]),
    ]
    out_copies = [
        pltpu.make_async_copy(part_s.at[0, pl.ds(0, 4)], keep_ref, o_sem.at[0]),
        pltpu.make_async_copy(part_s.at[0, pl.ds(4, 4)], send_ref, o_sem.at[1]),
    ] + [
        pltpu.make_async_copy(part_s.at[seq % 2], rest_ref.at[seq - 1], o_sem.at[seq + 1])
        for seq in range(1, total)
    ]
    for copy in part_copies[:16] + weight_copies + first_copies + part_copies[16:]:
        copy.start()
    vec_ref[...] = jnp.zeros_like(vec_ref)
    for seq in range(2 * total):
        vec_ref[3:4, :] += col_sum(cot_ref[seq])

    def norm_rows(first):
        for at in range(0, 256, 16):
            rows = slice(first + at, first + at + 16)
            normed, _ = normalize(h_s[rows, :].astype(f32))
            x_n[rows, :] = normed
            h_s[rows, :] = (normed * gain + shift).astype(bf16)

    for seq in range(total):
        rows = slice(seq * 1024, (seq + 1) * 1024)
        if seq == 0:
            for copy in part_copies[:16]:
                copy.wait()
            h_s[rows, :] = (x_n[rows, :] * gain + shift).astype(bf16)
            for copy in weight_copies:
                copy.wait()
        for cols in (slice(0, 512), slice(512, 768)):
            pre = nn(h_s[rows, :], w_in[:, cols]) + bias[:, cols]
            d_act = nt(c_s[rows, :], w_down[cols, :])
            cdf = 0.5 * (1.0 + lax.erf(pre * 0.7071067811865476))
            density = jnp.exp(-0.5 * pre * pre) * 0.3989422804014327
            act_s[rows, cols] = (pre * cdf).astype(bf16)
            d_pre = d_act * (cdf + pre * density)
            dpre_s[rows, cols] = d_pre.astype(bf16)
            vec_ref[0:1, cols] += col_sum(d_pre)
        if seq + 1 < total:
            for copy in part_copies[seq * 16 + 16 : seq * 16 + 32]:
                copy.wait()
        if seq == 0:
            for copy in first_copies:
                copy.wait()
        if seq == 2:
            out_copies[0].wait()
            out_copies[1].wait()
        for block in range(4):
            part_rows = slice(seq * 1024 + block * 256, seq * 1024 + (block + 1) * 256)
            out = nn(act_s[part_rows, :], w_down[...])
            d_hidden = nt(dpre_s[part_rows, :], w_in[...])
            if seq + 1 < total:
                norm_rows((seq + 1) * 1024 + block * 256)
            vec_ref[1:2, :] += col_sum(d_hidden * x_n[part_rows, :])
            vec_ref[2:3, :] += col_sum(d_hidden)
            for kind, value in ((0, out), (1, d_hidden * gain)):
                for half in range(2):
                    piece = block * 2 + half
                    part = value[half * ROWS : (half + 1) * ROWS]
                    if seq == 0:
                        part = part + first_s[piece, kind].astype(f32)
                    part_s[seq % 2, piece, kind] = part.astype(bf16)
        if seq + 1 < total:
            norm_copies[seq].start()
        if seq == 0:
            out_copies[0].start()
            out_copies[1].start()
        else:
            out_copies[seq + 1].start()

    g_in[...] = tn(h_s[...], dpre_s[...])
    g_down[...] = tn(act_s[...], c_s[...])
    for at in range(8):
        seg_s[at, :, :96] = jnp.broadcast_to(vec_ref[0:1, at * 96 : (at + 1) * 96], (16, 96))
    for half, target in ((0, gkeep_ref), (1, gsend_ref)):
        for zz in range(4):
            at = zz * 2 + (row_ref[24] ^ half)
            rows = pl.ds(pl.multiple_of(at * 96, 16), 96)
            target[zz, :96, :] = g_in[rows, :].astype(target.dtype)
            target[zz, 96:192, :] = g_down[rows, :].astype(target.dtype)
            target[zz, 192:, :] = jnp.zeros((16, 768), target.dtype)
            target[zz, 192:, :96] = seg_s[at, :, :96].astype(target.dtype)
    for copy in out_copies[2:] + norm_copies:
        copy.wait()


def whole(shape):
    return pl.BlockSpec(shape, lambda *_: (0,) * len(shape))


def mlp_call(row_offsets, parts, weights, vecs, cot, first_send, first_keep, first_norm):
    chunks = tuple(part[0].shape[1] for part in parts)
    total = sum(chunks)
    width = vecs.shape[-1]
    f32, bf16 = jnp.float32, jnp.bfloat16

    anywhere = pl.BlockSpec(memory_space=pl.ANY)
    dma = pltpu.SemaphoreType.DMA
    rows = total * 8 * ROWS
    half = (4, 2, ROWS, width)
    grads = (4, 208, width)
    return pl.pallas_call(
        functools.partial(mlp_kernel, chunks),
        grid_spec=pltpu.PrefetchScalarGridSpec(
            num_scalar_prefetch=1,
            grid=(1,),
            in_specs=[anywhere] * (8 * len(parts) + 8)
            + [whole(vecs.shape), whole(cot.shape)]
            + [anywhere] * 3,
            out_specs=[anywhere] * 4 + [whole(grads), whole(grads), whole((8, width))],
            scratch_shapes=[pltpu.VMEM((width, width), bf16)] * 2
            + [pltpu.VMEM((rows, width), bf16)] * 4
            + [pltpu.VMEM((rows, width), f32)]
            + [pltpu.VMEM((8, 2, ROWS, width), bf16), pltpu.VMEM((2, 8, 2, ROWS, width), bf16)]
            + [pltpu.VMEM((width, width), f32)] * 2
            + [pltpu.VMEM((8, 16, 128), f32)]
            + [dma((16,)), dma((total * 16,)), dma((2,)), dma((2 * total,))],
        ),
        out_shape=[
            jax.ShapeDtypeStruct(half, bf16),
            jax.ShapeDtypeStruct(half, bf16),
            jax.ShapeDtypeStruct((total - 1, 8, 2, ROWS, width), bf16),
            jax.ShapeDtypeStruct((total - 1, 8 * ROWS, width), f32),
            jax.ShapeDtypeStruct(grads, bf16),
            jax.ShapeDtypeStruct(grads, f32),
            jax.ShapeDtypeStruct((8, width), f32),
        ],
        compiler_params=pltpu.CompilerParams(vmem_limit_bytes=58 << 20),
        cost_estimate=pl.CostEstimate(
            flops=30_000_000_000, transcendentals=0, bytes_accessed=30_000_000
        ),
        name="mlp",
    )(row_offsets, *[a for part in parts for a in part], *weights, vecs, cot, first_send, first_keep, first_norm)


def rotary_tables():
    f32 = jnp.float32
    lane = lax.broadcasted_iota(jnp.int32, (32, 128), 1)
    dim = lane & 63
    power = (dim & 7).astype(f32) * (-2.0 / ROT_DIM)
    freq = jnp.where(dim < ROT_DIM, jnp.exp(power * math.log(BASE_FREQ)), 0.0)
    row = lax.broadcasted_iota(jnp.int32, (32, 128), 0).astype(f32)
    fine, coarse = row * freq, row * 32.0 * freq
    cos_fine, sin_fine = jnp.cos(fine), jnp.sin(fine)
    scale = jnp.where(lane < 64, HEAD_DIM ** (-0.5), 1.0)
    cos_coarse, sin_coarse = jnp.cos(coarse) * scale, jnp.sin(coarse) * scale
    first, second = dim[:1] < 8, (dim[:1] >= 8) & (dim[:1] < ROT_DIM)
    return cos_fine, sin_fine, cos_coarse, sin_coarse, first, second


def attn_kernel(has_prev, last, at_seq, inside, row_ref, *refs):
    refs = list(refs)
    parts = [refs.pop(0) for _ in range(8)]
    weights = [refs.pop(0) for _ in range(8)]
    o_own, o_other, vecs = [refs.pop(0) for _ in range(3)]
    if has_prev:
        partial, norm_ref, pq_ref, po_ref, pv_ref = [refs.pop(0) for _ in range(5)]
    if last:
        mv_ref, at_ref, col_ref = [refs.pop(0) for _ in range(3)]
        send_ref, keep_ref, qsend_ref, qkeep_ref, osend_ref, okeep_ref = [refs.pop(0) for _ in range(6)]
    else:
        send_ref, keep_ref, gq_ref, go_ref, vec_ref = [refs.pop(0) for _ in range(5)]
    if not has_prev:
        norm_out_ref = refs.pop(0)
    wq, wo, x_s, c_s, x_n, h_s = [refs.pop(0) for _ in range(6)]
    q_s, k_s, v_s, g_s, kt_s, vt_s, gt_s = [refs.pop(0) for _ in range(7)]
    dq_s, dk_s, dv_s, at_s, att_s, dp_s, res_s, tab = [refs.pop(0) for _ in range(8)]
    w_sem, x_sem, r_sem = [refs.pop(0) for _ in range(3)]
    if has_prev:
        pp_s, pq_s, po_s, p_sem = [refs.pop(0) for _ in range(4)]
    f32, bf16 = jnp.float32, jnp.bfloat16
    seq = 8 * ROWS
    blocks = seq // BLOCK
    gain, shift, bias = vecs[0:1, :], vecs[1:2, :], vecs[5:6, :640]

    def place(piece):
        return pl.ds(pl.multiple_of(row_ref[16 + piece], ROWS), ROWS)

    weight_copies = [
        pltpu.make_async_copy(
            source,
            wq.at[pl.ds(pl.multiple_of(row_ref[at], 16), 96)],
            w_sem.at[at],
        )
        for at, source in enumerate(weights)
    ]
    out_weight_copies = [
        pltpu.make_async_copy(
            source, wo.at[pl.ds(pl.multiple_of(row_ref[8 + at], 16), 96)], w_sem.at[8 + at]
        )
        for at, source in enumerate((o_own, o_other))
    ]
    part_copies = [
        [
            pltpu.make_async_copy(
                parts[piece].at[kind, inside], target.at[place(piece)], x_sem.at[kind * 8 + piece]
            )
            for piece in range(8)
        ]
        for kind, target in (((1, c_s),) if has_prev else ((0, x_s), (1, c_s)))
    ]
    if has_prev:
        norm_part_copies = [
            pltpu.make_async_copy(
                norm_ref.at[at_seq - 1, pl.ds(piece * ROWS, ROWS)], x_n.at[place(piece)], x_sem.at[piece]
            )
            for piece in range(8)
        ]
        part_copies.insert(0, norm_part_copies)
    for copy in part_copies[0] + weight_copies + part_copies[1] + out_weight_copies:
        copy.start()
    if has_prev:
        prev_copies = [
            pltpu.make_async_copy(
                partial.at[at_seq - 1, piece, kind], pp_s.at[kind, place(piece)], p_sem.at[kind * 8 + piece]
            )
            for piece in range(8)
            for kind in range(2)
        ]
        prev_copies.append(pltpu.make_async_copy(pq_ref, pq_s, p_sem.at[16]))
        prev_copies.append(pltpu.make_async_copy(po_ref, po_s, p_sem.at[17]))
        for copy in prev_copies:
            copy.start()

    wo[192:, :] = jnp.zeros((64, 768), bf16)
    cos_f, sin_f, cos_c, sin_c, first, second = rotary_tables()
    for at in range(seq // 32):
        rows = slice(at * 32, (at + 1) * 32)
        cosine = cos_f * cos_c[at : at + 1] - sin_f * sin_c[at : at + 1]
        sine = sin_f * cos_c[at : at + 1] + cos_f * sin_c[at : at + 1]
        tab[0, rows, :] = cosine
        tab[1, rows, :] = jnp.where(first, -sine, 0.0)
        tab[2, rows, :] = jnp.where(second, sine, 0.0)

    lane = lax.broadcasted_iota(jnp.int32, (256, 128), 1)
    left = lane < 64

    def heads_of(block, project, grad):
        rows = slice(block * 256, (block + 1) * 256)
        cosine, low, high = tab[0, rows, :], tab[1, rows, :], tab[2, rows, :]
        for head in range(3):
            pair = project[:, head * 128 : (head + 1) * 128]
            pair = pair * cosine + pltpu.roll(pair, 120, 1) * low + pltpu.roll(pair, 8, 1) * high
            k_s[head, rows, :] = jnp.where(left, 0.0, pair).astype(bf16)
            q_s[head, rows, :] = jnp.where(left, 0.0, pltpu.roll(pair, 64, 1)).astype(bf16)
            kt_s[head, :, rows] = jnp.transpose(pair)[64:].astype(bf16)
        v_pair, v_last = project[:, 384:512], jnp.where(left, project[:, 512:640], 0.0)
        vt_s[:128, rows] = jnp.transpose(v_pair).astype(bf16)
        vt_s[128:, rows] = jnp.transpose(v_last)[:64].astype(bf16)
        for target, pair_value, last_value in ((v_s, v_pair, v_last), (g_s, grad[:, :128], grad[:, 128:])):
            target[0, rows, :] = jnp.where(left, pair_value, 0.0).astype(bf16)
            target[1, rows, :] = jnp.where(left, 0.0, pair_value).astype(bf16)
            target[2, rows, :] = last_value.astype(bf16)

    for copy in part_copies[0] + weight_copies + part_copies[1] + out_weight_copies:
        copy.wait()
    for block in (1, 3):
        wide = slice((block - 1) * 256, (block + 1) * 256)
        if has_prev:
            h_s[wide, :] = (x_n[wide, :] * gain + shift).astype(bf16)
        else:
            for part in range(32):
                rows = slice((block - 1) * 256 + part * 16, (block - 1) * 256 + (part + 1) * 16)
                normed, _ = normalize(x_s[rows, :].astype(f32))
                x_n[rows, :] = normed
                h_s[rows, :] = (normed * gain + shift).astype(bf16)
        project_wide = nn(h_s[wide, :], wq[...]) + bias
        grad_wide = nt(c_s[wide, :], wo[...])
        gt_s[:, wide] = nt(wo[:192, :], c_s[wide, :]).astype(bf16)
        for half in range(2):
            heads_of(block - 1 + half, project_wide[half * 256 : half * 256 + 256], grad_wide[half * 256 : half * 256 + 256])

    allowed = lax.broadcasted_iota(jnp.int32, (BLOCK, BLOCK), 0) <= lax.broadcasted_iota(
        jnp.int32, (BLOCK, BLOCK), 1
    )

    def rows_of(block):
        return slice(block * BLOCK, (block + 1) * BLOCK)

    def scores_of(head, block):
        query, grad = q_s[head, rows_of(block), :], g_s[head, rows_of(block), :]
        upto = (block + 1) * BLOCK
        scores = nt(k_s[head, :upto, :], query)
        scores = [scores[rows_of(at)] for at in range(block + 1)]
        scores[block] = jnp.where(allowed, scores[block], -1e30)
        d_prob = nt(v_s[head, :upto, :], grad)
        return scores, [d_prob[rows_of(at)] for at in range(block + 1)]

    def softmax_of(scores):
        top = jnp.max(scores[0], axis=0, keepdims=True)
        for part in scores[1:]:
            top = jnp.maximum(top, jnp.max(part, axis=0, keepdims=True))
        probs = [jnp.exp(part - top) for part in scores]
        total = col_sum(probs[0])
        for part in probs[1:]:
            total = total + col_sum(part)
        scale = 1.0 / total
        probs = [part * scale for part in probs]
        return probs, [part.astype(bf16) for part in probs]

    def values_of(head, block, probs, lows, d_prob):
        rows, upto = rows_of(block), (block + 1) * BLOCK
        low = jnp.concatenate(lows, axis=0) if block else lows[0]
        att_t = nn(vt_s[head * 64 : (head + 1) * 64, :upto], low)
        att_low = att_t.astype(bf16)
        att_s[head * 64 : (head + 1) * 64, rows] = att_low
        d_value = nn(low, g_s[head, rows, :])
        into = head // 2
        keep = slice(0, upto if head == 1 else upto - BLOCK)
        if keep.stop:
            dv_s[into, keep, :] += d_value[keep]
        if head != 1:
            dv_s[into, rows, :] = d_value[upto - BLOCK :]
        delta = col_sum(gt_s[head * 64 : (head + 1) * 64, rows].astype(f32) * att_low.astype(f32))
        return [(p * (d - delta)).astype(bf16) for p, d in zip(probs, d_prob)]

    def grads_of(head, block, d_scores):
        rows, upto = rows_of(block), (block + 1) * BLOCK
        d_score = jnp.concatenate(d_scores, axis=0) if block else d_scores[0]
        d_key = nn(d_score, q_s[head, rows, :])
        if block:
            dk_s[head, : upto - BLOCK, :] += d_key[: upto - BLOCK]
        dk_s[head, rows, :] = d_key[upto - BLOCK :]
        dq_s[head, rows, :64] = jnp.transpose(nn(kt_s[head, :, :upto], d_score))

    order = [(head, block) for block in range(blocks) for head in range(3)]
    ahead = scores_of(*order[0])
    waiting = None
    for at, (head, block) in enumerate(order):
        scores, d_prob = ahead
        if at + 1 < len(order):
            ahead = scores_of(*order[at + 1])
        probs, lows = softmax_of(scores)
        if waiting is not None:
            grads_of(*waiting)
        waiting = (head, block, values_of(head, block, probs, lows, d_prob))
    grads_of(*waiting)

    project_sums = []
    for head in range(3):
        total = jnp.zeros((1, 128), f32)
        for block in range(4):
            rows = slice(block * 256, (block + 1) * 256)
            pair = jnp.concatenate([dq_s[head, rows, :64], dk_s[head, rows, 64:]], axis=1)
            cosine, low, high = tab[0, rows, :], tab[1, rows, :], tab[2, rows, :]
            pair = pair * cosine - pltpu.roll(pair, 120, 1) * low - pltpu.roll(pair, 8, 1) * high
            total = total + col_sum(pair)
            dp_s[rows, head * 128 : (head + 1) * 128] = pair.astype(bf16)
        project_sums.append(total)
    for into in range(2):
        dp_s[:, 384 + into * 128 : 512 + into * 128] = dv_s[into].astype(bf16)
        project_sums.append(col_sum(dv_s[into]))
    if has_prev:
        for copy in prev_copies:
            copy.wait()
    for block in range(4):
        rows = slice(block * 256, (block + 1) * 256)
        at_s[rows, :128] = jnp.transpose(att_s[:128, rows].astype(f32)).astype(bf16)
        at_s[rows, 128:] = jnp.concatenate(
            [jnp.transpose(att_s[128:, rows].astype(f32)), jnp.zeros((256, 64), f32)], axis=1
        ).astype(bf16)
    out = nn(at_s[...], wo[...])
    d_hidden = nt(dp_s[...], wq[...])
    s = d_hidden * gain
    if has_prev:
        out = out + pp_s[0].astype(f32)
        s = s + pp_s[1].astype(f32)
    res_s[0] = out.astype(bf16)
    res_s[1] = s.astype(bf16)
    sums = [
        jnp.concatenate(project_sums, axis=1),
        col_sum(d_hidden * x_n[...]),
        col_sum(d_hidden),
    ]
    result_copies = [
        pltpu.make_async_copy(
            res_s.at[kind, place(piece)],
            (keep_ref if piece < 4 else send_ref).at[piece % 4, kind],
            r_sem.at[piece * 2 + kind],
        )
        for piece in (4, 5, 6, 7, 0, 1, 2, 3)
        for kind in range(2)
    ]
    if not has_prev:
        result_copies.append(pltpu.make_async_copy(x_n, norm_out_ref, r_sem.at[16]))
    for copy in result_copies:
        copy.start()
    g_query = tn(h_s[...], dp_s[...])
    g_out = nn(att_s[...], c_s[...])
    if has_prev:
        g_query = g_query + pq_s[...]
        g_out = g_out + po_s[...]
        sums = [sums[0] + pv_ref[0:1, :640], sums[1] + pv_ref[1:2, :], sums[2] + pv_ref[2:3, :]]
    if last:
        gq_s, go_s, tr_s = refs
        gq_s[...] = g_query
        go_s[...] = g_out
        tr_s[...] = jnp.zeros_like(tr_s)
        tr_s[64:65, :] = sums[1]
        tr_s[65:66, :] = sums[2]
        tr_s[66:69, :] = mv_ref[1:4, :]
        columns = jnp.transpose(tr_s[...])
        lanes = lax.broadcasted_iota(jnp.int32, (768, 128), 1)
        target_at = col_ref[0:1, :576] + row_ref[25] * 192
        for third in range(3):
            hit = at_ref[:, third : third + 1] == target_at
            column = jnp.sum(jnp.where(hit, sums[0][:, :576], 0.0), axis=1, keepdims=True)
            columns = jnp.where(lanes == 69 + third, column, columns)
        gq_s[:, 512:640] = jnp.where(lanes < 64, gq_s[:, 512:640], columns)
        for half, target in ((0, qkeep_ref), (1, qsend_ref)):
            for zz in range(4):
                at = zz * 2 + (row_ref[24] ^ half)
                rows = pl.ds(pl.multiple_of(at * 96, 16), 96)
                target[zz] = gq_s[rows, :].astype(target.dtype)
        for half, target in ((0, okeep_ref), (1, osend_ref)):
            rows = pl.ds(pl.multiple_of((row_ref[24] ^ half) * 96, 16), 96)
            target[...] = go_s[rows, :].astype(target.dtype)
    else:
        gq_ref[...] = g_query
        go_ref[...] = g_out
        vec_ref[...] = jnp.zeros_like(vec_ref)
        vec_ref[0:1, :640] = sums[0]
        vec_ref[1:2, :] = sums[1]
        vec_ref[2:3, :] = sums[2]
    for copy in result_copies:
        copy.wait()


def attn_call(row_offsets, parts, inside, weights, o_own, o_other, vecs, partial, seq, prev, tail):
    width = vecs.shape[-1]
    f32, bf16 = jnp.float32, jnp.bfloat16
    anywhere = pl.BlockSpec(memory_space=pl.ANY)
    dma = pltpu.SemaphoreType.DMA
    has_prev, last = prev is not None, tail is not None
    rows = 8 * ROWS
    half = (4, 2, ROWS, width)
    shapes = [(half, bf16), (half, bf16)]
    if last:
        shapes += [((4, 96, 640), bf16), ((4, 96, 640), f32), ((96, width), bf16), ((96, width), f32)]
    else:
        shapes += [((width, 640), f32), ((192, width), f32), ((8, width), f32)]
    out_specs = [anywhere] * 2 + [whole(shape) for shape, _ in shapes[2:]]
    if not has_prev:
        shapes.append(((rows, width), f32))
        out_specs.append(anywhere)
    operands = [*parts, *weights, o_own, o_other, vecs]
    in_specs = [anywhere] * 18 + [whole(vecs.shape)]
    scratch = [
        pltpu.VMEM((width, 640), bf16),
        pltpu.VMEM((256, width), bf16),
        pltpu.VMEM((rows, width), bf16),
        pltpu.VMEM((rows, width), bf16),
        pltpu.VMEM((rows, width), f32),
        pltpu.VMEM((rows, width), bf16),
    ]
    scratch += [pltpu.VMEM((3, rows, 128), bf16)] * 4
    scratch += [
        pltpu.VMEM((3, 64, rows), bf16),
        pltpu.VMEM((192, rows), bf16),
        pltpu.VMEM((192, rows), bf16),
        pltpu.VMEM((3, rows, 128), f32),
        pltpu.VMEM((3, rows, 128), f32),
        pltpu.VMEM((2, rows, 128), f32),
        pltpu.VMEM((rows, 256), bf16),
        pltpu.VMEM((192, rows), bf16),
        pltpu.VMEM((rows, 640), bf16),
        pltpu.VMEM((2, rows, width), bf16),
        pltpu.VMEM((3, rows, 128), f32),
        dma((10,)),
        dma((16,)),
        dma((17,)),
    ]
    if has_prev:
        operands += [*partial, *prev]
        in_specs += [anywhere] * 4 + [whole(prev[2].shape)]
        scratch += [
            pltpu.VMEM((2, rows, width), bf16),
            pltpu.VMEM((width, 640), f32),
            pltpu.VMEM((192, width), f32),
            dma((18,)),
        ]
    if last:
        operands += list(tail)
        in_specs += [whole(a.shape) for a in tail]
        scratch += [pltpu.VMEM((width, 640), f32), pltpu.VMEM((192, width), f32), pltpu.VMEM((128, width), f32)]
    return pl.pallas_call(
        functools.partial(attn_kernel, has_prev, last, seq, inside),
        grid_spec=pltpu.PrefetchScalarGridSpec(
            num_scalar_prefetch=1,
            grid=(1,),
            in_specs=in_specs,
            out_specs=out_specs,
            scratch_shapes=scratch,
        ),
        out_shape=[jax.ShapeDtypeStruct(shape, kind) for shape, kind in shapes],
        compiler_params=pltpu.CompilerParams(vmem_limit_bytes=58 << 20),
        cost_estimate=pl.CostEstimate(
            flops=24_000_000_000, transcendentals=0, bytes_accessed=15_000_000
        ),
        name="attn",
    )(row_offsets, *operands)


def finish_kernel(seqs, half_ref, x_ref, c_ref, *refs):
    refs = list(refs)
    terms = [[refs.pop(0) for _ in range(4)] for _ in seqs]
    bias = refs.pop(0)
    out_ref, grad_ref = refs[-2:]
    f32 = jnp.float32

    def write(sources):
        total = [source[0].astype(f32) for source in sources]
        total = sum(total[1:], total[0])
        x = x_ref[0].astype(f32)
        normed, inverse = normalize(x)
        out_ref[0] = x + bias[4:5, :] + total[0]
        s = total[1]
        mean_s = jnp.mean(s, axis=-1, keepdims=True)
        mean_sn = jnp.mean(s * normed, axis=-1, keepdims=True)
        grad_ref[0] = c_ref[0] + inverse * (s - mean_s - normed * mean_sn)

    for at in range(len(seqs)):
        for other in range(2):
            @pl.when(pl.program_id(0) == at * 2 + other)
            def _(at=at, other=other):
                write(terms[at][3:] if other else terms[at][:3])


def finish_call(half, seqs, x, cot, terms, bias, done):
    _, rows, width = x.shape
    f32 = jnp.float32
    seq_spec = pl.BlockSpec(
        (1, rows, width),
        lambda i, at: (jnp.where(i % 2 == 0, at[0], 1 - at[0]) * 3 + seqs[0] + i // 2, 0, 0),
    )
    part_spec = pl.BlockSpec((1, 2, rows, width), lambda i, at: (0, 0, 0, 0))
    before = list(done) if done is not None else []
    operands = [x, cot, *[a for parts in terms for a in parts], bias]
    return pl.pallas_call(
        functools.partial(finish_kernel, seqs),
        grid_spec=pltpu.PrefetchScalarGridSpec(
            num_scalar_prefetch=1,
            grid=(2 * len(seqs),),
            in_specs=[seq_spec, seq_spec]
            + [part_spec] * (4 * len(seqs))
            + [whole(bias.shape)]
            + [pl.BlockSpec(memory_space=pl.ANY)] * len(before),
            out_specs=[seq_spec, seq_spec],
        ),
        out_shape=[jax.ShapeDtypeStruct(x.shape, f32)] * 2,
        input_output_aliases={len(operands) + 1: 0, len(operands) + 2: 1} if before else {},
        name="finish",
    )(half, *operands, *before)


def pick(value, index, axis=0):
    return lax.dynamic_index_in_dim(value, index, axis, keepdims=False)


def prep_kernel(at_ref, in_ref, q_ref, small_ref, own_ref, send_ref, pack_s):
    for h in range(4):
        parts = [in_ref[:, zy * 384 + h * 96 : zy * 384 + (h + 1) * 96] for zy in range(8)]
        for head in range(3):
            for kind in range(2):
                first = kind * 768 + h * 192 + head * 64
                parts.append(q_ref[:, first : first + 64])
        first = 1536 + h * 192
        parts.append(q_ref[:, first : first + 192])
        parts.append(small_ref[...])
        at = 0
        for part in parts:
            pack_s[h, :, at : at + part.shape[1]] = part
            at += part.shape[1]
    for core in range(2):
        own_ref[core] = pack_s[at_ref[26] * 2 + core]
        send_ref[core] = pack_s[(1 - at_ref[26]) * 2 + core]


def prep_call(row_offsets, w_in, w_qkv, small):
    half = jax.ShapeDtypeStruct((2, 24, 1408), jnp.bfloat16)
    return pl.pallas_call(
        prep_kernel,
        grid_spec=pltpu.PrefetchScalarGridSpec(
            num_scalar_prefetch=1,
            grid=(1,),
            in_specs=[whole(a.shape) for a in (w_in, w_qkv, small)],
            out_specs=[whole(half.shape)] * 2,
            scratch_shapes=[pltpu.VMEM((4, 24, 1408), jnp.bfloat16)],
        ),
        out_shape=[half, half],
        name="prep",
    )(row_offsets, w_in, w_qkv, small)


def join_kernel(at_ref, own_ref, got_ref, far_ref, down_ref, attn_ref, mlp_ref, four, rows_s):
    f32, bf16 = jnp.float32, jnp.bfloat16
    x, c = at_ref[26], at_ref[27]
    four[0] = own_ref[c].astype(f32)
    four[1] = got_ref[c].astype(f32)
    four[2] = far_ref[0].astype(f32)
    four[3] = far_ref[1].astype(f32)
    for source in range(4):
        near = ((source & 1) ^ c) * 2 + ((source >> 1) ^ x)
        rows_s[source * 24 : (source + 1) * 24, :] = four[near]
    mlp_ref[:96, :] = rows_s[:, :768].astype(bf16)
    mlp_ref[96:, :] = down_ref[...]
    attn_ref[...] = rows_s[:, 768:].astype(bf16)


def join_call(row_offsets, own, got, far, w_down):
    f32, bf16 = jnp.float32, jnp.bfloat16
    outs = [jax.ShapeDtypeStruct((96, 640), bf16), jax.ShapeDtypeStruct((192, 768), bf16)]
    return pl.pallas_call(
        join_kernel,
        grid_spec=pltpu.PrefetchScalarGridSpec(
            num_scalar_prefetch=1,
            grid=(1,),
            in_specs=[whole(a.shape) for a in (own, got, far, w_down)],
            out_specs=[whole(a.shape) for a in outs],
            scratch_shapes=[pltpu.VMEM((4, 24, 1408), f32), pltpu.VMEM((96, 1408), f32)],
        ),
        out_shape=outs,
        name="join",
    )(row_offsets, own, got, far, w_down)


def pick_out_kernel(at_ref, one, two, three, four, own_ref, send_ref, all_s):
    for at, source in enumerate((one, two, three, four)):
        all_s[at] = source[...]
    for core in range(2):
        own_ref[core] = all_s[(at_ref[28] - at_ref[26] * 2 - core + 4) % 4]
        send_ref[core] = all_s[(at_ref[28] - (1 - at_ref[26]) * 2 - core + 4) % 4]


def pick_out_call(row_offsets, pieces):
    half = jax.ShapeDtypeStruct((2, 24, 768), jnp.bfloat16)
    return pl.pallas_call(
        pick_out_kernel,
        grid_spec=pltpu.PrefetchScalarGridSpec(
            num_scalar_prefetch=1,
            grid=(1,),
            in_specs=[whole((24, 768))] * 4,
            out_specs=[whole(half.shape)] * 2,
            scratch_shapes=[pltpu.VMEM((4, 24, 768), jnp.bfloat16)],
        ),
        out_shape=[half, half],
        name="out_pick",
    )(row_offsets, *pieces)


def join_out_kernel(at_ref, own_ref, got_ref, far_ref, out_ref, four, rows_s):
    f32, bf16 = jnp.float32, jnp.bfloat16
    x, c = at_ref[26], at_ref[27]
    four[0] = own_ref[c].astype(f32)
    four[1] = got_ref[c].astype(f32)
    four[2] = far_ref[0].astype(f32)
    four[3] = far_ref[1].astype(f32)
    for source in range(4):
        near = ((source & 1) ^ c) * 2 + ((source >> 1) ^ x)
        rows_s[source * 24 : (source + 1) * 24, :] = four[near]
    out_ref[...] = rows_s[...].astype(bf16)


def join_out_call(row_offsets, own, got, far):
    f32, bf16 = jnp.float32, jnp.bfloat16
    return pl.pallas_call(
        join_out_kernel,
        grid_spec=pltpu.PrefetchScalarGridSpec(
            num_scalar_prefetch=1,
            grid=(1,),
            in_specs=[whole(a.shape) for a in (own, got, far)],
            out_specs=whole((96, 768)),
            scratch_shapes=[pltpu.VMEM((4, 24, 768), f32), pltpu.VMEM((96, 768), f32)],
        ),
        out_shape=jax.ShapeDtypeStruct((96, 768), bf16),
        name="join_out",
    )(row_offsets, own, got, far)


def vector_tables():
    row = np.arange(768)
    at_q = np.stack([(row // 24) * 72 + third * 24 + row % 24 for third in range(3)], axis=1)
    at_in = np.stack([(row // 24) * 96 + third * 24 + row % 24 for third in range(4)], axis=1)
    lane = np.arange(576)
    head, kind = lane // 128, (lane % 128) // 64
    col_q = np.where(lane < 384, kind * 768 + head * 64 + lane % 64, 1536 + lane - 384)
    col_in = (row // 96) * 384 + row % 96
    cols = np.zeros((8, 768), np.int32)
    cols[0, :576] = col_q
    cols[1] = col_in
    rows = np.concatenate([at_q, at_in, np.zeros((768, 1))], axis=1).astype(np.int32)
    return rows, cols


def vec_kernel(at_ref, *refs):
    refs = list(refs)
    pieces = [refs.pop(0) for _ in range(8)]
    rows_ref, cols_ref, out_ref, all_s = refs
    f32 = jnp.float32
    for at, source in enumerate(pieces):
        rows = pl.ds(pl.multiple_of(at_ref[at], 16), 96)
        all_s[rows, :] = source[...].astype(f32)
    flipped = jnp.transpose(all_s[...])
    out_ref[0:4, :] = flipped[64:68]
    out_ref[4:5, :] = flipped[68:69] + flipped[69:70]
    for row, kinds, target, width, step in ((5, (0, 1, 2), 0, 576, 192), (6, (3, 4, 5, 6), 1, 768, 96)):
        wanted = cols_ref[target : target + 1, :width] + at_ref[25] * step
        total = jnp.zeros((1, width), f32)
        for kind in kinds:
            hit = rows_ref[:, kind : kind + 1] == wanted
            total += col_sum(jnp.where(hit, all_s[:, 70 + kind : 71 + kind], 0.0))
        out_ref[row : row + 1, :width] = total
    out_ref[7:8, :] = jnp.zeros((1, 768), f32)
    out_ref[5:6, 576:] = jnp.zeros((1, 192), f32)


def vec_call(row_offsets, pieces, rows, cols):
    f32 = jnp.float32
    return pl.pallas_call(
        vec_kernel,
        grid_spec=pltpu.PrefetchScalarGridSpec(
            num_scalar_prefetch=1,
            grid=(1,),
            in_specs=[pl.BlockSpec((96, 128), lambda i, *_: (0, 4))] * 8
            + [whole(rows.shape), whole(cols.shape)],
            out_specs=whole((8, 768)),
            scratch_shapes=[pltpu.VMEM((768, 128), f32)],
        ),
        out_shape=jax.ShapeDtypeStruct((8, 768), f32),
        name="vectors",
    )(row_offsets, *pieces, rows, cols)


def spread_kernel(at_ref, mine, far, q_ref, in_ref, o_ref, *refs):
    f32 = jnp.float32
    out_refs, four = refs[:6], refs[6]
    x, c, z = at_ref[26], at_ref[27], at_ref[28]
    for side in range(2):
        four[side] = mine[side]
        four[2 + side] = far[side]
    o_ref[...] = four[((z & 1) ^ c) * 2 + ((z >> 1) ^ x), :, 1408:].astype(f32)
    total = None
    for h in range(4):
        block = four[((h & 1) ^ c) * 2 + ((h >> 1) ^ x)][:, :1408].astype(f32)
        for zy in range(8):
            first = zy * 384 + h * 96
            in_ref[:, first : first + 96] = block[:, 640 + zy * 96 : 640 + (zy + 1) * 96]
        for head in range(3):
            for kind in range(2):
                first = kind * 768 + h * 192 + head * 64
                at = head * 128 + kind * 64
                q_ref[:, first : first + 64] = block[:, at : at + 64]
        first = 1536 + h * 192
        q_ref[:, first : first + 192] = block[:, 384:576]
        part = block[:, 576:584]
        total = part if total is None else total + part
    same = lax.broadcasted_iota(jnp.int32, (24, 24), 0) == lax.broadcasted_iota(jnp.int32, (24, 24), 1)
    rows = [col_sum(jnp.where(same, total[:, t : t + 1], 0.0)) for t in range(8)]
    for t in range(5):
        out_refs[t][...] = rows[t]
    out_refs[5][...] = jnp.concatenate(rows[5:], axis=1)


def spread_call(row_offsets, mine, far):
    f32, bf16 = jnp.float32, jnp.bfloat16
    shapes = [(24, 2304), (24, 3072), (24, 768)] + [(1, 24)] * 5 + [(1, 72)]
    return pl.pallas_call(
        spread_kernel,
        grid_spec=pltpu.PrefetchScalarGridSpec(
            num_scalar_prefetch=1,
            grid=(1,),
            in_specs=[whole(mine.shape), whole(far.shape)],
            out_specs=[whole(shape) for shape in shapes],
            scratch_shapes=[pltpu.VMEM((4, 24, 2176), bf16)],
        ),
        out_shape=[jax.ShapeDtypeStruct(shape, f32) for shape in shapes],
        name="spread",
    )(row_offsets, mine, far)


def exchange_four(blocks, x, c):
    blocks = blocks.reshape((2, 2) + blocks.shape[1:])
    own = pick(blocks, x)
    got = swap(pick(blocks, 1 - x), 2)
    both = jnp.stack([own, got])
    mine = pick(both, c, 1)
    send = pick(both, 1 - c, 1)
    return mine, swap(send, 1)


def fast(*args):
    return fast_body(*args)


def fast_body(
    inputs, cotangent, ln1_gain, ln1_bias, ln2_gain, ln2_bias, w_qkv, b_qkv, w_out, b_out, w_in, b_in, w_mlp_out, b_mlp_out
):
    f32, bf16 = jnp.float32, jnp.bfloat16
    z = lax.axis_index("fsdp")
    ctx = lax.axis_index("ctx")
    y, x, c = ctx // 4, (ctx // 2) % 2, ctx % 2
    h = ctx % 4

    zs = jnp.stack([(z - k) % 4 for k in range(4)])
    rows_w = jnp.concatenate([(zs * 2 + y) * 96, (zs * 2 + 1 - y) * 96])
    rows_o = jnp.stack([y * 96, (1 - y) * 96])
    rows_p = jnp.stack([(ctx ^ piece_bits(k)) * ROWS for k in range(8)])
    row_offsets = jnp.concatenate(
        [rows_w, rows_o, jnp.zeros((6,), jnp.int32), rows_p, jnp.stack([y, h, x, c, z])]
    ).astype(jnp.int32)

    small = jnp.concatenate(
        [ln1_gain, ln1_bias, ln2_gain, ln2_bias, b_out, b_mlp_out, b_qkv, b_in, jnp.zeros((51 * 24,), bf16)]
    ).reshape(64, 24).T
    pack_own, pack_send = prep_call(row_offsets, w_in, w_qkv, small)

    def rows_of(half, first, count):
        at = half * 3 + first
        return jnp.stack(
            [
                lax.dynamic_slice_in_dim(inputs, at, count),
                lax.dynamic_slice_in_dim(cotangent, at, count).astype(bf16),
            ]
        )

    parts = []
    first = 0
    for count in CHUNKS:
        got = swap(rows_of(1 - y, first, count), 4)
        own = rows_of(y, first, count)
        side, side_got = swap(own, 2), swap(got, 2)
        near = (own, got, side, side_got)
        parts.append(near + tuple(swap(a, 1) for a in near))
        first += count

    pack_got = swap(pack_send, 2)
    pack_far = swap(jnp.stack([pick(pack_own, 1 - c), pick(pack_got, 1 - c)]), 1)
    out_all = [w_out] + [shift_z(w_out, k) for k in (1, 2, 3)]
    attn_w, mlp_w = join_call(row_offsets, pack_own, pack_got, pack_far, w_mlp_out)
    attn_own = [attn_w] + [shift_z(attn_w, k) for k in (1, 2, 3)]
    mlp_own = [mlp_w] + [shift_z(mlp_w, k) for k in (1, 2, 3)]
    attn_all = attn_own + [swap(part, 4) for part in attn_own]
    mlp_all = mlp_own + [swap(part, 4) for part in mlp_own]
    out_mine, out_send = pick_out_call(row_offsets, out_all)
    out_got = swap(out_send, 2)
    out_far = swap(jnp.stack([pick(out_mine, 1 - c), pick(out_got, 1 - c)]), 1)
    out_own = join_out_call(row_offsets, out_mine, out_got, out_far)
    out_other = swap(out_own, 4)
    at_rows, at_cols = vector_tables()
    vecs = vec_call(row_offsets, attn_all, at_rows, at_cols)

    where = [(at, inside) for at, count in enumerate(CHUNKS) for inside in range(count)]

    def attention(seq, partial, prev, tail=None):
        at, inside = where[seq]
        return attn_call(
            row_offsets, parts[at], inside, attn_all, out_own, out_other,
            vecs, partial, seq, prev, tail,
        )

    def reduce_z(blocks, cols):
        def total(at):
            value = pick(blocks[0], at)[:, :cols].astype(f32)
            for block in blocks[1:]:
                value = value + pick(block, at)[:, :cols].astype(f32)
            return value

        low = [total((z + k) % 4).astype(bf16) for k in (1, 2, 3)]
        sent = [shift_z(part, k + 1) for k, part in enumerate(low)]

        def rows_of_sum(first, count):
            result = total(z)[first : first + count]
            for part in sent:
                result = result + part[first : first + count].astype(f32)
            return result

        return rows_of_sum

    def to_owner_z(value):
        total = value
        low = value.astype(bf16)
        for k in (1, 2, 3):
            pairs = [
                (zz * 8 + i, (zz + k) % 4 * 8 + i) for zz in range(4) for i in range(8) if (zz + k) % 4 == i % 4
            ]
            total = total + lax.ppermute(low, ("fsdp", "ctx"), pairs).astype(f32)
        return total

    half = jnp.reshape(y, (1,)).astype(jnp.int32)

    def scatter(send, keep):
        got = swap(send, 1)
        side = swap((keep[2:].astype(f32) + got[2:].astype(f32)).astype(bf16), 2)
        far = (keep[1:2].astype(f32) + got[1:2].astype(f32) + side[1:2].astype(f32)).astype(bf16)
        return keep, got, side, swap(far, 4)

    def finish(seqs, terms, done):
        return finish_call(half, seqs, inputs, cotangent, terms, vecs, done)

    first_send, first_keep, g_q, g_o, vec, first_norm = attention(0, None, None)
    prev = (g_q, g_o, vec)
    send, keep, rest_part, rest_norm, g_send, g_keep, mlp_vec = mlp_call(
        row_offsets, parts, mlp_all, vecs, cotangent, first_send, first_keep, first_norm
    )
    g_got = swap(g_send, 4)
    terms = [scatter(send, keep)]
    send, keep, g_q, g_o, vec = attention(1, (rest_part, rest_norm), prev)
    terms.append(scatter(send, keep))
    mlp_rows = reduce_z((g_keep, g_got), 768)
    grad_w_mlp = mlp_rows(96, 96)
    grad_b_in = mlp_rows(192, 1)[0, :96]
    send, keep, q_send, q_keep, o_send, o_keep = attention(
        2, (rest_part, rest_norm), (g_q, g_o, vec), (mlp_vec, at_rows, at_cols)
    )
    terms.append(scatter(send, keep))
    done = None
    for seq in range(3):
        done = finish((seq,), terms[seq : seq + 1], done)
    q_got, o_got = swap(q_send, 4), swap(o_send, 4)
    q_rows = reduce_z((q_keep, q_got), 640)
    o_sum = o_keep + o_got.astype(f32)
    o_grad = to_owner_z(o_sum)
    low = [part.astype(bf16) for part in (q_rows(0, 96), mlp_rows(0, 96), o_grad)]
    blocks = jnp.concatenate(low, axis=1).reshape(4, 24, 2176)
    grad_w_qkv, grad_w_in, grad_w_out, *spread = spread_call(row_offsets, *exchange_four(blocks, x, c))
    one_gain, one_bias, two_gain, two_bias, grad_bias, grad_bq = [v.reshape(-1) for v in spread]

    outputs, grad_inputs = done
    return (
        outputs,
        grad_inputs,
        one_gain,
        one_bias,
        two_gain,
        two_bias,
        grad_w_qkv,
        grad_bq,
        grad_w_out,
        grad_bias,
        grad_w_in,
        grad_b_in,
        grad_w_mlp,
        grad_bias,
    )


def fast_fits(mesh):
    sizes = dict(mesh.shape)
    return sizes["fsdp"] == 4 and sizes["ctx"] == 8


def solution(mesh):
    return jax.shard_map(
        fast if fast_fits(mesh) else local,
        mesh=mesh,
        in_specs=(
            P("fsdp", "ctx", None),
            P("fsdp", "ctx", None),
            P(("fsdp", "ctx")),
            P(("fsdp", "ctx")),
            P(("fsdp", "ctx")),
            P(("fsdp", "ctx")),
            P(("fsdp", "ctx"), None),
            P(("fsdp", "ctx")),
            P(("fsdp", "ctx"), None),
            P(("fsdp", "ctx")),
            P(("fsdp", "ctx"), None),
            P(("fsdp", "ctx")),
            P(("fsdp", "ctx"), None),
            P(("fsdp", "ctx")),
        ),
        out_specs=(
            P("fsdp", "ctx", None),
            P("fsdp", "ctx", None),
            P(("fsdp", "ctx")),
            P(("fsdp", "ctx")),
            P(("fsdp", "ctx")),
            P(("fsdp", "ctx")),
            P(("fsdp", "ctx"), None),
            P(("fsdp", "ctx")),
            P(("fsdp", "ctx"), None),
            P(("fsdp", "ctx")),
            P(("fsdp", "ctx"), None),
            P(("fsdp", "ctx")),
            P(("fsdp", "ctx"), None),
            P(("fsdp", "ctx")),
        ),
        check_vma=False,
    )
```

```python
import functools
import math

import jax
import jax.numpy as jnp
import numpy as np
from jax import lax
from jax.experimental import pallas as pl
from jax.experimental.pallas import tpu as pltpu
from jax.sharding import PartitionSpec as P


HEADS = 12
HEAD_DIM = 64
ROT_DIM = 16
MICRO = 2
SEQ_MB = 3
CHUNKS = (1, 2)


EPS = 1e-05
BASE_FREQ = 10000.0


def layer_norm(values, gain_row, shift_row):
    centre = jnp.mean(values, axis=-1, keepdims=True)
    centred = values - centre
    inverse = lax.rsqrt(jnp.mean(centred * centred, axis=-1, keepdims=True) + EPS)
    normed = centred * inverse
    return (normed * gain_row + shift_row, normed, inverse)


def norm_back(grad_out, normed, inverse, gain_row):
    scaled = grad_out * gain_row
    return inverse * (
        scaled
        - jnp.mean(scaled, axis=-1, keepdims=True)
        - normed * jnp.mean(scaled * normed, axis=-1, keepdims=True)
    )


def angles(positions):
    half_rot = ROT_DIM // 2
    inv_freq = BASE_FREQ ** (-(2.0 * jnp.arange(half_rot, dtype=jnp.float32)) / ROT_DIM)
    phase_angle = positions.astype(jnp.float32)[:, None] * inv_freq[None, :]
    return (jnp.cos(phase_angle), jnp.sin(phase_angle))


def rotate(head_field, cosine, sine_rot, direction):
    half_rot = ROT_DIM // 2
    lead_half = head_field[..., :half_rot]
    trail_half = head_field[..., half_rot:ROT_DIM]
    cos_wide = cosine[:, None, :]
    sin_wide = direction * sine_rot[:, None, :]
    return jnp.concatenate(
        [
            lead_half * cos_wide - trail_half * sin_wide,
            trail_half * cos_wide + lead_half * sin_wide,
            head_field[..., ROT_DIM:],
        ],
        axis=-1,
    )


def gelu_parts(pre_act):
    normal_cdf = 0.5 * (1.0 + jax.scipy.special.erf(pre_act * 0.7071067811865476))
    density = jnp.exp(-0.5 * pre_act * pre_act) * 0.3989422804014327
    return (pre_act * normal_cdf, normal_cdf + pre_act * density)


def outer_rows(left, right):
    return lax.dot_general(
        left, right, (((0,), (0,)), ((), ())), preferred_element_type=jnp.float32
    )


def times_transpose(left, right):
    return lax.dot_general(
        left, right, (((1,), (1,)), ((), ())), preferred_element_type=jnp.float32
    )


def attend_block(soft_state, kv_block, first_row, query_low, positions, score_scale):
    run_max, run_sum, weighted = soft_state
    seq_count, block_rows, double_width = kv_block.shape
    model_width = double_width // 2
    key_low = kv_block[..., :model_width].reshape(seq_count, block_rows, HEADS, HEAD_DIM)
    value_low = kv_block[..., model_width:].reshape(seq_count, block_rows, HEADS, HEAD_DIM)
    scores = (
        jnp.einsum("sqhd,skhd->shqk", query_low, key_low, preferred_element_type=jnp.float32)
        * score_scale
    )
    allowed = (first_row + jnp.arange(block_rows, dtype=jnp.int32))[None, :] <= positions[:, None]
    scores = jnp.where(allowed, scores, -jnp.inf)
    new_max = jnp.maximum(run_max, jnp.max(scores, axis=-1))
    safe_max = jnp.where(new_max == -jnp.inf, 0.0, new_max)
    exp_scores = jnp.exp(scores - safe_max[..., None])
    factor = jnp.exp(run_max - safe_max)
    run_sum = run_sum * factor + jnp.sum(exp_scores, axis=-1)
    weighted = weighted * factor[..., None] + jnp.einsum(
        "shqk,skhd->shqd",
        exp_scores.astype(jnp.bfloat16),
        value_low,
        preferred_element_type=jnp.float32,
    )
    return (new_max, run_sum, weighted)


def attend_piece(soft_state, kv_piece, query_low, positions, score_scale):
    piece_rows = kv_piece.shape[1]
    step_rows = math.gcd(piece_rows, 512)

    def one_block(block_index, inner_state):
        offset = block_index * step_rows
        kv_block = lax.dynamic_slice_in_dim(kv_piece, offset, step_rows, 1)
        return attend_block(inner_state, kv_block, offset, query_low, positions, score_scale)

    return lax.fori_loop(0, piece_rows // step_rows, one_block, soft_state)


def local(
    inputs,
    cotangent,
    ln1_gain,
    ln1_bias,
    ln2_gain,
    ln2_bias,
    w_qkv,
    b_qkv,
    w_out,
    b_out,
    w_in,
    b_in,
    w_mlp_out,
    b_mlp_out,
):
    f32 = jnp.float32
    bf16 = jnp.bfloat16
    group_rows = inputs.shape[1]
    model_width = inputs.shape[2]
    seq_len = group_rows * lax.axis_size("ctx")
    key_block = math.gcd(seq_len, 512)
    score_scale = HEAD_DIM ** (-0.5)
    positions = lax.axis_index("ctx") * group_rows + jnp.arange(group_rows, dtype=jnp.int32)
    cosine, sine_rot = angles(positions)

    def gather_params():
        return (
            lax.all_gather(ln1_gain, ("fsdp", "ctx"), axis=0, tiled=True),
            lax.all_gather(ln1_bias, ("fsdp", "ctx"), axis=0, tiled=True),
            lax.all_gather(ln2_gain, ("fsdp", "ctx"), axis=0, tiled=True),
            lax.all_gather(ln2_bias, ("fsdp", "ctx"), axis=0, tiled=True),
            lax.all_gather(w_qkv, ("fsdp", "ctx"), axis=0, tiled=True),
            lax.all_gather(b_qkv, ("fsdp", "ctx"), axis=0, tiled=True),
            lax.all_gather(w_out, ("fsdp", "ctx"), axis=0, tiled=True),
            lax.all_gather(b_out, ("fsdp", "ctx"), axis=0, tiled=True),
            lax.all_gather(w_in, ("fsdp", "ctx"), axis=0, tiled=True),
            lax.all_gather(b_in, ("fsdp", "ctx"), axis=0, tiled=True),
            lax.all_gather(w_mlp_out, ("fsdp", "ctx"), axis=0, tiled=True),
            lax.all_gather(b_mlp_out, ("fsdp", "ctx"), axis=0, tiled=True),
        )

    weight_sums = None
    output_list = []
    grad_list = []
    for micro_index in range(MICRO):
        batch_rows = inputs[micro_index * SEQ_MB : (micro_index + 1) * SEQ_MB]
        cot_rows = cotangent[micro_index * SEQ_MB : (micro_index + 1) * SEQ_MB]
        seq_count = batch_rows.shape[0]
        flat_rows = seq_count * group_rows
        params_fwd = gather_params()
        (
            gain_one,
            shift_one,
            gain_two,
            shift_two,
            weight_qkv,
            bias_qkv,
            weight_out,
            bias_out,
            weight_in,
            bias_in,
            weight_mlp,
            bias_mlp,
        ) = params_fwd
        residual = batch_rows.reshape(flat_rows, model_width).astype(f32)
        normal_one, normed_one, inverse_one = layer_norm(
            residual, gain_one.astype(f32), shift_one.astype(f32)
        )
        normal_two, normed_two, inverse_two = layer_norm(
            residual, gain_two.astype(f32), shift_two.astype(f32)
        )
        hidden_one = normal_one.astype(bf16)
        hidden_two = normal_two.astype(bf16)
        project = jnp.dot(hidden_one, weight_qkv, preferred_element_type=f32) + bias_qkv.astype(f32)
        head_shape = (seq_count, group_rows, HEADS, HEAD_DIM)
        query_low = rotate(
            project[:, :model_width].reshape(head_shape), cosine, sine_rot, 1.0
        ).astype(bf16)
        key_low = rotate(
            project[:, model_width : 2 * model_width].reshape(head_shape), cosine, sine_rot, 1.0
        ).astype(bf16)
        value_low = project[:, 2 * model_width :].astype(bf16)
        kv_pack = jnp.concatenate(
            [
                key_low.reshape(seq_count, group_rows, model_width),
                value_low.reshape(seq_count, group_rows, model_width),
            ],
            axis=-1,
        )
        start_state = (
            jnp.full((seq_count, HEADS, group_rows), -jnp.inf, f32),
            jnp.zeros((seq_count, HEADS, group_rows), f32),
            jnp.zeros((seq_count, HEADS, group_rows, HEAD_DIM), f32),
        )
        soft_state = attend_piece(
            start_state,
            lax.all_gather(kv_pack, "ctx", axis=1, tiled=True),
            query_low,
            positions,
            score_scale,
        )
        run_max, run_sum, weighted = soft_state
        log_total = run_max + jnp.log(run_sum)
        attended = jnp.transpose(weighted / run_sum[..., None], (0, 2, 1, 3)).astype(bf16)
        att_flat = attended.reshape(flat_rows, model_width)
        pre_act = jnp.dot(hidden_two, weight_in, preferred_element_type=f32) + bias_in.astype(f32)
        activation_f, gelu_slope = gelu_parts(pre_act)
        activation = activation_f.astype(bf16)
        output = (
            residual
            + jnp.dot(att_flat, weight_out, preferred_element_type=f32)
            + bias_out.astype(f32)
            + jnp.dot(activation, weight_mlp, preferred_element_type=f32)
            + bias_mlp.astype(f32)
        )
        output_list.append(output.reshape(seq_count, group_rows, model_width))
        params_back = gather_params()
        (
            gain_one,
            shift_one,
            gain_two,
            shift_two,
            weight_qkv,
            bias_qkv,
            weight_out,
            bias_out,
            weight_in,
            bias_in,
            weight_mlp,
            bias_mlp,
        ) = params_back
        kv_rows = lax.all_gather(kv_pack, "ctx", axis=1, tiled=True)
        cot_flat = cot_rows.reshape(flat_rows, model_width)
        cot_low = cot_flat.astype(bf16)
        cot_sum = jnp.sum(cot_flat, axis=0)
        grad_w_out = outer_rows(att_flat, cot_low)
        grad_w_mlp = outer_rows(activation, cot_low)
        d_pre = times_transpose(cot_low, weight_mlp) * gelu_slope
        d_pre_low = d_pre.astype(bf16)
        grad_w_in = outer_rows(hidden_two, d_pre_low)
        d_hidden_two = times_transpose(d_pre_low, weight_in)
        grad_att = times_transpose(cot_low, weight_out).astype(bf16).reshape(head_shape)
        row_delta = jnp.einsum("sqhd,sqhd->shq", grad_att, attended, preferred_element_type=f32)

        def back_block(block_index, loop_carry):
            grad_query, buffer = loop_carry
            offset = block_index * key_block
            kv_block = lax.dynamic_slice_in_dim(kv_rows, offset, key_block, 1)
            key_part = kv_block[..., :model_width].reshape(seq_count, key_block, HEADS, HEAD_DIM)
            value_part = kv_block[..., model_width:].reshape(seq_count, key_block, HEADS, HEAD_DIM)
            scores = (
                jnp.einsum("sqhd,skhd->shqk", query_low, key_part, preferred_element_type=f32)
                * score_scale
            )
            allowed = (offset + jnp.arange(key_block, dtype=jnp.int32))[None, :] <= positions[
                :, None
            ]
            prob_block = jnp.where(allowed, jnp.exp(scores - log_total[..., None]), 0.0)
            grad_value = jnp.einsum(
                "shqk,sqhd->skhd", prob_block.astype(bf16), grad_att, preferred_element_type=f32
            )
            grad_prob = jnp.einsum(
                "sqhd,skhd->shqk", grad_att, value_part, preferred_element_type=f32
            )
            grad_score = (prob_block * (grad_prob - row_delta[..., None]) * score_scale).astype(
                bf16
            )
            grad_query = grad_query + jnp.einsum(
                "shqk,skhd->sqhd", grad_score, key_part, preferred_element_type=f32
            )
            grad_key = jnp.einsum(
                "shqk,sqhd->skhd", grad_score, query_low, preferred_element_type=f32
            )
            key_value_grad = jnp.concatenate(
                [
                    grad_key.reshape(seq_count, key_block, model_width),
                    grad_value.reshape(seq_count, key_block, model_width),
                ],
                axis=-1,
            )
            return (grad_query, lax.dynamic_update_slice_in_dim(buffer, key_value_grad, offset, 1))

        start_carry = (
            jnp.zeros(head_shape, f32),
            jnp.zeros((seq_count, seq_len, 2 * model_width), f32),
        )
        grad_query, buffer = lax.fori_loop(0, seq_len // key_block, back_block, start_carry)
        kv_grad_own = lax.psum_scatter(
            buffer.astype(jnp.bfloat16), "ctx", scatter_dimension=1, tiled=True
        ).astype(jnp.float32)
        key_grad_raw = kv_grad_own[..., :model_width].reshape(head_shape)
        value_grad_flat = kv_grad_own[..., model_width:].reshape(flat_rows, model_width)
        grad_query = rotate(grad_query, cosine, sine_rot, -1.0)
        grad_key = rotate(key_grad_raw, cosine, sine_rot, -1.0)
        d_project = jnp.concatenate(
            [
                grad_query.reshape(flat_rows, model_width),
                grad_key.reshape(flat_rows, model_width),
                value_grad_flat,
            ],
            axis=-1,
        )
        d_project_low = d_project.astype(bf16)
        grad_w_qkv = outer_rows(hidden_one, d_project_low)
        d_hidden_one = times_transpose(d_project_low, weight_qkv)
        grad_rows = (
            cot_flat
            + norm_back(d_hidden_one, normed_one, inverse_one, gain_one.astype(f32))
            + norm_back(d_hidden_two, normed_two, inverse_two, gain_two.astype(f32))
        )
        grad_list.append(grad_rows.reshape(seq_count, group_rows, model_width))
        terms = (
            jnp.sum(d_hidden_one * normed_one, axis=0),
            jnp.sum(d_hidden_one, axis=0),
            jnp.sum(d_hidden_two * normed_two, axis=0),
            jnp.sum(d_hidden_two, axis=0),
            grad_w_qkv,
            jnp.sum(d_project, axis=0),
            grad_w_out,
            cot_sum,
            grad_w_in,
            jnp.sum(d_pre, axis=0),
            grad_w_mlp,
            cot_sum,
        )
        if weight_sums is None:
            weight_sums = terms
        else:
            weight_sums = jax.tree.map(lambda total, term: total + term, weight_sums, terms)
    owned = (
        lax.psum_scatter(weight_sums[0], ("fsdp", "ctx"), scatter_dimension=0, tiled=True),
        lax.psum_scatter(weight_sums[1], ("fsdp", "ctx"), scatter_dimension=0, tiled=True),
        lax.psum_scatter(weight_sums[2], ("fsdp", "ctx"), scatter_dimension=0, tiled=True),
        lax.psum_scatter(weight_sums[3], ("fsdp", "ctx"), scatter_dimension=0, tiled=True),
        lax.psum_scatter(weight_sums[4], ("fsdp", "ctx"), scatter_dimension=0, tiled=True),
        lax.psum_scatter(weight_sums[5], ("fsdp", "ctx"), scatter_dimension=0, tiled=True),
        lax.psum_scatter(weight_sums[6], ("fsdp", "ctx"), scatter_dimension=0, tiled=True),
        lax.psum_scatter(weight_sums[7], ("fsdp", "ctx"), scatter_dimension=0, tiled=True),
        lax.psum_scatter(weight_sums[8], ("fsdp", "ctx"), scatter_dimension=0, tiled=True),
        lax.psum_scatter(weight_sums[9], ("fsdp", "ctx"), scatter_dimension=0, tiled=True),
        lax.psum_scatter(weight_sums[10], ("fsdp", "ctx"), scatter_dimension=0, tiled=True),
        lax.psum_scatter(weight_sums[11], ("fsdp", "ctx"), scatter_dimension=0, tiled=True),
    )
    outputs = jnp.concatenate(output_list, axis=0)
    grad_inputs = jnp.concatenate(grad_list, axis=0)
    return (
        outputs,
        grad_inputs,
        owned[0],
        owned[1],
        owned[2],
        owned[3],
        owned[4],
        owned[5],
        owned[6],
        owned[7],
        owned[8],
        owned[9],
        owned[10],
        owned[11],
    )


ROWS = 128
BLOCK = 256


def swap(value, bit):
    return lax.ppermute(value, "ctx", [(i, i ^ bit) for i in range(8)])


def shift_z(value, step):
    return lax.ppermute(value, "fsdp", [(i, (i + step) % 4) for i in range(4)])


def nt(left, right):
    return lax.dot_general(
        left, right, (((1,), (1,)), ((), ())), preferred_element_type=jnp.float32
    )


def nn(left, right):
    return lax.dot_general(
        left, right, (((1,), (0,)), ((), ())), preferred_element_type=jnp.float32
    )


def tn(left, right):
    return lax.dot_general(
        left, right, (((0,), (0,)), ((), ())), preferred_element_type=jnp.float32
    )


def normalize(values):
    centred = values - jnp.mean(values, axis=-1, keepdims=True)
    inverse = lax.rsqrt(jnp.mean(centred * centred, axis=-1, keepdims=True) + EPS)
    return centred * inverse, inverse


def col_sum(values):
    return jnp.sum(values, axis=0, keepdims=True)


def piece_bits(index):
    return ((index & 1) << 2) | (index & 2) | (index >> 2)


def mlp_kernel(chunks, row_ref, *refs):
    refs = list(refs)
    parts = [[refs.pop(0) for _ in range(8)] for _ in chunks]
    weights = [refs.pop(0) for _ in range(8)]
    vecs, cot_ref, first_send, first_keep, first_norm = [refs.pop(0) for _ in range(5)]
    send_ref, keep_ref, rest_ref, norm_ref, gsend_ref, gkeep_ref, vec_ref = [refs.pop(0) for _ in range(7)]
    w_in, w_down, h_s, c_s, act_s, dpre_s, x_n, first_s, part_s, g_in, g_down, seg_s, w_sem, x_sem, p_sem, o_sem = refs
    f32, bf16 = jnp.float32, jnp.bfloat16
    gain, shift, bias = vecs[2:3, :], vecs[3:4, :], vecs[6:7, :]
    where = [(at, inside) for at, count in enumerate(chunks) for inside in range(count)]
    total = len(where)

    weight_copies = []
    for at, source in enumerate(weights):
        rows = pl.ds(pl.multiple_of(row_ref[at], 16), 96)
        for kind, target in ((0, w_in), (1, w_down)):
            weight_copies.append(
                pltpu.make_async_copy(
                    source.at[pl.ds(kind * 96, 96)], target.at[rows], w_sem.at[at * 2 + kind]
                )
            )
    part_copies = []
    for seq, (at, inside) in enumerate(where):
        for piece in range(8):
            rows = pl.ds((seq * 8 + piece) * ROWS, ROWS)
            sem = x_sem.at[(seq * 8 + piece) * 2]
            if seq == 0:
                source_rows = pl.ds(pl.multiple_of(row_ref[16 + piece], ROWS), ROWS)
                part_copies.append(pltpu.make_async_copy(first_norm.at[source_rows], x_n.at[rows], sem))
            else:
                part_copies.append(
                    pltpu.make_async_copy(parts[at][piece].at[0, inside], h_s.at[rows], sem)
                )
            part_copies.append(
                pltpu.make_async_copy(
                    parts[at][piece].at[1, inside], c_s.at[rows], x_sem.at[(seq * 8 + piece) * 2 + 1]
                )
            )
    norm_copies = [
        pltpu.make_async_copy(x_n.at[pl.ds(seq * 1024, 1024)], norm_ref.at[seq - 1], o_sem.at[total + seq])
        for seq in range(1, total)
    ]
    first_copies = [
        pltpu.make_async_copy(first_keep, first_s.at[pl.ds(0, 4)], p_sem.at[0]),
        pltpu.make_async_copy(first_send, first_s.at[pl.ds(4, 4)], p_sem.at[1]),
    ]
    out_copies = [
        pltpu.make_async_copy(part_s.at[0, pl.ds(0, 4)], keep_ref, o_sem.at[0]),
        pltpu.make_async_copy(part_s.at[0, pl.ds(4, 4)], send_ref, o_sem.at[1]),
    ] + [
        pltpu.make_async_copy(part_s.at[seq % 2], rest_ref.at[seq - 1], o_sem.at[seq + 1])
        for seq in range(1, total)
    ]
    for copy in part_copies[:16] + weight_copies + first_copies + part_copies[16:]:
        copy.start()
    vec_ref[...] = jnp.zeros_like(vec_ref)
    for seq in range(2 * total):
        vec_ref[3:4, :] += col_sum(cot_ref[seq])

    def norm_rows(first):
        for at in range(0, 256, 16):
            rows = slice(first + at, first + at + 16)
            normed, _ = normalize(h_s[rows, :].astype(f32))
            x_n[rows, :] = normed
            h_s[rows, :] = (normed * gain + shift).astype(bf16)

    for seq in range(total):
        rows = slice(seq * 1024, (seq + 1) * 1024)
        if seq == 0:
            for copy in part_copies[:16]:
                copy.wait()
            h_s[rows, :] = (x_n[rows, :] * gain + shift).astype(bf16)
            for copy in weight_copies:
                copy.wait()
        for cols in (slice(0, 512), slice(512, 768)):
            pre = nn(h_s[rows, :], w_in[:, cols]) + bias[:, cols]
            d_act = nt(c_s[rows, :], w_down[cols, :])
            cdf = 0.5 * (1.0 + lax.erf(pre * 0.7071067811865476))
            density = jnp.exp(-0.5 * pre * pre) * 0.3989422804014327
            act_s[rows, cols] = (pre * cdf).astype(bf16)
            d_pre = d_act * (cdf + pre * density)
            dpre_s[rows, cols] = d_pre.astype(bf16)
            vec_ref[0:1, cols] += col_sum(d_pre)
        if seq + 1 < total:
            for copy in part_copies[seq * 16 + 16 : seq * 16 + 32]:
                copy.wait()
        if seq == 0:
            for copy in first_copies:
                copy.wait()
        if seq == 2:
            out_copies[0].wait()
            out_copies[1].wait()
        for block in range(4):
            part_rows = slice(seq * 1024 + block * 256, seq * 1024 + (block + 1) * 256)
            out = nn(act_s[part_rows, :], w_down[...])
            d_hidden = nt(dpre_s[part_rows, :], w_in[...])
            if seq + 1 < total:
                norm_rows((seq + 1) * 1024 + block * 256)
            vec_ref[1:2, :] += col_sum(d_hidden * x_n[part_rows, :])
            vec_ref[2:3, :] += col_sum(d_hidden)
            for kind, value in ((0, out), (1, d_hidden * gain)):
                for half in range(2):
                    piece = block * 2 + half
                    part = value[half * ROWS : (half + 1) * ROWS]
                    if seq == 0:
                        part = part + first_s[piece, kind].astype(f32)
                    part_s[seq % 2, piece, kind] = part.astype(bf16)
        if seq + 1 < total:
            norm_copies[seq].start()
        if seq == 0:
            out_copies[0].start()
            out_copies[1].start()
        else:
            out_copies[seq + 1].start()

    g_in[...] = tn(h_s[...], dpre_s[...])
    g_down[...] = tn(act_s[...], c_s[...])
    for at in range(8):
        seg_s[at, :, :96] = jnp.broadcast_to(vec_ref[0:1, at * 96 : (at + 1) * 96], (16, 96))
    for half, target in ((0, gkeep_ref), (1, gsend_ref)):
        for zz in range(4):
            at = zz * 2 + (row_ref[24] ^ half)
            rows = pl.ds(pl.multiple_of(at * 96, 16), 96)
            target[zz, :96, :] = g_in[rows, :].astype(target.dtype)
            target[zz, 96:192, :] = g_down[rows, :].astype(target.dtype)
            target[zz, 192:, :] = jnp.zeros((16, 768), target.dtype)
            target[zz, 192:, :96] = seg_s[at, :, :96].astype(target.dtype)
    for copy in out_copies[2:] + norm_copies:
        copy.wait()


def whole(shape):
    return pl.BlockSpec(shape, lambda *_: (0,) * len(shape))


def mlp_call(row_offsets, parts, weights, vecs, cot, first_send, first_keep, first_norm):
    chunks = tuple(part[0].shape[1] for part in parts)
    total = sum(chunks)
    width = vecs.shape[-1]
    f32, bf16 = jnp.float32, jnp.bfloat16

    anywhere = pl.BlockSpec(memory_space=pl.ANY)
    dma = pltpu.SemaphoreType.DMA
    rows = total * 8 * ROWS
    half = (4, 2, ROWS, width)
    grads = (4, 208, width)
    return pl.pallas_call(
        functools.partial(mlp_kernel, chunks),
        grid_spec=pltpu.PrefetchScalarGridSpec(
            num_scalar_prefetch=1,
            grid=(1,),
            in_specs=[anywhere] * (8 * len(parts) + 8)
            + [whole(vecs.shape), whole(cot.shape)]
            + [anywhere] * 3,
            out_specs=[anywhere] * 4 + [whole(grads), whole(grads), whole((8, width))],
            scratch_shapes=[pltpu.VMEM((width, width), bf16)] * 2
            + [pltpu.VMEM((rows, width), bf16)] * 4
            + [pltpu.VMEM((rows, width), f32)]
            + [pltpu.VMEM((8, 2, ROWS, width), bf16), pltpu.VMEM((2, 8, 2, ROWS, width), bf16)]
            + [pltpu.VMEM((width, width), f32)] * 2
            + [pltpu.VMEM((8, 16, 128), f32)]
            + [dma((16,)), dma((total * 16,)), dma((2,)), dma((2 * total,))],
        ),
        out_shape=[
            jax.ShapeDtypeStruct(half, bf16),
            jax.ShapeDtypeStruct(half, bf16),
            jax.ShapeDtypeStruct((total - 1, 8, 2, ROWS, width), bf16),
            jax.ShapeDtypeStruct((total - 1, 8 * ROWS, width), f32),
            jax.ShapeDtypeStruct(grads, bf16),
            jax.ShapeDtypeStruct(grads, f32),
            jax.ShapeDtypeStruct((8, width), f32),
        ],
        compiler_params=pltpu.CompilerParams(vmem_limit_bytes=58 << 20),
        cost_estimate=pl.CostEstimate(
            flops=30_000_000_000, transcendentals=0, bytes_accessed=30_000_000
        ),
        name="mlp",
    )(row_offsets, *[a for part in parts for a in part], *weights, vecs, cot, first_send, first_keep, first_norm)


def rotary_tables():
    f32 = jnp.float32
    lane = lax.broadcasted_iota(jnp.int32, (32, 128), 1)
    dim = lane & 63
    power = (dim & 7).astype(f32) * (-2.0 / ROT_DIM)
    freq = jnp.where(dim < ROT_DIM, jnp.exp(power * math.log(BASE_FREQ)), 0.0)
    row = lax.broadcasted_iota(jnp.int32, (32, 128), 0).astype(f32)
    fine, coarse = row * freq, row * 32.0 * freq
    cos_fine, sin_fine = jnp.cos(fine), jnp.sin(fine)
    scale = jnp.where(lane < 64, HEAD_DIM ** (-0.5), 1.0)
    cos_coarse, sin_coarse = jnp.cos(coarse) * scale, jnp.sin(coarse) * scale
    first, second = dim[:1] < 8, (dim[:1] >= 8) & (dim[:1] < ROT_DIM)
    return cos_fine, sin_fine, cos_coarse, sin_coarse, first, second


def attn_kernel(has_prev, last, at_seq, inside, row_ref, *refs):
    refs = list(refs)
    parts = [refs.pop(0) for _ in range(8)]
    weights = [refs.pop(0) for _ in range(8)]
    o_own, o_other, vecs = [refs.pop(0) for _ in range(3)]
    if has_prev:
        partial, norm_ref, pq_ref, po_ref, pv_ref = [refs.pop(0) for _ in range(5)]
    if last:
        mv_ref, at_ref, col_ref = [refs.pop(0) for _ in range(3)]
        send_ref, keep_ref, qsend_ref, qkeep_ref, osend_ref, okeep_ref = [refs.pop(0) for _ in range(6)]
    else:
        send_ref, keep_ref, gq_ref, go_ref, vec_ref = [refs.pop(0) for _ in range(5)]
    if not has_prev:
        norm_out_ref = refs.pop(0)
    wq, wo, x_s, c_s, x_n, h_s = [refs.pop(0) for _ in range(6)]
    q_s, k_s, v_s, g_s, kt_s, vt_s, gt_s = [refs.pop(0) for _ in range(7)]
    dq_s, dk_s, dv_s, at_s, att_s, dp_s, res_s, tab = [refs.pop(0) for _ in range(8)]
    w_sem, x_sem, r_sem = [refs.pop(0) for _ in range(3)]
    if has_prev:
        pp_s, pq_s, po_s, p_sem = [refs.pop(0) for _ in range(4)]
    f32, bf16 = jnp.float32, jnp.bfloat16
    seq = 8 * ROWS
    blocks = seq // BLOCK
    gain, shift, bias = vecs[0:1, :], vecs[1:2, :], vecs[5:6, :640]

    def place(piece):
        return pl.ds(pl.multiple_of(row_ref[16 + piece], ROWS), ROWS)

    weight_copies = [
        pltpu.make_async_copy(
            source,
            wq.at[pl.ds(pl.multiple_of(row_ref[at], 16), 96)],
            w_sem.at[at],
        )
        for at, source in enumerate(weights)
    ]
    out_weight_copies = [
        pltpu.make_async_copy(
            source, wo.at[pl.ds(pl.multiple_of(row_ref[8 + at], 16), 96)], w_sem.at[8 + at]
        )
        for at, source in enumerate((o_own, o_other))
    ]
    part_copies = [
        [
            pltpu.make_async_copy(
                parts[piece].at[kind, inside], target.at[place(piece)], x_sem.at[kind * 8 + piece]
            )
            for piece in range(8)
        ]
        for kind, target in (((1, c_s),) if has_prev else ((0, x_s), (1, c_s)))
    ]
    if has_prev:
        norm_part_copies = [
            pltpu.make_async_copy(
                norm_ref.at[at_seq - 1, pl.ds(piece * ROWS, ROWS)], x_n.at[place(piece)], x_sem.at[piece]
            )
            for piece in range(8)
        ]
        part_copies.insert(0, norm_part_copies)
    for copy in part_copies[0] + weight_copies + part_copies[1] + out_weight_copies:
        copy.start()
    if has_prev:
        prev_copies = [
            pltpu.make_async_copy(
                partial.at[at_seq - 1, piece, kind], pp_s.at[kind, place(piece)], p_sem.at[kind * 8 + piece]
            )
            for piece in range(8)
            for kind in range(2)
        ]
        prev_copies.append(pltpu.make_async_copy(pq_ref, pq_s, p_sem.at[16]))
        prev_copies.append(pltpu.make_async_copy(po_ref, po_s, p_sem.at[17]))
        for copy in prev_copies:
            copy.start()

    wo[192:, :] = jnp.zeros((64, 768), bf16)
    cos_f, sin_f, cos_c, sin_c, first, second = rotary_tables()
    for at in range(seq // 32):
        rows = slice(at * 32, (at + 1) * 32)
        cosine = cos_f * cos_c[at : at + 1] - sin_f * sin_c[at : at + 1]
        sine = sin_f * cos_c[at : at + 1] + cos_f * sin_c[at : at + 1]
        tab[0, rows, :] = cosine
        tab[1, rows, :] = jnp.where(first, -sine, 0.0)
        tab[2, rows, :] = jnp.where(second, sine, 0.0)

    lane = lax.broadcasted_iota(jnp.int32, (256, 128), 1)
    left = lane < 64

    def heads_of(block, project, grad):
        rows = slice(block * 256, (block + 1) * 256)
        cosine, low, high = tab[0, rows, :], tab[1, rows, :], tab[2, rows, :]
        for head in range(3):
            pair = project[:, head * 128 : (head + 1) * 128]
            pair = pair * cosine + pltpu.roll(pair, 120, 1) * low + pltpu.roll(pair, 8, 1) * high
            k_s[head, rows, :] = jnp.where(left, 0.0, pair).astype(bf16)
            q_s[head, rows, :] = jnp.where(left, 0.0, pltpu.roll(pair, 64, 1)).astype(bf16)
            kt_s[head, :, rows] = jnp.transpose(pair)[64:].astype(bf16)
        v_pair, v_last = project[:, 384:512], jnp.where(left, project[:, 512:640], 0.0)
        vt_s[:128, rows] = jnp.transpose(v_pair).astype(bf16)
        vt_s[128:, rows] = jnp.transpose(v_last)[:64].astype(bf16)
        for target, pair_value, last_value in ((v_s, v_pair, v_last), (g_s, grad[:, :128], grad[:, 128:])):
            target[0, rows, :] = jnp.where(left, pair_value, 0.0).astype(bf16)
            target[1, rows, :] = jnp.where(left, 0.0, pair_value).astype(bf16)
            target[2, rows, :] = last_value.astype(bf16)

    for copy in part_copies[0] + weight_copies + part_copies[1] + out_weight_copies:
        copy.wait()
    for block in (1, 3):
        wide = slice((block - 1) * 256, (block + 1) * 256)
        if has_prev:
            h_s[wide, :] = (x_n[wide, :] * gain + shift).astype(bf16)
        else:
            for part in range(32):
                rows = slice((block - 1) * 256 + part * 16, (block - 1) * 256 + (part + 1) * 16)
                normed, _ = normalize(x_s[rows, :].astype(f32))
                x_n[rows, :] = normed
                h_s[rows, :] = (normed * gain + shift).astype(bf16)
        project_wide = nn(h_s[wide, :], wq[...]) + bias
        grad_wide = nt(c_s[wide, :], wo[...])
        gt_s[:, wide] = nt(wo[:192, :], c_s[wide, :]).astype(bf16)
        for half in range(2):
            heads_of(block - 1 + half, project_wide[half * 256 : half * 256 + 256], grad_wide[half * 256 : half * 256 + 256])

    allowed = lax.broadcasted_iota(jnp.int32, (BLOCK, BLOCK), 0) <= lax.broadcasted_iota(
        jnp.int32, (BLOCK, BLOCK), 1
    )

    def rows_of(block):
        return slice(block * BLOCK, (block + 1) * BLOCK)

    def scores_of(head, block):
        query, grad = q_s[head, rows_of(block), :], g_s[head, rows_of(block), :]
        upto = (block + 1) * BLOCK
        scores = nt(k_s[head, :upto, :], query)
        scores = [scores[rows_of(at)] for at in range(block + 1)]
        scores[block] = jnp.where(allowed, scores[block], -1e30)
        d_prob = nt(v_s[head, :upto, :], grad)
        return scores, [d_prob[rows_of(at)] for at in range(block + 1)]

    def softmax_of(scores):
        top = jnp.max(scores[0], axis=0, keepdims=True)
        for part in scores[1:]:
            top = jnp.maximum(top, jnp.max(part, axis=0, keepdims=True))
        probs = [jnp.exp(part - top) for part in scores]
        total = col_sum(probs[0])
        for part in probs[1:]:
            total = total + col_sum(part)
        scale = 1.0 / total
        probs = [part * scale for part in probs]
        return probs, [part.astype(bf16) for part in probs]

    def values_of(head, block, probs, lows, d_prob):
        rows, upto = rows_of(block), (block + 1) * BLOCK
        low = jnp.concatenate(lows, axis=0) if block else lows[0]
        att_t = nn(vt_s[head * 64 : (head + 1) * 64, :upto], low)
        att_low = att_t.astype(bf16)
        att_s[head * 64 : (head + 1) * 64, rows] = att_low
        d_value = nn(low, g_s[head, rows, :])
        into = head // 2
        keep = slice(0, upto if head == 1 else upto - BLOCK)
        if keep.stop:
            dv_s[into, keep, :] += d_value[keep]
        if head != 1:
            dv_s[into, rows, :] = d_value[upto - BLOCK :]
        delta = col_sum(gt_s[head * 64 : (head + 1) * 64, rows].astype(f32) * att_low.astype(f32))
        return [(p * (d - delta)).astype(bf16) for p, d in zip(probs, d_prob)]

    def grads_of(head, block, d_scores):
        rows, upto = rows_of(block), (block + 1) * BLOCK
        d_score = jnp.concatenate(d_scores, axis=0) if block else d_scores[0]
        d_key = nn(d_score, q_s[head, rows, :])
        if block:
            dk_s[head, : upto - BLOCK, :] += d_key[: upto - BLOCK]
        dk_s[head, rows, :] = d_key[upto - BLOCK :]
        dq_s[head, rows, :64] = jnp.transpose(nn(kt_s[head, :, :upto], d_score))

    order = [(head, block) for block in range(blocks) for head in range(3)]
    ahead = scores_of(*order[0])
    waiting = None
    for at, (head, block) in enumerate(order):
        scores, d_prob = ahead
        if at + 1 < len(order):
            ahead = scores_of(*order[at + 1])
        probs, lows = softmax_of(scores)
        if waiting is not None:
            grads_of(*waiting)
        waiting = (head, block, values_of(head, block, probs, lows, d_prob))
    grads_of(*waiting)

    project_sums = []
    for head in range(3):
        total = jnp.zeros((1, 128), f32)
        for block in range(4):
            rows = slice(block * 256, (block + 1) * 256)
            pair = jnp.concatenate([dq_s[head, rows, :64], dk_s[head, rows, 64:]], axis=1)
            cosine, low, high = tab[0, rows, :], tab[1, rows, :], tab[2, rows, :]
            pair = pair * cosine - pltpu.roll(pair, 120, 1) * low - pltpu.roll(pair, 8, 1) * high
            total = total + col_sum(pair)
            dp_s[rows, head * 128 : (head + 1) * 128] = pair.astype(bf16)
        project_sums.append(total)
    for into in range(2):
        dp_s[:, 384 + into * 128 : 512 + into * 128] = dv_s[into].astype(bf16)
        project_sums.append(col_sum(dv_s[into]))
    if has_prev:
        for copy in prev_copies:
            copy.wait()
    for block in range(4):
        rows = slice(block * 256, (block + 1) * 256)
        at_s[rows, :128] = jnp.transpose(att_s[:128, rows].astype(f32)).astype(bf16)
        at_s[rows, 128:] = jnp.concatenate(
            [jnp.transpose(att_s[128:, rows].astype(f32)), jnp.zeros((256, 64), f32)], axis=1
        ).astype(bf16)
    out = nn(at_s[...], wo[...])
    d_hidden = nt(dp_s[...], wq[...])
    s = d_hidden * gain
    if has_prev:
        out = out + pp_s[0].astype(f32)
        s = s + pp_s[1].astype(f32)
    res_s[0] = out.astype(bf16)
    res_s[1] = s.astype(bf16)
    sums = [
        jnp.concatenate(project_sums, axis=1),
        col_sum(d_hidden * x_n[...]),
        col_sum(d_hidden),
    ]
    result_copies = [
        pltpu.make_async_copy(
            res_s.at[kind, place(piece)],
            (keep_ref if piece < 4 else send_ref).at[piece % 4, kind],
            r_sem.at[piece * 2 + kind],
        )
        for piece in (4, 5, 6, 7, 0, 1, 2, 3)
        for kind in range(2)
    ]
    if not has_prev:
        result_copies.append(pltpu.make_async_copy(x_n, norm_out_ref, r_sem.at[16]))
    for copy in result_copies:
        copy.start()
    g_query = tn(h_s[...], dp_s[...])
    g_out = nn(att_s[...], c_s[...])
    if has_prev:
        g_query = g_query + pq_s[...]
        g_out = g_out + po_s[...]
        sums = [sums[0] + pv_ref[0:1, :640], sums[1] + pv_ref[1:2, :], sums[2] + pv_ref[2:3, :]]
    if last:
        gq_s, go_s, tr_s = refs
        gq_s[...] = g_query
        go_s[...] = g_out
        tr_s[...] = jnp.zeros_like(tr_s)
        tr_s[64:65, :] = sums[1]
        tr_s[65:66, :] = sums[2]
        tr_s[66:69, :] = mv_ref[1:4, :]
        columns = jnp.transpose(tr_s[...])
        lanes = lax.broadcasted_iota(jnp.int32, (768, 128), 1)
        target_at = col_ref[0:1, :576] + row_ref[25] * 192
        for third in range(3):
            hit = at_ref[:, third : third + 1] == target_at
            column = jnp.sum(jnp.where(hit, sums[0][:, :576], 0.0), axis=1, keepdims=True)
            columns = jnp.where(lanes == 69 + third, column, columns)
        gq_s[:, 512:640] = jnp.where(lanes < 64, gq_s[:, 512:640], columns)
        for half, target in ((0, qkeep_ref), (1, qsend_ref)):
            for zz in range(4):
                at = zz * 2 + (row_ref[24] ^ half)
                rows = pl.ds(pl.multiple_of(at * 96, 16), 96)
                target[zz] = gq_s[rows, :].astype(target.dtype)
        for half, target in ((0, okeep_ref), (1, osend_ref)):
            rows = pl.ds(pl.multiple_of((row_ref[24] ^ half) * 96, 16), 96)
            target[...] = go_s[rows, :].astype(target.dtype)
    else:
        gq_ref[...] = g_query
        go_ref[...] = g_out
        vec_ref[...] = jnp.zeros_like(vec_ref)
        vec_ref[0:1, :640] = sums[0]
        vec_ref[1:2, :] = sums[1]
        vec_ref[2:3, :] = sums[2]
    for copy in result_copies:
        copy.wait()


def attn_call(row_offsets, parts, inside, weights, o_own, o_other, vecs, partial, seq, prev, tail):
    width = vecs.shape[-1]
    f32, bf16 = jnp.float32, jnp.bfloat16
    anywhere = pl.BlockSpec(memory_space=pl.ANY)
    dma = pltpu.SemaphoreType.DMA
    has_prev, last = prev is not None, tail is not None
    rows = 8 * ROWS
    half = (4, 2, ROWS, width)
    shapes = [(half, bf16), (half, bf16)]
    if last:
        shapes += [((4, 96, 640), bf16), ((4, 96, 640), f32), ((96, width), bf16), ((96, width), f32)]
    else:
        shapes += [((width, 640), f32), ((192, width), f32), ((8, width), f32)]
    out_specs = [anywhere] * 2 + [whole(shape) for shape, _ in shapes[2:]]
    if not has_prev:
        shapes.append(((rows, width), f32))
        out_specs.append(anywhere)
    operands = [*parts, *weights, o_own, o_other, vecs]
    in_specs = [anywhere] * 18 + [whole(vecs.shape)]
    scratch = [
        pltpu.VMEM((width, 640), bf16),
        pltpu.VMEM((256, width), bf16),
        pltpu.VMEM((rows, width), bf16),
        pltpu.VMEM((rows, width), bf16),
        pltpu.VMEM((rows, width), f32),
        pltpu.VMEM((rows, width), bf16),
    ]
    scratch += [pltpu.VMEM((3, rows, 128), bf16)] * 4
    scratch += [
        pltpu.VMEM((3, 64, rows), bf16),
        pltpu.VMEM((192, rows), bf16),
        pltpu.VMEM((192, rows), bf16),
        pltpu.VMEM((3, rows, 128), f32),
        pltpu.VMEM((3, rows, 128), f32),
        pltpu.VMEM((2, rows, 128), f32),
        pltpu.VMEM((rows, 256), bf16),
        pltpu.VMEM((192, rows), bf16),
        pltpu.VMEM((rows, 640), bf16),
        pltpu.VMEM((2, rows, width), bf16),
        pltpu.VMEM((3, rows, 128), f32),
        dma((10,)),
        dma((16,)),
        dma((17,)),
    ]
    if has_prev:
        operands += [*partial, *prev]
        in_specs += [anywhere] * 4 + [whole(prev[2].shape)]
        scratch += [
            pltpu.VMEM((2, rows, width), bf16),
            pltpu.VMEM((width, 640), f32),
            pltpu.VMEM((192, width), f32),
            dma((18,)),
        ]
    if last:
        operands += list(tail)
        in_specs += [whole(a.shape) for a in tail]
        scratch += [pltpu.VMEM((width, 640), f32), pltpu.VMEM((192, width), f32), pltpu.VMEM((128, width), f32)]
    return pl.pallas_call(
        functools.partial(attn_kernel, has_prev, last, seq, inside),
        grid_spec=pltpu.PrefetchScalarGridSpec(
            num_scalar_prefetch=1,
            grid=(1,),
            in_specs=in_specs,
            out_specs=out_specs,
            scratch_shapes=scratch,
        ),
        out_shape=[jax.ShapeDtypeStruct(shape, kind) for shape, kind in shapes],
        compiler_params=pltpu.CompilerParams(vmem_limit_bytes=58 << 20),
        cost_estimate=pl.CostEstimate(
            flops=24_000_000_000, transcendentals=0, bytes_accessed=15_000_000
        ),
        name="attn",
    )(row_offsets, *operands)


def finish_kernel(half_ref, x_ref, c_ref, *refs):
    refs = list(refs)
    terms = [[refs.pop(0) for _ in range(4)] for _ in range(3)]
    bias, out_ref, grad_ref = refs
    f32 = jnp.float32

    def write(seq, sources):
        total = [source[0].astype(f32) for source in sources]
        total = sum(total[1:], total[0])
        x = x_ref[seq].astype(f32)
        normed, inverse = normalize(x)
        out_ref[seq] = x + bias[4:5, :] + total[0]
        s = total[1]
        mean_s = jnp.mean(s, axis=-1, keepdims=True)
        mean_sn = jnp.mean(s * normed, axis=-1, keepdims=True)
        grad_ref[seq] = c_ref[seq] + inverse * (s - mean_s - normed * mean_sn)

    @pl.when(pl.program_id(0) == 0)
    def _():
        for seq in range(3):
            write(seq, terms[seq][:3])

    @pl.when(pl.program_id(0) == 1)
    def _():
        for seq in range(3):
            write(seq, terms[seq][3:])


def finish_call(half, x, cot, terms, bias):
    _, rows, width = x.shape
    f32 = jnp.float32
    seq_spec = pl.BlockSpec((3, rows, width), lambda i, at: (jnp.where(i == 0, at[0], 1 - at[0]), 0, 0))
    part_spec = pl.BlockSpec((1, 2, rows, width), lambda i, at: (0, 0, 0, 0))
    operands = [x, cot, *[a for parts in terms for a in parts], bias]
    return pl.pallas_call(
        finish_kernel,
        grid_spec=pltpu.PrefetchScalarGridSpec(
            num_scalar_prefetch=1,
            grid=(2,),
            in_specs=[seq_spec, seq_spec] + [part_spec] * 12 + [whole(bias.shape)],
            out_specs=[seq_spec, seq_spec],
        ),
        out_shape=[jax.ShapeDtypeStruct(x.shape, f32)] * 2,
        name="finish",
    )(half, *operands)


def pick(value, index, axis=0):
    return lax.dynamic_index_in_dim(value, index, axis, keepdims=False)


def prep_kernel(at_ref, in_ref, q_ref, small_ref, own_ref, send_ref, pack_s):
    for h in range(4):
        parts = [in_ref[:, zy * 384 + h * 96 : zy * 384 + (h + 1) * 96] for zy in range(8)]
        for head in range(3):
            for kind in range(2):
                first = kind * 768 + h * 192 + head * 64
                parts.append(q_ref[:, first : first + 64])
        first = 1536 + h * 192
        parts.append(q_ref[:, first : first + 192])
        parts.append(small_ref[...])
        at = 0
        for part in parts:
            pack_s[h, :, at : at + part.shape[1]] = part
            at += part.shape[1]
    for core in range(2):
        own_ref[core] = pack_s[at_ref[26] * 2 + core]
        send_ref[core] = pack_s[(1 - at_ref[26]) * 2 + core]


def prep_call(row_offsets, w_in, w_qkv, small):
    half = jax.ShapeDtypeStruct((2, 24, 1408), jnp.bfloat16)
    return pl.pallas_call(
        prep_kernel,
        grid_spec=pltpu.PrefetchScalarGridSpec(
            num_scalar_prefetch=1,
            grid=(1,),
            in_specs=[whole(a.shape) for a in (w_in, w_qkv, small)],
            out_specs=[whole(half.shape)] * 2,
            scratch_shapes=[pltpu.VMEM((4, 24, 1408), jnp.bfloat16)],
        ),
        out_shape=[half, half],
        name="prep",
    )(row_offsets, w_in, w_qkv, small)


def join_kernel(at_ref, own_ref, got_ref, far_ref, down_ref, attn_ref, mlp_ref, four, rows_s):
    f32, bf16 = jnp.float32, jnp.bfloat16
    x, c = at_ref[26], at_ref[27]
    four[0] = own_ref[c].astype(f32)
    four[1] = got_ref[c].astype(f32)
    four[2] = far_ref[0].astype(f32)
    four[3] = far_ref[1].astype(f32)
    for source in range(4):
        near = ((source & 1) ^ c) * 2 + ((source >> 1) ^ x)
        rows_s[source * 24 : (source + 1) * 24, :] = four[near]
    mlp_ref[:96, :] = rows_s[:, :768].astype(bf16)
    mlp_ref[96:, :] = down_ref[...]
    attn_ref[...] = rows_s[:, 768:].astype(bf16)


def join_call(row_offsets, own, got, far, w_down):
    f32, bf16 = jnp.float32, jnp.bfloat16
    outs = [jax.ShapeDtypeStruct((96, 640), bf16), jax.ShapeDtypeStruct((192, 768), bf16)]
    return pl.pallas_call(
        join_kernel,
        grid_spec=pltpu.PrefetchScalarGridSpec(
            num_scalar_prefetch=1,
            grid=(1,),
            in_specs=[whole(a.shape) for a in (own, got, far, w_down)],
            out_specs=[whole(a.shape) for a in outs],
            scratch_shapes=[pltpu.VMEM((4, 24, 1408), f32), pltpu.VMEM((96, 1408), f32)],
        ),
        out_shape=outs,
        name="join",
    )(row_offsets, own, got, far, w_down)


def pick_out_kernel(at_ref, one, two, three, four, own_ref, send_ref, all_s):
    for at, source in enumerate((one, two, three, four)):
        all_s[at] = source[...]
    for core in range(2):
        own_ref[core] = all_s[(at_ref[28] - at_ref[26] * 2 - core + 4) % 4]
        send_ref[core] = all_s[(at_ref[28] - (1 - at_ref[26]) * 2 - core + 4) % 4]


def pick_out_call(row_offsets, pieces):
    half = jax.ShapeDtypeStruct((2, 24, 768), jnp.bfloat16)
    return pl.pallas_call(
        pick_out_kernel,
        grid_spec=pltpu.PrefetchScalarGridSpec(
            num_scalar_prefetch=1,
            grid=(1,),
            in_specs=[whole((24, 768))] * 4,
            out_specs=[whole(half.shape)] * 2,
            scratch_shapes=[pltpu.VMEM((4, 24, 768), jnp.bfloat16)],
        ),
        out_shape=[half, half],
        name="out_pick",
    )(row_offsets, *pieces)


def join_out_kernel(at_ref, own_ref, got_ref, far_ref, out_ref, four, rows_s):
    f32, bf16 = jnp.float32, jnp.bfloat16
    x, c = at_ref[26], at_ref[27]
    four[0] = own_ref[c].astype(f32)
    four[1] = got_ref[c].astype(f32)
    four[2] = far_ref[0].astype(f32)
    four[3] = far_ref[1].astype(f32)
    for source in range(4):
        near = ((source & 1) ^ c) * 2 + ((source >> 1) ^ x)
        rows_s[source * 24 : (source + 1) * 24, :] = four[near]
    out_ref[...] = rows_s[...].astype(bf16)


def join_out_call(row_offsets, own, got, far):
    f32, bf16 = jnp.float32, jnp.bfloat16
    return pl.pallas_call(
        join_out_kernel,
        grid_spec=pltpu.PrefetchScalarGridSpec(
            num_scalar_prefetch=1,
            grid=(1,),
            in_specs=[whole(a.shape) for a in (own, got, far)],
            out_specs=whole((96, 768)),
            scratch_shapes=[pltpu.VMEM((4, 24, 768), f32), pltpu.VMEM((96, 768), f32)],
        ),
        out_shape=jax.ShapeDtypeStruct((96, 768), bf16),
        name="join_out",
    )(row_offsets, own, got, far)


def vector_tables():
    row = np.arange(768)
    at_q = np.stack([(row // 24) * 72 + third * 24 + row % 24 for third in range(3)], axis=1)
    at_in = np.stack([(row // 24) * 96 + third * 24 + row % 24 for third in range(4)], axis=1)
    lane = np.arange(576)
    head, kind = lane // 128, (lane % 128) // 64
    col_q = np.where(lane < 384, kind * 768 + head * 64 + lane % 64, 1536 + lane - 384)
    col_in = (row // 96) * 384 + row % 96
    cols = np.zeros((8, 768), np.int32)
    cols[0, :576] = col_q
    cols[1] = col_in
    rows = np.concatenate([at_q, at_in, np.zeros((768, 1))], axis=1).astype(np.int32)
    return rows, cols


def vec_kernel(at_ref, *refs):
    refs = list(refs)
    pieces = [refs.pop(0) for _ in range(8)]
    rows_ref, cols_ref, out_ref, all_s = refs
    f32 = jnp.float32
    for at, source in enumerate(pieces):
        rows = pl.ds(pl.multiple_of(at_ref[at], 16), 96)
        all_s[rows, :] = source[...].astype(f32)
    flipped = jnp.transpose(all_s[...])
    out_ref[0:4, :] = flipped[64:68]
    out_ref[4:5, :] = flipped[68:69] + flipped[69:70]
    for row, kinds, target, width, step in ((5, (0, 1, 2), 0, 576, 192), (6, (3, 4, 5, 6), 1, 768, 96)):
        wanted = cols_ref[target : target + 1, :width] + at_ref[25] * step
        total = jnp.zeros((1, width), f32)
        for kind in kinds:
            hit = rows_ref[:, kind : kind + 1] == wanted
            total += col_sum(jnp.where(hit, all_s[:, 70 + kind : 71 + kind], 0.0))
        out_ref[row : row + 1, :width] = total
    out_ref[7:8, :] = jnp.zeros((1, 768), f32)
    out_ref[5:6, 576:] = jnp.zeros((1, 192), f32)


def vec_call(row_offsets, pieces, rows, cols):
    f32 = jnp.float32
    return pl.pallas_call(
        vec_kernel,
        grid_spec=pltpu.PrefetchScalarGridSpec(
            num_scalar_prefetch=1,
            grid=(1,),
            in_specs=[pl.BlockSpec((96, 128), lambda i, *_: (0, 4))] * 8
            + [whole(rows.shape), whole(cols.shape)],
            out_specs=whole((8, 768)),
            scratch_shapes=[pltpu.VMEM((768, 128), f32)],
        ),
        out_shape=jax.ShapeDtypeStruct((8, 768), f32),
        name="vectors",
    )(row_offsets, *pieces, rows, cols)


def spread_kernel(at_ref, q_mine, q_far, in_mine, in_far, q_ref, in_ref, *refs):
    f32 = jnp.float32
    out_refs, (q_four, in_four) = refs[:6], refs[6:]
    x, c = at_ref[26], at_ref[27]
    for four, near, far in ((q_four, q_mine, q_far), (in_four, in_mine, in_far)):
        for side in range(2):
            four[side] = near[side]
            four[2 + side] = far[side]
    total = None
    for h in range(4):
        near = ((h & 1) ^ c) * 2 + ((h >> 1) ^ x)
        block = in_four[near].astype(f32)
        for zy in range(8):
            first = zy * 384 + h * 96
            in_ref[:, first : first + 96] = block[:, zy * 96 : (zy + 1) * 96]
        block = q_four[near].astype(f32)
        for head in range(3):
            for kind in range(2):
                first = kind * 768 + h * 192 + head * 64
                at = head * 128 + kind * 64
                q_ref[:, first : first + 64] = block[:, at : at + 64]
        first = 1536 + h * 192
        q_ref[:, first : first + 192] = block[:, 384:576]
        part = block[:, 576:584]
        total = part if total is None else total + part
    same = lax.broadcasted_iota(jnp.int32, (24, 24), 0) == lax.broadcasted_iota(jnp.int32, (24, 24), 1)
    rows = [col_sum(jnp.where(same, total[:, t : t + 1], 0.0)) for t in range(8)]
    for t in range(5):
        out_refs[t][...] = rows[t]
    out_refs[5][...] = jnp.concatenate(rows[5:], axis=1)


def spread_call(row_offsets, q_pair, in_pair):
    f32, bf16 = jnp.float32, jnp.bfloat16
    shapes = [(24, 2304), (24, 3072)] + [(1, 24)] * 5 + [(1, 72)]
    operands = [*q_pair, *in_pair]
    return pl.pallas_call(
        spread_kernel,
        grid_spec=pltpu.PrefetchScalarGridSpec(
            num_scalar_prefetch=1,
            grid=(1,),
            in_specs=[whole(a.shape) for a in operands],
            out_specs=[whole(shape) for shape in shapes],
            scratch_shapes=[pltpu.VMEM((4, 24, 640), bf16), pltpu.VMEM((4, 24, 768), bf16)],
        ),
        out_shape=[jax.ShapeDtypeStruct(shape, f32) for shape in shapes],
        name="spread",
    )(row_offsets, *operands)


def exchange_four(blocks, x, c):
    blocks = blocks.reshape((2, 2) + blocks.shape[1:])
    own = pick(blocks, x)
    got = swap(pick(blocks, 1 - x), 2)
    both = jnp.stack([own, got])
    mine = pick(both, c, 1)
    send = pick(both, 1 - c, 1)
    return mine, swap(send, 1)


def fast(*args):
    return fast_body(*args)


def fast_body(
    inputs, cotangent, ln1_gain, ln1_bias, ln2_gain, ln2_bias, w_qkv, b_qkv, w_out, b_out, w_in, b_in, w_mlp_out, b_mlp_out
):
    f32, bf16 = jnp.float32, jnp.bfloat16
    z = lax.axis_index("fsdp")
    ctx = lax.axis_index("ctx")
    y, x, c = ctx // 4, (ctx // 2) % 2, ctx % 2
    h = ctx % 4

    zs = jnp.stack([(z - k) % 4 for k in range(4)])
    rows_w = jnp.concatenate([(zs * 2 + y) * 96, (zs * 2 + 1 - y) * 96])
    rows_o = jnp.stack([y * 96, (1 - y) * 96])
    rows_p = jnp.stack([(ctx ^ piece_bits(k)) * ROWS for k in range(8)])
    row_offsets = jnp.concatenate(
        [rows_w, rows_o, jnp.zeros((6,), jnp.int32), rows_p, jnp.stack([y, h, x, c, z])]
    ).astype(jnp.int32)

    small = jnp.concatenate(
        [ln1_gain, ln1_bias, ln2_gain, ln2_bias, b_out, b_mlp_out, b_qkv, b_in, jnp.zeros((51 * 24,), bf16)]
    ).reshape(64, 24).T
    pack_own, pack_send = prep_call(row_offsets, w_in, w_qkv, small)

    def rows_of(half, first, count):
        at = half * 3 + first
        return jnp.stack(
            [
                lax.dynamic_slice_in_dim(inputs, at, count),
                lax.dynamic_slice_in_dim(cotangent, at, count).astype(bf16),
            ]
        )

    parts = []
    first = 0
    for count in CHUNKS:
        got = swap(rows_of(1 - y, first, count), 4)
        own = rows_of(y, first, count)
        side, side_got = swap(own, 2), swap(got, 2)
        near = (own, got, side, side_got)
        parts.append(near + tuple(swap(a, 1) for a in near))
        first += count

    pack_got = swap(pack_send, 2)
    pack_far = swap(jnp.stack([pick(pack_own, 1 - c), pick(pack_got, 1 - c)]), 1)
    out_all = [w_out] + [shift_z(w_out, k) for k in (1, 2, 3)]
    attn_w, mlp_w = join_call(row_offsets, pack_own, pack_got, pack_far, w_mlp_out)
    attn_own = [attn_w] + [shift_z(attn_w, k) for k in (1, 2, 3)]
    mlp_own = [mlp_w] + [shift_z(mlp_w, k) for k in (1, 2, 3)]
    attn_all = attn_own + [swap(part, 4) for part in attn_own]
    mlp_all = mlp_own + [swap(part, 4) for part in mlp_own]
    out_mine, out_send = pick_out_call(row_offsets, out_all)
    out_got = swap(out_send, 2)
    out_far = swap(jnp.stack([pick(out_mine, 1 - c), pick(out_got, 1 - c)]), 1)
    out_own = join_out_call(row_offsets, out_mine, out_got, out_far)
    out_other = swap(out_own, 4)
    at_rows, at_cols = vector_tables()
    vecs = vec_call(row_offsets, attn_all, at_rows, at_cols)

    where = [(at, inside) for at, count in enumerate(CHUNKS) for inside in range(count)]

    def attention(seq, partial, prev, tail=None):
        at, inside = where[seq]
        return attn_call(
            row_offsets, parts[at], inside, attn_all, out_own, out_other,
            vecs, partial, seq, prev, tail,
        )

    def reduce_z(blocks, place=lambda at: at):
        def total(at):
            at = place(at)
            value = pick(blocks[0], at).astype(f32)
            for block in blocks[1:]:
                value = value + pick(block, at).astype(f32)
            return value

        low = [total((z + k) % 4).astype(bf16) for k in (1, 2, 3)]
        sent = [shift_z(part, k + 1) for k, part in enumerate(low)]
        result = total(z)
        for part in sent:
            result = result + part.astype(f32)
        return result

    half = jnp.reshape(y, (1,)).astype(jnp.int32)

    def scatter(send, keep):
        got = swap(send, 1)
        side = swap((keep[2:].astype(f32) + got[2:].astype(f32)).astype(bf16), 2)
        far = (keep[1:2].astype(f32) + got[1:2].astype(f32) + side[1:2].astype(f32)).astype(bf16)
        return keep, got, side, swap(far, 4)

    first_send, first_keep, g_q, g_o, vec, first_norm = attention(0, None, None)
    prev = (g_q, g_o, vec)
    send, keep, rest_part, rest_norm, g_send, g_keep, mlp_vec = mlp_call(
        row_offsets, parts, mlp_all, vecs, cotangent, first_send, first_keep, first_norm
    )
    g_got = swap(g_send, 4)
    terms = [scatter(send, keep)]
    send, keep, g_q, g_o, vec = attention(1, (rest_part, rest_norm), prev)
    terms.append(scatter(send, keep))
    mlp_grad = reduce_z((g_keep, g_got))
    grad_w_mlp = mlp_grad[96:192]
    grad_b_in = mlp_grad[192, :96]
    in_pair = exchange_four(mlp_grad[:96].astype(bf16).reshape(4, 24, 768), x, c)
    send, keep, q_send, q_keep, o_send, o_keep = attention(
        2, (rest_part, rest_norm), (g_q, g_o, vec), (mlp_vec, at_rows, at_cols)
    )
    terms.append(scatter(send, keep))
    done = finish_call(half, inputs, cotangent, terms, vecs)
    q_grad = reduce_z((q_keep, swap(q_send, 4)))
    q_low = q_grad.astype(bf16).reshape(4, 24, 640)
    q_pair = exchange_four(q_low, x, c)
    grad_w_qkv, grad_w_in, *spread = spread_call(row_offsets, q_pair, in_pair)
    one_gain, one_bias, two_gain, two_bias, grad_bias, grad_bq = [v.reshape(-1) for v in spread]

    o_parts = o_keep + swap(o_send, 4).astype(f32)
    o_low = o_parts.astype(bf16).reshape(4, 24, 768)
    o_blocks = jnp.concatenate(exchange_four(o_low, x, c))
    grad_w_out = reduce_z((o_blocks,), lambda at: ((at & 1) ^ c) * 2 + ((at >> 1) ^ x))

    outputs, grad_inputs = done
    return (
        outputs,
        grad_inputs,
        one_gain,
        one_bias,
        two_gain,
        two_bias,
        grad_w_qkv,
        grad_bq,
        grad_w_out,
        grad_bias,
        grad_w_in,
        grad_b_in,
        grad_w_mlp,
        grad_bias,
    )


def fast_fits(mesh):
    sizes = dict(mesh.shape)
    return sizes["fsdp"] == 4 and sizes["ctx"] == 8


def solution(mesh):
    return jax.shard_map(
        fast if fast_fits(mesh) else local,
        mesh=mesh,
        in_specs=(
            P("fsdp", "ctx", None),
            P("fsdp", "ctx", None),
            P(("fsdp", "ctx")),
            P(("fsdp", "ctx")),
            P(("fsdp", "ctx")),
            P(("fsdp", "ctx")),
            P(("fsdp", "ctx"), None),
            P(("fsdp", "ctx")),
            P(("fsdp", "ctx"), None),
            P(("fsdp", "ctx")),
            P(("fsdp", "ctx"), None),
            P(("fsdp", "ctx")),
            P(("fsdp", "ctx"), None),
            P(("fsdp", "ctx")),
        ),
        out_specs=(
            P("fsdp", "ctx", None),
            P("fsdp", "ctx", None),
            P(("fsdp", "ctx")),
            P(("fsdp", "ctx")),
            P(("fsdp", "ctx")),
            P(("fsdp", "ctx")),
            P(("fsdp", "ctx"), None),
            P(("fsdp", "ctx")),
            P(("fsdp", "ctx"), None),
            P(("fsdp", "ctx")),
            P(("fsdp", "ctx"), None),
            P(("fsdp", "ctx")),
            P(("fsdp", "ctx"), None),
            P(("fsdp", "ctx")),
        ),
        check_vma=False,
    )
```
